32 devices in a mesh: dp: 8 (over z, y), filt: 4 (over x, core).
Axes of the slice: x: 2, y: 2, z: 4, core: 2. Of those that a mesh axis runs over, the one named last changes fastest.
Arguments:
- chars: int32 [8, 512, 50], P('dp'), may hold values from 0 to 261
- lengths: int32 [8], P('dp'), may hold values from 385 to 512, as said below
- char_table: bfloat16 [262, 16], replicated, may hold values from -6 to 6
- conv_weight: bfloat16 [112, 2048], P(None, 'filt'), may hold values from -0.5 to 0.5
- conv_bias: bfloat16 [2048], P('filt'), may hold values from -3 to 3
- highway_weight: bfloat16 [1, 2048, 4096], P(None, 'dp'), may hold values from -0.125 to 0.125
- highway_bias: bfloat16 [1, 4096], P(None, 'dp'), may hold values from -3 to 3
- proj_weight: bfloat16 [2048, 768], P('dp'), may hold values from -0.125 to 0.125
- proj_bias: bfloat16 [768], P('dp'), may hold values from -3 to 3
- position: bfloat16 [512, 768], P('filt'), may hold values from -3 to 3
- norm_gain: bfloat16 [3, 768], P(None, 'dp'), may hold values from 0.099609375 to 1.8984375
- norm_bias: bfloat16 [3, 768], P(None, 'dp'), may hold values from -2 to 2
- query_key_value_weight: bfloat16 [768, 2304], P('dp'), may hold values from -0.21875 to 0.21875
- attention_output_weight: bfloat16 [768, 768], P('dp'), may hold values from -0.875 to 0.875
- feedforward_input_weight: bfloat16 [768, 3072], P('dp'), may hold values from -0.21875 to 0.21875
- feedforward_input_bias: bfloat16 [3072], P('dp'), may hold values from -3 to 3
- feedforward_output_weight: bfloat16 [3072, 768], P('dp'), may hold values from -0.109375 to 0.109375
- cotangent: bfloat16 [8, 512, 768], P('dp', 'filt'), may hold values from -6 to 6
Outputs:
- encoded: bfloat16 [8, 512, 768], P('dp', 'filt')
- grad_char_table: float32 [262, 16], replicated
- grad_conv_weight: float32 [112, 2048], P(None, 'filt')
- grad_conv_bias: float32 [2048], P('filt')
- grad_highway_weight: float32 [1, 2048, 4096], P(None, 'dp')
- grad_highway_bias: float32 [1, 4096], P(None, 'dp')
- grad_proj_weight: float32 [2048, 768], P('dp')
- grad_proj_bias: float32 [768], P('dp')
- grad_position: float32 [512, 768], P('filt')
- grad_norm_gain: float32 [3, 768], P(None, 'dp')
- grad_norm_bias: float32 [3, 768], P(None, 'dp')
- grad_qkv_weight: float32 [768, 2304], P('dp')
- grad_out_weight: float32 [768, 768], P('dp')
- grad_ffn_in_weight: float32 [768, 3072], P('dp')
- grad_ffn_in_bias: float32 [3072], P('dp')
- grad_ffn_out_weight: float32 [3072, 768], P('dp')
The draws below stay inside these ranges and needn't reach their ends.
Inputs may be any that keep to these rules, and one draw needn't show every extreme that they name: `lengths`: every sequence fills more than three quarters of its 512 slots, and some sequence fills all of them.
All inputs are finite; a program needn't handle non-finite values.
Results may differ from the reference program's by a relative error of at most 0.017.
Values may be sent and summed in bfloat16 or wider, within the bound.
A program may use at most 256 MiB of HBM per device.

```python
import jax
import jax.numpy as jnp
from jax import lax

CV = 262
CD = 16
CL = 50
KW = 7
NF = 2048
D = 768
H = 12
HD = 64
FF = 3072
HW = 1
L = 512
SEQS = 8


def draw_lengths(key, part):
    first_key, second_key = jax.random.split(jax.random.fold_in(key, 17))
    drawn = jax.random.randint(first_key, (SEQS,), L - L // 4 + 1, L + 1)
    picked = jax.random.randint(second_key, (), 0, SEQS)
    return jnp.where(jnp.arange(SEQS) == picked, L, drawn).astype(jnp.int32)


def plant(values, stream_key, least, top_value):
    shape = values.shape
    index_at = [jax.random.randint(jax.random.fold_in(stream_key, axis), (), 0, shape[axis]) for axis in range(len(shape))]
    values = values.at[tuple(index_at)].set(least)
    longest = shape.index(max(shape))
    index_at[longest] = (index_at[longest] + 1) % shape[longest]
    return values.at[tuple(index_at)].set(top_value)


def shard_levels(own_key, extent, cuts, least, largest):
    factor_of = 1.0
    for dim, shards_of in cuts:
        heights = jax.random.uniform(jax.random.fold_in(jax.random.fold_in(own_key, 6), dim), (shards_of,), jnp.float32, least / len(cuts), largest / len(cuts))
        factor_of = factor_of * jnp.repeat(jnp.exp(heights), extent[dim] // shards_of).reshape((-1,) + (1,) * (len(extent) - 1 - dim))
    return factor_of


def noise(rng, dims, scale, limit, cuts=(), kind=jnp.bfloat16):
    values = jax.random.normal(rng, dims, jnp.float32) * scale
    if len(cuts) > 0:
        values = shard_levels(rng, dims, cuts, -0.22, 0.18) * values
    return jnp.clip(values, min=-limit, max=limit).astype(kind)


def setup_inputs(seed: int = 0) -> dict:
    seeds = jax.random.split(jax.random.key(seed), 19)
    return {
        "chars": plant(jax.random.randint(seeds[0], (SEQS, L, CL), 0, CV), jax.random.fold_in(seeds[0], 1), 0, CV - 1).astype(jnp.int32),
        "lengths": draw_lengths(jax.random.fold_in(seeds[18], 71), 0),
        "char_table": noise(seeds[2], (CV, CD), 1.0, 6.0),
        "conv_weight": noise(seeds[3], (KW * CD, NF), (KW * CD) ** -0.5, 0.5, ((1, 4),)),
        "conv_bias": noise(seeds[4], (NF,), 0.5, 3.0, ((0, 4),)),
        "highway_weight": noise(seeds[5], (HW, NF, 2 * NF), NF ** -0.5, 0.125, ((1, 8),)),
        "highway_bias": noise(seeds[6], (HW, 2 * NF), 0.5, 3.0, ((1, 8),)),
        "proj_weight": noise(seeds[7], (NF, D), NF ** -0.5, 0.125, ((0, 8),)),
        "proj_bias": noise(seeds[8], (D,), 0.5, 3.0, ((0, 8),)),
        "position": noise(seeds[9], (L, D), 0.5, 3.0, ((0, 4),)),
        "norm_gain": jnp.clip(1.0 + 0.18 * jax.random.normal(seeds[10], (3, D), jnp.float32), 0.099609375, 1.8984375).astype(jnp.bfloat16),
        "norm_bias": noise(seeds[11], (3, D), 0.3, 2.0, ((1, 8),)),
        "query_key_value_weight": noise(seeds[12], (D, 3 * D), D ** -0.5, 0.21875, ((0, 8),)),
        "attention_output_weight": noise(seeds[13], (D, D), (D // 16) ** -0.5, 0.875, ((0, 8),)),
        "feedforward_input_weight": noise(seeds[14], (D, FF), D ** -0.5, 0.21875, ((0, 8),)),
        "feedforward_input_bias": noise(seeds[15], (FF,), 0.5, 3.0, ((0, 8),)),
        "feedforward_output_weight": noise(seeds[16], (FF, D), FF ** -0.5, 0.109375, ((0, 8),)),
        "cotangent": noise(seeds[17], (SEQS, L, D), 1.0, 6.0, ((0, 8), (1, 4))),
    }


eps_norm = 1e-12
highest_precision = lax.Precision.HIGHEST

@jax.custom_vjp
def lowered_precision(v):
    return lax.optimization_barrier(v.astype(jnp.bfloat16)).astype(jnp.float32)

@jax.custom_vjp
def lowered_backward(v):
    return v

def low_keep(v):
    return (lowered_precision(v), None)

def low_pass(kept, grad):
    return (grad,)

def back_keep(v):
    return (v, None)

def back_low(kept, grad):
    return (lowered_precision(grad),)
lowered_precision.defvjp(low_keep, low_pass)
lowered_backward.defvjp(back_keep, back_low)

def exact_gaussian_activation(values):
    return jax.nn.gelu(values, approximate=False)

def layer_norm(values, scale, offset):
    center = values - lax.optimization_barrier(jnp.mean(values, axis=-1, keepdims=True))
    spread = lax.optimization_barrier(jnp.mean(center * center, axis=-1, keepdims=True))
    return center * lax.rsqrt(spread + eps_norm) * scale + offset

def channel_widths(channels):
    widths = jnp.ones_like(channels)
    for power in range(6):
        widths = widths + (channels >= NF * 2 ** power // 64).astype(jnp.int32)
    return widths

def forward(params, char_ids, seq_lengths):
    char_table, conv_weight, conv_bias, highway_weight, highway_bias, proj_weight, proj_bias, position, norm_gain, norm_bias, query_key_value_weight, attention_output_weight, feedforward_input_weight, feedforward_input_bias, feedforward_output_weight = params
    widths = channel_widths(jnp.arange(NF, dtype=jnp.int32))
    tap_index = jnp.arange(KW * CD, dtype=jnp.int32) // CD
    masked_weight = jnp.where(tap_index[:, None] < widths[None, :], conv_weight, 0.0)
    valid = jnp.arange(CL, dtype=jnp.int32)[:, None] <= CL - widths[None, :]
    counts = (CL - widths + 1).astype(jnp.float32)

    def embed(word_ids):
        embedded = char_table[word_ids]
        padded = jnp.pad(embedded, ((0, 0), (0, KW - 1), (0, 0)))
        patches = jnp.concatenate([padded[:, shift_tap:shift_tap + CL, :] for shift_tap in range(KW)], axis=2)
        grid = jnp.einsum('wpk,kc->wpc', patches, masked_weight, precision=highest_precision) + conv_bias
        grid = lowered_backward(grid)
        pooled = jax.nn.logsumexp(jnp.where(valid, grid, -1e+30), axis=1) - jnp.log(counts)
        return lowered_backward(lowered_precision(exact_gaussian_activation(pooled)))
    acts = lax.map(jax.checkpoint(embed), char_ids)
    seqs = char_ids.shape[0]
    hidden = acts.reshape(seqs * L, NF)
    for layer in range(HW):
        gates = lowered_backward(jnp.dot(lowered_precision(hidden), highway_weight[layer], precision=highest_precision) + highway_bias[layer])
        carry_gate = jax.nn.sigmoid(gates[:, NF:])
        hidden = carry_gate * hidden + (1.0 - carry_gate) * exact_gaussian_activation(gates[:, :NF])
    projected = lowered_backward(jnp.dot(lowered_precision(hidden), proj_weight, precision=highest_precision) + proj_bias)
    summed = projected.reshape(seqs, L, D) + position
    first_operand = layer_norm(summed, norm_gain[0], norm_bias[0])
    packed_projection = lowered_backward(lowered_precision(jnp.einsum('zhx,xn->zhn', lowered_precision(first_operand), query_key_value_weight, precision=highest_precision)))
    queries = packed_projection[..., :D].reshape(seqs, L, H, HD)
    keys = packed_projection[..., D:2 * D].reshape(seqs, L, H, HD)
    values = packed_projection[..., 2 * D:].reshape(seqs, L, H, HD)
    scores = jnp.einsum('sqhd,skhd->shqk', queries, keys, precision=highest_precision) * HD ** (-0.5)
    key_ok = jnp.arange(L, dtype=jnp.int32)[None, :] < seq_lengths[:, None]
    scores = lowered_backward(jnp.where(key_ok[:, None, None, :], scores, -1e+30))
    probs = lowered_precision(jax.nn.softmax(scores, axis=-1))
    attention_result = lowered_backward(lowered_precision(jnp.einsum('shqk,skhd->sqhd', probs, values, precision=highest_precision))).reshape(seqs, L, D)
    mixed_hidden = lowered_backward(jnp.einsum('zhx,xn->zhn', attention_result, attention_output_weight, precision=highest_precision))
    second_operand = layer_norm(first_operand + mixed_hidden, norm_gain[1], norm_bias[1])
    inner_activation = lowered_backward(jnp.einsum('cnv,vu->cnu', lowered_precision(second_operand), feedforward_input_weight, precision=highest_precision) + feedforward_input_bias)
    outer_projection = lowered_backward(jnp.einsum('gzw,wa->gza', lowered_precision(exact_gaussian_activation(inner_activation)), feedforward_output_weight, precision=highest_precision))
    return layer_norm(second_operand + outer_projection, norm_gain[2], norm_bias[2])

def reference(chars, lengths, char_table, conv_weight, conv_bias, highway_weight, highway_bias, proj_weight, proj_bias, position, norm_gain, norm_bias, query_key_value_weight, attention_output_weight, feedforward_input_weight, feedforward_input_bias, feedforward_output_weight, cotangent):
    params = tuple((item.astype(jnp.float32) for item in (char_table, conv_weight, conv_bias, highway_weight, highway_bias, proj_weight, proj_bias, position, norm_gain, norm_bias, query_key_value_weight, attention_output_weight, feedforward_input_weight, feedforward_input_bias, feedforward_output_weight)))
    stride = 8 if SEQS % 8 == 0 else 1
    blocks = SEQS // stride
    inputs = (chars.reshape(blocks, stride, L, CL), lengths.reshape(blocks, stride), cotangent.reshape(blocks, stride, L, D))

    def one_block(totals, item):
        block_chars, block_lengths, block_cot = item
        result, pull = jax.vjp(lambda *weights: forward(weights, block_chars, block_lengths), *params)
        grads = pull(block_cot.astype(jnp.float32))
        return (tuple((left + right for left, right in zip(totals, grads))), result.astype(jnp.bfloat16))
    totals, encoded = lax.scan(one_block, tuple((jnp.zeros_like(item) for item in params)), inputs)
    return (encoded.reshape(SEQS, L, D), totals[0], totals[1], totals[2], totals[3], totals[4], totals[5], totals[6], totals[7], totals[8], totals[9], totals[10], totals[11], totals[12], totals[13], totals[14])
```

```python
from functools import reduce
import math

import jax
import jax.numpy as jnp
from jax import lax
from jax.sharding import PartitionSpec as P

KW = 7
NF = 2048
HD = 64


eps_norm = 1e-12


def exact_gaussian_activation(values):
    return jax.nn.gelu(values, approximate=False)


def gelu_back(values, upstream):
    return jax.vjp(exact_gaussian_activation, values)[1](upstream)[0]


def layer_norm(values, scale, offset):
    center = values - jnp.mean(values, axis=-1, keepdims=True)
    spread = jnp.mean(center * center, axis=-1, keepdims=True)
    return center * lax.rsqrt(spread + eps_norm) * scale + offset


def channel_widths(channels):
    widths = jnp.ones_like(channels)
    for power in range(6):
        widths = widths + (channels >= NF * 2**power // 64).astype(jnp.int32)
    return widths


def highway_mix(hidden, gates):
    width = hidden.shape[1]
    carry_gate = jax.nn.sigmoid(gates[:, width:])
    return carry_gate * hidden + (1.0 - carry_gate) * exact_gaussian_activation(gates[:, :width])


def char_grid(word_ids, char_table, masked_weight, bias_row, valid):
    vocab = jnp.arange(char_table.shape[0], dtype=jnp.int32)
    onehot = (word_ids[..., None] == vocab).astype(jnp.bfloat16)
    embedded = jnp.einsum(
        "wpv,vd->wpd", onehot, char_table, preferred_element_type=jnp.float32
    ).astype(jnp.bfloat16)
    letters = word_ids.shape[1]
    padded = jnp.pad(embedded, ((0, 0), (0, KW - 1), (0, 0)))
    patches = jnp.concatenate(
        [padded[:, shift_tap : shift_tap + letters, :] for shift_tap in range(KW)], axis=2
    )
    grid = (
        jnp.einsum("wpk,kc->wpc", patches, masked_weight, preferred_element_type=jnp.float32)
        + bias_row
    )
    grid = jnp.where(valid, grid, -1e30)
    row_top = jnp.max(grid, axis=1, keepdims=True)
    log_total = row_top[:, 0, :] + jnp.log(jnp.sum(jnp.exp(grid - row_top), axis=1))
    return (onehot, patches, grid, log_total)


def low_dot(left, right):
    return jnp.dot(left, right, preferred_element_type=jnp.float32)


def dot_tn(left, right):
    return lax.dot_general(
        left, right, (((0,), (0,)), ((), ())), preferred_element_type=jnp.float32
    )


def dot_nt(left, right):
    return lax.dot_general(
        left, right, (((1,), (1,)), ((), ())), preferred_element_type=jnp.float32
    )


def per_device(
    chars,
    lengths,
    char_table,
    conv_weight,
    conv_bias,
    highway_weight,
    highway_bias,
    proj_weight,
    proj_bias,
    position,
    norm_gain,
    norm_bias,
    query_key_value_weight,
    attention_output_weight,
    feedforward_input_weight,
    feedforward_input_bias,
    feedforward_output_weight,
    cotangent,
):
    parts = lax.axis_size("filt")
    slices = lax.axis_size("dp")
    part = lax.axis_index("filt")
    slot = lax.axis_index("dp")
    seqs, quarter, dmodel = cotangent.shape
    full_len = chars.shape[1]
    letters = chars.shape[2]
    words = seqs * full_len
    tokens = seqs * quarter
    filters = conv_weight.shape[1]
    heads = dmodel // HD // parts
    width = heads * HD
    hidden_units = feedforward_output_weight.shape[0] * slices
    unit_rows = feedforward_output_weight.shape[0] // parts
    units = hidden_units // parts

    def own_columns(array, blocks):
        rows = array.shape[0]
        split = array.reshape(rows, blocks, parts, -1)
        return lax.dynamic_index_in_dim(split, part, 2, keepdims=False).reshape(rows, -1)

    def gather_rows(array):
        return lax.all_gather(array, "dp", axis=0, tiled=True)

    def to_rows(array):
        return lax.all_to_all(array, "filt", split_axis=0, concat_axis=1, tiled=True)

    def to_columns(array):
        return lax.all_to_all(array, "filt", split_axis=1, concat_axis=0, tiled=True)

    highway_own = gather_rows(own_columns(highway_weight[0], 2))
    small = jnp.concatenate(
        [
            highway_bias.reshape(-1),
            proj_bias,
            norm_gain.reshape(-1),
            norm_bias.reshape(-1),
            feedforward_input_bias,
        ]
    )
    small = lax.all_gather(small, "dp", axis=0, tiled=False)
    proj_own = to_rows(gather_rows(own_columns(proj_weight, 1)))
    qkv_own = gather_rows(own_columns(query_key_value_weight, 3))
    out_own = to_rows(gather_rows(own_columns(attention_output_weight, 1)))
    inner_own = gather_rows(own_columns(feedforward_input_weight, slices))
    outer_own = gather_rows(
        lax.dynamic_slice_in_dim(feedforward_output_weight, part * unit_rows, unit_rows, 0)
    )
    small = small.astype(jnp.float32)
    hb, pb, nd = highway_bias.shape[1], proj_bias.shape[0], norm_gain.shape[1]
    ib = feedforward_input_bias.shape[0]
    cuts = [hb, hb + pb, hb + pb + 3 * nd, hb + pb + 6 * nd]
    highway_b, proj_b, gain, shift, inner_b = jnp.split(small, cuts, axis=1)
    highway_b_own = own_columns(highway_b.reshape(1, -1), 2)
    proj_b = proj_b.reshape(-1)
    gain = gain.reshape(slices, 3, nd).transpose(1, 0, 2).reshape(3, dmodel)
    shift = shift.reshape(slices, 3, nd).transpose(1, 0, 2).reshape(3, dmodel)
    inner_b_own = own_columns(inner_b.reshape(1, -1), slices)

    def gather_tokens(array):
        array = array.reshape(seqs, quarter, -1)
        return lax.all_gather(array, "filt", axis=1, tiled=True).reshape(words, -1)

    def scatter_tokens(array):
        array = array.astype(jnp.bfloat16).reshape(seqs, full_len, -1)
        array = lax.psum_scatter(array, "filt", scatter_dimension=1, tiled=True)
        return array.reshape(tokens, -1).astype(jnp.float32)

    offset = part * filters
    word_ids = chars.reshape(words, letters)
    channels = offset + jnp.arange(filters, dtype=jnp.int32)
    widths = channel_widths(channels)
    tap_index = jnp.arange(conv_weight.shape[0], dtype=jnp.int32) // char_table.shape[1]
    tap_keep = tap_index[:, None] < widths[None, :]
    masked_weight = jnp.where(tap_keep, conv_weight, 0)
    valid = jnp.arange(letters, dtype=jnp.int32)[:, None] <= letters - widths[None, :]
    counts = (letters - widths + 1).astype(jnp.float32)
    bias_row = conv_bias.astype(jnp.float32)
    block_rows = math.gcd(words, 128)
    block_count = words // block_rows
    id_blocks = word_ids.reshape(block_count, block_rows, letters)

    def forward_block(carried, block_ids):
        onehot, patches, grid, log_total = char_grid(
            block_ids, char_table, masked_weight, bias_row, valid
        )
        return (
            carried,
            exact_gaussian_activation(log_total - jnp.log(counts)).astype(jnp.bfloat16),
        )

    unused, acts = lax.scan(forward_block, jnp.zeros((), jnp.float32), id_blocks)
    acts = acts.reshape(words, filters)
    features = lax.all_gather(acts, "filt", axis=1, tiled=True)
    gates = low_dot(features, highway_own) + highway_b_own
    feature_own = acts.astype(jnp.float32)
    hidden_low = highway_mix(feature_own, gates).astype(jnp.bfloat16)
    projected = scatter_tokens(low_dot(hidden_low, proj_own)) + proj_b
    summed = (projected.reshape(seqs, quarter, dmodel) + position.astype(jnp.float32)).reshape(
        tokens, dmodel
    )
    first_operand, norm_zero_pull = jax.vjp(layer_norm, summed, gain[0], shift[0])
    first_low = gather_tokens(first_operand.astype(jnp.bfloat16))
    packed = low_dot(first_low, qkv_own).astype(jnp.bfloat16)
    queries, keys, values = (
        packed[:, block * width : (block + 1) * width].reshape(seqs, full_len, heads, HD)
        for block in range(3)
    )
    key_ok = jnp.arange(full_len, dtype=jnp.int32)[None, :] < lengths[:, None]
    scale = HD ** (-0.5)
    scores = (
        jnp.einsum("sqhd,skhd->shqk", queries, keys, preferred_element_type=jnp.float32) * scale
    )
    scores = jnp.where(key_ok[:, None, None, :], scores, -1e30)
    row_top = jnp.max(scores, axis=-1, keepdims=True)
    log_total = row_top + jnp.log(jnp.sum(jnp.exp(scores - row_top), axis=-1, keepdims=True))
    probs = jnp.exp(scores - log_total)
    probs_low = probs.astype(jnp.bfloat16)
    attended = (
        jnp.einsum("shqk,skhd->sqhd", probs_low, values, preferred_element_type=jnp.float32)
        .astype(jnp.bfloat16)
        .reshape(words, width)
    )
    mixed = scatter_tokens(low_dot(attended, out_own))
    second_operand, norm_one_pull = jax.vjp(layer_norm, first_operand + mixed, gain[1], shift[1])
    second_low = gather_tokens(second_operand.astype(jnp.bfloat16))
    inner = low_dot(second_low, inner_own) + inner_b_own
    active = exact_gaussian_activation(inner).astype(jnp.bfloat16)
    outer = scatter_tokens(low_dot(active, outer_own))
    top_out, norm_two_pull = jax.vjp(layer_norm, second_operand + outer, gain[2], shift[2])
    encoded = top_out.astype(jnp.bfloat16).reshape(seqs, quarter, dmodel)
    upstream = cotangent.reshape(tokens, dmodel).astype(jnp.float32)
    d_res_two, d_gain_two, d_shift_two = norm_two_pull(upstream)
    d_outer = gather_tokens(d_res_two.astype(jnp.bfloat16))

    def reduce_rows(array):
        return lax.psum_scatter(
            array.astype(jnp.bfloat16), "dp", scatter_dimension=0, tiled=True
        )

    grad_outer = reduce_rows(dot_tn(active, d_outer))
    d_active = dot_nt(d_outer, outer_own)
    d_inner = gelu_back(inner, d_active).astype(jnp.bfloat16)
    grad_inner = reduce_rows(dot_tn(second_low, d_inner))
    grad_inner_b = jnp.sum(d_inner.astype(jnp.float32), axis=0)
    d_second = d_res_two + scatter_tokens(dot_nt(d_inner, inner_own))
    d_res_one, d_gain_one, d_shift_one = norm_one_pull(d_second)
    d_mixed = gather_tokens(d_res_one.astype(jnp.bfloat16))
    grad_out = reduce_rows(to_columns(dot_tn(attended, d_mixed).astype(jnp.bfloat16)))
    d_attended = dot_nt(d_mixed, out_own).astype(jnp.bfloat16)
    d_attended = d_attended.reshape(seqs, full_len, heads, HD)
    d_values = jnp.einsum(
        "shqk,sqhd->skhd", probs_low, d_attended, preferred_element_type=jnp.float32
    )
    d_probs = jnp.einsum(
        "sqhd,skhd->shqk", d_attended, values, preferred_element_type=jnp.float32
    )
    row_inner = jnp.sum(d_probs * probs, axis=-1, keepdims=True)
    d_scores = (probs * (d_probs - row_inner)).astype(jnp.bfloat16)
    d_queries = (
        jnp.einsum("shqk,skhd->sqhd", d_scores, keys, preferred_element_type=jnp.float32) * scale
    )
    d_keys = (
        jnp.einsum("shqk,sqhd->skhd", d_scores, queries, preferred_element_type=jnp.float32) * scale
    )
    d_packed = jnp.concatenate(
        [item.reshape(words, width) for item in (d_queries, d_keys, d_values)], axis=1
    ).astype(jnp.bfloat16)
    grad_qkv = reduce_rows(dot_tn(first_low, d_packed))
    d_first = d_res_one + scatter_tokens(dot_nt(d_packed, qkv_own))
    d_summed, d_gain_zero, d_shift_zero = norm_zero_pull(d_first)
    grad_pos = jnp.sum(d_summed.reshape(seqs, quarter, dmodel), axis=0)
    d_projected_own = d_summed.astype(jnp.bfloat16)
    d_projected = gather_tokens(d_projected_own)
    grad_proj_b = jnp.sum(d_projected_own.astype(jnp.float32), axis=0)
    grad_proj = reduce_rows(to_columns(dot_tn(hidden_low, d_projected).astype(jnp.bfloat16)))
    d_hidden = dot_nt(d_projected, proj_own)
    d_in, d_gates = jax.vjp(highway_mix, feature_own, gates)[1](d_hidden)
    d_gates = d_gates.astype(jnp.bfloat16)
    grad_highway = reduce_rows(dot_tn(features, d_gates))
    grad_highway_b = jnp.sum(d_gates.astype(jnp.float32), axis=0)
    d_mixed_in = lax.psum_scatter(
        dot_nt(d_gates, highway_own).astype(jnp.bfloat16), "filt", scatter_dimension=1, tiled=True
    )
    d_features = (d_in + d_mixed_in.astype(jnp.float32)).astype(jnp.bfloat16)
    d_blocks = d_features.reshape(block_count, block_rows, -1)
    depth = char_table.shape[1]

    def backward_block(totals, item):
        block_ids, block_grad = item
        onehot, patches, grid, log_total = char_grid(
            block_ids, char_table, masked_weight, bias_row, valid
        )
        d_pooled = gelu_back(log_total - jnp.log(counts), block_grad.astype(jnp.float32))
        position_weights = jnp.exp(grid - log_total[:, None, :])
        d_grid = (position_weights * d_pooled[:, None, :]).astype(jnp.bfloat16)
        grad_weight = totals[0] + jnp.einsum(
            "wpk,wpc->kc", patches, d_grid, preferred_element_type=jnp.float32
        )
        grad_bias = totals[1] + jnp.sum(d_grid.astype(jnp.float32), axis=(0, 1))
        d_patch = jnp.einsum(
            "wpc,kc->wpk", d_grid, masked_weight, preferred_element_type=jnp.float32
        )
        pieces = [
            jnp.pad(
                d_patch[:, :, shift_tap * depth : (shift_tap + 1) * depth],
                ((0, 0), (shift_tap, KW - 1 - shift_tap), (0, 0)),
            )
            for shift_tap in range(KW)
        ]
        d_embedded = reduce(jnp.add, pieces)[:, :letters, :]
        grad_table = totals[2] + jnp.einsum(
            "wpv,wpd->vd", onehot.astype(jnp.float32), d_embedded, precision=lax.Precision.HIGHEST
        )
        return ((grad_weight, grad_bias, grad_table), None)

    start = (
        jnp.zeros(masked_weight.shape, jnp.float32),
        jnp.zeros(bias_row.shape, jnp.float32),
        jnp.zeros(char_table.shape, jnp.float32),
    )
    char_totals, unused_rows = lax.scan(backward_block, start, (id_blocks, d_blocks))
    conv_grad_w = jnp.where(tap_keep, char_totals[0], 0.0)
    conv_grad_w, conv_grad_b, grad_pos = lax.psum((conv_grad_w, char_totals[1], grad_pos), "dp")

    def place_columns(own, blocks):
        piece = own.reshape(blocks, 1, -1)
        whole = jnp.zeros((blocks, parts, piece.shape[2]), own.dtype)
        return lax.dynamic_update_slice_in_dim(whole, piece, part, 1).reshape(-1)

    d_gain = jnp.stack([d_gain_zero, d_gain_one, d_gain_two])
    d_shift = jnp.stack([d_shift_zero, d_shift_one, d_shift_two])
    pieces = [
        place_columns(grad_highway_b, 2).reshape(slices, -1),
        grad_proj_b.reshape(slices, -1),
        d_gain.reshape(3, slices, nd).transpose(1, 0, 2).reshape(slices, -1),
        d_shift.reshape(3, slices, nd).transpose(1, 0, 2).reshape(slices, -1),
        place_columns(grad_inner_b, slices).reshape(slices, -1),
    ]
    rows = jnp.concatenate(pieces, axis=1)
    row_size = rows.shape[1]
    table_size = char_totals[2].size
    sums = lax.psum(
        jnp.concatenate([rows.reshape(-1), char_totals[2].reshape(-1)]), ("dp", "filt")
    )
    g_table = sums[rows.size :].reshape(char_totals[2].shape)
    own = lax.dynamic_slice_in_dim(sums, slot * row_size, row_size, 0)
    g_highway_b, g_proj_b, g_gain, g_shift, g_inner_b = jnp.split(own, cuts)

    def join_columns(array, blocks):
        rows_here = array.shape[0]
        whole = lax.all_gather(array, "filt", axis=0, tiled=False)
        whole = whole.reshape(parts, rows_here, blocks, -1).transpose(1, 2, 0, 3)
        return whole.reshape(rows_here, -1).astype(jnp.float32)

    g_outer = lax.all_gather(grad_outer, "filt", axis=0, tiled=True).astype(jnp.float32)
    g_inner = join_columns(grad_inner, slices)
    g_out = join_columns(grad_out, 1)
    g_qkv = join_columns(grad_qkv, 3)
    g_proj = join_columns(grad_proj, 1)
    g_highway = join_columns(grad_highway, 2)
    return (
        encoded,
        g_table,
        conv_grad_w,
        conv_grad_b,
        g_highway[None],
        g_highway_b[None],
        g_proj,
        g_proj_b,
        grad_pos,
        g_gain.reshape(3, nd),
        g_shift.reshape(3, nd),
        g_qkv,
        g_out,
        g_inner,
        g_inner_b,
        g_outer,
    )


def solution(mesh):
    return jax.shard_map(
        per_device,
        mesh=mesh,
        in_specs=(
            P("dp", None, None),
            P("dp"),
            P(),
            P(None, "filt"),
            P("filt"),
            P(None, "dp", None),
            P(None, "dp"),
            P("dp", None),
            P("dp"),
            P("filt", None),
            P(None, "dp"),
            P(None, "dp"),
            P("dp", None),
            P("dp", None),
            P("dp", None),
            P("dp"),
            P("dp", None),
            P("dp", "filt", None),
        ),
        out_specs=(
            P("dp", "filt", None),
            P(),
            P(None, "filt"),
            P("filt"),
            P(None, "dp", None),
            P(None, "dp"),
            P("dp", None),
            P("dp"),
            P("filt", None),
            P(None, "dp"),
            P(None, "dp"),
            P("dp", None),
            P("dp", None),
            P("dp", None),
            P("dp"),
            P("dp", None),
        ),
        check_vma=False,
    )
```

```python
import functools

import jax
import jax.numpy as jnp
from jax import lax
from jax.experimental import pallas as pl
from jax.experimental.pallas import tpu as pltpu
from jax.sharding import PartitionSpec as P

KW = 7
NF = 2048
HD = 64
EPS = 1e-12
ROOT_HALF = 0.7071067811865476
DENSITY = 0.3989422804014327

def nt_dot(left, right):
    return lax.dot_general(left, right, (((1,), (1,)), ((), ())), preferred_element_type=jnp.float32)

def nn_dot(left, right):
    return jnp.dot(left, right, preferred_element_type=jnp.float32)

def normal_cdf(values):
    return 0.5 * (1.0 + lax.erf(values * ROOT_HALF))

def char_parts(chars_ref, position, block):
    ids = chars_ref[pl.ds(position, 1), :]
    low = ids & 127
    group = ids >> 7
    onehot = (lax.broadcasted_iota(jnp.int32, (128, block), 0) == low)
    onehot = jnp.where(onehot, 1.0, 0.0).astype(jnp.bfloat16)
    return onehot, group

def conv_forward(letters, depth, chars_ref, table_ref, weight_ref, limit_ref, count_ref,
                 acts_ref, lse_ref, embed_ref, patch_ref, grid_ref):
    block = chars_ref.shape[1]
    filters = weight_ref.shape[0]
    groups = table_ref.shape[0] // depth
    lead = KW - 1
    rows = KW * depth

    @pl.when(pl.program_id(0) == 0)
    def _():
        patch_ref[:, :rows, :] = jnp.zeros((patch_ref.shape[0], rows, block), jnp.bfloat16)
        ones = lax.broadcasted_iota(jnp.int32, (128 - rows, block), 0) == 0
        tail = jnp.where(ones, 1.0, 0.0).astype(jnp.bfloat16)
        patch_ref[:, rows:, :] = jnp.broadcast_to(tail[None], (patch_ref.shape[0],) + tail.shape)

    def embed(position, carry):
        onehot, group = char_parts(chars_ref, position, block)
        looked = nn_dot(table_ref[...], onehot)
        row = looked[:depth]
        for index in range(1, groups):
            row = jnp.where(group == index, looked[index * depth : (index + 1) * depth], row)
        row = row.astype(jnp.bfloat16)
        embed_ref[pl.ds(pl.multiple_of(position * depth, depth), depth), :] = row
        for tap in range(KW):
            patch_ref[position + lead - tap, tap * depth : (tap + 1) * depth, :] = row
        return carry

    lax.fori_loop(0, letters, embed, 0, unroll=5)
    chunk = grid_ref.shape[1]
    always = letters - KW + 1
    for start in range(0, filters, chunk):
        weight = weight_ref[start : start + chunk, :]
        limit = limit_ref[start : start + chunk, :]

        def product(position, top):
            grid = nn_dot(weight, patch_ref[position + lead])
            grid_ref[position] = grid
            return jnp.maximum(top, grid)

        top = lax.fori_loop(0, always, product, jnp.full((chunk, block), -1e30, jnp.float32), unroll=11)
        for position in range(always, letters):
            grid = nn_dot(weight, patch_ref[position + lead])
            grid = jnp.where(limit >= position, grid, -1e30)
            grid_ref[position] = grid
            top = jnp.maximum(top, grid)

        def total(position, acc):
            return acc + jnp.exp(grid_ref[position] - top)

        acc = lax.fori_loop(0, letters, total, jnp.zeros((chunk, block), jnp.float32), unroll=10)
        lse = top + jnp.log(acc)
        lse_ref[start : start + chunk, :] = lse
        pooled = lse - count_ref[start : start + chunk, :]
        acts_ref[:, start : start + chunk] = (pooled * normal_cdf(pooled)).astype(jnp.bfloat16).T

def conv_backward(letters, depth, chars_ref, embed_ref, lse_ref, up_ref, weight_ref, back_ref,
                  limit_ref, count_ref, wgrad_ref, tgrad_ref, patch_ref, down_ref, pull_ref):
    block = chars_ref.shape[1]
    filters = weight_ref.shape[0]
    lead = KW - 1
    rows = KW * depth
    groups = tgrad_ref.shape[0] // (2 * depth)
    step = pl.program_id(0)

    @pl.when(step == 0)
    def _():
        wgrad_ref[...] = jnp.zeros(wgrad_ref.shape, jnp.float32)
        tgrad_ref[...] = jnp.zeros(tgrad_ref.shape, jnp.float32)
        patch_ref[letters * depth :, :] = jnp.zeros((patch_ref.shape[0] - letters * depth, block), jnp.bfloat16)

    patch_ref[: letters * depth, :] = embed_ref[...]
    down_ref[...] = jnp.zeros(down_ref.shape, jnp.float32)
    pooled = lse_ref[...] - count_ref[...]
    slope = normal_cdf(pooled) + pooled * (DENSITY * jnp.exp(-0.5 * pooled * pooled))
    pull_ref[...] = slope * up_ref[...].T.astype(jnp.float32)
    ones = jnp.where(lax.broadcasted_iota(jnp.int32, (128 - rows, block), 0) == 0, 1.0, 0.0).astype(jnp.bfloat16)

    def one(position, masked):
        start = position * depth
        if not isinstance(position, int):
            start = pl.multiple_of(start, depth)
        patch = jnp.concatenate([patch_ref[pl.ds(start, rows), :], ones], axis=0)
        grid = nn_dot(weight_ref[...], patch)
        spread = jnp.exp(grid - lse_ref[...]) * pull_ref[...]
        if masked:
            spread = jnp.where(limit_ref[...] >= position, spread, 0.0)
        spread = spread.astype(jnp.bfloat16)
        down = nn_dot(back_ref[...], spread)
        down_ref[pl.ds(start, rows), :] += down[:rows]
        wgrad_ref[...] += nt_dot(spread, patch)

    always = letters - KW + 1

    def body(position, carry):
        one(position, False)
        return carry

    lax.fori_loop(0, always, body, 0, unroll=2)
    for position in range(always, letters):
        one(position, True)

    def table(position, carry):
        onehot, group = char_parts(chars_ref, position, block)
        down = down_ref[pl.ds(pl.multiple_of(position * depth, depth), depth), :]
        high = down.astype(jnp.bfloat16)
        low = (down - high.astype(jnp.float32)).astype(jnp.bfloat16)
        zero = jnp.zeros_like(high)
        parts = [jnp.where(group == index, item, zero) for item in (high, low) for index in range(groups)]
        tgrad_ref[...] += nt_dot(jnp.concatenate(parts, axis=0), onehot)
        return carry

    lax.fori_loop(0, letters, table, 0, unroll=5)

def conv_prep(chars, char_table, conv_weight, conv_bias, widths):
    letters = chars.shape[1]
    vocab, depth = char_table.shape
    groups = -(-vocab // 128)
    table = jnp.pad(char_table, ((0, groups * 128 - vocab), (0, 0)))
    table = table.reshape(groups, 128, depth).transpose(0, 2, 1).reshape(groups * depth, 128)
    tap = jnp.arange(conv_weight.shape[0], dtype=jnp.int32) // depth
    masked = jnp.where(tap[:, None] < widths[None, :], conv_weight, 0)
    back = jnp.concatenate([masked, conv_bias[None, :], jnp.zeros((127 - masked.shape[0], masked.shape[1]), masked.dtype)], axis=0)
    limit = (letters - widths)[:, None].astype(jnp.int32)
    count = jnp.log((letters - widths + 1).astype(jnp.float32))[:, None]
    ids = jnp.pad(chars, ((0, 0), (0, -letters % 8))).T
    return ids, table, back.T, back, limit, count

def conv_forward_call(ids, table, weight, limit, count, letters, depth, block=256):
    words = ids.shape[1]
    filters = weight.shape[0]
    full = lambda a: pl.BlockSpec(a.shape, lambda i: (0,) * a.ndim)
    return pl.pallas_call(
        functools.partial(conv_forward, letters, depth),
        grid=(words // block,),
        in_specs=[pl.BlockSpec((ids.shape[0], block), lambda i: (0, i)), full(table), full(weight), full(limit), full(count)],
        out_specs=[pl.BlockSpec((block, filters), lambda i: (i, 0)), pl.BlockSpec((filters, block), lambda i: (0, i)),
                   pl.BlockSpec((letters * depth, block), lambda i: (0, i))],
        out_shape=[jax.ShapeDtypeStruct((words, filters), jnp.bfloat16), jax.ShapeDtypeStruct((filters, words), jnp.float32),
                   jax.ShapeDtypeStruct((letters * depth, words), jnp.bfloat16)],
        scratch_shapes=[pltpu.VMEM((letters + KW - 1, 128, block), jnp.bfloat16), pltpu.VMEM((letters, 128, block), jnp.float32)],
        compiler_params=pltpu.CompilerParams(vmem_limit_bytes=48 << 20),
        name="conv_forward",
    )(ids, table, weight, limit, count)

def conv_backward_call(ids, embed, lse, up, weight, back, limit, count, groups, letters, depth, block=256):
    words = ids.shape[1]
    filters = weight.shape[0]
    full = lambda a: pl.BlockSpec(a.shape, lambda i: (0,) * a.ndim)
    return pl.pallas_call(
        functools.partial(conv_backward, letters, depth),
        grid=(words // block,),
        in_specs=[pl.BlockSpec((ids.shape[0], block), lambda i: (0, i)), pl.BlockSpec((letters * depth, block), lambda i: (0, i)),
                  pl.BlockSpec((filters, block), lambda i: (0, i)), pl.BlockSpec((block, filters), lambda i: (i, 0)),
                  full(weight), full(back), full(limit), full(count)],
        out_specs=[pl.BlockSpec((filters, 128), lambda i: (0, 0)), pl.BlockSpec((2 * groups * depth, 128), lambda i: (0, 0))],
        out_shape=[jax.ShapeDtypeStruct((filters, 128), jnp.float32), jax.ShapeDtypeStruct((2 * groups * depth, 128), jnp.float32)],
        scratch_shapes=[pltpu.VMEM(((letters + KW - 1) * depth, block), jnp.bfloat16), pltpu.VMEM(((letters + KW - 1) * depth, block), jnp.float32),
                        pltpu.VMEM((filters, block), jnp.float32)],
        compiler_params=pltpu.CompilerParams(vmem_limit_bytes=48 << 20),
        name="conv_backward",
    )(ids, embed, lse, up, weight, back, limit, count)


MESH = pl.DeviceIdType.MESH

def greet(peers):
    barrier = pltpu.get_barrier_semaphore()
    for peer in peers:
        pl.semaphore_signal(barrier, inc=1, device_id=peer, device_id_type=MESH)
    pl.semaphore_wait(barrier, len(peers))

def remote(source, target, send, recv, peer):
    return pltpu.make_async_remote_copy(
        src_ref=source, dst_ref=target, send_sem=send, recv_sem=recv,
        device_id=peer, device_id_type=MESH)

def comm_call(kernel, out_shape, scratch, ident, *args, name):
    vmem = pl.BlockSpec(memory_space=pltpu.VMEM)
    return pl.pallas_call(
        kernel, out_shape=out_shape, in_specs=[vmem] * len(args), out_specs=jax.tree.map(lambda _: vmem, out_shape),
        scratch_shapes=scratch,
        compiler_params=pltpu.CompilerParams(collective_id=ident, has_side_effects=True, vmem_limit_bytes=40 << 20),
        name=name)(*args)

DMA = pltpu.SemaphoreType.DMA

def scatter_sum(part_ref, inbox, send, recv, me):
    copies = []
    for hop in (3, 2, 1):
        copy = remote(part_ref.at[me ^ hop], inbox.at[hop - 1], send.at[hop - 1], recv.at[hop - 1], {"filt": me ^ hop})
        copy.start()
        copies.append(copy)
    total = part_ref[me].astype(jnp.float32)
    for copy, hop in reversed(list(zip(copies, (3, 2, 1)))):
        copy.wait()
        total = total + inbox[hop - 1].astype(jnp.float32)
    return total

def gather_blocks(low, all_ref, send, recv, me):
    all_ref[me] = low
    far = remote(all_ref.at[me], all_ref.at[me], send.at[0], recv.at[0], {"filt": me ^ 2})
    near = remote(all_ref.at[me], all_ref.at[me], send.at[1], recv.at[1], {"filt": me ^ 1})
    far.start()
    near.start()
    far.wait_recv()
    relay = remote(all_ref.at[me ^ 2], all_ref.at[me ^ 2], send.at[2], recv.at[2], {"filt": me ^ 1})
    relay.start()
    far.wait_send()
    near.wait()
    relay.wait()

def norm(values, gain, shift, eps):
    center = values - jnp.mean(values, axis=-1, keepdims=True)
    scale = lax.rsqrt(jnp.mean(center * center, axis=-1, keepdims=True) + eps)
    unit = center * scale
    return unit * gain + shift, unit, scale

def norm_back(upstream, unit, scale, gain):
    lifted = upstream * gain
    drop = jnp.mean(lifted, axis=-1, keepdims=True)
    lean = jnp.mean(lifted * unit, axis=-1, keepdims=True)
    return scale * (lifted - drop - unit * lean)

def forward_stage(part_ref, base_ref, gain_ref, shift_ref, value_ref, unit_ref, scale_ref, all_ref, inbox, send, recv, eps):
    me = lax.axis_index("filt")
    greet([{"filt": me ^ hop} for hop in (1, 2, 3)])
    total = scatter_sum(part_ref, inbox, send, recv, me) + base_ref[...]
    value, unit, scale = norm(total, gain_ref[...], shift_ref[...], eps)
    value_ref[...] = value
    unit_ref[...] = unit
    scale_ref[...] = scale
    gather_blocks(value.astype(jnp.bfloat16), all_ref, send.at[pl.ds(3, 3)], recv.at[pl.ds(3, 3)], me)

def top_stage(part_ref, base_ref, up_ref, gain_ref, shift_ref, top_ref, down_ref, dgain_ref, dshift_ref, all_ref, inbox, send, recv, eps):
    me = lax.axis_index("filt")
    greet([{"filt": me ^ hop} for hop in (1, 2, 3)])
    total = scatter_sum(part_ref, inbox, send, recv, me) + base_ref[...]
    top, unit, scale = norm(total, gain_ref[...], shift_ref[...], eps)
    top_ref[...] = top.astype(jnp.bfloat16)
    up = up_ref[...].astype(jnp.float32)
    dgain_ref[...] = jnp.sum(up * unit, axis=0, keepdims=True)
    dshift_ref[...] = jnp.sum(up, axis=0, keepdims=True)
    down = norm_back(up, unit, scale, gain_ref[...])
    down_ref[...] = down
    gather_blocks(down.astype(jnp.bfloat16), all_ref, send.at[pl.ds(3, 3)], recv.at[pl.ds(3, 3)], me)

def backward_stage(part_ref, base_ref, unit_ref, scale_ref, gain_ref, down_ref, dgain_ref, dshift_ref, dlow_ref, all_ref, inbox, send, recv):
    me = lax.axis_index("filt")
    greet([{"filt": me ^ hop} for hop in (1, 2, 3)])
    up = scatter_sum(part_ref, inbox, send, recv, me) + base_ref[...]
    unit = unit_ref[...]
    dgain_ref[...] = jnp.sum(up * unit, axis=0, keepdims=True)
    dshift_ref[...] = jnp.sum(up, axis=0, keepdims=True)
    down = norm_back(up, unit, scale_ref[...], gain_ref[...])
    down_ref[...] = down
    low = down.astype(jnp.bfloat16)
    dlow_ref[...] = jnp.sum(low.astype(jnp.float32), axis=0, keepdims=True)
    gather_blocks(low, all_ref, send.at[pl.ds(3, 3)], recv.at[pl.ds(3, 3)], me)

def stage_scratch(block):
    return [pltpu.VMEM((3,) + block, jnp.bfloat16), DMA((6,)), DMA((6,))]

def f32(*shape): return jax.ShapeDtypeStruct(shape, jnp.float32)
def bf16(*shape): return jax.ShapeDtypeStruct(shape, jnp.bfloat16)

def forward_stage_call(part, base, gain, shift, eps, ident):
    parts, rows, cols = part.shape
    return comm_call(functools.partial(forward_stage, eps=eps),
        (f32(rows, cols), f32(rows, cols), f32(rows, 1), bf16(parts, rows, cols)), stage_scratch((rows, cols)), ident,
        part, base, gain, shift, name="forward_stage")

def top_stage_call(part, base, up, gain, shift, eps, ident):
    parts, rows, cols = part.shape
    return comm_call(functools.partial(top_stage, eps=eps),
        (bf16(rows, cols), f32(rows, cols), f32(1, cols), f32(1, cols), bf16(parts, rows, cols)), stage_scratch((rows, cols)), ident,
        part, base, up, gain, shift, name="top_stage")

def backward_stage_call(part, base, unit, scale, gain, ident):
    parts, rows, cols = part.shape
    return comm_call(backward_stage,
        (f32(rows, cols), f32(1, cols), f32(1, cols), f32(1, cols), bf16(parts, rows, cols)), stage_scratch((rows, cols)), ident,
        part, base, unit, scale, gain, name="backward_stage")

def gather_channels(own_ref, all_ref, send, recv, *, chunks):
    me = lax.axis_index("filt")
    greet([{"filt": me ^ hop} for hop in (1, 2)])
    rows, cols = own_ref.shape
    size = rows // chunks

    def lanes(index):
        return pl.ds(pl.multiple_of(index * cols, cols), cols)

    far, near, relay = [], [], []
    for chunk in range(chunks):
        span = pl.ds(chunk * size, size)
        copy = remote(own_ref.at[span, :], all_ref.at[span, lanes(me)], send.at[0, chunk], recv.at[0, chunk], {"filt": me ^ 2})
        copy.start()
        far.append(copy)
    for chunk in range(chunks):
        span = pl.ds(chunk * size, size)
        copy = remote(own_ref.at[span, :], all_ref.at[span, lanes(me)], send.at[1, chunk], recv.at[1, chunk], {"filt": me ^ 1})
        copy.start()
        near.append(copy)
    all_ref[:, lanes(me)] = own_ref[...]
    for chunk in range(chunks):
        span = pl.ds(chunk * size, size)
        far[chunk].wait_recv()
        piece = all_ref.at[span, lanes(me ^ 2)]
        copy = remote(piece, piece, send.at[2, chunk], recv.at[2, chunk], {"filt": me ^ 1})
        copy.start()
        relay.append(copy)
    for chunk in range(chunks):
        far[chunk].wait_send()
        near[chunk].wait()
        relay[chunk].wait()

def gather_channels_call(own, parts, ident, chunks=4):
    rows, cols = own.shape
    return comm_call(functools.partial(gather_channels, chunks=chunks), bf16(rows, cols * parts),
        [DMA((3, chunks)), DMA((3, chunks))], ident, own, name="gather_channels")

def scatter_channels(part_ref, base_ref, out_ref, inbox, merged, send, recv, *, chunks):
    me = lax.axis_index("filt")
    greet([{"filt": me ^ hop} for hop in (1, 2)])
    rows, cols = base_ref.shape
    size = rows // chunks

    def lanes(index):
        return pl.ds(pl.multiple_of(index * cols, cols), cols)

    def hop(source, slot, chunk, peer):
        span = pl.ds(chunk * size, size)
        copy = remote(source, inbox.at[slot, span, :], send.at[slot, chunk], recv.at[slot, chunk], {"filt": peer})
        copy.start()
        return copy

    first, second, third = [], [], []
    for chunk in range(chunks):
        span = pl.ds(chunk * size, size)
        first.append(hop(part_ref.at[span, lanes(me ^ 3)], 0, chunk, me ^ 1))
    for chunk in range(chunks):
        span = pl.ds(chunk * size, size)
        second.append(hop(part_ref.at[span, lanes(me ^ 1)], 1, chunk, me ^ 1))
    for chunk in range(chunks):
        span = pl.ds(chunk * size, size)
        first[chunk].wait_recv()
        both = part_ref[span, lanes(me ^ 2)].astype(jnp.float32) + inbox[0, span, :].astype(jnp.float32)
        merged[span, :] = both.astype(jnp.bfloat16)
        third.append(hop(merged.at[span, :], 2, chunk, me ^ 2))
    for chunk in range(chunks):
        span = pl.ds(chunk * size, size)
        second[chunk].wait_recv()
        third[chunk].wait_recv()
        total = part_ref[span, lanes(me)].astype(jnp.float32) + inbox[1, span, :].astype(jnp.float32)
        total = total + inbox[2, span, :].astype(jnp.float32) + base_ref[span, :]
        out_ref[span, :] = total.astype(jnp.bfloat16)
    for copy in first + second + third:
        copy.wait_send()

def scatter_channels_call(part, base, ident, chunks=4):
    rows, cols = base.shape
    return comm_call(functools.partial(scatter_channels, chunks=chunks), bf16(rows, cols),
        [pltpu.VMEM((3, rows, cols), jnp.bfloat16), pltpu.VMEM((rows, cols), jnp.bfloat16), DMA((3, chunks)), DMA((3, chunks))],
        ident, part, base, name="scatter_channels")

def total_all(rows_ref, table_ref, rows_out, table_out, inbox, tbox, sbox, low, tlow, tsum, send, recv):
    count = lax.axis_size("dp")
    slot = lax.axis_index("dp")
    me = lax.axis_index("filt")
    size = rows_out.shape[1]
    tsize = table_out.shape[1]
    low[...] = rows_ref[...].astype(jnp.bfloat16)
    tlow[...] = table_ref[...].astype(jnp.bfloat16)
    greet([{"dp": slot ^ hop} for hop in range(1, count)] + [{"filt": me ^ hop} for hop in (1, 2, 3)])
    copies = []
    for hop in range(1, count):
        peer = {"dp": slot ^ hop}
        copy = remote(low.at[slot ^ hop], inbox.at[hop - 1], send.at[0, hop - 1], recv.at[0, hop - 1], peer)
        copy.start()
        also = remote(tlow.at[slot ^ hop], tbox.at[hop - 1], send.at[1, hop - 1], recv.at[1, hop - 1], peer)
        also.start()
        copies += [copy, also]
    total = rows_ref[slot]
    part = table_ref[slot]
    for hop in range(1, count):
        copies[2 * hop - 2].wait()
        copies[2 * hop - 1].wait()
        total = total + inbox[hop - 1].astype(jnp.float32)
        part = part + tbox[hop - 1].astype(jnp.float32)
    rows_out[slot] = total.astype(jnp.bfloat16)
    tsum[...] = part.astype(jnp.bfloat16)
    sides = []
    for hop in (1, 2, 3):
        copy = remote(tsum, sbox.at[hop - 1], send.at[2, hop - 1], recv.at[2, hop - 1], {"filt": me ^ hop})
        copy.start()
        sides.append(copy)
    outs = []
    for hop in range(1, count):
        copy = remote(rows_out.at[slot], rows_out.at[slot], send.at[3, hop - 1], recv.at[3, hop - 1], {"dp": slot ^ hop})
        copy.start()
        outs.append(copy)
    for hop in (1, 2, 3):
        sides[hop - 1].wait()
    ordered = tsum[...].astype(jnp.float32)
    near = sbox[0].astype(jnp.float32)
    ordered = (ordered + near) + (sbox[1].astype(jnp.float32) + sbox[2].astype(jnp.float32))
    table_out[slot] = ordered.astype(jnp.bfloat16)
    for hop in range(1, count):
        copy = remote(table_out.at[slot], table_out.at[slot], send.at[4, hop - 1], recv.at[4, hop - 1], {"dp": slot ^ hop})
        copy.start()
        outs.append(copy)
    for copy in outs:
        copy.wait()

def total_all_call(rows, table, ident):
    count, size, lanes = rows.shape
    tsize = table.shape[1]
    return comm_call(total_all, (bf16(count, size, lanes), bf16(count, tsize, lanes)),
        [pltpu.VMEM((count - 1, size, lanes), jnp.bfloat16), pltpu.VMEM((count - 1, tsize, lanes), jnp.bfloat16),
         pltpu.VMEM((3, tsize, lanes), jnp.bfloat16), pltpu.VMEM((count, size, lanes), jnp.bfloat16), pltpu.VMEM((count, tsize, lanes), jnp.bfloat16),
         pltpu.VMEM((tsize, lanes), jnp.bfloat16), DMA((5, count - 1)), DMA((5, count - 1))],
        ident, rows, table, name="total_all")


def exact_gaussian_activation(values):
    return jax.nn.gelu(values, approximate=False)


def gelu_back(values, upstream):
    return jax.vjp(exact_gaussian_activation, values)[1](upstream)[0]


def channel_widths(channels):
    widths = jnp.ones_like(channels)
    for power in range(6):
        widths = widths + (channels >= NF * 2**power // 64).astype(jnp.int32)
    return widths


def highway_mix(hidden, gates):
    width = hidden.shape[1]
    carry_gate = jax.nn.sigmoid(gates[:, width:])
    return carry_gate * hidden + (1.0 - carry_gate) * exact_gaussian_activation(gates[:, :width])


def tn_dot(left, right):
    return lax.dot_general(left, right, (((0,), (0,)), ((), ())), preferred_element_type=jnp.float32)


def swap(array, axis, bit):
    size = lax.axis_size(axis)
    return lax.ppermute(array, axis, [(index, index ^ bit) for index in range(size)])


def reduce_rows(array):
    count = lax.axis_size("dp")
    slot = lax.axis_index("dp")
    bits = count.bit_length() - 1
    rows, cols = array.shape
    if count != 1 << bits:
        return lax.psum_scatter(array.astype(jnp.bfloat16), "dp", scatter_dimension=0, tiled=True)
    array = array.reshape((2,) * bits + (rows // count, cols))
    for bit in range(bits):
        axis = bits - 1 - bit
        mine = (slot >> bit) & 1
        keep = lax.dynamic_index_in_dim(array, mine, axis, keepdims=False)
        give = lax.dynamic_index_in_dim(array, 1 - mine, axis, keepdims=False)
        got = swap(give.astype(jnp.bfloat16), "dp", 1 << bit)
        array = (keep.astype(jnp.float32) + got.astype(jnp.float32)).astype(jnp.bfloat16)
    return array


def join_parts(array):
    part = lax.axis_index("filt")
    low = (part & 1) == 1
    high = (part >> 1) == 1
    far = swap(array, "filt", 2)
    near = swap(array, "filt", 1)
    both = swap(far, "filt", 1)
    here = (jnp.where(low, near, array), jnp.where(low, array, near))
    there = (jnp.where(low, both, far), jnp.where(low, far, both))
    first = [jnp.where(high, b, a) for a, b in zip(here, there)]
    second = [jnp.where(high, a, b) for a, b in zip(here, there)]
    return first + second


def per_device(
    chars,
    lengths,
    char_table,
    conv_weight,
    conv_bias,
    highway_weight,
    highway_bias,
    proj_weight,
    proj_bias,
    position,
    norm_gain,
    norm_bias,
    query_key_value_weight,
    attention_output_weight,
    feedforward_input_weight,
    feedforward_input_bias,
    feedforward_output_weight,
    cotangent,
):
    parts = lax.axis_size("filt")
    slices = lax.axis_size("dp")
    part = lax.axis_index("filt")
    slot = lax.axis_index("dp")
    seqs, quarter, dmodel = cotangent.shape
    full_len = chars.shape[1]
    letters = chars.shape[2]
    words = seqs * full_len
    tokens = seqs * quarter
    filters = conv_weight.shape[1]
    depth = char_table.shape[1]
    heads = dmodel // HD // parts
    width = heads * HD
    unit_rows = feedforward_output_weight.shape[0] // parts

    def own_columns(array, blocks):
        rows = array.shape[0]
        split = array.reshape(rows, blocks, parts, -1)
        return lax.dynamic_index_in_dim(split, part, 2, keepdims=False).reshape(rows, -1)

    def gather_rows(array):
        return lax.all_gather(array, "dp", axis=0, tiled=True)

    def to_rows(array):
        return lax.all_to_all(array, "filt", split_axis=0, concat_axis=1, tiled=True)

    def to_columns(array):
        return lax.all_to_all(array, "filt", split_axis=1, concat_axis=0, tiled=True)

    highway_own = gather_rows(own_columns(highway_weight[0], 2))
    small = jnp.concatenate(
        [
            highway_bias.reshape(-1),
            proj_bias,
            norm_gain.reshape(-1),
            norm_bias.reshape(-1),
            feedforward_input_bias,
        ]
    )
    small = lax.all_gather(small, "dp", axis=0, tiled=False)
    proj_own = to_rows(gather_rows(own_columns(proj_weight, 1)))
    qkv_own = gather_rows(own_columns(query_key_value_weight, 3))
    out_own = to_rows(gather_rows(own_columns(attention_output_weight, 1)))
    inner_own = gather_rows(own_columns(feedforward_input_weight, slices))
    outer_own = gather_rows(
        lax.dynamic_slice_in_dim(feedforward_output_weight, part * unit_rows, unit_rows, 0)
    )
    small = small.astype(jnp.float32)
    hb, pb, nd = highway_bias.shape[1], proj_bias.shape[0], norm_gain.shape[1]
    ib = feedforward_input_bias.shape[0]
    cuts = [hb, hb + pb, hb + pb + 3 * nd, hb + pb + 6 * nd]
    highway_b, proj_b, gain, shift, inner_b = jnp.split(small, cuts, axis=1)
    highway_b_own = own_columns(highway_b.reshape(1, -1), 2)
    proj_b = proj_b.reshape(-1)
    gain = gain.reshape(slices, 3, nd).transpose(1, 0, 2).reshape(3, dmodel)
    shift = shift.reshape(slices, 3, nd).transpose(1, 0, 2).reshape(3, dmodel)
    inner_b_own = own_columns(inner_b.reshape(1, -1), slices)

    def blocks_of(array):
        return array.astype(jnp.bfloat16).reshape(parts, tokens, -1)

    widths = channel_widths(part * filters + jnp.arange(filters, dtype=jnp.int32))
    ids, table, weight, back, limit, count = conv_prep(
        chars.reshape(words, letters), char_table, conv_weight, conv_bias, widths
    )
    acts, lse, embed = conv_forward_call(ids, table, weight, limit, count, letters, depth)
    features = gather_channels_call(acts, parts, 0)
    gates = nn_dot(features, highway_own) + highway_b_own
    feature_own = acts.astype(jnp.float32)
    hidden_low = highway_mix(feature_own, gates).astype(jnp.bfloat16)
    base = position.astype(jnp.float32) + proj_b[None, :]
    first, unit_zero, scale_zero, first_all = forward_stage_call(
        blocks_of(nn_dot(hidden_low, proj_own)), base, gain[0:1], shift[0:1], EPS, 1
    )
    first_all = first_all.reshape(words, dmodel)
    packed = nn_dot(first_all, qkv_own).astype(jnp.bfloat16)
    queries, keys, values = (
        packed[:, block * width : (block + 1) * width].reshape(seqs, full_len, heads, HD)
        for block in range(3)
    )
    key_ok = jnp.arange(full_len, dtype=jnp.int32)[None, :] < lengths[:, None]
    scale = HD ** (-0.5)
    scores = (
        jnp.einsum("sqhd,skhd->shqk", queries, keys, preferred_element_type=jnp.float32) * scale
    )
    scores = jnp.where(key_ok[:, None, None, :], scores, -1e30)
    row_top = jnp.max(scores, axis=-1, keepdims=True)
    log_total = row_top + jnp.log(jnp.sum(jnp.exp(scores - row_top), axis=-1, keepdims=True))
    probs = jnp.exp(scores - log_total)
    probs_low = probs.astype(jnp.bfloat16)
    attended = (
        jnp.einsum("shqk,skhd->sqhd", probs_low, values, preferred_element_type=jnp.float32)
        .astype(jnp.bfloat16)
        .reshape(words, width)
    )
    second, unit_one, scale_one, second_all = forward_stage_call(
        blocks_of(nn_dot(attended, out_own)), first, gain[1:2], shift[1:2], EPS, 2
    )
    second_all = second_all.reshape(words, dmodel)
    inner = nn_dot(second_all, inner_own) + inner_b_own
    active = exact_gaussian_activation(inner).astype(jnp.bfloat16)
    top, d_res_two, d_gain_two, d_shift_two, d_outer = top_stage_call(
        blocks_of(nn_dot(active, outer_own)),
        second,
        cotangent.reshape(tokens, dmodel),
        gain[2:3],
        shift[2:3],
        EPS,
        3,
    )
    encoded = top.reshape(seqs, quarter, dmodel)
    d_outer = d_outer.reshape(words, dmodel)
    grad_outer = reduce_rows(tn_dot(active, d_outer))
    d_active = nt_dot(d_outer, outer_own)
    d_inner = gelu_back(inner, d_active).astype(jnp.bfloat16)
    grad_inner = reduce_rows(tn_dot(second_all, d_inner))
    grad_inner_b = jnp.sum(d_inner.astype(jnp.float32), axis=0)
    d_res_one, d_gain_one, d_shift_one, unused_sum, d_mixed = backward_stage_call(
        blocks_of(nt_dot(d_inner, inner_own)), d_res_two, unit_one, scale_one, gain[1:2], 4
    )
    d_mixed = d_mixed.reshape(words, dmodel)
    grad_out = reduce_rows(to_columns(tn_dot(attended, d_mixed).astype(jnp.bfloat16)))
    d_attended = nt_dot(d_mixed, out_own).astype(jnp.bfloat16)
    d_attended = d_attended.reshape(seqs, full_len, heads, HD)
    d_values = jnp.einsum(
        "shqk,sqhd->skhd", probs_low, d_attended, preferred_element_type=jnp.float32
    )
    d_probs = jnp.einsum(
        "sqhd,skhd->shqk", d_attended, values, preferred_element_type=jnp.float32
    )
    row_inner = jnp.sum(d_probs * probs, axis=-1, keepdims=True)
    d_scores = (probs * (d_probs - row_inner)).astype(jnp.bfloat16)
    d_queries = (
        jnp.einsum("shqk,skhd->sqhd", d_scores, keys, preferred_element_type=jnp.float32) * scale
    )
    d_keys = (
        jnp.einsum("shqk,sqhd->skhd", d_scores, queries, preferred_element_type=jnp.float32) * scale
    )
    d_packed = jnp.concatenate(
        [item.reshape(words, width) for item in (d_queries, d_keys, d_values)], axis=1
    ).astype(jnp.bfloat16)
    grad_qkv = reduce_rows(tn_dot(first_all, d_packed))
    d_summed, d_gain_zero, d_shift_zero, grad_proj_b, d_projected = backward_stage_call(
        blocks_of(nt_dot(d_packed, qkv_own)), d_res_one, unit_zero, scale_zero, gain[0:1], 5
    )
    grad_pos = jnp.sum(d_summed.reshape(seqs, quarter, dmodel), axis=0)
    d_projected = d_projected.reshape(words, dmodel)
    grad_proj = reduce_rows(to_columns(tn_dot(hidden_low, d_projected).astype(jnp.bfloat16)))
    d_hidden = nt_dot(d_projected, proj_own)
    d_in, d_gates = jax.vjp(highway_mix, feature_own, gates)[1](d_hidden)
    d_gates = d_gates.astype(jnp.bfloat16)
    grad_highway = reduce_rows(tn_dot(features, d_gates))
    grad_highway_b = jnp.sum(d_gates.astype(jnp.float32), axis=0)
    d_features = scatter_channels_call(
        nt_dot(d_gates, highway_own).astype(jnp.bfloat16), d_in, 6
    )
    groups = table.shape[0] // depth
    conv_sums, table_sums = conv_backward_call(
        ids, embed, lse, d_features, weight, back, limit, count, groups, letters, depth
    )
    table_sums = table_sums.reshape(2, groups * depth, -1).sum(0)
    if slices == 8:
        table_rows = -(-table_sums.shape[0] // slices)
        table_rows = -(-table_rows // 8) * 8
        padded = jnp.pad(table_sums, ((0, table_rows * slices - table_sums.shape[0]), (0, 0)))
        conv_all, table_all = total_all_call(
            conv_sums.reshape(slices, -1, 128), padded.reshape(slices, table_rows, 128), 7
        )
        conv_all = conv_all.reshape(filters, 128).astype(jnp.float32)
        table_all = table_all.reshape(-1, 128)[: table_sums.shape[0]].astype(jnp.float32)
    else:
        conv_all = lax.psum(conv_sums, "dp")
        table_all = lax.psum(table_sums, ("dp", "filt"))
    tap_rows = conv_weight.shape[0]
    tap_keep = (jnp.arange(tap_rows, dtype=jnp.int32) // depth)[:, None] < widths[None, :]
    conv_grad_w = jnp.where(tap_keep, conv_all[:, :tap_rows].T, 0.0)
    conv_grad_b = conv_all[:, tap_rows]
    g_table = table_all.reshape(groups, depth, 128).transpose(0, 2, 1).reshape(-1, depth)
    g_table = g_table[: char_table.shape[0]]
    grad_pos = lax.psum(grad_pos, "dp")

    def place_columns(own, blocks):
        piece = own.reshape(blocks, 1, -1)
        whole = jnp.zeros((blocks, parts, piece.shape[2]), own.dtype)
        return lax.dynamic_update_slice_in_dim(whole, piece, part, 1).reshape(-1)

    d_gain = jnp.concatenate([d_gain_zero, d_gain_one, d_gain_two])
    d_shift = jnp.concatenate([d_shift_zero, d_shift_one, d_shift_two])
    pieces = [
        place_columns(grad_highway_b, 2).reshape(slices, -1),
        grad_proj_b.reshape(slices, -1),
        d_gain.reshape(3, slices, nd).transpose(1, 0, 2).reshape(slices, -1),
        d_shift.reshape(3, slices, nd).transpose(1, 0, 2).reshape(slices, -1),
        place_columns(grad_inner_b, slices).reshape(slices, -1),
    ]
    rows = jnp.concatenate(pieces, axis=1)
    sums = lax.psum(rows, ("dp", "filt"))
    own = lax.dynamic_index_in_dim(sums, slot, 0, keepdims=False)
    g_highway_b, g_proj_b, g_gain, g_shift, g_inner_b = jnp.split(own, cuts)

    def join_columns(array, blocks):
        rows_here = array.shape[0]
        split = [item.reshape(rows_here, blocks, 1, -1) for item in join_parts(array)]
        return jnp.concatenate(split, axis=2).reshape(rows_here, -1).astype(jnp.float32)

    g_outer = jnp.concatenate(join_parts(grad_outer), axis=0).astype(jnp.float32)
    g_inner = join_columns(grad_inner, slices)
    g_out = join_columns(grad_out, 1)
    g_qkv = join_columns(grad_qkv, 3)
    g_proj = join_columns(grad_proj, 1)
    g_highway = join_columns(grad_highway, 2)
    return (
        encoded,
        g_table,
        conv_grad_w,
        conv_grad_b,
        g_highway[None],
        g_highway_b[None],
        g_proj,
        g_proj_b,
        grad_pos,
        g_gain.reshape(3, nd),
        g_shift.reshape(3, nd),
        g_qkv,
        g_out,
        g_inner,
        g_inner_b,
        g_outer,
    )


def solution(mesh):
    return jax.shard_map(
        per_device,
        mesh=mesh,
        in_specs=(
            P("dp", None, None),
            P("dp"),
            P(),
            P(None, "filt"),
            P("filt"),
            P(None, "dp", None),
            P(None, "dp"),
            P("dp", None),
            P("dp"),
            P("filt", None),
            P(None, "dp"),
            P(None, "dp"),
            P("dp", None),
            P("dp", None),
            P("dp", None),
            P("dp"),
            P("dp", None),
            P("dp", "filt", None),
        ),
        out_specs=(
            P("dp", "filt", None),
            P(),
            P(None, "filt"),
            P("filt"),
            P(None, "dp", None),
            P(None, "dp"),
            P("dp", None),
            P("dp"),
            P("filt", None),
            P(None, "dp"),
            P(None, "dp"),
            P("dp", None),
            P("dp", None),
            P("dp", None),
            P("dp"),
            P("dp", None),
        ),
        check_vma=False,
    )
```

```python
import functools

import jax
import jax.numpy as jnp
from jax import lax
from jax.experimental import pallas as pl
from jax.experimental.pallas import tpu as pltpu
from jax.sharding import PartitionSpec as P

KW = 7
NF = 2048
HD = 64
EPS = 1e-12
ROOT_HALF = 0.7071067811865476
DENSITY = 0.3989422804014327

def nt_dot(left, right):
    return lax.dot_general(left, right, (((1,), (1,)), ((), ())), preferred_element_type=jnp.float32)

def nn_dot(left, right):
    return jnp.dot(left, right, preferred_element_type=jnp.float32)

def normal_cdf(values):
    return 0.5 * (1.0 + lax.erf(values * ROOT_HALF))

def char_parts(chars_ref, position, block):
    ids = chars_ref[pl.ds(position, 1), :]
    low = ids & 127
    group = ids >> 7
    onehot = (lax.broadcasted_iota(jnp.int32, (128, block), 0) == low)
    onehot = jnp.where(onehot, 1.0, 0.0).astype(jnp.bfloat16)
    return onehot, group

def conv_forward(letters, depth, chars_ref, table_ref, weight_ref, limit_ref, count_ref,
                 acts_ref, lse_ref, embed_ref, patch_ref, grid_ref):
    block = chars_ref.shape[1]
    filters = weight_ref.shape[0]
    groups = table_ref.shape[0] // depth
    lead = KW - 1
    rows = KW * depth

    @pl.when(pl.program_id(0) == 0)
    def _():
        patch_ref[:, :rows, :] = jnp.zeros((patch_ref.shape[0], rows, block), jnp.bfloat16)
        ones = lax.broadcasted_iota(jnp.int32, (128 - rows, block), 0) == 0
        tail = jnp.where(ones, 1.0, 0.0).astype(jnp.bfloat16)
        patch_ref[:, rows:, :] = jnp.broadcast_to(tail[None], (patch_ref.shape[0],) + tail.shape)

    def embed(position, carry):
        onehot, group = char_parts(chars_ref, position, block)
        looked = nn_dot(table_ref[...], onehot)
        row = looked[:depth]
        for index in range(1, groups):
            row = jnp.where(group == index, looked[index * depth : (index + 1) * depth], row)
        row = row.astype(jnp.bfloat16)
        embed_ref[pl.ds(pl.multiple_of(position * depth, depth), depth), :] = row
        for tap in range(KW):
            patch_ref[position + lead - tap, tap * depth : (tap + 1) * depth, :] = row
        return carry

    lax.fori_loop(0, letters, embed, 0, unroll=5)
    chunk = grid_ref.shape[1]
    always = letters - KW + 1
    for start in range(0, filters, chunk):
        weight = weight_ref[start : start + chunk, :]
        limit = limit_ref[start : start + chunk, :]

        def product(position, top):
            grid = nn_dot(weight, patch_ref[position + lead])
            grid_ref[position] = grid
            return jnp.maximum(top, grid)

        top = lax.fori_loop(0, always, product, jnp.full((chunk, block), -1e30, jnp.float32), unroll=11)
        for position in range(always, letters):
            grid = nn_dot(weight, patch_ref[position + lead])
            grid = jnp.where(limit >= position, grid, -1e30)
            grid_ref[position] = grid
            top = jnp.maximum(top, grid)

        def total(position, acc):
            return acc + jnp.exp(grid_ref[position] - top)

        acc = lax.fori_loop(0, letters, total, jnp.zeros((chunk, block), jnp.float32), unroll=10)
        lse = top + jnp.log(acc)
        lse_ref[start : start + chunk, :] = lse
        pooled = lse - count_ref[start : start + chunk, :]
        acts_ref[:, start : start + chunk] = (pooled * normal_cdf(pooled)).astype(jnp.bfloat16).T

def conv_backward(letters, depth, chars_ref, embed_ref, lse_ref, up_ref, weight_ref, back_ref,
                  limit_ref, count_ref, wgrad_ref, tgrad_ref, patch_ref, down_ref, pull_ref):
    block = chars_ref.shape[1]
    filters = weight_ref.shape[0]
    lead = KW - 1
    rows = KW * depth
    groups = tgrad_ref.shape[0] // (2 * depth)
    step = pl.program_id(0)

    @pl.when(step == 0)
    def _():
        wgrad_ref[...] = jnp.zeros(wgrad_ref.shape, jnp.float32)
        tgrad_ref[...] = jnp.zeros(tgrad_ref.shape, jnp.float32)
        patch_ref[letters * depth :, :] = jnp.zeros((patch_ref.shape[0] - letters * depth, block), jnp.bfloat16)

    patch_ref[: letters * depth, :] = embed_ref[...]
    down_ref[...] = jnp.zeros(down_ref.shape, jnp.float32)
    pooled = lse_ref[...] - count_ref[...]
    slope = normal_cdf(pooled) + pooled * (DENSITY * jnp.exp(-0.5 * pooled * pooled))
    pull_ref[...] = slope * up_ref[...].T.astype(jnp.float32)
    ones = jnp.where(lax.broadcasted_iota(jnp.int32, (128 - rows, block), 0) == 0, 1.0, 0.0).astype(jnp.bfloat16)

    def one(position, masked):
        start = position * depth
        if not isinstance(position, int):
            start = pl.multiple_of(start, depth)
        patch = jnp.concatenate([patch_ref[pl.ds(start, rows), :], ones], axis=0)
        grid = nn_dot(weight_ref[...], patch)
        spread = jnp.exp(grid - lse_ref[...]) * pull_ref[...]
        if masked:
            spread = jnp.where(limit_ref[...] >= position, spread, 0.0)
        spread = spread.astype(jnp.bfloat16)
        down = nn_dot(back_ref[...], spread)
        down_ref[pl.ds(start, rows), :] += down[:rows]
        wgrad_ref[...] += nt_dot(spread, patch)

    always = letters - KW + 1

    def body(position, carry):
        one(position, False)
        return carry

    lax.fori_loop(0, always, body, 0, unroll=2)
    for position in range(always, letters):
        one(position, True)

    def table(position, carry):
        onehot, group = char_parts(chars_ref, position, block)
        down = down_ref[pl.ds(pl.multiple_of(position * depth, depth), depth), :]
        high = down.astype(jnp.bfloat16)
        low = (down - high.astype(jnp.float32)).astype(jnp.bfloat16)
        zero = jnp.zeros_like(high)
        parts = [jnp.where(group == index, item, zero) for item in (high, low) for index in range(groups)]
        tgrad_ref[...] += nt_dot(jnp.concatenate(parts, axis=0), onehot)
        return carry

    lax.fori_loop(0, letters, table, 0, unroll=5)

def conv_prep(chars, char_table, conv_weight, conv_bias, widths):
    letters = chars.shape[1]
    vocab, depth = char_table.shape
    groups = -(-vocab // 128)
    table = jnp.pad(char_table, ((0, groups * 128 - vocab), (0, 0)))
    table = table.reshape(groups, 128, depth).transpose(0, 2, 1).reshape(groups * depth, 128)
    tap = jnp.arange(conv_weight.shape[0], dtype=jnp.int32) // depth
    masked = jnp.where(tap[:, None] < widths[None, :], conv_weight, 0)
    back = jnp.concatenate([masked, conv_bias[None, :], jnp.zeros((127 - masked.shape[0], masked.shape[1]), masked.dtype)], axis=0)
    limit = (letters - widths)[:, None].astype(jnp.int32)
    count = jnp.log((letters - widths + 1).astype(jnp.float32))[:, None]
    ids = jnp.pad(chars, ((0, 0), (0, -letters % 8))).T
    return ids, table, back.T, back, limit, count

def conv_forward_call(ids, table, weight, limit, count, letters, depth, block=256):
    words = ids.shape[1]
    filters = weight.shape[0]
    full = lambda a: pl.BlockSpec(a.shape, lambda i: (0,) * a.ndim)
    return pl.pallas_call(
        functools.partial(conv_forward, letters, depth),
        grid=(words // block,),
        in_specs=[pl.BlockSpec((ids.shape[0], block), lambda i: (0, i)), full(table), full(weight), full(limit), full(count)],
        out_specs=[pl.BlockSpec((block, filters), lambda i: (i, 0)), pl.BlockSpec((filters, block), lambda i: (0, i)),
                   pl.BlockSpec((letters * depth, block), lambda i: (0, i))],
        out_shape=[jax.ShapeDtypeStruct((words, filters), jnp.bfloat16), jax.ShapeDtypeStruct((filters, words), jnp.float32),
                   jax.ShapeDtypeStruct((letters * depth, words), jnp.bfloat16)],
        scratch_shapes=[pltpu.VMEM((letters + KW - 1, 128, block), jnp.bfloat16), pltpu.VMEM((letters, 128, block), jnp.float32)],
        compiler_params=pltpu.CompilerParams(vmem_limit_bytes=48 << 20),
        name="conv_forward",
    )(ids, table, weight, limit, count)

def conv_backward_call(ids, embed, lse, up, weight, back, limit, count, groups, letters, depth, block=256):
    words = ids.shape[1]
    filters = weight.shape[0]
    full = lambda a: pl.BlockSpec(a.shape, lambda i: (0,) * a.ndim)
    return pl.pallas_call(
        functools.partial(conv_backward, letters, depth),
        grid=(words // block,),
        in_specs=[pl.BlockSpec((ids.shape[0], block), lambda i: (0, i)), pl.BlockSpec((letters * depth, block), lambda i: (0, i)),
                  pl.BlockSpec((filters, block), lambda i: (0, i)), pl.BlockSpec((block, filters), lambda i: (i, 0)),
                  full(weight), full(back), full(limit), full(count)],
        out_specs=[pl.BlockSpec((filters, 128), lambda i: (0, 0)), pl.BlockSpec((2 * groups * depth, 128), lambda i: (0, 0))],
        out_shape=[jax.ShapeDtypeStruct((filters, 128), jnp.float32), jax.ShapeDtypeStruct((2 * groups * depth, 128), jnp.float32)],
        scratch_shapes=[pltpu.VMEM(((letters + KW - 1) * depth, block), jnp.bfloat16), pltpu.VMEM(((letters + KW - 1) * depth, block), jnp.float32),
                        pltpu.VMEM((filters, block), jnp.float32)],
        compiler_params=pltpu.CompilerParams(vmem_limit_bytes=48 << 20),
        name="conv_backward",
    )(ids, embed, lse, up, weight, back, limit, count)


MESH = pl.DeviceIdType.MESH

def greet(peers):
    barrier = pltpu.get_barrier_semaphore()
    for peer in peers:
        pl.semaphore_signal(barrier, inc=1, device_id=peer, device_id_type=MESH)
    pl.semaphore_wait(barrier, len(peers))

def remote(source, target, send, recv, peer):
    return pltpu.make_async_remote_copy(
        src_ref=source, dst_ref=target, send_sem=send, recv_sem=recv,
        device_id=peer, device_id_type=MESH)

def comm_call(kernel, out_shape, scratch, ident, *args, name):
    vmem = pl.BlockSpec(memory_space=pltpu.VMEM)
    return pl.pallas_call(
        kernel, out_shape=out_shape, in_specs=[vmem] * len(args), out_specs=jax.tree.map(lambda _: vmem, out_shape),
        scratch_shapes=scratch,
        compiler_params=pltpu.CompilerParams(collective_id=ident, has_side_effects=True, vmem_limit_bytes=40 << 20),
        name=name)(*args)

DMA = pltpu.SemaphoreType.DMA

def scatter_sum(part_ref, inbox, send, recv, me):
    copies = []
    for hop in (3, 2, 1):
        copy = remote(part_ref.at[me ^ hop], inbox.at[hop - 1], send.at[hop - 1], recv.at[hop - 1], {"filt": me ^ hop})
        copy.start()
        copies.append(copy)
    total = part_ref[me].astype(jnp.float32)
    for copy, hop in reversed(list(zip(copies, (3, 2, 1)))):
        copy.wait()
        total = total + inbox[hop - 1].astype(jnp.float32)
    return total

def gather_blocks(low, all_ref, send, recv, me):
    all_ref[me] = low
    far = remote(all_ref.at[me], all_ref.at[me], send.at[0], recv.at[0], {"filt": me ^ 2})
    near = remote(all_ref.at[me], all_ref.at[me], send.at[1], recv.at[1], {"filt": me ^ 1})
    far.start()
    near.start()
    far.wait_recv()
    relay = remote(all_ref.at[me ^ 2], all_ref.at[me ^ 2], send.at[2], recv.at[2], {"filt": me ^ 1})
    relay.start()
    far.wait_send()
    near.wait()
    relay.wait()

def norm(values, gain, shift, eps):
    center = values - jnp.mean(values, axis=-1, keepdims=True)
    scale = lax.rsqrt(jnp.mean(center * center, axis=-1, keepdims=True) + eps)
    unit = center * scale
    return unit * gain + shift, unit, scale

def norm_back(upstream, unit, scale, gain):
    lifted = upstream * gain
    drop = jnp.mean(lifted, axis=-1, keepdims=True)
    lean = jnp.mean(lifted * unit, axis=-1, keepdims=True)
    return scale * (lifted - drop - unit * lean)

def forward_stage(part_ref, base_ref, gain_ref, shift_ref, value_ref, unit_ref, scale_ref, all_ref, inbox, send, recv, eps):
    me = lax.axis_index("filt")
    greet([{"filt": me ^ hop} for hop in (1, 2, 3)])
    total = scatter_sum(part_ref, inbox, send, recv, me) + base_ref[...]
    value, unit, scale = norm(total, gain_ref[...], shift_ref[...], eps)
    value_ref[...] = value
    unit_ref[...] = unit
    scale_ref[...] = scale
    gather_blocks(value.astype(jnp.bfloat16), all_ref, send.at[pl.ds(3, 3)], recv.at[pl.ds(3, 3)], me)

def top_stage(part_ref, base_ref, up_ref, gain_ref, shift_ref, top_ref, down_ref, dgain_ref, dshift_ref, all_ref, inbox, send, recv, eps):
    me = lax.axis_index("filt")
    greet([{"filt": me ^ hop} for hop in (1, 2, 3)])
    total = scatter_sum(part_ref, inbox, send, recv, me) + base_ref[...]
    top, unit, scale = norm(total, gain_ref[...], shift_ref[...], eps)
    top_ref[...] = top.astype(jnp.bfloat16)
    up = up_ref[...].astype(jnp.float32)
    dgain_ref[...] = jnp.sum(up * unit, axis=0, keepdims=True)
    dshift_ref[...] = jnp.sum(up, axis=0, keepdims=True)
    down = norm_back(up, unit, scale, gain_ref[...])
    down_ref[...] = down
    gather_blocks(down.astype(jnp.bfloat16), all_ref, send.at[pl.ds(3, 3)], recv.at[pl.ds(3, 3)], me)

def backward_stage(kind, part_ref, base_ref, unit_ref, scale_ref, gain_ref, *refs):
    job_in, job_out, job_send, job_recv = None, None, None, None
    if kind is not None:
        (job_in, down_ref, dgain_ref, dshift_ref, dlow_ref, all_ref, job_out, inbox, send, recv, job_send, job_recv) = refs
    else:
        (down_ref, dgain_ref, dshift_ref, dlow_ref, all_ref, inbox, send, recv) = refs
    me = lax.axis_index("filt")
    slot = lax.axis_index("dp")
    others = [] if kind is None else [{"dp": slot ^ hop} for hop in job_hops(kind)]
    greet([{"filt": me ^ hop} for hop in (1, 2, 3)] + others)
    copies = [] if kind is None else start_job(kind, job_in, job_out, job_send, job_recv)
    up = scatter_sum(part_ref, inbox, send, recv, me) + base_ref[...]
    unit = unit_ref[...]
    dgain_ref[...] = jnp.sum(up * unit, axis=0, keepdims=True)
    dshift_ref[...] = jnp.sum(up, axis=0, keepdims=True)
    down = norm_back(up, unit, scale_ref[...], gain_ref[...])
    down_ref[...] = down
    low = down.astype(jnp.bfloat16)
    dlow_ref[...] = jnp.sum(low.astype(jnp.float32), axis=0, keepdims=True)
    gather_blocks(low, all_ref, send.at[pl.ds(3, 3)], recv.at[pl.ds(3, 3)], me)
    for copy in copies:
        copy.wait()

def start_job(kind, source, target, send, recv):
    slot = lax.axis_index("dp")
    ring, side = slot // 2, slot % 2
    if kind == "side":
        moves = [(source.at[:, 1 - side], target, 1)]
    else:
        moves = [(source.at[ring ^ hop], target.at[hop - 1], 2 * hop) for hop in (2, 3, 1)]
    copies = []
    for index, (piece, place, hop) in enumerate(moves):
        copy = remote(piece, place, send.at[index], recv.at[index], {"dp": slot ^ hop})
        copy.start()
        copies.append(copy)
    return copies

def job_hops(kind):
    return (1,) if kind == "side" else (2, 4, 6)

def stage_scratch(block):
    return [pltpu.VMEM((3,) + block, jnp.bfloat16), DMA((6,)), DMA((6,))]

def f32(*shape): return jax.ShapeDtypeStruct(shape, jnp.float32)
def bf16(*shape): return jax.ShapeDtypeStruct(shape, jnp.bfloat16)

def forward_stage_call(part, base, gain, shift, eps, ident):
    parts, rows, cols = part.shape
    return comm_call(functools.partial(forward_stage, eps=eps),
        (f32(rows, cols), f32(rows, cols), f32(rows, 1), bf16(parts, rows, cols)), stage_scratch((rows, cols)), ident,
        part, base, gain, shift, name="forward_stage")

def top_stage_call(part, base, up, gain, shift, eps, ident):
    parts, rows, cols = part.shape
    return comm_call(functools.partial(top_stage, eps=eps),
        (bf16(rows, cols), f32(rows, cols), f32(1, cols), f32(1, cols), bf16(parts, rows, cols)), stage_scratch((rows, cols)), ident,
        part, base, up, gain, shift, name="top_stage")

def backward_stage_call(part, base, unit, scale, gain, ident, kind=None, job=None):
    parts, rows, cols = part.shape
    vmem = pl.BlockSpec(memory_space=pltpu.VMEM)
    hbm = pl.BlockSpec(memory_space=pl.ANY)
    args = (part, base, unit, scale, gain)
    out_shape = [f32(rows, cols), f32(1, cols), f32(1, cols), f32(1, cols), bf16(parts, rows, cols)]
    in_specs, out_specs, scratch = [vmem] * 5, [vmem] * 5, stage_scratch((rows, cols))
    if kind is not None:
        ring = job.shape[0]
        args += (job,)
        in_specs.append(hbm)
        out_specs.append(hbm)
        out_shape.append(bf16(ring, *job.shape[2:]) if kind == "side" else bf16(ring - 1, *job.shape[1:]))
        scratch += [DMA((3,)), DMA((3,))]
    return pl.pallas_call(
        functools.partial(backward_stage, kind), out_shape=out_shape, in_specs=in_specs, out_specs=out_specs,
        scratch_shapes=scratch,
        compiler_params=pltpu.CompilerParams(collective_id=ident, has_side_effects=True, vmem_limit_bytes=24 << 20),
        name="backward_stage")(*args)

def gather_channels(own_ref, all_ref, send, recv, *, chunks):
    me = lax.axis_index("filt")
    greet([{"filt": me ^ hop} for hop in (1, 2)])
    rows, cols = own_ref.shape
    size = rows // chunks

    def lanes(index):
        return pl.ds(pl.multiple_of(index * cols, cols), cols)

    far, near, relay = [], [], []
    for chunk in range(chunks):
        span = pl.ds(chunk * size, size)
        copy = remote(own_ref.at[span, :], all_ref.at[span, lanes(me)], send.at[0, chunk], recv.at[0, chunk], {"filt": me ^ 2})
        copy.start()
        far.append(copy)
    for chunk in range(chunks):
        span = pl.ds(chunk * size, size)
        copy = remote(own_ref.at[span, :], all_ref.at[span, lanes(me)], send.at[1, chunk], recv.at[1, chunk], {"filt": me ^ 1})
        copy.start()
        near.append(copy)
    all_ref[:, lanes(me)] = own_ref[...]
    for chunk in range(chunks):
        span = pl.ds(chunk * size, size)
        far[chunk].wait_recv()
        piece = all_ref.at[span, lanes(me ^ 2)]
        copy = remote(piece, piece, send.at[2, chunk], recv.at[2, chunk], {"filt": me ^ 1})
        copy.start()
        relay.append(copy)
    for chunk in range(chunks):
        far[chunk].wait_send()
        near[chunk].wait()
        relay[chunk].wait()

def gather_channels_call(own, parts, ident, chunks=4):
    rows, cols = own.shape
    return comm_call(functools.partial(gather_channels, chunks=chunks), bf16(rows, cols * parts),
        [DMA((3, chunks)), DMA((3, chunks))], ident, own, name="gather_channels")

def scatter_channels(part_ref, base_ref, out_ref, inbox, merged, send, recv, *, chunks):
    me = lax.axis_index("filt")
    greet([{"filt": me ^ hop} for hop in (1, 2)])
    rows, cols = base_ref.shape
    size = rows // chunks

    def lanes(index):
        return pl.ds(pl.multiple_of(index * cols, cols), cols)

    def hop(source, slot, chunk, peer):
        span = pl.ds(chunk * size, size)
        copy = remote(source, inbox.at[slot, span, :], send.at[slot, chunk], recv.at[slot, chunk], {"filt": peer})
        copy.start()
        return copy

    first, second, third = [], [], []
    for chunk in range(chunks):
        span = pl.ds(chunk * size, size)
        first.append(hop(part_ref.at[span, lanes(me ^ 3)], 0, chunk, me ^ 1))
    for chunk in range(chunks):
        span = pl.ds(chunk * size, size)
        second.append(hop(part_ref.at[span, lanes(me ^ 1)], 1, chunk, me ^ 1))
    for chunk in range(chunks):
        span = pl.ds(chunk * size, size)
        first[chunk].wait_recv()
        both = part_ref[span, lanes(me ^ 2)].astype(jnp.float32) + inbox[0, span, :].astype(jnp.float32)
        merged[span, :] = both.astype(jnp.bfloat16)
        third.append(hop(merged.at[span, :], 2, chunk, me ^ 2))
    for chunk in range(chunks):
        span = pl.ds(chunk * size, size)
        second[chunk].wait_recv()
        third[chunk].wait_recv()
        total = part_ref[span, lanes(me)].astype(jnp.float32) + inbox[1, span, :].astype(jnp.float32)
        total = total + inbox[2, span, :].astype(jnp.float32) + base_ref[span, :]
        out_ref[span, :] = total.astype(jnp.bfloat16)
    for copy in first + second + third:
        copy.wait_send()

def scatter_channels_call(part, base, ident, chunks=4):
    rows, cols = base.shape
    return comm_call(functools.partial(scatter_channels, chunks=chunks), bf16(rows, cols),
        [pltpu.VMEM((3, rows, cols), jnp.bfloat16), pltpu.VMEM((rows, cols), jnp.bfloat16), DMA((3, chunks)), DMA((3, chunks))],
        ident, part, base, name="scatter_channels")

def total_all(rows_ref, table_ref, rows_out, table_out, inbox, tbox, sbox, low, tlow, tsum, send, recv):
    count = lax.axis_size("dp")
    slot = lax.axis_index("dp")
    me = lax.axis_index("filt")
    size = rows_out.shape[1]
    tsize = table_out.shape[1]
    low[...] = rows_ref[...].astype(jnp.bfloat16)
    tlow[...] = table_ref[...].astype(jnp.bfloat16)
    greet([{"dp": slot ^ hop} for hop in range(1, count)] + [{"filt": me ^ hop} for hop in (1, 2, 3)])
    copies = []
    for hop in range(1, count):
        peer = {"dp": slot ^ hop}
        copy = remote(low.at[slot ^ hop], inbox.at[hop - 1], send.at[0, hop - 1], recv.at[0, hop - 1], peer)
        copy.start()
        also = remote(tlow.at[slot ^ hop], tbox.at[hop - 1], send.at[1, hop - 1], recv.at[1, hop - 1], peer)
        also.start()
        copies += [copy, also]
    total = rows_ref[slot]
    part = table_ref[slot]
    for hop in range(1, count):
        copies[2 * hop - 2].wait()
        copies[2 * hop - 1].wait()
        total = total + inbox[hop - 1].astype(jnp.float32)
        part = part + tbox[hop - 1].astype(jnp.float32)
    rows_out[slot] = total.astype(jnp.bfloat16)
    tsum[...] = part.astype(jnp.bfloat16)
    sides = []
    for hop in (1, 2, 3):
        copy = remote(tsum, sbox.at[hop - 1], send.at[2, hop - 1], recv.at[2, hop - 1], {"filt": me ^ hop})
        copy.start()
        sides.append(copy)
    outs = []
    for hop in range(1, count):
        copy = remote(rows_out.at[slot], rows_out.at[slot], send.at[3, hop - 1], recv.at[3, hop - 1], {"dp": slot ^ hop})
        copy.start()
        outs.append(copy)
    for hop in (1, 2, 3):
        sides[hop - 1].wait()
    ordered = tsum[...].astype(jnp.float32)
    near = sbox[0].astype(jnp.float32)
    ordered = (ordered + near) + (sbox[1].astype(jnp.float32) + sbox[2].astype(jnp.float32))
    table_out[slot] = ordered.astype(jnp.bfloat16)
    for hop in range(1, count):
        copy = remote(table_out.at[slot], table_out.at[slot], send.at[4, hop - 1], recv.at[4, hop - 1], {"dp": slot ^ hop})
        copy.start()
        outs.append(copy)
    for copy in outs:
        copy.wait()

def total_all_call(rows, table, ident):
    count, size, lanes = rows.shape
    tsize = table.shape[1]
    return comm_call(total_all, (bf16(count, size, lanes), bf16(count, tsize, lanes)),
        [pltpu.VMEM((count - 1, size, lanes), jnp.bfloat16), pltpu.VMEM((count - 1, tsize, lanes), jnp.bfloat16),
         pltpu.VMEM((3, tsize, lanes), jnp.bfloat16), pltpu.VMEM((count, size, lanes), jnp.bfloat16), pltpu.VMEM((count, tsize, lanes), jnp.bfloat16),
         pltpu.VMEM((tsize, lanes), jnp.bfloat16), DMA((5, count - 1)), DMA((5, count - 1))],
        ident, rows, table, name="total_all")


def prologue(letters, depth, block, chunks, window, first, chars_ref, table_ref, weight_ref, limit_ref, count_ref, shard_ref,
             acts_ref, lse_ref, embed_ref, all_ref, full_ref, patch_ref, grid_ref,
             zsend, zrecv, local, ysend, yrecv, fsend, frecv):
    words = chars_ref.shape[1]
    filters = weight_ref.shape[0]
    me = lax.axis_index("filt")
    slot = lax.axis_index("dp")
    ring, side = slot // 2, slot % 2
    greet([{"filt": me ^ hop} for hop in (1, 2)] + [{"dp": slot ^ hop} for hop in (1, 2, 4, 6)])
    parts = all_ref.shape[1] // filters
    span = shard_ref.shape[0] // (chunks // 2)

    def spot(chunk):
        return pl.ds((chunk // 2) * span, span), chunk % 2

    own, far = [], []

    def start_chunk(chunk):
        if chunk >= chunks:
            return
        rows, half = spot(chunk)
        source = shard_ref.at[rows, pl.ds(pl.multiple_of(half * filters * parts + me * filters, filters), filters)]
        target = full_ref.at[half, ring, side, rows, :]
        copy = pltpu.make_async_copy(source, target, local.at[chunk])
        copy.start()
        own.append(copy)
        for hop in (2, 1, 3):
            copy = remote(source, target, zsend.at[chunk, hop - 1], zrecv.at[chunk, hop - 1], {"dp": slot ^ (2 * hop)})
            copy.start()
            far.append(copy)

    for chunk in range(window):
        start_chunk(chunk)
    cross = []

    def forward_chunk(chunk):
        rows, half = spot(chunk)
        own[chunk].wait()
        for copy in far[3 * chunk : 3 * chunk + 3]:
            copy.wait_recv()
        start_chunk(chunk + window)
        piece = full_ref.at[half, :, side, rows, :]
        copy = remote(piece, piece, ysend.at[chunk], yrecv.at[chunk], {"dp": slot ^ 1})
        copy.start()
        cross.append(copy)

    lead = KW - 1
    rows = KW * depth
    groups = table_ref.shape[0] // depth
    patch_ref[:, :rows, :] = jnp.zeros((patch_ref.shape[0], rows, block), jnp.bfloat16)
    ones = lax.broadcasted_iota(jnp.int32, (128 - rows, block), 0) == 0
    tail = jnp.where(ones, 1.0, 0.0).astype(jnp.bfloat16)
    patch_ref[:, rows:, :] = jnp.broadcast_to(tail[None], (patch_ref.shape[0],) + tail.shape)
    chunk = grid_ref.shape[1]
    always = letters - KW + 1
    steps = filters // chunk
    polls = {(step // steps, step % steps): step - first for step in range(first, min(first + chunks, words // block * steps))}
    gathers = ChannelGather(acts_ref, all_ref, fsend, frecv, words // block)
    for index in range(words // block):
        cols = pl.ds(index * block, block)

        def embed(position, carry):
            ids = chars_ref[pl.ds(position, 1), cols]
            low = ids & 127
            group = ids >> 7
            onehot = lax.broadcasted_iota(jnp.int32, (128, block), 0) == low
            onehot = jnp.where(onehot, 1.0, 0.0).astype(jnp.bfloat16)
            looked = nn_dot(table_ref[...], onehot)
            row = looked[:depth]
            for part in range(1, groups):
                row = jnp.where(group == part, looked[part * depth : (part + 1) * depth], row)
            row = row.astype(jnp.bfloat16)
            embed_ref[pl.ds(pl.multiple_of(position * depth, depth), depth), cols] = row
            for tap in range(KW):
                patch_ref[position + lead - tap, tap * depth : (tap + 1) * depth, :] = row
            return carry

        lax.fori_loop(0, letters, embed, 0, unroll=5)
        for start in range(0, filters, chunk):
            weight = weight_ref[start : start + chunk, :]
            limit = limit_ref[start : start + chunk, :]

            def product(position, top):
                grid = nn_dot(weight, patch_ref[position + lead])
                grid_ref[position] = grid
                return jnp.maximum(top, grid)

            top = lax.fori_loop(0, always, product, jnp.full((chunk, block), -1e30, jnp.float32), unroll=11)
            for position in range(always, letters):
                grid = nn_dot(weight, patch_ref[position + lead])
                grid = jnp.where(limit >= position, grid, -1e30)
                grid_ref[position] = grid
                top = jnp.maximum(top, grid)

            def total(position, acc):
                return acc + jnp.exp(grid_ref[position] - top)

            acc = lax.fori_loop(0, letters, total, jnp.zeros((chunk, block), jnp.float32), unroll=10)
            lse = top + jnp.log(acc)
            lse_ref[start : start + chunk, cols] = lse
            pooled = lse - count_ref[start : start + chunk, :]
            acts_ref[cols, start : start + chunk] = (pooled * normal_cdf(pooled)).astype(jnp.bfloat16).T
            poll = polls.get((index, start // chunk))
            if poll is not None:
                forward_chunk(poll)
        gathers.send(index)
    for index in range(len(polls), chunks):
        forward_chunk(index)
    for index in range(words // block):
        gathers.relay(index)
    gathers.finish()
    for copy in far:
        copy.wait_send()
    for copy in cross:
        copy.wait()

class ChannelGather:
    def __init__(self, own_ref, all_ref, send, recv, pieces):
        self.me = lax.axis_index("filt")
        self.own, self.all, self.sems = own_ref, all_ref, (send, recv)
        self.size = own_ref.shape[0] // pieces
        self.copies = []

    def view(self, index, piece):
        cols = self.own.shape[1]
        return self.all.at[pl.ds(piece * self.size, self.size), pl.ds(pl.multiple_of(index * cols, cols), cols)]

    def push(self, source, target, kind, piece, hop):
        send, recv = self.sems
        copy = remote(source, target, send.at[kind, piece], recv.at[kind, piece], {"filt": self.me ^ hop})
        copy.start()
        self.copies.append(copy)
        return copy

    def send(self, piece):
        source = self.own.at[pl.ds(piece * self.size, self.size), :]
        target = self.view(self.me, piece)
        self.push(source, target, 0, piece, 2)
        self.push(source, target, 1, piece, 1)
        cols = self.own.shape[1]
        self.all[pl.ds(piece * self.size, self.size), pl.ds(pl.multiple_of(self.me * cols, cols), cols)] = self.own[pl.ds(piece * self.size, self.size), :]

    def relay(self, piece):
        self.copies[2 * piece].wait_recv()
        view = self.view(self.me ^ 2, piece)
        self.push(view, view, 2, piece, 1)

    def finish(self):
        for index, copy in enumerate(self.copies):
            copy.wait_send()
            if index % 2 == 1 or index >= 2 * (len(self.copies) // 3):
                copy.wait_recv()

def prologue_call(ids, table, weight, limit, count, shard, parts, letters, depth, ident, block=256, chunks=8, window=2, first=2):
    words = ids.shape[1]
    filters = weight.shape[0]
    rows = shard.shape[0]
    vmem = pl.BlockSpec(memory_space=pltpu.VMEM)
    hbm = pl.BlockSpec(memory_space=pl.ANY)
    pieces = words // block
    return pl.pallas_call(
        functools.partial(prologue, letters, depth, block, chunks, window, first),
        in_specs=[vmem] * 5 + [hbm],
        out_specs=[vmem] * 4 + [hbm],
        out_shape=[bf16(words, filters), f32(filters, words), bf16(letters * depth, words), bf16(words, filters * parts),
                   bf16(2, 4, 2, rows, filters)],
        scratch_shapes=[pltpu.VMEM((letters + KW - 1, 128, block), jnp.bfloat16), pltpu.VMEM((letters, 128, block), jnp.float32),
                        DMA((chunks, 3)), DMA((chunks, 3)), DMA((chunks,)), DMA((chunks,)), DMA((chunks,)), DMA((3, pieces)), DMA((3, pieces))],
        compiler_params=pltpu.CompilerParams(collective_id=ident, has_side_effects=True, vmem_limit_bytes=48 << 20),
        name="prologue",
    )(ids, table, weight, limit, count, shard)


class RowReduce:
    def __init__(self, grad, yin, pair, zin, joined, span, sems):
        self.grad, self.yin, self.pair, self.zin, self.joined = grad, yin, pair, zin, joined
        self.span, self.sems = span, sems
        self.me, self.slot = lax.axis_index("filt"), lax.axis_index("dp")
        self.ring, self.side = self.slot // 2, self.slot % 2
        self.copies = []

    def push(self, source, target, index, peer):
        send, recv = self.sems
        copy = remote(source, target, send.at[index], recv.at[index], peer)
        copy.start()
        self.copies.append(copy)
        return copy

    def across(self):
        span = self.span
        self.first = self.push(
            self.grad.at[:, 1 - self.side, span, :], self.yin.at[:, span, :], 0, {"dp": self.slot ^ 1}
        )

    def along(self):
        span = self.span
        self.first.wait_recv()
        both = self.grad[:, self.side, span, :].astype(jnp.float32) + self.yin[:, span, :].astype(jnp.float32)
        self.pair[:, span, :] = both.astype(jnp.bfloat16)
        self.rest = [
            self.push(self.pair.at[self.ring ^ hop, span, :], self.zin.at[hop - 1, span, :], hop, {"dp": self.slot ^ (2 * hop)})
            for hop in (2, 3, 1)
        ]

    def join(self):
        span = self.span
        for copy in self.rest:
            copy.wait_recv()
        total = self.pair[self.ring, span, :].astype(jnp.float32)
        for hop in (1, 2, 3):
            total = total + self.zin[hop - 1, span, :].astype(jnp.float32)
        self.joined[self.me, span, :] = total.astype(jnp.bfloat16)
        self.share()

    def share(self):
        piece = self.joined.at[self.me, self.span, :]
        self.far = self.push(piece, piece, 4, {"filt": self.me ^ 2})
        self.near = self.push(piece, piece, 5, {"filt": self.me ^ 1})

    def relay(self):
        self.far.wait_recv()
        piece = self.joined.at[self.me ^ 2, self.span, :]
        self.last = self.push(piece, piece, 6, {"filt": self.me ^ 1})

    def finish(self):
        self.near.wait_recv()
        self.last.wait_recv()
        for copy in self.copies:
            copy.wait_send()


def epilogue(letters, depth, block, plan, *refs):
    (part_ref, base_ref, chars_ref, embed_ref, lse_ref, weight_ref, back_ref, limit_ref, count_ref, wide_ref, slim_ref, ffn_ref,
     wgrad_ref, tgrad_ref, wide_out, slim_out, ffn_out,
     inbox, merged, up_ref, patch_ref, down_ref, pull_ref, wide_y, wide_p, wide_z, slim_y, slim_p, slim_z,
     csend, crecv, rsend, rrecv) = refs
    me = lax.axis_index("filt")
    slot = lax.axis_index("dp")
    greet([{"filt": me ^ hop} for hop in (1, 2)] + [{"dp": slot ^ hop} for hop in (1, 2, 4, 6)])
    items = []
    slim_rows = slim_out.shape[1] // 2
    wide_rows = wide_out.shape[1] // 4
    for index in range(2):
        items.append(RowReduce(slim_ref, slim_y, slim_p, slim_z, slim_out, pl.ds(index * slim_rows, slim_rows),
                               (rsend.at[index], rrecv.at[index])))
    for index in range(4):
        items.append(RowReduce(wide_ref, wide_y, wide_p, wide_z, wide_out, pl.ds(index * wide_rows, wide_rows),
                               (rsend.at[2 + index], rrecv.at[2 + index])))
    for item in items:
        item.across()
    ffn = RowReduce(None, None, None, None, ffn_out, pl.ds(0, ffn_out.shape[1]), (rsend.at[6], rrecv.at[6]))
    ffn_out[me] = ffn_ref[...]
    scatter = ChannelScatter(part_ref, base_ref, up_ref, inbox, merged, csend, crecv)
    scatter.run()
    ffn.share()
    steps = iter([(ffn, "relay") if code == "F" else (items[int(code[1:])], {"A": "along", "J": "join", "R": "relay"}[code[0]])
                  for code in plan])

    def advance(many):
        for unused in range(many):
            step = next(steps, None)
            if step is not None:
                getattr(*step)()

    filters = weight_ref.shape[0]
    rows = KW * depth
    groups = tgrad_ref.shape[0] // (2 * depth)
    wgrad_ref[...] = jnp.zeros(wgrad_ref.shape, jnp.float32)
    tgrad_ref[...] = jnp.zeros(tgrad_ref.shape, jnp.float32)
    patch_ref[letters * depth :, :] = jnp.zeros((patch_ref.shape[0] - letters * depth, block), jnp.bfloat16)
    ones = jnp.where(lax.broadcasted_iota(jnp.int32, (128 - rows, block), 0) == 0, 1.0, 0.0).astype(jnp.bfloat16)
    always = letters - KW + 1
    quarter = always // 4
    for index in range(chars_ref.shape[1] // block):
        cols = pl.ds(index * block, block)
        patch_ref[: letters * depth, :] = embed_ref[:, cols]
        down_ref[...] = jnp.zeros(down_ref.shape, jnp.float32)
        pooled = lse_ref[:, cols] - count_ref[...]
        slope = normal_cdf(pooled) + pooled * (DENSITY * jnp.exp(-0.5 * pooled * pooled))
        pull_ref[...] = slope * up_ref[cols, :].T.astype(jnp.float32)

        def one(position, masked):
            start = position * depth
            if not isinstance(position, int):
                start = pl.multiple_of(start, depth)
            patch = jnp.concatenate([patch_ref[pl.ds(start, rows), :], ones], axis=0)
            grid = nn_dot(weight_ref[...], patch)
            spread = jnp.exp(grid - lse_ref[:, cols]) * pull_ref[...]
            if masked:
                spread = jnp.where(limit_ref[...] >= position, spread, 0.0)
            spread = spread.astype(jnp.bfloat16)
            down = nn_dot(back_ref[...], spread)
            down_ref[pl.ds(start, rows), :] += down[:rows]
            wgrad_ref[...] += nt_dot(spread, patch)

        def body(position, carry):
            one(position, False)
            return carry

        for lap in range(4):
            stop = always if lap == 3 else (lap + 1) * quarter
            lax.fori_loop(lap * quarter, stop, body, 0)
            advance(2)
        for position in range(always, letters):
            one(position, True)

        def table(position, carry):
            ids = chars_ref[pl.ds(position, 1), cols]
            low = ids & 127
            group = ids >> 7
            onehot = lax.broadcasted_iota(jnp.int32, (128, block), 0) == low
            onehot = jnp.where(onehot, 1.0, 0.0).astype(jnp.bfloat16)
            down = down_ref[pl.ds(pl.multiple_of(position * depth, depth), depth), :]
            high = down.astype(jnp.bfloat16)
            rest = (down - high.astype(jnp.float32)).astype(jnp.bfloat16)
            zero = jnp.zeros_like(high)
            parts = [jnp.where(group == part, item, zero) for item in (high, rest) for part in range(groups)]
            tgrad_ref[...] += nt_dot(jnp.concatenate(parts, axis=0), onehot)
            return carry

        lax.fori_loop(0, letters, table, 0, unroll=5)
        advance(2)
    advance(len(plan))
    ffn.finish()
    for item in items:
        item.finish()


class ChannelScatter:
    def __init__(self, part_ref, base_ref, out_ref, inbox, merged, send, recv):
        self.part, self.base, self.out, self.inbox, self.merged = part_ref, base_ref, out_ref, inbox, merged
        self.sems = (send, recv)
        self.me = lax.axis_index("filt")

    def run(self):
        me = self.me
        rows, cols = self.base.shape
        pieces = self.sems[0].shape[1]
        size = rows // pieces

        def lanes(index):
            return pl.ds(pl.multiple_of(index * cols, cols), cols)

        def hop(source, kind, piece, peer):
            span = pl.ds(piece * size, size)
            send, recv = self.sems
            copy = remote(source, self.inbox.at[kind, span, :], send.at[kind, piece], recv.at[kind, piece], {"filt": peer})
            copy.start()
            return copy

        spans = [pl.ds(piece * size, size) for piece in range(pieces)]
        first = [hop(self.part.at[span, lanes(me ^ 3)], 0, piece, me ^ 1) for piece, span in enumerate(spans)]
        second = [hop(self.part.at[span, lanes(me ^ 1)], 1, piece, me ^ 1) for piece, span in enumerate(spans)]
        third = []
        for piece, span in enumerate(spans):
            first[piece].wait_recv()
            both = self.part[span, lanes(me ^ 2)].astype(jnp.float32) + self.inbox[0, span, :].astype(jnp.float32)
            self.merged[span, :] = both.astype(jnp.bfloat16)
            third.append(hop(self.merged.at[span, :], 2, piece, me ^ 2))
        for piece, span in enumerate(spans):
            second[piece].wait_recv()
            third[piece].wait_recv()
            total = self.part[span, lanes(me)].astype(jnp.float32) + self.inbox[1, span, :].astype(jnp.float32)
            total = total + self.inbox[2, span, :].astype(jnp.float32) + self.base[span, :]
            self.out[span, :] = total.astype(jnp.bfloat16)
        for copy in first + second + third:
            copy.wait_send()


PLAN = ("A0", "F", "A1", "J0", "A2", "J1", "R0", "A3", "J2", "R1", "A4", "J3", "R2", "A5", "J4", "R3", "J5", "R4", "R5")


def epilogue_call(part, base, ids, embed, lse, weight, back, limit, count, wide, slim, ffn, letters, depth, groups, ident, block=256):
    filters, words = lse.shape
    args = (part, base, ids, embed, lse, weight, back, limit, count, wide, slim, ffn)
    parts = part.shape[1] // filters
    pieces = 4
    vmem = pl.BlockSpec(memory_space=pltpu.VMEM)

    def space(shape, dtype=jnp.bfloat16):
        return pltpu.VMEM(shape, dtype)

    def stages(array):
        ring, side, rows, cols = array.shape
        return [space((ring, rows, cols)), space((ring, rows, cols)), space((ring - 1, rows, cols))]

    out_shape = [f32(filters, 128), f32(2 * groups * depth, 128), bf16(parts, *wide.shape[2:]), bf16(parts, *slim.shape[2:]),
                 bf16(parts, *ffn.shape)]
    padded = (letters + KW - 1) * depth
    return pl.pallas_call(
        functools.partial(epilogue, letters, depth, block, PLAN),
        in_specs=[vmem] * len(args),
        out_specs=[vmem] * len(out_shape),
        out_shape=out_shape,
        scratch_shapes=[space((3, words, filters)), space((words, filters)), space((words, filters)), space((padded, block)),
                        space((padded, block), jnp.float32), space((filters, block), jnp.float32)]
        + stages(wide) + stages(slim) + [DMA((3, pieces)), DMA((3, pieces)), DMA((7, 7)), DMA((7, 7))],
        compiler_params=pltpu.CompilerParams(collective_id=ident, has_side_effects=True, vmem_limit_bytes=56 << 20),
        name="epilogue",
    )(*args)


def exact_gaussian_activation(values):
    return jax.nn.gelu(values, approximate=False)


def gelu_back(values, upstream):
    return jax.vjp(exact_gaussian_activation, values)[1](upstream)[0]


def channel_widths(channels):
    widths = jnp.ones_like(channels)
    for power in range(6):
        widths = widths + (channels >= NF * 2**power // 64).astype(jnp.int32)
    return widths


def highway_mix(hidden, gates):
    width = hidden.shape[1]
    carry_gate = jax.nn.sigmoid(gates[:, width:])
    return carry_gate * hidden + (1.0 - carry_gate) * exact_gaussian_activation(gates[:, :width])


def tn_dot(left, right):
    return lax.dot_general(left, right, (((0,), (0,)), ((), ())), preferred_element_type=jnp.float32)


def swap(array, axis, bit):
    size = lax.axis_size(axis)
    return lax.ppermute(array, axis, [(index, index ^ bit) for index in range(size)])


def reduce_rows(array):
    count = lax.axis_size("dp")
    slot = lax.axis_index("dp")
    bits = count.bit_length() - 1
    rows, cols = array.shape
    if count != 1 << bits:
        return lax.psum_scatter(array.astype(jnp.bfloat16), "dp", scatter_dimension=0, tiled=True)
    array = array.reshape((2,) * bits + (rows // count, cols))
    for bit in range(bits):
        axis = bits - 1 - bit
        mine = (slot >> bit) & 1
        keep = lax.dynamic_index_in_dim(array, mine, axis, keepdims=False)
        give = lax.dynamic_index_in_dim(array, 1 - mine, axis, keepdims=False)
        got = swap(give.astype(jnp.bfloat16), "dp", 1 << bit)
        array = (keep.astype(jnp.float32) + got.astype(jnp.float32)).astype(jnp.bfloat16)
    return array


def join_parts(array):
    part = lax.axis_index("filt")
    low = (part & 1) == 1
    high = (part >> 1) == 1
    far = swap(array, "filt", 2)
    near = swap(array, "filt", 1)
    both = swap(far, "filt", 1)
    here = (jnp.where(low, near, array), jnp.where(low, array, near))
    there = (jnp.where(low, both, far), jnp.where(low, far, both))
    first = [jnp.where(high, b, a) for a, b in zip(here, there)]
    second = [jnp.where(high, a, b) for a, b in zip(here, there)]
    return first + second


def per_device(
    chars,
    lengths,
    char_table,
    conv_weight,
    conv_bias,
    highway_weight,
    highway_bias,
    proj_weight,
    proj_bias,
    position,
    norm_gain,
    norm_bias,
    query_key_value_weight,
    attention_output_weight,
    feedforward_input_weight,
    feedforward_input_bias,
    feedforward_output_weight,
    cotangent,
):
    parts = lax.axis_size("filt")
    slices = lax.axis_size("dp")
    part = lax.axis_index("filt")
    slot = lax.axis_index("dp")
    seqs, quarter, dmodel = cotangent.shape
    full_len = chars.shape[1]
    letters = chars.shape[2]
    words = seqs * full_len
    tokens = seqs * quarter
    filters = conv_weight.shape[1]
    depth = char_table.shape[1]
    heads = dmodel // HD // parts
    width = heads * HD
    inner_rows = feedforward_input_weight.shape[0]
    unit_rows = feedforward_output_weight.shape[0] // parts

    def own_columns(array, blocks):
        rows = array.shape[0]
        split = array.reshape(rows, blocks, parts, -1)
        return lax.dynamic_index_in_dim(split, part, 2, keepdims=False).reshape(rows, -1)

    def gather_rows(array):
        return lax.all_gather(array, "dp", axis=0, tiled=True)

    def rows_from_columns(proj_cols, out_cols):
        stack = jnp.concatenate([item.reshape(parts, -1, width) for item in (proj_cols, out_cols)], axis=1)
        stack = lax.all_to_all(stack, "filt", split_axis=0, concat_axis=0, tiled=True)
        whole = stack.transpose(1, 0, 2).reshape(-1, dmodel)
        return whole[: proj_cols.shape[0] // parts], whole[proj_cols.shape[0] // parts :]

    def columns_from_rows(proj_rows, out_rows):
        stack = jnp.concatenate([proj_rows, out_rows], axis=0).astype(jnp.bfloat16)
        stack = stack.reshape(-1, parts, width).transpose(1, 0, 2)
        stack = lax.all_to_all(stack, "filt", split_axis=0, concat_axis=0, tiled=True)
        split = proj_rows.shape[0]
        return stack[:, :split].reshape(-1, width), stack[:, split:].reshape(-1, width)

    fast = slices == 8 and parts == 4
    hb, pb, nd = highway_bias.shape[1], proj_bias.shape[0], norm_gain.shape[1]
    small = jnp.concatenate(
        [
            highway_bias.reshape(-1),
            proj_bias,
            norm_gain.reshape(-1),
            norm_bias.reshape(-1),
            feedforward_input_bias,
        ]
    )
    small_size = small.shape[0]
    small = jnp.pad(small, (0, -small_size % dmodel))
    slim_parts = [
        item.reshape(-1, dmodel)
        for item in (
            own_columns(query_key_value_weight, 3),
            own_columns(proj_weight, 1),
            own_columns(attention_output_weight, 1),
            small,
        )
    ]
    slim_cuts = [slim_parts[0].shape[0]]
    for item in slim_parts[1:3]:
        slim_cuts.append(slim_cuts[-1] + item.shape[0])
    slim_all = lax.all_gather(jnp.concatenate(slim_parts, axis=0), "dp", axis=0, tiled=False)
    qkv_own, proj_cols, out_cols, small = jnp.split(slim_all, slim_cuts, axis=1)
    qkv_own = qkv_own.reshape(dmodel, 3 * width)
    proj_own, out_own = rows_from_columns(proj_cols.reshape(-1, width), out_cols.reshape(-1, width))
    small = small.reshape(slices, -1)[:, :small_size].astype(jnp.float32)
    cuts = [hb, hb + pb, hb + pb + 3 * nd, hb + pb + 6 * nd]
    highway_b, proj_b, gain, shift, inner_b = jnp.split(small, cuts, axis=1)
    highway_b_own = own_columns(highway_b.reshape(1, -1), 2)
    proj_b = proj_b.reshape(-1)
    gain = gain.reshape(slices, 3, nd).transpose(1, 0, 2).reshape(3, dmodel)
    shift = shift.reshape(slices, 3, nd).transpose(1, 0, 2).reshape(3, dmodel)
    inner_b_own = own_columns(inner_b.reshape(1, -1), slices)
    ffn_own = jnp.concatenate(
        [
            own_columns(feedforward_input_weight, slices),
            lax.dynamic_slice_in_dim(feedforward_output_weight, part * unit_rows, unit_rows, 0),
        ],
        axis=0,
    )

    def blocks_of(array):
        return array.astype(jnp.bfloat16).reshape(parts, tokens, -1)

    widths = channel_widths(part * filters + jnp.arange(filters, dtype=jnp.int32))
    ids, table, weight, back, limit, count = conv_prep(
        chars.reshape(words, letters), char_table, conv_weight, conv_bias, widths
    )
    if fast:
        acts, lse, embed, features, highway_own = prologue_call(
            ids, table, weight, limit, count, highway_weight[0], parts, letters, depth, 0
        )
        highway_own = highway_own.reshape(2, -1, filters)
        gates = jnp.concatenate([nn_dot(features, item) for item in highway_own], axis=1) + highway_b_own
    else:
        acts, lse, embed = conv_forward_call(ids, table, weight, limit, count, letters, depth)
        features = gather_channels_call(acts, parts, 0)
        highway_own = gather_rows(own_columns(highway_weight[0], 2))
        gates = nn_dot(features, highway_own) + highway_b_own
    ffn_own, features = lax.optimization_barrier((ffn_own, features))
    ffn_all = lax.all_gather(ffn_own, "dp", axis=0, tiled=False)
    inner_own = ffn_all[:, : inner_rows].reshape(dmodel, -1)
    outer_own = ffn_all[:, inner_rows :].reshape(-1, dmodel)
    feature_own = acts.astype(jnp.float32)
    hidden_low = highway_mix(feature_own, gates).astype(jnp.bfloat16)
    base = position.astype(jnp.float32) + proj_b[None, :]
    first, unit_zero, scale_zero, first_all = forward_stage_call(
        blocks_of(nn_dot(hidden_low, proj_own)), base, gain[0:1], shift[0:1], EPS, 1
    )
    first_all = first_all.reshape(words, dmodel)
    packed = nn_dot(first_all, qkv_own).astype(jnp.bfloat16)
    queries, keys, values = (
        packed[:, block * width : (block + 1) * width].reshape(seqs, full_len, heads, HD)
        for block in range(3)
    )
    key_ok = jnp.arange(full_len, dtype=jnp.int32)[None, :] < lengths[:, None]
    scale = HD ** (-0.5)
    scores = (
        jnp.einsum("sqhd,skhd->shqk", queries, keys, preferred_element_type=jnp.float32) * scale
    )
    scores = jnp.where(key_ok[:, None, None, :], scores, -1e30)
    row_top = jnp.max(scores, axis=-1, keepdims=True)
    log_total = row_top + jnp.log(jnp.sum(jnp.exp(scores - row_top), axis=-1, keepdims=True))
    probs = jnp.exp(scores - log_total)
    probs_low = probs.astype(jnp.bfloat16)
    attended = (
        jnp.einsum("shqk,skhd->sqhd", probs_low, values, preferred_element_type=jnp.float32)
        .astype(jnp.bfloat16)
        .reshape(words, width)
    )
    second, unit_one, scale_one, second_all = forward_stage_call(
        blocks_of(nn_dot(attended, out_own)), first, gain[1:2], shift[1:2], EPS, 2
    )
    second_all = second_all.reshape(words, dmodel)
    inner = nn_dot(second_all, inner_own) + inner_b_own
    active = exact_gaussian_activation(inner).astype(jnp.bfloat16)
    top, d_res_two, d_gain_two, d_shift_two, d_outer = top_stage_call(
        blocks_of(nn_dot(active, outer_own)),
        second,
        cotangent.reshape(tokens, dmodel),
        gain[2:3],
        shift[2:3],
        EPS,
        3,
    )
    encoded = top.reshape(seqs, quarter, dmodel)
    d_outer = d_outer.reshape(words, dmodel)
    grad_outer = tn_dot(active, d_outer)
    d_active = nt_dot(d_outer, outer_own)
    d_inner = gelu_back(inner, d_active).astype(jnp.bfloat16)
    grad_inner = tn_dot(second_all, d_inner)
    grad_ffn = jnp.concatenate(
        [item.astype(jnp.bfloat16).reshape(slices, -1, dmodel) for item in (grad_inner, grad_outer)], axis=1
    )
    kinds = ("side", "ring") if fast else (None, None)
    if fast:
        grad_ffn = grad_ffn.reshape(4, 2, -1, dmodel)
    grad_inner_b = jnp.sum(d_inner.astype(jnp.float32), axis=0)
    d_res_one, d_gain_one, d_shift_one, unused_sum, d_mixed, *got = backward_stage_call(
        blocks_of(nt_dot(d_inner, inner_own)), d_res_two, unit_one, scale_one, gain[1:2], 4, kinds[0], grad_ffn
    )
    if fast:
        keep = lax.dynamic_index_in_dim(grad_ffn, slot % 2, 1, keepdims=False)
        grad_ffn = (keep.astype(jnp.float32) + got[0].astype(jnp.float32)).astype(jnp.bfloat16)
    d_mixed = d_mixed.reshape(words, dmodel)
    grad_out = tn_dot(attended, d_mixed)
    d_attended = nt_dot(d_mixed, out_own).astype(jnp.bfloat16)
    d_attended = d_attended.reshape(seqs, full_len, heads, HD)
    d_values = jnp.einsum(
        "shqk,sqhd->skhd", probs_low, d_attended, preferred_element_type=jnp.float32
    )
    d_probs = jnp.einsum(
        "sqhd,skhd->shqk", d_attended, values, preferred_element_type=jnp.float32
    )
    row_inner = jnp.sum(d_probs * probs, axis=-1, keepdims=True)
    d_scores = (probs * (d_probs - row_inner)).astype(jnp.bfloat16)
    d_queries = (
        jnp.einsum("shqk,skhd->sqhd", d_scores, keys, preferred_element_type=jnp.float32) * scale
    )
    d_keys = (
        jnp.einsum("shqk,sqhd->skhd", d_scores, queries, preferred_element_type=jnp.float32) * scale
    )
    d_packed = jnp.concatenate(
        [item.reshape(words, width) for item in (d_queries, d_keys, d_values)], axis=1
    ).astype(jnp.bfloat16)
    grad_qkv = tn_dot(first_all, d_packed)
    d_summed, d_gain_zero, d_shift_zero, grad_proj_b, d_projected, *got = backward_stage_call(
        blocks_of(nt_dot(d_packed, qkv_own)), d_res_one, unit_zero, scale_zero, gain[0:1], 5, kinds[1], grad_ffn
    )
    if fast:
        keep = lax.dynamic_index_in_dim(grad_ffn, slot // 2, 0, keepdims=False)
        grad_ffn = sum([item.astype(jnp.float32) for item in got[0]], keep.astype(jnp.float32))
        grad_ffn = grad_ffn.astype(jnp.bfloat16)
    grad_pos = jnp.sum(d_summed.reshape(seqs, quarter, dmodel), axis=0)
    d_projected = d_projected.reshape(words, dmodel)
    grad_proj = tn_dot(hidden_low, d_projected)
    grad_slim = jnp.concatenate(
        [
            item.astype(jnp.bfloat16).reshape(slices, -1, dmodel)
            for item in (grad_qkv, *columns_from_rows(grad_proj, grad_out))
        ],
        axis=1,
    )
    d_hidden = nt_dot(d_projected, proj_own)
    d_in, d_gates = jax.vjp(highway_mix, feature_own, gates)[1](d_hidden)
    d_gates = d_gates.astype(jnp.bfloat16)
    grad_highway = tn_dot(features, d_gates).astype(jnp.bfloat16)
    grad_highway_b = jnp.sum(d_gates.astype(jnp.float32), axis=0)
    if fast:
        d_partial = nt_dot(d_gates[:, :filters], highway_own[0]) + nt_dot(d_gates[:, filters:], highway_own[1])
    else:
        d_partial = nt_dot(d_gates, highway_own)
    d_partial = d_partial.astype(jnp.bfloat16)
    groups = table.shape[0] // depth
    if fast:
        conv_sums, table_sums, wide_all, slim_all, ffn_all = epilogue_call(
            d_partial,
            d_in,
            ids,
            embed,
            lse,
            weight,
            back,
            limit,
            count,
            grad_highway.reshape(4, 2, -1, 2 * filters),
            grad_slim.reshape(4, 2, -1, dmodel),
            grad_ffn,
            letters,
            depth,
            groups,
            6,
        )
    else:
        d_features = scatter_channels_call(d_partial, d_in, 6)
        conv_sums, table_sums = conv_backward_call(
            ids, embed, lse, d_features, weight, back, limit, count, groups, letters, depth
        )
        wide_all = jnp.stack(join_parts(reduce_rows(grad_highway)))
        slim_all = jnp.stack(join_parts(reduce_rows(grad_slim.reshape(-1, dmodel))))
        ffn_all = jnp.stack(join_parts(reduce_rows(grad_ffn.reshape(-1, dmodel))))
    table_sums = table_sums.reshape(2, groups * depth, -1).sum(0)

    def place_columns(own, blocks):
        piece = own.reshape(blocks, 1, -1)
        whole = jnp.zeros((blocks, parts, piece.shape[2]), own.dtype)
        return lax.dynamic_update_slice_in_dim(whole, piece, part, 1).reshape(-1)

    d_gain = jnp.concatenate([d_gain_zero, d_gain_one, d_gain_two])
    d_shift = jnp.concatenate([d_shift_zero, d_shift_one, d_shift_two])
    pieces = [
        place_columns(grad_highway_b, 2).reshape(slices, -1),
        grad_proj_b.reshape(slices, -1),
        d_gain.reshape(3, slices, nd).transpose(1, 0, 2).reshape(slices, -1),
        d_shift.reshape(3, slices, nd).transpose(1, 0, 2).reshape(slices, -1),
        place_columns(grad_inner_b, slices).reshape(slices, -1),
    ]
    rows = jnp.concatenate(pieces, axis=1)
    if fast:
        table_rows = -(-table_sums.shape[0] // slices)
        table_rows = -(-table_rows // 8) * 8
        padded = jnp.pad(table_sums, ((0, table_rows * slices - table_sums.shape[0]), (0, 0)))
        small_rows = -(-rows.shape[1] // 1024) * 8
        packed_rows = jnp.pad(rows, ((0, 0), (0, small_rows * 128 - rows.shape[1])))
        few = jnp.concatenate(
            [padded.reshape(slices, table_rows, 128), packed_rows.reshape(slices, small_rows, 128)], axis=1
        )
        conv_rows = filters // slices
        many = jnp.concatenate(
            [conv_sums.reshape(slices, conv_rows, 128), grad_pos.reshape(slices, -1, 128)], axis=1
        )
        many, few = total_all_call(many, few, 7)
        conv_all = many[:, :conv_rows].reshape(filters, 128).astype(jnp.float32)
        grad_pos = many[:, conv_rows:].reshape(grad_pos.shape).astype(jnp.float32)
        table_all = few[:, :table_rows].reshape(-1, 128)[: table_sums.shape[0]].astype(jnp.float32)
        own = lax.dynamic_index_in_dim(few[:, table_rows:].reshape(slices, -1), slot, 0, keepdims=False)
        own = own[: rows.shape[1]].astype(jnp.float32)
    else:
        conv_all = lax.psum(conv_sums, "dp")
        table_all, sums = lax.psum((table_sums, rows), ("dp", "filt"))
        grad_pos = lax.psum(grad_pos, "dp")
        own = lax.dynamic_index_in_dim(sums, slot, 0, keepdims=False)
    tap_rows = conv_weight.shape[0]
    tap_keep = (jnp.arange(tap_rows, dtype=jnp.int32) // depth)[:, None] < widths[None, :]
    conv_grad_w = jnp.where(tap_keep, conv_all[:, :tap_rows].T, 0.0)
    conv_grad_b = conv_all[:, tap_rows]
    g_table = table_all.reshape(groups, depth, 128).transpose(0, 2, 1).reshape(-1, depth)
    g_table = g_table[: char_table.shape[0]]

    g_highway_b, g_proj_b, g_gain, g_shift, g_inner_b = jnp.split(own, cuts)

    def join_columns(array, blocks, rows_here):
        split = array.reshape(parts, rows_here, blocks, -1).transpose(1, 2, 0, 3)
        return split.reshape(rows_here, -1).astype(jnp.float32)

    g_outer = ffn_all[:, inner_rows:].reshape(-1, dmodel).astype(jnp.float32)
    g_inner = join_columns(ffn_all[:, :inner_rows], slices, inner_rows)
    slim_list = jnp.split(slim_all, slim_cuts[:2], axis=1)
    g_qkv = join_columns(slim_list[0], 3, query_key_value_weight.shape[0])
    g_proj = join_columns(slim_list[1], 1, proj_weight.shape[0])
    g_out = join_columns(slim_list[2], 1, attention_output_weight.shape[0])
    g_highway = join_columns(wide_all, 2, highway_weight.shape[1])
    return (
        encoded,
        g_table,
        conv_grad_w,
        conv_grad_b,
        g_highway[None],
        g_highway_b[None],
        g_proj,
        g_proj_b,
        grad_pos,
        g_gain.reshape(3, nd),
        g_shift.reshape(3, nd),
        g_qkv,
        g_out,
        g_inner,
        g_inner_b,
        g_outer,
    )


def solution(mesh):
    return jax.shard_map(
        per_device,
        mesh=mesh,
        in_specs=(
            P("dp", None, None),
            P("dp"),
            P(),
            P(None, "filt"),
            P("filt"),
            P(None, "dp", None),
            P(None, "dp"),
            P("dp", None),
            P("dp"),
            P("filt", None),
            P(None, "dp"),
            P(None, "dp"),
            P("dp", None),
            P("dp", None),
            P("dp", None),
            P("dp"),
            P("dp", None),
            P("dp", "filt", None),
        ),
        out_specs=(
            P("dp", "filt", None),
            P(),
            P(None, "filt"),
            P("filt"),
            P(None, "dp", None),
            P(None, "dp"),
            P("dp", None),
            P("dp"),
            P("filt", None),
            P(None, "dp"),
            P(None, "dp"),
            P("dp", None),
            P("dp", None),
            P("dp", None),
            P("dp"),
            P("dp", None),
        ),
        check_vma=False,
    )
```

```python
import functools

import jax
import jax.numpy as jnp
from jax import lax
from jax.experimental import pallas as pl
from jax.experimental.pallas import tpu as pltpu
from jax.sharding import PartitionSpec as P

KW = 7
NF = 2048
HD = 64
EPS = 1e-12
ROOT_HALF = 0.7071067811865476
DENSITY = 0.3989422804014327

def nt_dot(left, right):
    return lax.dot_general(left, right, (((1,), (1,)), ((), ())), preferred_element_type=jnp.float32)

def nn_dot(left, right):
    return jnp.dot(left, right, preferred_element_type=jnp.float32)

def normal_cdf(values):
    return 0.5 * (1.0 + lax.erf(values * ROOT_HALF))

def char_parts(chars_ref, position, block):
    ids = chars_ref[pl.ds(position, 1), :]
    low = ids & 127
    group = ids >> 7
    onehot = (lax.broadcasted_iota(jnp.int32, (128, block), 0) == low)
    onehot = jnp.where(onehot, 1.0, 0.0).astype(jnp.bfloat16)
    return onehot, group

def conv_forward(letters, depth, chars_ref, table_ref, weight_ref, limit_ref, count_ref,
                 acts_ref, lse_ref, embed_ref, patch_ref, grid_ref):
    block = chars_ref.shape[1]
    filters = weight_ref.shape[0]
    groups = table_ref.shape[0] // depth
    lead = KW - 1
    rows = KW * depth

    @pl.when(pl.program_id(0) == 0)
    def _():
        patch_ref[:, :rows, :] = jnp.zeros((patch_ref.shape[0], rows, block), jnp.bfloat16)
        ones = lax.broadcasted_iota(jnp.int32, (128 - rows, block), 0) == 0
        tail = jnp.where(ones, 1.0, 0.0).astype(jnp.bfloat16)
        patch_ref[:, rows:, :] = jnp.broadcast_to(tail[None], (patch_ref.shape[0],) + tail.shape)

    def embed(position, carry):
        onehot, group = char_parts(chars_ref, position, block)
        looked = nn_dot(table_ref[...], onehot)
        row = looked[:depth]
        for index in range(1, groups):
            row = jnp.where(group == index, looked[index * depth : (index + 1) * depth], row)
        row = row.astype(jnp.bfloat16)
        embed_ref[pl.ds(pl.multiple_of(position * depth, depth), depth), :] = row
        for tap in range(KW):
            patch_ref[position + lead - tap, tap * depth : (tap + 1) * depth, :] = row
        return carry

    lax.fori_loop(0, letters, embed, 0, unroll=5)
    chunk = grid_ref.shape[1]
    always = letters - KW + 1
    for start in range(0, filters, chunk):
        weight = weight_ref[start : start + chunk, :]
        limit = limit_ref[start : start + chunk, :]

        def product(position, top):
            grid = nn_dot(weight, patch_ref[position + lead])
            grid_ref[position] = grid
            return jnp.maximum(top, grid)

        top = lax.fori_loop(0, always, product, jnp.full((chunk, block), -1e30, jnp.float32), unroll=11)
        for position in range(always, letters):
            grid = nn_dot(weight, patch_ref[position + lead])
            grid = jnp.where(limit >= position, grid, -1e30)
            grid_ref[position] = grid
            top = jnp.maximum(top, grid)

        def total(position, acc):
            return acc + jnp.exp(grid_ref[position] - top)

        acc = lax.fori_loop(0, letters, total, jnp.zeros((chunk, block), jnp.float32), unroll=10)
        lse = top + jnp.log(acc)
        lse_ref[start : start + chunk, :] = lse
        pooled = lse - count_ref[start : start + chunk, :]
        acts_ref[:, start : start + chunk] = (pooled * normal_cdf(pooled)).astype(jnp.bfloat16).T

def conv_backward(letters, depth, chars_ref, embed_ref, lse_ref, up_ref, weight_ref, back_ref,
                  limit_ref, count_ref, wgrad_ref, tgrad_ref, patch_ref, down_ref, pull_ref):
    block = chars_ref.shape[1]
    filters = weight_ref.shape[0]
    lead = KW - 1
    rows = KW * depth
    groups = tgrad_ref.shape[0] // (2 * depth)
    step = pl.program_id(0)

    @pl.when(step == 0)
    def _():
        wgrad_ref[...] = jnp.zeros(wgrad_ref.shape, jnp.float32)
        tgrad_ref[...] = jnp.zeros(tgrad_ref.shape, jnp.float32)
        patch_ref[letters * depth :, :] = jnp.zeros((patch_ref.shape[0] - letters * depth, block), jnp.bfloat16)

    patch_ref[: letters * depth, :] = embed_ref[...]
    down_ref[...] = jnp.zeros(down_ref.shape, jnp.float32)
    pooled = lse_ref[...] - count_ref[...]
    slope = normal_cdf(pooled) + pooled * (DENSITY * jnp.exp(-0.5 * pooled * pooled))
    pull_ref[...] = slope * up_ref[...].T.astype(jnp.float32)
    ones = jnp.where(lax.broadcasted_iota(jnp.int32, (128 - rows, block), 0) == 0, 1.0, 0.0).astype(jnp.bfloat16)

    def one(position, masked):
        start = position * depth
        if not isinstance(position, int):
            start = pl.multiple_of(start, depth)
        patch = jnp.concatenate([patch_ref[pl.ds(start, rows), :], ones], axis=0)
        grid = nn_dot(weight_ref[...], patch)
        spread = jnp.exp(grid - lse_ref[...]) * pull_ref[...]
        if masked:
            spread = jnp.where(limit_ref[...] >= position, spread, 0.0)
        spread = spread.astype(jnp.bfloat16)
        down = nn_dot(back_ref[...], spread)
        down_ref[pl.ds(start, rows), :] += down[:rows]
        wgrad_ref[...] += nt_dot(spread, patch)

    always = letters - KW + 1

    def body(position, carry):
        one(position, False)
        return carry

    lax.fori_loop(0, always, body, 0, unroll=2)
    for position in range(always, letters):
        one(position, True)

    def table(position, carry):
        onehot, group = char_parts(chars_ref, position, block)
        down = down_ref[pl.ds(pl.multiple_of(position * depth, depth), depth), :]
        high = down.astype(jnp.bfloat16)
        low = (down - high.astype(jnp.float32)).astype(jnp.bfloat16)
        zero = jnp.zeros_like(high)
        parts = [jnp.where(group == index, item, zero) for item in (high, low) for index in range(groups)]
        tgrad_ref[...] += nt_dot(jnp.concatenate(parts, axis=0), onehot)
        return carry

    lax.fori_loop(0, letters, table, 0, unroll=5)

def conv_prep(chars, char_table, conv_weight, conv_bias, widths):
    letters = chars.shape[1]
    vocab, depth = char_table.shape
    groups = -(-vocab // 128)
    table = jnp.pad(char_table, ((0, groups * 128 - vocab), (0, 0)))
    table = table.reshape(groups, 128, depth).transpose(0, 2, 1).reshape(groups * depth, 128)
    tap = jnp.arange(conv_weight.shape[0], dtype=jnp.int32) // depth
    masked = jnp.where(tap[:, None] < widths[None, :], conv_weight, 0)
    back = jnp.concatenate([masked, conv_bias[None, :], jnp.zeros((127 - masked.shape[0], masked.shape[1]), masked.dtype)], axis=0)
    limit = (letters - widths)[:, None].astype(jnp.int32)
    count = jnp.log((letters - widths + 1).astype(jnp.float32))[:, None]
    ids = jnp.pad(chars, ((0, 0), (0, -letters % 8))).T
    return ids, table, back.T, back, limit, count

def conv_forward_call(ids, table, weight, limit, count, letters, depth, block=256):
    words = ids.shape[1]
    filters = weight.shape[0]
    full = lambda a: pl.BlockSpec(a.shape, lambda i: (0,) * a.ndim)
    return pl.pallas_call(
        functools.partial(conv_forward, letters, depth),
        grid=(words // block,),
        in_specs=[pl.BlockSpec((ids.shape[0], block), lambda i: (0, i)), full(table), full(weight), full(limit), full(count)],
        out_specs=[pl.BlockSpec((block, filters), lambda i: (i, 0)), pl.BlockSpec((filters, block), lambda i: (0, i)),
                   pl.BlockSpec((letters * depth, block), lambda i: (0, i))],
        out_shape=[jax.ShapeDtypeStruct((words, filters), jnp.bfloat16), jax.ShapeDtypeStruct((filters, words), jnp.float32),
                   jax.ShapeDtypeStruct((letters * depth, words), jnp.bfloat16)],
        scratch_shapes=[pltpu.VMEM((letters + KW - 1, 128, block), jnp.bfloat16), pltpu.VMEM((letters, 128, block), jnp.float32)],
        compiler_params=pltpu.CompilerParams(vmem_limit_bytes=48 << 20),
        name="conv_forward",
    )(ids, table, weight, limit, count)

def conv_backward_call(ids, embed, lse, up, weight, back, limit, count, groups, letters, depth, block=256):
    words = ids.shape[1]
    filters = weight.shape[0]
    full = lambda a: pl.BlockSpec(a.shape, lambda i: (0,) * a.ndim)
    return pl.pallas_call(
        functools.partial(conv_backward, letters, depth),
        grid=(words // block,),
        in_specs=[pl.BlockSpec((ids.shape[0], block), lambda i: (0, i)), pl.BlockSpec((letters * depth, block), lambda i: (0, i)),
                  pl.BlockSpec((filters, block), lambda i: (0, i)), pl.BlockSpec((block, filters), lambda i: (i, 0)),
                  full(weight), full(back), full(limit), full(count)],
        out_specs=[pl.BlockSpec((filters, 128), lambda i: (0, 0)), pl.BlockSpec((2 * groups * depth, 128), lambda i: (0, 0))],
        out_shape=[jax.ShapeDtypeStruct((filters, 128), jnp.float32), jax.ShapeDtypeStruct((2 * groups * depth, 128), jnp.float32)],
        scratch_shapes=[pltpu.VMEM(((letters + KW - 1) * depth, block), jnp.bfloat16), pltpu.VMEM(((letters + KW - 1) * depth, block), jnp.float32),
                        pltpu.VMEM((filters, block), jnp.float32)],
        compiler_params=pltpu.CompilerParams(vmem_limit_bytes=48 << 20),
        name="conv_backward",
    )(ids, embed, lse, up, weight, back, limit, count)


MESH = pl.DeviceIdType.MESH

def greet(peers):
    barrier = pltpu.get_barrier_semaphore()
    for peer in peers:
        pl.semaphore_signal(barrier, inc=1, device_id=peer, device_id_type=MESH)
    pl.semaphore_wait(barrier, len(peers))

def greet_all():
    slot, me = lax.axis_index("dp"), lax.axis_index("filt")
    count, parts = lax.axis_size("dp"), lax.axis_size("filt")
    greet([{"dp": slot ^ far, "filt": me ^ near} for far in range(count) for near in range(parts) if far or near])

def remote(source, target, send, recv, peer):
    return pltpu.make_async_remote_copy(
        src_ref=source, dst_ref=target, send_sem=send, recv_sem=recv,
        device_id=peer, device_id_type=MESH)

def comm_call(kernel, out_shape, scratch, ident, *args, name):
    vmem = pl.BlockSpec(memory_space=pltpu.VMEM)
    return pl.pallas_call(
        kernel, out_shape=out_shape, in_specs=[vmem] * len(args), out_specs=jax.tree.map(lambda _: vmem, out_shape),
        scratch_shapes=scratch,
        compiler_params=pltpu.CompilerParams(collective_id=ident, has_side_effects=True, vmem_limit_bytes=40 << 20),
        name=name)(*args)

DMA = pltpu.SemaphoreType.DMA

def scatter_sum(part_ref, inbox, send, recv, me):
    copies = []
    for hop in (3, 2, 1):
        copy = remote(part_ref.at[me ^ hop], inbox.at[hop - 1], send.at[hop - 1], recv.at[hop - 1], {"filt": me ^ hop})
        copy.start()
        copies.append(copy)
    total = part_ref[me].astype(jnp.float32)
    for copy, hop in reversed(list(zip(copies, (3, 2, 1)))):
        copy.wait()
        total = total + inbox[hop - 1].astype(jnp.float32)
    return total

def gather_blocks(low, all_ref, send, recv, me):
    all_ref[me] = low
    far = remote(all_ref.at[me], all_ref.at[me], send.at[0], recv.at[0], {"filt": me ^ 2})
    near = remote(all_ref.at[me], all_ref.at[me], send.at[1], recv.at[1], {"filt": me ^ 1})
    far.start()
    near.start()
    far.wait_recv()
    relay = remote(all_ref.at[me ^ 2], all_ref.at[me ^ 2], send.at[2], recv.at[2], {"filt": me ^ 1})
    relay.start()
    far.wait_send()
    near.wait()
    relay.wait()

def norm(values, gain, shift, eps):
    center = values - jnp.mean(values, axis=-1, keepdims=True)
    scale = lax.rsqrt(jnp.mean(center * center, axis=-1, keepdims=True) + eps)
    unit = center * scale
    return unit * gain + shift, unit, scale

def norm_back(upstream, unit, scale, gain):
    lifted = upstream * gain
    drop = jnp.mean(lifted, axis=-1, keepdims=True)
    lean = jnp.mean(lifted * unit, axis=-1, keepdims=True)
    return scale * (lifted - drop - unit * lean)

def forward_stage(part_ref, base_ref, gain_ref, shift_ref, value_ref, unit_ref, scale_ref, all_ref, inbox, send, recv, eps):
    me = lax.axis_index("filt")
    greet([{"filt": me ^ hop} for hop in (1, 2, 3)])
    total = scatter_sum(part_ref, inbox, send, recv, me) + base_ref[...]
    value, unit, scale = norm(total, gain_ref[...], shift_ref[...], eps)
    value_ref[...] = value
    unit_ref[...] = unit
    scale_ref[...] = scale
    gather_blocks(value.astype(jnp.bfloat16), all_ref, send.at[pl.ds(3, 3)], recv.at[pl.ds(3, 3)], me)

def top_stage(part_ref, base_ref, up_ref, gain_ref, shift_ref, top_ref, down_ref, dgain_ref, dshift_ref, all_ref, inbox, send, recv, eps):
    me = lax.axis_index("filt")
    greet([{"filt": me ^ hop} for hop in (1, 2, 3)])
    total = scatter_sum(part_ref, inbox, send, recv, me) + base_ref[...]
    top, unit, scale = norm(total, gain_ref[...], shift_ref[...], eps)
    top_ref[...] = top.astype(jnp.bfloat16)
    up = up_ref[...].astype(jnp.float32)
    dgain_ref[...] = jnp.sum(up * unit, axis=0, keepdims=True)
    dshift_ref[...] = jnp.sum(up, axis=0, keepdims=True)
    down = norm_back(up, unit, scale, gain_ref[...])
    down_ref[...] = down
    gather_blocks(down.astype(jnp.bfloat16), all_ref, send.at[pl.ds(3, 3)], recv.at[pl.ds(3, 3)], me)

def backward_stage(kind, part_ref, base_ref, unit_ref, scale_ref, gain_ref, *refs):
    job_in, job_out, job_send, job_recv = None, None, None, None
    if kind is not None:
        (job_in, down_ref, dgain_ref, dshift_ref, dlow_ref, all_ref, job_out, inbox, send, recv, job_send, job_recv) = refs
    else:
        (down_ref, dgain_ref, dshift_ref, dlow_ref, all_ref, inbox, send, recv) = refs
    me = lax.axis_index("filt")
    slot = lax.axis_index("dp")
    others = [] if kind is None else [{"dp": slot ^ hop} for hop in job_hops(kind)]
    greet([{"filt": me ^ hop} for hop in (1, 2, 3)] + others)
    copies = [] if kind is None else start_job(kind, job_in, job_out, job_send, job_recv)
    up = scatter_sum(part_ref, inbox, send, recv, me) + base_ref[...]
    unit = unit_ref[...]
    dgain_ref[...] = jnp.sum(up * unit, axis=0, keepdims=True)
    dshift_ref[...] = jnp.sum(up, axis=0, keepdims=True)
    down = norm_back(up, unit, scale_ref[...], gain_ref[...])
    down_ref[...] = down
    low = down.astype(jnp.bfloat16)
    dlow_ref[...] = jnp.sum(low.astype(jnp.float32), axis=0, keepdims=True)
    gather_blocks(low, all_ref, send.at[pl.ds(3, 3)], recv.at[pl.ds(3, 3)], me)
    for copy in copies:
        copy.wait()

def start_job(kind, source, target, send, recv):
    slot = lax.axis_index("dp")
    ring, side = slot // 2, slot % 2
    if kind == "side":
        moves = [(source.at[:, 1 - side], target, 1)]
    else:
        moves = [(source.at[ring ^ hop], target.at[hop - 1], 2 * hop) for hop in (2, 3, 1)]
    copies = []
    for index, (piece, place, hop) in enumerate(moves):
        copy = remote(piece, place, send.at[index], recv.at[index], {"dp": slot ^ hop})
        copy.start()
        copies.append(copy)
    return copies

def job_hops(kind):
    return (1,) if kind == "side" else (2, 4, 6)

def stage_scratch(block):
    return [pltpu.VMEM((3,) + block, jnp.bfloat16), DMA((6,)), DMA((6,))]

def f32(*shape): return jax.ShapeDtypeStruct(shape, jnp.float32)
def bf16(*shape): return jax.ShapeDtypeStruct(shape, jnp.bfloat16)

def forward_stage_call(part, base, gain, shift, eps, ident):
    parts, rows, cols = part.shape
    return comm_call(functools.partial(forward_stage, eps=eps),
        (f32(rows, cols), f32(rows, cols), f32(rows, 1), bf16(parts, rows, cols)), stage_scratch((rows, cols)), ident,
        part, base, gain, shift, name="forward_stage")

def top_stage_call(part, base, up, gain, shift, eps, ident):
    parts, rows, cols = part.shape
    return comm_call(functools.partial(top_stage, eps=eps),
        (bf16(rows, cols), f32(rows, cols), f32(1, cols), f32(1, cols), bf16(parts, rows, cols)), stage_scratch((rows, cols)), ident,
        part, base, up, gain, shift, name="top_stage")

def backward_stage_call(part, base, unit, scale, gain, ident, kind=None, job=None):
    parts, rows, cols = part.shape
    vmem = pl.BlockSpec(memory_space=pltpu.VMEM)
    hbm = pl.BlockSpec(memory_space=pl.ANY)
    args = (part, base, unit, scale, gain)
    out_shape = [f32(rows, cols), f32(1, cols), f32(1, cols), f32(1, cols), bf16(parts, rows, cols)]
    in_specs, out_specs, scratch = [vmem] * 5, [vmem] * 5, stage_scratch((rows, cols))
    if kind is not None:
        ring = job.shape[0]
        args += (job,)
        in_specs.append(hbm)
        out_specs.append(hbm)
        out_shape.append(bf16(ring, *job.shape[2:]) if kind == "side" else bf16(ring - 1, *job.shape[1:]))
        scratch += [DMA((3,)), DMA((3,))]
    return pl.pallas_call(
        functools.partial(backward_stage, kind), out_shape=out_shape, in_specs=in_specs, out_specs=out_specs,
        scratch_shapes=scratch,
        compiler_params=pltpu.CompilerParams(collective_id=ident, has_side_effects=True, vmem_limit_bytes=24 << 20),
        name="backward_stage")(*args)

def gather_channels(own_ref, all_ref, send, recv, *, chunks):
    me = lax.axis_index("filt")
    greet([{"filt": me ^ hop} for hop in (1, 2)])
    rows, cols = own_ref.shape
    size = rows // chunks

    def lanes(index):
        return pl.ds(pl.multiple_of(index * cols, cols), cols)

    far, near, relay = [], [], []
    for chunk in range(chunks):
        span = pl.ds(chunk * size, size)
        copy = remote(own_ref.at[span, :], all_ref.at[span, lanes(me)], send.at[0, chunk], recv.at[0, chunk], {"filt": me ^ 2})
        copy.start()
        far.append(copy)
    for chunk in range(chunks):
        span = pl.ds(chunk * size, size)
        copy = remote(own_ref.at[span, :], all_ref.at[span, lanes(me)], send.at[1, chunk], recv.at[1, chunk], {"filt": me ^ 1})
        copy.start()
        near.append(copy)
    all_ref[:, lanes(me)] = own_ref[...]
    for chunk in range(chunks):
        span = pl.ds(chunk * size, size)
        far[chunk].wait_recv()
        piece = all_ref.at[span, lanes(me ^ 2)]
        copy = remote(piece, piece, send.at[2, chunk], recv.at[2, chunk], {"filt": me ^ 1})
        copy.start()
        relay.append(copy)
    for chunk in range(chunks):
        far[chunk].wait_send()
        near[chunk].wait()
        relay[chunk].wait()

def gather_channels_call(own, parts, ident, chunks=4):
    rows, cols = own.shape
    return comm_call(functools.partial(gather_channels, chunks=chunks), bf16(rows, cols * parts),
        [DMA((3, chunks)), DMA((3, chunks))], ident, own, name="gather_channels")

def scatter_channels(part_ref, base_ref, out_ref, inbox, merged, send, recv, *, chunks):
    me = lax.axis_index("filt")
    greet([{"filt": me ^ hop} for hop in (1, 2)])
    rows, cols = base_ref.shape
    size = rows // chunks

    def lanes(index):
        return pl.ds(pl.multiple_of(index * cols, cols), cols)

    def hop(source, slot, chunk, peer):
        span = pl.ds(chunk * size, size)
        copy = remote(source, inbox.at[slot, span, :], send.at[slot, chunk], recv.at[slot, chunk], {"filt": peer})
        copy.start()
        return copy

    first, second, third = [], [], []
    for chunk in range(chunks):
        span = pl.ds(chunk * size, size)
        first.append(hop(part_ref.at[span, lanes(me ^ 3)], 0, chunk, me ^ 1))
    for chunk in range(chunks):
        span = pl.ds(chunk * size, size)
        second.append(hop(part_ref.at[span, lanes(me ^ 1)], 1, chunk, me ^ 1))
    for chunk in range(chunks):
        span = pl.ds(chunk * size, size)
        first[chunk].wait_recv()
        both = part_ref[span, lanes(me ^ 2)].astype(jnp.float32) + inbox[0, span, :].astype(jnp.float32)
        merged[span, :] = both.astype(jnp.bfloat16)
        third.append(hop(merged.at[span, :], 2, chunk, me ^ 2))
    for chunk in range(chunks):
        span = pl.ds(chunk * size, size)
        second[chunk].wait_recv()
        third[chunk].wait_recv()
        total = part_ref[span, lanes(me)].astype(jnp.float32) + inbox[1, span, :].astype(jnp.float32)
        total = total + inbox[2, span, :].astype(jnp.float32) + base_ref[span, :]
        out_ref[span, :] = total.astype(jnp.bfloat16)
    for copy in first + second + third:
        copy.wait_send()

def scatter_channels_call(part, base, ident, chunks=4):
    rows, cols = base.shape
    return comm_call(functools.partial(scatter_channels, chunks=chunks), bf16(rows, cols),
        [pltpu.VMEM((3, rows, cols), jnp.bfloat16), pltpu.VMEM((rows, cols), jnp.bfloat16), DMA((3, chunks)), DMA((3, chunks))],
        ident, part, base, name="scatter_channels")


class Total:
    def __init__(self, low, inbox, out, send, recv, sides=None):
        self.low, self.inbox, self.out, self.sides = low, inbox, out, sides
        self.send, self.recv = send, recv
        self.me, self.slot = lax.axis_index("filt"), lax.axis_index("dp")
        self.count = low.shape[0]
        self.copies = []

    def push(self, source, target, kind, hop, peer):
        copy = remote(source, target, self.send.at[kind, hop - 1], self.recv.at[kind, hop - 1], peer)
        copy.start()
        self.copies.append(copy)
        return copy

    def start(self, value):
        self.low[...] = value.astype(jnp.bfloat16)
        self.first = [
            self.push(self.low.at[self.slot ^ hop], self.inbox.at[hop - 1], 0, hop, {"dp": self.slot ^ hop})
            for hop in range(1, self.count)
        ]

    def combine(self):
        for copy in self.first:
            copy.wait_recv()
        total = self.low[self.slot].astype(jnp.float32)
        for hop in range(1, self.count):
            total = total + self.inbox[hop - 1].astype(jnp.float32)
        self.out[self.slot] = total.astype(jnp.bfloat16)
        if self.sides is None:
            self.spread()
            return
        self.sides[0] = total.astype(jnp.bfloat16)
        self.second = [self.push(self.sides.at[0], self.sides.at[hop], 1, hop, {"filt": self.me ^ hop}) for hop in (1, 2, 3)]

    def across(self):
        for copy in self.second:
            copy.wait_recv()
        left = self.sides[0].astype(jnp.float32) + self.sides[1].astype(jnp.float32)
        right = self.sides[2].astype(jnp.float32) + self.sides[3].astype(jnp.float32)
        self.out[self.slot] = (left + right).astype(jnp.bfloat16)
        self.spread()

    def spread(self):
        piece = self.out.at[self.slot]
        self.third = [self.push(piece, piece, 2, hop, {"dp": self.slot ^ hop}) for hop in range(1, self.count)]

    def finish(self):
        for copy in self.third:
            copy.wait_recv()
        for copy in self.copies:
            copy.wait_send()


def prologue(letters, depth, block, chunks, window, first, chars_ref, table_ref, weight_ref, limit_ref, count_ref, shard_ref,
             acts_ref, lse_ref, embed_ref, all_ref, full_ref, patch_ref, grid_ref,
             zsend, zrecv, local, ysend, yrecv, fsend, frecv):
    words = chars_ref.shape[1]
    filters = weight_ref.shape[0]
    me = lax.axis_index("filt")
    slot = lax.axis_index("dp")
    ring, side = slot // 2, slot % 2
    greet([{"filt": me ^ hop} for hop in (1, 2)] + [{"dp": slot ^ hop} for hop in (1, 2, 4, 6)])
    parts = all_ref.shape[1] // filters
    span = shard_ref.shape[0] // (chunks // 2)

    def spot(chunk):
        return pl.ds((chunk // 2) * span, span), chunk % 2

    own, far = [], []

    def start_chunk(chunk):
        if chunk >= chunks:
            return
        rows, half = spot(chunk)
        source = shard_ref.at[rows, pl.ds(pl.multiple_of(half * filters * parts + me * filters, filters), filters)]
        target = full_ref.at[half, ring, side, rows, :]
        copy = pltpu.make_async_copy(source, target, local.at[chunk])
        copy.start()
        own.append(copy)
        for hop in (2, 1, 3):
            copy = remote(source, target, zsend.at[chunk, hop - 1], zrecv.at[chunk, hop - 1], {"dp": slot ^ (2 * hop)})
            copy.start()
            far.append(copy)

    for chunk in range(window):
        start_chunk(chunk)
    cross = []

    def forward_chunk(chunk):
        rows, half = spot(chunk)
        own[chunk].wait()
        for copy in far[3 * chunk : 3 * chunk + 3]:
            copy.wait_recv()
        start_chunk(chunk + window)
        piece = full_ref.at[half, :, side, rows, :]
        copy = remote(piece, piece, ysend.at[chunk], yrecv.at[chunk], {"dp": slot ^ 1})
        copy.start()
        cross.append(copy)

    lead = KW - 1
    rows = KW * depth
    groups = table_ref.shape[0] // depth
    patch_ref[:, :rows, :] = jnp.zeros((patch_ref.shape[0], rows, block), jnp.bfloat16)
    ones = lax.broadcasted_iota(jnp.int32, (128 - rows, block), 0) == 0
    tail = jnp.where(ones, 1.0, 0.0).astype(jnp.bfloat16)
    patch_ref[:, rows:, :] = jnp.broadcast_to(tail[None], (patch_ref.shape[0],) + tail.shape)
    chunk = grid_ref.shape[1]
    always = letters - KW + 1
    steps = filters // chunk
    polls = {(step // steps, step % steps): step - first for step in range(first, min(first + chunks, words // block * steps))}
    gathers = ChannelGather(acts_ref, all_ref, fsend, frecv, words // block)
    for index in range(words // block):
        cols = pl.ds(index * block, block)

        def embed(position, carry):
            ids = chars_ref[pl.ds(position, 1), cols]
            low = ids & 127
            group = ids >> 7
            onehot = lax.broadcasted_iota(jnp.int32, (128, block), 0) == low
            onehot = jnp.where(onehot, 1.0, 0.0).astype(jnp.bfloat16)
            looked = nn_dot(table_ref[...], onehot)
            row = looked[:depth]
            for part in range(1, groups):
                row = jnp.where(group == part, looked[part * depth : (part + 1) * depth], row)
            row = row.astype(jnp.bfloat16)
            embed_ref[pl.ds(pl.multiple_of(position * depth, depth), depth), cols] = row
            for tap in range(KW):
                patch_ref[position + lead - tap, tap * depth : (tap + 1) * depth, :] = row
            return carry

        lax.fori_loop(0, letters, embed, 0, unroll=5)
        for start in range(0, filters, chunk):
            weight = weight_ref[start : start + chunk, :]
            limit = limit_ref[start : start + chunk, :]

            def product(position, top):
                grid = nn_dot(weight, patch_ref[position + lead])
                grid_ref[position] = grid
                return jnp.maximum(top, grid)

            top = lax.fori_loop(0, always, product, jnp.full((chunk, block), -1e30, jnp.float32), unroll=11)
            for position in range(always, letters):
                grid = nn_dot(weight, patch_ref[position + lead])
                grid = jnp.where(limit >= position, grid, -1e30)
                grid_ref[position] = grid
                top = jnp.maximum(top, grid)

            def total(position, acc):
                return acc + jnp.exp(grid_ref[position] - top)

            acc = lax.fori_loop(0, letters, total, jnp.zeros((chunk, block), jnp.float32), unroll=10)
            lse = top + jnp.log(acc)
            lse_ref[start : start + chunk, cols] = lse
            pooled = lse - count_ref[start : start + chunk, :]
            acts_ref[cols, start : start + chunk] = (pooled * normal_cdf(pooled)).astype(jnp.bfloat16).T
            poll = polls.get((index, start // chunk))
            if poll is not None:
                forward_chunk(poll)
        gathers.send(index)
    for index in range(len(polls), chunks):
        forward_chunk(index)
    for index in range(words // block):
        gathers.relay(index)
    gathers.finish()
    for copy in far:
        copy.wait_send()
    for copy in cross:
        copy.wait()

class ChannelGather:
    def __init__(self, own_ref, all_ref, send, recv, pieces):
        self.me = lax.axis_index("filt")
        self.own, self.all, self.sems = own_ref, all_ref, (send, recv)
        self.size = own_ref.shape[0] // pieces
        self.copies = []

    def view(self, index, piece):
        cols = self.own.shape[1]
        return self.all.at[pl.ds(piece * self.size, self.size), pl.ds(pl.multiple_of(index * cols, cols), cols)]

    def push(self, source, target, kind, piece, hop):
        send, recv = self.sems
        copy = remote(source, target, send.at[kind, piece], recv.at[kind, piece], {"filt": self.me ^ hop})
        copy.start()
        self.copies.append(copy)
        return copy

    def send(self, piece):
        source = self.own.at[pl.ds(piece * self.size, self.size), :]
        target = self.view(self.me, piece)
        self.push(source, target, 0, piece, 2)
        self.push(source, target, 1, piece, 1)
        cols = self.own.shape[1]
        self.all[pl.ds(piece * self.size, self.size), pl.ds(pl.multiple_of(self.me * cols, cols), cols)] = self.own[pl.ds(piece * self.size, self.size), :]

    def relay(self, piece):
        self.copies[2 * piece].wait_recv()
        view = self.view(self.me ^ 2, piece)
        self.push(view, view, 2, piece, 1)

    def finish(self):
        for index, copy in enumerate(self.copies):
            copy.wait_send()
            if index % 2 == 1 or index >= 2 * (len(self.copies) // 3):
                copy.wait_recv()

def prologue_call(ids, table, weight, limit, count, shard, parts, letters, depth, ident, block=256, chunks=8, window=2, first=2):
    words = ids.shape[1]
    filters = weight.shape[0]
    rows = shard.shape[0]
    vmem = pl.BlockSpec(memory_space=pltpu.VMEM)
    hbm = pl.BlockSpec(memory_space=pl.ANY)
    pieces = words // block
    return pl.pallas_call(
        functools.partial(prologue, letters, depth, block, chunks, window, first),
        in_specs=[vmem] * 5 + [hbm],
        out_specs=[vmem] * 4 + [hbm],
        out_shape=[bf16(words, filters), f32(filters, words), bf16(letters * depth, words), bf16(words, filters * parts),
                   bf16(2, 4, 2, rows, filters)],
        scratch_shapes=[pltpu.VMEM((letters + KW - 1, 128, block), jnp.bfloat16), pltpu.VMEM((letters, 128, block), jnp.float32),
                        DMA((chunks, 3)), DMA((chunks, 3)), DMA((chunks,)), DMA((chunks,)), DMA((chunks,)), DMA((3, pieces)), DMA((3, pieces))],
        compiler_params=pltpu.CompilerParams(collective_id=ident, has_side_effects=True, vmem_limit_bytes=48 << 20),
        name="prologue",
    )(ids, table, weight, limit, count, shard)


class RowReduce:
    def __init__(self, grad, yin, pair, zin, joined, span, sems):
        self.grad, self.yin, self.pair, self.zin, self.joined = grad, yin, pair, zin, joined
        self.span, self.sems = span, sems
        self.me, self.slot = lax.axis_index("filt"), lax.axis_index("dp")
        self.ring, self.side = self.slot // 2, self.slot % 2
        self.copies = []

    def push(self, source, target, index, peer):
        send, recv = self.sems
        copy = remote(source, target, send.at[index], recv.at[index], peer)
        copy.start()
        self.copies.append(copy)
        return copy

    def across(self):
        span = self.span
        self.first = self.push(
            self.grad.at[:, 1 - self.side, span, :], self.yin.at[:, span, :], 0, {"dp": self.slot ^ 1}
        )

    def along(self):
        span = self.span
        self.first.wait_recv()
        if self.after is not None:
            self.after.across()
        both = self.grad[:, self.side, span, :].astype(jnp.float32) + self.yin[:, span, :].astype(jnp.float32)
        self.pair[:, span, :] = both.astype(jnp.bfloat16)
        self.rest = [
            self.push(self.pair.at[self.ring ^ hop, span, :], self.zin.at[hop - 1, span, :], hop, {"dp": self.slot ^ (2 * hop)})
            for hop in (2, 3, 1)
        ]

    def join(self):
        span = self.span
        for copy in self.rest:
            copy.wait_recv()
        total = self.pair[self.ring, span, :].astype(jnp.float32)
        for hop in (1, 2, 3):
            total = total + self.zin[hop - 1, span, :].astype(jnp.float32)
        self.joined[self.me, span, :] = total.astype(jnp.bfloat16)
        self.share()

    def share(self):
        piece = self.joined.at[self.me, self.span, :]
        self.far = self.push(piece, piece, 4, {"filt": self.me ^ 2})
        self.near = self.push(piece, piece, 5, {"filt": self.me ^ 1})

    def relay(self):
        self.far.wait_recv()
        piece = self.joined.at[self.me ^ 2, self.span, :]
        self.last = self.push(piece, piece, 6, {"filt": self.me ^ 1})

    def finish(self):
        self.near.wait_recv()
        self.last.wait_recv()
        for copy in self.copies:
            copy.wait_send()


AHEAD = 2


def epilogue(letters, depth, block, *refs):
    (part_ref, base_ref, chars_ref, embed_ref, lse_ref, weight_ref, back_ref, limit_ref, count_ref, wide_ref, slim_ref,
     rows_ref, ffn_ref, pos_ref, few_ref,
     wide_out, slim_out, rows_out, ffn_out, conv_out, table_out, pos_out, few_out,
     inbox, merged, up_ref, patch_ref, down_ref, pull_ref, wgrad_ref, tgrad_ref, wide_y, wide_p, wide_z, slim_y, slim_p, slim_z,
     rows_y, rows_p, rows_z, conv_low, conv_in, table_low, table_in, table_side, pos_low, pos_in, few_low, few_in, few_side,
     csend, crecv, rsend, rrecv, tsend, trecv) = refs
    me = lax.axis_index("filt")
    greet_all()
    pos = Total(pos_low, pos_in, pos_out, tsend.at[0], trecv.at[0])
    few = Total(few_low, few_in, few_out, tsend.at[1], trecv.at[1], few_side)
    conv_total = Total(conv_low, conv_in, conv_out, tsend.at[2], trecv.at[2])
    table_total = Total(table_low, table_in, table_out, tsend.at[3], trecv.at[3], table_side)
    wide_rows = wide_out.shape[1] // 4
    slim = RowReduce(slim_ref, slim_y, slim_p, slim_z, slim_out, pl.ds(0, slim_out.shape[1]), (rsend.at[4], rrecv.at[4]))
    both = RowReduce(rows_ref, rows_y, rows_p, rows_z, rows_out, pl.ds(0, rows_out.shape[1]), (rsend.at[6], rrecv.at[6]))
    wide = [
        RowReduce(wide_ref, wide_y, wide_p, wide_z, wide_out, pl.ds(index * wide_rows, wide_rows), (rsend.at[index], rrecv.at[index]))
        for index in range(4)
    ]
    ffn = RowReduce(None, None, None, None, ffn_out, pl.ds(0, ffn_out.shape[1]), (rsend.at[5], rrecv.at[5]))
    pos.start(pos_ref[...])
    few.start(few_ref[...])
    queue = [slim, both] + wide
    for index, item in enumerate(queue):
        item.after = queue[index + AHEAD] if index + AHEAD < len(queue) else None
    for item in queue[:AHEAD]:
        item.across()
    ffn_out[me] = ffn_ref[...]
    scatter = ChannelScatter(part_ref, base_ref, up_ref, inbox, merged, csend, crecv)
    scatter.run()
    pos.combine()
    few.combine()
    ffn.share()
    steps = iter([
        [slim.along, ffn.relay], [], [both.along, slim.join], [slim.relay], [wide[0].along, both.join],
        [both.relay, few.across], [wide[1].along, wide[0].join], [wide[0].relay], [], [],
    ])

    def advance():
        for step in next(steps):
            step()

    filters = weight_ref.shape[0]
    rows = KW * depth
    groups = tgrad_ref.shape[0] // (2 * depth)
    wgrad_ref[...] = jnp.zeros(wgrad_ref.shape, jnp.float32)
    tgrad_ref[...] = jnp.zeros(tgrad_ref.shape, jnp.float32)
    patch_ref[letters * depth :, :] = jnp.zeros((patch_ref.shape[0] - letters * depth, block), jnp.bfloat16)
    ones = jnp.where(lax.broadcasted_iota(jnp.int32, (128 - rows, block), 0) == 0, 1.0, 0.0).astype(jnp.bfloat16)
    always = letters - KW + 1
    quarter = always // 4
    for index in range(chars_ref.shape[1] // block):
        cols = pl.ds(index * block, block)
        patch_ref[: letters * depth, :] = embed_ref[:, cols]
        down_ref[...] = jnp.zeros(down_ref.shape, jnp.float32)
        pooled = lse_ref[:, cols] - count_ref[...]
        slope = normal_cdf(pooled) + pooled * (DENSITY * jnp.exp(-0.5 * pooled * pooled))
        pull_ref[...] = slope * up_ref[cols, :].T.astype(jnp.float32)

        def one(position, masked):
            start = position * depth
            if not isinstance(position, int):
                start = pl.multiple_of(start, depth)
            patch = jnp.concatenate([patch_ref[pl.ds(start, rows), :], ones], axis=0)
            grid = nn_dot(weight_ref[...], patch)
            spread = jnp.exp(grid - lse_ref[:, cols]) * pull_ref[...]
            if masked:
                spread = jnp.where(limit_ref[...] >= position, spread, 0.0)
            spread = spread.astype(jnp.bfloat16)
            down = nn_dot(back_ref[...], spread)
            down_ref[pl.ds(start, rows), :] += down[:rows]
            wgrad_ref[...] += nt_dot(spread, patch)

        def body(position, carry):
            one(position, False)
            return carry

        for lap in range(4):
            stop = always if lap == 3 else (lap + 1) * quarter
            lax.fori_loop(lap * quarter, stop, body, 0, unroll=11)
            advance()
        for position in range(always, letters):
            one(position, True)

        def table(position, carry):
            ids = chars_ref[pl.ds(position, 1), cols]
            low = ids & 127
            group = ids >> 7
            onehot = lax.broadcasted_iota(jnp.int32, (128, block), 0) == low
            onehot = jnp.where(onehot, 1.0, 0.0).astype(jnp.bfloat16)
            down = down_ref[pl.ds(pl.multiple_of(position * depth, depth), depth), :]
            high = down.astype(jnp.bfloat16)
            rest = (down - high.astype(jnp.float32)).astype(jnp.bfloat16)
            zero = jnp.zeros_like(high)
            parts = [jnp.where(group == part, item, zero) for item in (high, rest) for part in range(groups)]
            tgrad_ref[...] += nt_dot(jnp.concatenate(parts, axis=0), onehot)
            return carry

        lax.fori_loop(0, letters, table, 0, unroll=5)
        advance()
    table_rows = tgrad_ref.shape[0] // 2
    slices, size = table_low.shape[:2]
    conv_total.start(wgrad_ref[...].reshape(conv_low.shape))
    sums = tgrad_ref[:table_rows, :] + tgrad_ref[table_rows:, :]
    sums = jnp.concatenate([sums, jnp.zeros((slices * size - table_rows, sums.shape[1]), jnp.float32)], axis=0)
    table_total.start(sums.reshape(table_low.shape))
    for step in (
        wide[2].along, wide[1].join, wide[1].relay, wide[3].along, conv_total.combine, table_total.combine, wide[2].join,
        wide[2].relay, table_total.across, wide[3].join, wide[3].relay,
    ):
        step()
    for item in [ffn, slim, both, pos, few, conv_total, table_total] + wide:
        item.finish()


class ChannelScatter:
    def __init__(self, part_ref, base_ref, out_ref, inbox, merged, send, recv):
        self.part, self.base, self.out, self.inbox, self.merged = part_ref, base_ref, out_ref, inbox, merged
        self.sems = (send, recv)
        self.me = lax.axis_index("filt")

    def run(self):
        me = self.me
        rows, cols = self.base.shape
        pieces = self.sems[0].shape[1]
        size = rows // pieces

        def lanes(index):
            return pl.ds(pl.multiple_of(index * cols, cols), cols)

        def hop(source, kind, piece, peer):
            span = pl.ds(piece * size, size)
            send, recv = self.sems
            copy = remote(source, self.inbox.at[kind, span, :], send.at[kind, piece], recv.at[kind, piece], {"filt": peer})
            copy.start()
            return copy

        spans = [pl.ds(piece * size, size) for piece in range(pieces)]
        first = [hop(self.part.at[span, lanes(me ^ 3)], 0, piece, me ^ 1) for piece, span in enumerate(spans)]
        second = [hop(self.part.at[span, lanes(me ^ 1)], 1, piece, me ^ 1) for piece, span in enumerate(spans)]
        third = []
        for piece, span in enumerate(spans):
            first[piece].wait_recv()
            both = self.part[span, lanes(me ^ 2)].astype(jnp.float32) + self.inbox[0, span, :].astype(jnp.float32)
            self.merged[span, :] = both.astype(jnp.bfloat16)
            third.append(hop(self.merged.at[span, :], 2, piece, me ^ 2))
        for piece, span in enumerate(spans):
            second[piece].wait_recv()
            third[piece].wait_recv()
            total = self.part[span, lanes(me)].astype(jnp.float32) + self.inbox[1, span, :].astype(jnp.float32)
            total = total + self.inbox[2, span, :].astype(jnp.float32) + self.base[span, :]
            self.out[span, :] = total.astype(jnp.bfloat16)
        for copy in first + second + third:
            copy.wait_send()


def epilogue_call(part, base, ids, embed, lse, weight, back, limit, count, wide, slim, both, ffn, pos, few, letters, depth, groups, ident, block=256):
    filters, words = lse.shape
    args = (part, base, ids, embed, lse, weight, back, limit, count, wide, slim, both, ffn, pos, few)
    parts = part.shape[1] // filters
    slices = pos.shape[0]
    pieces = 4
    vmem = pl.BlockSpec(memory_space=pltpu.VMEM)
    table_size = -(-(-(-groups * depth // slices)) // 8) * 8

    def space(shape, dtype=jnp.bfloat16):
        return pltpu.VMEM(tuple(shape), dtype)

    def stages(array):
        ring, side, rows, cols = array.shape
        return [space((ring, rows, cols)), space((ring, rows, cols)), space((ring - 1, rows, cols))]

    def totals(shape, sides):
        spaces = [space(shape), space((shape[0] - 1,) + shape[1:])]
        return spaces + ([space((4,) + shape[1:])] if sides else [])

    conv_shape = (slices, filters // slices, 128)
    table_shape = (slices, table_size, 128)
    out_shape = [bf16(parts, *wide.shape[2:]), bf16(parts, *slim.shape[2:]), bf16(parts, *both.shape[2:]), bf16(parts, *ffn.shape), bf16(*conv_shape), bf16(*table_shape), bf16(*pos.shape), bf16(*few.shape)]
    padded = (letters + KW - 1) * depth
    return pl.pallas_call(
        functools.partial(epilogue, letters, depth, block),
        in_specs=[vmem] * len(args),
        out_specs=[vmem] * len(out_shape),
        out_shape=out_shape,
        scratch_shapes=[space((3, words, filters)), space((words, filters)), space((words, filters)), space((padded, block)),
                        space((padded, block), jnp.float32), space((filters, block), jnp.float32),
                        space((filters, 128), jnp.float32), space((2 * groups * depth, 128), jnp.float32)]
        + stages(wide) + stages(slim) + stages(both)
        + totals(conv_shape, False) + totals(table_shape, True) + totals(pos.shape, False) + totals(few.shape, True)
        + [DMA((3, pieces)), DMA((3, pieces)), DMA((7, 7)), DMA((7, 7)), DMA((4, 3, slices - 1)), DMA((4, 3, slices - 1))],
        compiler_params=pltpu.CompilerParams(collective_id=ident, has_side_effects=True, vmem_limit_bytes=56 << 20),
        name="epilogue",
    )(*args)


def assemble(wide_ref, slim_ref, both_ref, ffn_ref, wide_out, slim_out, proj_out, out_out, inner_out, outer_out):
    parts = wide_ref.shape[0]
    inner_rows = inner_out.shape[0]
    proj_rows, out_rows = proj_out.shape[0] // parts, out_out.shape[0] // parts
    filters = wide_ref.shape[2] // 2
    width = slim_ref.shape[2] // 3
    for part in range(parts):
        for half in range(2):
            start = (half * parts + part) * filters
            wide_out[:, start : start + filters] = wide_ref[part, :, half * filters : (half + 1) * filters].astype(jnp.float32)
        for block in range(3):
            start = (block * parts + part) * width
            slim_out[:, start : start + width] = slim_ref[part, :, block * width : (block + 1) * width].astype(jnp.float32)
        cols = slice(part * width, (part + 1) * width)
        for block in range(parts):
            lanes = slice(block * width, (block + 1) * width)
            proj_out[block * proj_rows : (block + 1) * proj_rows, cols] = both_ref[part, :proj_rows, lanes].astype(jnp.float32)
            out_out[block * out_rows : (block + 1) * out_rows, cols] = both_ref[part, proj_rows:, lanes].astype(jnp.float32)
        units = ffn_ref.shape[1] - inner_rows
        outer_out[part * units : (part + 1) * units, :] = ffn_ref[part, inner_rows:, :].astype(jnp.float32)
        for block in range(inner_out.shape[1] // (parts * units)):
            start = (block * parts + part) * units
            inner_out[:, start : start + units] = ffn_ref[part, :inner_rows, block * units : (block + 1) * units].astype(jnp.float32)


def assemble_call(wide, slim, both, ffn, inner_rows, out_rows):
    args = (wide, slim, both, ffn)
    parts = wide.shape[0]
    vmem = pl.BlockSpec(memory_space=pltpu.VMEM)
    units = ffn.shape[1] - inner_rows
    dmodel = both.shape[2]
    out_shape = [f32(wide.shape[1], wide.shape[2] * parts), f32(slim.shape[1], slim.shape[2] * parts),
                 f32(both.shape[1] * parts - out_rows, dmodel), f32(out_rows, dmodel), f32(inner_rows, dmodel * parts), f32(units * parts, dmodel)]
    return pl.pallas_call(
        assemble, in_specs=[vmem] * 4, out_specs=[vmem] * 6, out_shape=out_shape,
        compiler_params=pltpu.CompilerParams(vmem_limit_bytes=32 << 20), name="assemble",
    )(*args)


def exact_gaussian_activation(values):
    return jax.nn.gelu(values, approximate=False)


def gelu_back(values, upstream):
    return jax.vjp(exact_gaussian_activation, values)[1](upstream)[0]


def channel_widths(channels):
    widths = jnp.ones_like(channels)
    for power in range(6):
        widths = widths + (channels >= NF * 2**power // 64).astype(jnp.int32)
    return widths


def highway_mix(hidden, gates):
    width = hidden.shape[1]
    carry_gate = jax.nn.sigmoid(gates[:, width:])
    return carry_gate * hidden + (1.0 - carry_gate) * exact_gaussian_activation(gates[:, :width])


def tn_dot(left, right):
    return lax.dot_general(left, right, (((0,), (0,)), ((), ())), preferred_element_type=jnp.float32)


def swap(array, axis, bit):
    size = lax.axis_size(axis)
    return lax.ppermute(array, axis, [(index, index ^ bit) for index in range(size)])


def reduce_rows(array):
    count = lax.axis_size("dp")
    slot = lax.axis_index("dp")
    bits = count.bit_length() - 1
    rows, cols = array.shape
    if count != 1 << bits:
        return lax.psum_scatter(array.astype(jnp.bfloat16), "dp", scatter_dimension=0, tiled=True)
    array = array.reshape((2,) * bits + (rows // count, cols))
    for bit in range(bits):
        axis = bits - 1 - bit
        mine = (slot >> bit) & 1
        keep = lax.dynamic_index_in_dim(array, mine, axis, keepdims=False)
        give = lax.dynamic_index_in_dim(array, 1 - mine, axis, keepdims=False)
        got = swap(give.astype(jnp.bfloat16), "dp", 1 << bit)
        array = (keep.astype(jnp.float32) + got.astype(jnp.float32)).astype(jnp.bfloat16)
    return array


def join_parts(array):
    part = lax.axis_index("filt")
    low = (part & 1) == 1
    high = (part >> 1) == 1
    far = swap(array, "filt", 2)
    near = swap(array, "filt", 1)
    both = swap(far, "filt", 1)
    here = (jnp.where(low, near, array), jnp.where(low, array, near))
    there = (jnp.where(low, both, far), jnp.where(low, far, both))
    first = [jnp.where(high, b, a) for a, b in zip(here, there)]
    second = [jnp.where(high, a, b) for a, b in zip(here, there)]
    return first + second


def per_device(
    chars,
    lengths,
    char_table,
    conv_weight,
    conv_bias,
    highway_weight,
    highway_bias,
    proj_weight,
    proj_bias,
    position,
    norm_gain,
    norm_bias,
    query_key_value_weight,
    attention_output_weight,
    feedforward_input_weight,
    feedforward_input_bias,
    feedforward_output_weight,
    cotangent,
):
    parts = lax.axis_size("filt")
    slices = lax.axis_size("dp")
    part = lax.axis_index("filt")
    slot = lax.axis_index("dp")
    seqs, quarter, dmodel = cotangent.shape
    full_len = chars.shape[1]
    letters = chars.shape[2]
    words = seqs * full_len
    tokens = seqs * quarter
    filters = conv_weight.shape[1]
    depth = char_table.shape[1]
    heads = dmodel // HD // parts
    width = heads * HD
    inner_rows = feedforward_input_weight.shape[0]
    unit_rows = feedforward_output_weight.shape[0] // parts

    def own_columns(array, blocks):
        rows = array.shape[0]
        split = array.reshape(rows, blocks, parts, -1)
        return lax.dynamic_index_in_dim(split, part, 2, keepdims=False).reshape(rows, -1)

    def gather_rows(array):
        return lax.all_gather(array, "dp", axis=0, tiled=True)

    def rows_from_columns(both, split):
        rows = both.shape[1]
        both = lax.all_to_all(both.reshape(parts, -1, dmodel), "filt", split_axis=0, concat_axis=0, tiled=True)
        both = both.reshape(parts, slices // parts, rows, parts, width)
        return [
            item.transpose(1, 2, 3, 0, 4).reshape(-1, dmodel) for item in (both[:, :, :split], both[:, :, split:])
        ]

    def columns_from_rows(*grads):
        items = [
            item.astype(jnp.bfloat16).reshape(slices // parts, parts, -1, parts, width).transpose(3, 0, 2, 1, 4)
            for item in grads
        ]
        both = jnp.concatenate([item.reshape(parts, slices // parts, -1, dmodel) for item in items], axis=2)
        rows = both.shape[2]
        both = lax.all_to_all(both.reshape(parts, -1, dmodel), "filt", split_axis=0, concat_axis=0, tiled=True)
        return both.reshape(slices, rows, dmodel)

    fast = slices == 8 and parts == 4
    hb, pb, nd = highway_bias.shape[1], proj_bias.shape[0], norm_gain.shape[1]
    small = jnp.concatenate(
        [
            highway_bias.reshape(-1),
            proj_bias,
            norm_gain.reshape(-1),
            norm_bias.reshape(-1),
            feedforward_input_bias,
        ]
    )
    small_size = small.shape[0]
    small = jnp.pad(small, (0, -small_size % dmodel))
    slim_parts = [
        item.reshape(-1, dmodel)
        for item in (
            own_columns(query_key_value_weight, 3),
            own_columns(proj_weight, 1),
            own_columns(attention_output_weight, 1),
            small,
        )
    ]
    slim_cuts = [slim_parts[0].shape[0]]
    for item in slim_parts[1:3]:
        slim_cuts.append(slim_cuts[-1] + item.shape[0])
    slim_all = lax.all_gather(jnp.concatenate(slim_parts, axis=0), "dp", axis=0, tiled=False)
    qkv_own = slim_all[:, : slim_cuts[0]].reshape(dmodel, 3 * width)
    proj_own, out_own = rows_from_columns(slim_all[:, slim_cuts[0] : slim_cuts[2]], slim_cuts[1] - slim_cuts[0])
    small = slim_all[:, slim_cuts[2] :]
    small = small.reshape(slices, -1)[:, :small_size].astype(jnp.float32)
    cuts = [hb, hb + pb, hb + pb + 3 * nd, hb + pb + 6 * nd]
    highway_b, proj_b, gain, shift, inner_b = jnp.split(small, cuts, axis=1)
    highway_b_own = own_columns(highway_b.reshape(1, -1), 2)
    proj_b = proj_b.reshape(-1)
    gain = gain.reshape(slices, 3, nd).transpose(1, 0, 2).reshape(3, dmodel)
    shift = shift.reshape(slices, 3, nd).transpose(1, 0, 2).reshape(3, dmodel)
    inner_b_own = own_columns(inner_b.reshape(1, -1), slices)
    ffn_own = jnp.concatenate(
        [
            own_columns(feedforward_input_weight, slices),
            lax.dynamic_slice_in_dim(feedforward_output_weight, part * unit_rows, unit_rows, 0),
        ],
        axis=0,
    )

    def blocks_of(array):
        return array.astype(jnp.bfloat16).reshape(parts, tokens, -1)

    widths = channel_widths(part * filters + jnp.arange(filters, dtype=jnp.int32))
    ids, table, weight, back, limit, count = conv_prep(
        chars.reshape(words, letters), char_table, conv_weight, conv_bias, widths
    )
    if fast:
        acts, lse, embed, features, highway_own = prologue_call(
            ids, table, weight, limit, count, highway_weight[0], parts, letters, depth, 0
        )
        highway_own = highway_own.reshape(2, -1, filters)
        gates = jnp.concatenate([nn_dot(features, item) for item in highway_own], axis=1) + highway_b_own
    else:
        acts, lse, embed = conv_forward_call(ids, table, weight, limit, count, letters, depth)
        features = gather_channels_call(acts, parts, 0)
        highway_own = gather_rows(own_columns(highway_weight[0], 2))
        gates = nn_dot(features, highway_own) + highway_b_own
    ffn_own, features = lax.optimization_barrier((ffn_own, features))
    ffn_all = lax.all_gather(ffn_own, "dp", axis=0, tiled=False)
    feature_own = acts.astype(jnp.float32)
    hidden_low = highway_mix(feature_own, gates).astype(jnp.bfloat16)
    base = position.astype(jnp.float32) + proj_b[None, :]
    first, unit_zero, scale_zero, first_all = forward_stage_call(
        blocks_of(nn_dot(hidden_low, proj_own)), base, gain[0:1], shift[0:1], EPS, 1
    )
    first_all = first_all.reshape(words, dmodel)
    packed = nn_dot(first_all, qkv_own).astype(jnp.bfloat16)
    queries, keys, values = (
        packed[:, block * width : (block + 1) * width].reshape(seqs, full_len, heads, HD)
        for block in range(3)
    )
    key_ok = jnp.arange(full_len, dtype=jnp.int32)[None, :] < lengths[:, None]
    scale = HD ** (-0.5)
    scores = (
        jnp.einsum("sqhd,skhd->shqk", queries, keys, preferred_element_type=jnp.float32) * scale
    )
    scores = jnp.where(key_ok[:, None, None, :], scores, -1e30)
    row_top = jnp.max(scores, axis=-1, keepdims=True)
    log_total = row_top + jnp.log(jnp.sum(jnp.exp(scores - row_top), axis=-1, keepdims=True))
    probs = jnp.exp(scores - log_total)
    probs_low = probs.astype(jnp.bfloat16)
    attended = (
        jnp.einsum("shqk,skhd->sqhd", probs_low, values, preferred_element_type=jnp.float32)
        .astype(jnp.bfloat16)
        .reshape(words, width)
    )
    second, unit_one, scale_one, second_all = forward_stage_call(
        blocks_of(nn_dot(attended, out_own)), first, gain[1:2], shift[1:2], EPS, 2
    )
    second_all = second_all.reshape(words, dmodel)
    ffn_all, second_all = lax.optimization_barrier((ffn_all, second_all))
    inner_own = ffn_all[:, :inner_rows].reshape(dmodel, -1)
    outer_own = ffn_all[:, inner_rows:].reshape(-1, dmodel)
    inner = nn_dot(second_all, inner_own) + inner_b_own
    active = exact_gaussian_activation(inner).astype(jnp.bfloat16)
    top, d_res_two, d_gain_two, d_shift_two, d_outer = top_stage_call(
        blocks_of(nn_dot(active, outer_own)),
        second,
        cotangent.reshape(tokens, dmodel),
        gain[2:3],
        shift[2:3],
        EPS,
        3,
    )
    encoded = top.reshape(seqs, quarter, dmodel)
    d_outer = d_outer.reshape(words, dmodel)
    grad_outer = tn_dot(active, d_outer)
    d_active = nt_dot(d_outer, outer_own)
    d_inner = gelu_back(inner, d_active).astype(jnp.bfloat16)
    grad_inner = tn_dot(second_all, d_inner)
    grad_ffn = jnp.concatenate(
        [item.astype(jnp.bfloat16).reshape(slices, -1, dmodel) for item in (grad_inner, grad_outer)], axis=1
    )
    kinds = ("side", "ring") if fast else (None, None)
    if fast:
        grad_ffn = grad_ffn.reshape(4, 2, -1, dmodel)
    grad_inner_b = jnp.sum(d_inner.astype(jnp.float32), axis=0)
    d_res_one, d_gain_one, d_shift_one, unused_sum, d_mixed, *got = backward_stage_call(
        blocks_of(nt_dot(d_inner, inner_own)), d_res_two, unit_one, scale_one, gain[1:2], 4, kinds[0], grad_ffn
    )
    if fast:
        keep = lax.dynamic_index_in_dim(grad_ffn, slot % 2, 1, keepdims=False)
        grad_ffn = (keep.astype(jnp.float32) + got[0].astype(jnp.float32)).astype(jnp.bfloat16)
    d_mixed = d_mixed.reshape(words, dmodel)
    grad_out = tn_dot(attended, d_mixed)
    d_attended = nt_dot(d_mixed, out_own).astype(jnp.bfloat16)
    d_attended = d_attended.reshape(seqs, full_len, heads, HD)
    d_values = jnp.einsum(
        "shqk,sqhd->skhd", probs_low, d_attended, preferred_element_type=jnp.float32
    )
    d_probs = jnp.einsum(
        "sqhd,skhd->shqk", d_attended, values, preferred_element_type=jnp.float32
    )
    row_inner = jnp.sum(d_probs * probs, axis=-1, keepdims=True)
    d_scores = (probs * (d_probs - row_inner)).astype(jnp.bfloat16)
    d_queries = (
        jnp.einsum("shqk,skhd->sqhd", d_scores, keys, preferred_element_type=jnp.float32) * scale
    )
    d_keys = (
        jnp.einsum("shqk,sqhd->skhd", d_scores, queries, preferred_element_type=jnp.float32) * scale
    )
    d_packed = jnp.concatenate(
        [item.reshape(words, width) for item in (d_queries, d_keys, d_values)], axis=1
    ).astype(jnp.bfloat16)
    grad_qkv = tn_dot(first_all, d_packed).astype(jnp.bfloat16)
    d_summed, d_gain_zero, d_shift_zero, grad_proj_b, d_projected, *got = backward_stage_call(
        blocks_of(nt_dot(d_packed, qkv_own)), d_res_one, unit_zero, scale_zero, gain[0:1], 5, kinds[1], grad_ffn
    )
    if fast:
        keep = lax.dynamic_index_in_dim(grad_ffn, slot // 2, 0, keepdims=False)
        grad_ffn = sum([item.astype(jnp.float32) for item in got[0]], keep.astype(jnp.float32))
        grad_ffn = grad_ffn.astype(jnp.bfloat16)
    grad_pos = jnp.sum(d_summed.reshape(seqs, quarter, dmodel), axis=0)
    d_projected = d_projected.reshape(words, dmodel)
    grad_proj = tn_dot(hidden_low, d_projected)
    grad_both = columns_from_rows(grad_proj, grad_out)
    d_hidden = nt_dot(d_projected, proj_own)
    d_in, d_gates = jax.vjp(highway_mix, feature_own, gates)[1](d_hidden)
    d_gates = d_gates.astype(jnp.bfloat16)
    grad_highway = tn_dot(features, d_gates).astype(jnp.bfloat16)
    grad_highway_b = jnp.sum(d_gates.astype(jnp.float32), axis=0)
    if fast:
        d_partial = nt_dot(d_gates[:, :filters], highway_own[0]) + nt_dot(d_gates[:, filters:], highway_own[1])
    else:
        d_partial = nt_dot(d_gates, highway_own)
    d_partial = d_partial.astype(jnp.bfloat16)
    groups = table.shape[0] // depth

    def place_columns(own, blocks):
        piece = own.reshape(blocks, 1, -1)
        whole = jnp.zeros((blocks, parts, piece.shape[2]), own.dtype)
        return lax.dynamic_update_slice_in_dim(whole, piece, part, 1).reshape(-1)

    d_gain = jnp.concatenate([d_gain_zero, d_gain_one, d_gain_two])
    d_shift = jnp.concatenate([d_shift_zero, d_shift_one, d_shift_two])
    pieces = [
        place_columns(grad_highway_b, 2).reshape(slices, -1),
        grad_proj_b.reshape(slices, -1),
        d_gain.reshape(3, slices, nd).transpose(1, 0, 2).reshape(slices, -1),
        d_shift.reshape(3, slices, nd).transpose(1, 0, 2).reshape(slices, -1),
        place_columns(grad_inner_b, slices).reshape(slices, -1),
    ]
    rows = jnp.concatenate(pieces, axis=1)
    if fast:
        few_rows = -(-rows.shape[1] // 1024) * 8
        few = jnp.pad(rows, ((0, 0), (0, few_rows * 128 - rows.shape[1]))).reshape(slices, few_rows, 128)
        wide_all, slim_all, both_all, ffn_all, conv_all, table_all, pos_all, few = epilogue_call(
            d_partial,
            d_in,
            ids,
            embed,
            lse,
            weight,
            back,
            limit,
            count,
            grad_highway.reshape(4, 2, -1, 2 * filters),
            grad_qkv.reshape(4, 2, -1, 3 * width),
            grad_both.reshape(4, 2, -1, dmodel),
            grad_ffn,
            grad_pos.reshape(slices, -1, 128),
            few,
            letters,
            depth,
            groups,
            6,
        )
        conv_all = conv_all.reshape(filters, 128).astype(jnp.float32)
        grad_pos = pos_all.reshape(grad_pos.shape).astype(jnp.float32)
        table_all = table_all.reshape(-1, 128)[: groups * depth].astype(jnp.float32)
        own = lax.dynamic_index_in_dim(few.reshape(slices, -1), slot, 0, keepdims=False)
        own = own[: rows.shape[1]].astype(jnp.float32)
    else:
        d_features = scatter_channels_call(d_partial, d_in, 6)
        conv_sums, table_sums = conv_backward_call(
            ids, embed, lse, d_features, weight, back, limit, count, groups, letters, depth
        )
        wide_all = jnp.stack(join_parts(reduce_rows(grad_highway)))
        slim_all = jnp.stack(join_parts(reduce_rows(grad_qkv)))
        both_all = jnp.stack(join_parts(reduce_rows(grad_both.reshape(-1, dmodel))))
        ffn_all = jnp.stack(join_parts(reduce_rows(grad_ffn.reshape(-1, dmodel))))
        table_sums = table_sums.reshape(2, groups * depth, -1).sum(0)
        conv_all = lax.psum(conv_sums, "dp")
        table_all, sums = lax.psum((table_sums, rows), ("dp", "filt"))
        grad_pos = lax.psum(grad_pos, "dp")
        own = lax.dynamic_index_in_dim(sums, slot, 0, keepdims=False)
    tap_rows = conv_weight.shape[0]
    tap_keep = (jnp.arange(tap_rows, dtype=jnp.int32) // depth)[:, None] < widths[None, :]
    conv_grad_w = jnp.where(tap_keep, conv_all[:, :tap_rows].T, 0.0)
    conv_grad_b = conv_all[:, tap_rows]
    g_table = table_all.reshape(groups, depth, 128).transpose(0, 2, 1).reshape(-1, depth)
    g_table = g_table[: char_table.shape[0]]
    g_highway_b, g_proj_b, g_gain, g_shift, g_inner_b = jnp.split(own, cuts)

    if fast:
        g_highway, g_qkv, g_proj, g_out, g_inner, g_outer = assemble_call(
            wide_all, slim_all, both_all, ffn_all, inner_rows, attention_output_weight.shape[0]
        )
    else:

        def join_columns(array, blocks, rows_here):
            split = array.reshape(parts, rows_here, blocks, -1).transpose(1, 2, 0, 3)
            return split.reshape(rows_here, -1).astype(jnp.float32)

        def join_groups(array):
            split = array.reshape(parts, array.shape[1], parts, width).transpose(2, 1, 0, 3)
            return split.reshape(-1, dmodel).astype(jnp.float32)

        split = proj_weight.shape[0] // parts
        g_outer = ffn_all[:, inner_rows:].reshape(-1, dmodel).astype(jnp.float32)
        g_inner = join_columns(ffn_all[:, :inner_rows], slices, inner_rows)
        g_qkv = join_columns(slim_all, 3, query_key_value_weight.shape[0])
        g_proj = join_groups(both_all[:, :split])
        g_out = join_groups(both_all[:, split:])
        g_highway = join_columns(wide_all, 2, highway_weight.shape[1])
    return (
        encoded,
        g_table,
        conv_grad_w,
        conv_grad_b,
        g_highway[None],
        g_highway_b[None],
        g_proj,
        g_proj_b,
        grad_pos,
        g_gain.reshape(3, nd),
        g_shift.reshape(3, nd),
        g_qkv,
        g_out,
        g_inner,
        g_inner_b,
        g_outer,
    )


def solution(mesh):
    return jax.shard_map(
        per_device,
        mesh=mesh,
        in_specs=(
            P("dp", None, None),
            P("dp"),
            P(),
            P(None, "filt"),
            P("filt"),
            P(None, "dp", None),
            P(None, "dp"),
            P("dp", None),
            P("dp"),
            P("filt", None),
            P(None, "dp"),
            P(None, "dp"),
            P("dp", None),
            P("dp", None),
            P("dp", None),
            P("dp"),
            P("dp", None),
            P("dp", "filt", None),
        ),
        out_specs=(
            P("dp", "filt", None),
            P(),
            P(None, "filt"),
            P("filt"),
            P(None, "dp", None),
            P(None, "dp"),
            P("dp", None),
            P("dp"),
            P("filt", None),
            P(None, "dp"),
            P(None, "dp"),
            P("dp", None),
            P("dp", None),
            P("dp", None),
            P("dp"),
            P("dp", None),
        ),
        check_vma=False,
    )
```

```python
import functools

import jax
import jax.numpy as jnp
from jax import lax
from jax.experimental import pallas as pl
from jax.experimental.pallas import tpu as pltpu
from jax.sharding import PartitionSpec as P

KW = 7
NF = 2048
HD = 64
EPS = 1e-12
ROOT_HALF = 0.7071067811865476
DENSITY = 0.3989422804014327

def nt_dot(left, right):
    return lax.dot_general(left, right, (((1,), (1,)), ((), ())), preferred_element_type=jnp.float32)

def tn_dot(left, right):
    return lax.dot_general(left, right, (((0,), (0,)), ((), ())), preferred_element_type=jnp.float32)

def nn_dot(left, right):
    return jnp.dot(left, right, preferred_element_type=jnp.float32)

def normal_cdf(values):
    return 0.5 * (1.0 + lax.erf(values * ROOT_HALF))

def char_parts(chars_ref, position, block):
    ids = chars_ref[pl.ds(position, 1), :]
    low = ids & 127
    group = ids >> 7
    onehot = (lax.broadcasted_iota(jnp.int32, (128, block), 0) == low)
    onehot = jnp.where(onehot, 1.0, 0.0).astype(jnp.bfloat16)
    return onehot, group

def conv_forward(letters, depth, chars_ref, table_ref, weight_ref, limit_ref, count_ref,
                 acts_ref, lse_ref, embed_ref, patch_ref, grid_ref):
    block = chars_ref.shape[1]
    filters = weight_ref.shape[0]
    groups = table_ref.shape[0] // depth
    lead = KW - 1
    rows = KW * depth

    @pl.when(pl.program_id(0) == 0)
    def _():
        patch_ref[:, :rows, :] = jnp.zeros((patch_ref.shape[0], rows, block), jnp.bfloat16)
        ones = lax.broadcasted_iota(jnp.int32, (128 - rows, block), 0) == 0
        tail = jnp.where(ones, 1.0, 0.0).astype(jnp.bfloat16)
        patch_ref[:, rows:, :] = jnp.broadcast_to(tail[None], (patch_ref.shape[0],) + tail.shape)

    def embed(position, carry):
        onehot, group = char_parts(chars_ref, position, block)
        looked = nn_dot(table_ref[...], onehot)
        row = looked[:depth]
        for index in range(1, groups):
            row = jnp.where(group == index, looked[index * depth : (index + 1) * depth], row)
        row = row.astype(jnp.bfloat16)
        embed_ref[pl.ds(pl.multiple_of(position * depth, depth), depth), :] = row
        for tap in range(KW):
            patch_ref[position + lead - tap, tap * depth : (tap + 1) * depth, :] = row
        return carry

    lax.fori_loop(0, letters, embed, 0, unroll=5)
    chunk = grid_ref.shape[1]
    always = letters - KW + 1
    for start in range(0, filters, chunk):
        weight = weight_ref[start : start + chunk, :]
        limit = limit_ref[start : start + chunk, :]

        def product(position, top):
            grid = nn_dot(weight, patch_ref[position + lead])
            grid_ref[position] = grid
            return jnp.maximum(top, grid)

        top = lax.fori_loop(0, always, product, jnp.full((chunk, block), -1e30, jnp.float32), unroll=11)
        for position in range(always, letters):
            grid = nn_dot(weight, patch_ref[position + lead])
            grid = jnp.where(limit >= position, grid, -1e30)
            grid_ref[position] = grid
            top = jnp.maximum(top, grid)

        def total(position, acc):
            return acc + jnp.exp(grid_ref[position] - top)

        acc = lax.fori_loop(0, letters, total, jnp.zeros((chunk, block), jnp.float32), unroll=10)
        lse = top + jnp.log(acc)
        lse_ref[start : start + chunk, :] = lse
        pooled = lse - count_ref[start : start + chunk, :]
        acts_ref[:, start : start + chunk] = (pooled * normal_cdf(pooled)).astype(jnp.bfloat16).T

def conv_backward(letters, depth, chars_ref, embed_ref, lse_ref, up_ref, weight_ref, back_ref,
                  limit_ref, count_ref, wgrad_ref, tgrad_ref, patch_ref, down_ref, pull_ref):
    block = chars_ref.shape[1]
    filters = weight_ref.shape[0]
    lead = KW - 1
    rows = KW * depth
    groups = tgrad_ref.shape[0] // (2 * depth)
    step = pl.program_id(0)

    @pl.when(step == 0)
    def _():
        wgrad_ref[...] = jnp.zeros(wgrad_ref.shape, jnp.float32)
        tgrad_ref[...] = jnp.zeros(tgrad_ref.shape, jnp.float32)
        patch_ref[letters * depth :, :] = jnp.zeros((patch_ref.shape[0] - letters * depth, block), jnp.bfloat16)

    patch_ref[: letters * depth, :] = embed_ref[...]
    down_ref[...] = jnp.zeros(down_ref.shape, jnp.float32)
    pooled = lse_ref[...] - count_ref[...]
    slope = normal_cdf(pooled) + pooled * (DENSITY * jnp.exp(-0.5 * pooled * pooled))
    pull_ref[...] = slope * up_ref[...].T.astype(jnp.float32)
    ones = jnp.where(lax.broadcasted_iota(jnp.int32, (128 - rows, block), 0) == 0, 1.0, 0.0).astype(jnp.bfloat16)

    def one(position, masked):
        start = position * depth
        if not isinstance(position, int):
            start = pl.multiple_of(start, depth)
        patch = jnp.concatenate([patch_ref[pl.ds(start, rows), :], ones], axis=0)
        grid = nn_dot(weight_ref[...], patch)
        spread = jnp.exp(grid - lse_ref[...]) * pull_ref[...]
        if masked:
            spread = jnp.where(limit_ref[...] >= position, spread, 0.0)
        spread = spread.astype(jnp.bfloat16)
        down = nn_dot(back_ref[...], spread)
        down_ref[pl.ds(start, rows), :] += down[:rows]
        wgrad_ref[...] += nt_dot(spread, patch)

    always = letters - KW + 1

    def body(position, carry):
        one(position, False)
        return carry

    lax.fori_loop(0, always, body, 0, unroll=2)
    for position in range(always, letters):
        one(position, True)

    def table(position, carry):
        onehot, group = char_parts(chars_ref, position, block)
        down = down_ref[pl.ds(pl.multiple_of(position * depth, depth), depth), :]
        high = down.astype(jnp.bfloat16)
        low = (down - high.astype(jnp.float32)).astype(jnp.bfloat16)
        zero = jnp.zeros_like(high)
        parts = [jnp.where(group == index, item, zero) for item in (high, low) for index in range(groups)]
        tgrad_ref[...] += nt_dot(jnp.concatenate(parts, axis=0), onehot)
        return carry

    lax.fori_loop(0, letters, table, 0, unroll=5)

def conv_prep(chars, char_table, conv_weight, conv_bias, widths):
    letters = chars.shape[1]
    vocab, depth = char_table.shape
    groups = -(-vocab // 128)
    table = jnp.pad(char_table, ((0, groups * 128 - vocab), (0, 0)))
    table = table.reshape(groups, 128, depth).transpose(0, 2, 1).reshape(groups * depth, 128)
    tap = jnp.arange(conv_weight.shape[0], dtype=jnp.int32) // depth
    masked = jnp.where(tap[:, None] < widths[None, :], conv_weight, 0)
    back = jnp.concatenate([masked, conv_bias[None, :], jnp.zeros((127 - masked.shape[0], masked.shape[1]), masked.dtype)], axis=0)
    limit = (letters - widths)[:, None].astype(jnp.int32)
    count = jnp.log((letters - widths + 1).astype(jnp.float32))[:, None]
    ids = jnp.pad(chars, ((0, 0), (0, -letters % 8))).T
    return ids, table, back.T, back, limit, count

def conv_forward_call(ids, table, weight, limit, count, letters, depth, block=256):
    words = ids.shape[1]
    filters = weight.shape[0]
    full = lambda a: pl.BlockSpec(a.shape, lambda i: (0,) * a.ndim)
    return pl.pallas_call(
        functools.partial(conv_forward, letters, depth),
        grid=(words // block,),
        in_specs=[pl.BlockSpec((ids.shape[0], block), lambda i: (0, i)), full(table), full(weight), full(limit), full(count)],
        out_specs=[pl.BlockSpec((block, filters), lambda i: (i, 0)), pl.BlockSpec((filters, block), lambda i: (0, i)),
                   pl.BlockSpec((letters * depth, block), lambda i: (0, i))],
        out_shape=[jax.ShapeDtypeStruct((words, filters), jnp.bfloat16), jax.ShapeDtypeStruct((filters, words), jnp.float32),
                   jax.ShapeDtypeStruct((letters * depth, words), jnp.bfloat16)],
        scratch_shapes=[pltpu.VMEM((letters + KW - 1, 128, block), jnp.bfloat16), pltpu.VMEM((letters, 128, block), jnp.float32)],
        compiler_params=pltpu.CompilerParams(vmem_limit_bytes=48 << 20),
        name="conv_forward",
    )(ids, table, weight, limit, count)

def conv_backward_call(ids, embed, lse, up, weight, back, limit, count, groups, letters, depth, block=256):
    words = ids.shape[1]
    filters = weight.shape[0]
    full = lambda a: pl.BlockSpec(a.shape, lambda i: (0,) * a.ndim)
    return pl.pallas_call(
        functools.partial(conv_backward, letters, depth),
        grid=(words // block,),
        in_specs=[pl.BlockSpec((ids.shape[0], block), lambda i: (0, i)), pl.BlockSpec((letters * depth, block), lambda i: (0, i)),
                  pl.BlockSpec((filters, block), lambda i: (0, i)), pl.BlockSpec((block, filters), lambda i: (i, 0)),
                  full(weight), full(back), full(limit), full(count)],
        out_specs=[pl.BlockSpec((filters, 128), lambda i: (0, 0)), pl.BlockSpec((2 * groups * depth, 128), lambda i: (0, 0))],
        out_shape=[jax.ShapeDtypeStruct((filters, 128), jnp.float32), jax.ShapeDtypeStruct((2 * groups * depth, 128), jnp.float32)],
        scratch_shapes=[pltpu.VMEM(((letters + KW - 1) * depth, block), jnp.bfloat16), pltpu.VMEM(((letters + KW - 1) * depth, block), jnp.float32),
                        pltpu.VMEM((filters, block), jnp.float32)],
        compiler_params=pltpu.CompilerParams(vmem_limit_bytes=48 << 20),
        name="conv_backward",
    )(ids, embed, lse, up, weight, back, limit, count)


MESH = pl.DeviceIdType.MESH

def greet(peers):
    barrier = pltpu.get_barrier_semaphore()
    for peer in peers:
        pl.semaphore_signal(barrier, inc=1, device_id=peer, device_id_type=MESH)
    pl.semaphore_wait(barrier, len(peers))

def greet_all():
    slot, me = lax.axis_index("dp"), lax.axis_index("filt")
    count, parts = lax.axis_size("dp"), lax.axis_size("filt")
    greet([{"dp": slot ^ far, "filt": me ^ near} for far in range(count) for near in range(parts) if far or near])

def remote(source, target, send, recv, peer):
    return pltpu.make_async_remote_copy(
        src_ref=source, dst_ref=target, send_sem=send, recv_sem=recv,
        device_id=peer, device_id_type=MESH)

def comm_call(kernel, out_shape, scratch, ident, *args, name):
    vmem = pl.BlockSpec(memory_space=pltpu.VMEM)
    return pl.pallas_call(
        kernel, out_shape=out_shape, in_specs=[vmem] * len(args), out_specs=jax.tree.map(lambda _: vmem, out_shape),
        scratch_shapes=scratch,
        compiler_params=pltpu.CompilerParams(collective_id=ident, has_side_effects=True, vmem_limit_bytes=40 << 20),
        name=name)(*args)

DMA = pltpu.SemaphoreType.DMA

def scatter_sum(part_ref, inbox, send, recv, me):
    copies = []
    for hop in (3, 2, 1):
        copy = remote(part_ref.at[me ^ hop], inbox.at[hop - 1], send.at[hop - 1], recv.at[hop - 1], {"filt": me ^ hop})
        copy.start()
        copies.append(copy)
    total = part_ref[me].astype(jnp.float32)
    for copy, hop in reversed(list(zip(copies, (3, 2, 1)))):
        copy.wait()
        total = total + inbox[hop - 1].astype(jnp.float32)
    return total

def gather_blocks(low, all_ref, send, recv, me):
    all_ref[me] = low
    far = remote(all_ref.at[me], all_ref.at[me], send.at[0], recv.at[0], {"filt": me ^ 2})
    near = remote(all_ref.at[me], all_ref.at[me], send.at[1], recv.at[1], {"filt": me ^ 1})
    far.start()
    near.start()
    far.wait_recv()
    relay = remote(all_ref.at[me ^ 2], all_ref.at[me ^ 2], send.at[2], recv.at[2], {"filt": me ^ 1})
    relay.start()
    far.wait_send()
    near.wait()
    relay.wait()

def norm(values, gain, shift, eps):
    center = values - jnp.mean(values, axis=-1, keepdims=True)
    scale = lax.rsqrt(jnp.mean(center * center, axis=-1, keepdims=True) + eps)
    unit = center * scale
    return unit * gain + shift, unit, scale

def norm_back(upstream, unit, scale, gain):
    lifted = upstream * gain
    drop = jnp.mean(lifted, axis=-1, keepdims=True)
    lean = jnp.mean(lifted * unit, axis=-1, keepdims=True)
    return scale * (lifted - drop - unit * lean)

def forward_stage(part_ref, base_ref, gain_ref, shift_ref, value_ref, unit_ref, scale_ref, all_ref, inbox, send, recv, eps):
    me = lax.axis_index("filt")
    greet([{"filt": me ^ hop} for hop in (1, 2, 3)])
    total = scatter_sum(part_ref, inbox, send, recv, me) + base_ref[...]
    value, unit, scale = norm(total, gain_ref[...], shift_ref[...], eps)
    value_ref[...] = value
    unit_ref[...] = unit
    scale_ref[...] = scale
    gather_blocks(value.astype(jnp.bfloat16), all_ref, send.at[pl.ds(3, 3)], recv.at[pl.ds(3, 3)], me)

def top_stage(part_ref, base_ref, up_ref, gain_ref, shift_ref, top_ref, down_ref, dgain_ref, dshift_ref, all_ref, inbox, send, recv, eps):
    me = lax.axis_index("filt")
    greet([{"filt": me ^ hop} for hop in (1, 2, 3)])
    total = scatter_sum(part_ref, inbox, send, recv, me) + base_ref[...]
    top, unit, scale = norm(total, gain_ref[...], shift_ref[...], eps)
    top_ref[...] = top.astype(jnp.bfloat16)
    up = up_ref[...].astype(jnp.float32)
    dgain_ref[...] = jnp.sum(up * unit, axis=0, keepdims=True)
    dshift_ref[...] = jnp.sum(up, axis=0, keepdims=True)
    down = norm_back(up, unit, scale, gain_ref[...])
    down_ref[...] = down
    gather_blocks(down.astype(jnp.bfloat16), all_ref, send.at[pl.ds(3, 3)], recv.at[pl.ds(3, 3)], me)

def start_job(kind, source, target, send, recv):
    slot = lax.axis_index("dp")
    ring, side = slot // 2, slot % 2
    if kind == "side":
        moves = [(source.at[:, 1 - side], target, 1)]
    else:
        moves = [(source.at[ring ^ hop], target.at[hop - 1], 2 * hop) for hop in (2, 3, 1)]
    copies = []
    for index, (piece, place, hop) in enumerate(moves):
        copy = remote(piece, place, send.at[index], recv.at[index], {"dp": slot ^ hop})
        copy.start()
        copies.append(copy)
    return copies

def job_hops(kind):
    return (1,) if kind == "side" else (2, 4, 6)

def backward_stage(kinds, part_ref, base_ref, unit_ref, scale_ref, gain_ref, *refs):
    many = len(kinds)
    job_in, refs = refs[:many], refs[many:]
    (down_ref, dgain_ref, dshift_ref, dlow_ref, all_ref), refs = refs[:5], refs[5:]
    job_out, refs = refs[:many], refs[many:]
    inbox, send, recv = refs[:3]
    me = lax.axis_index("filt")
    slot = lax.axis_index("dp")
    hops = sorted({hop for kind in kinds for hop in job_hops(kind)})
    greet([{"filt": me ^ hop} for hop in (1, 2, 3)] + [{"dp": slot ^ hop} for hop in hops])
    copies = []
    for index, kind in enumerate(kinds):
        copies += start_job(kind, job_in[index], job_out[index], refs[3].at[index], refs[4].at[index])
    up = scatter_sum(part_ref, inbox, send, recv, me) + base_ref[...]
    unit = unit_ref[...]
    dgain_ref[...] = jnp.sum(up * unit, axis=0, keepdims=True)
    dshift_ref[...] = jnp.sum(up, axis=0, keepdims=True)
    down = norm_back(up, unit, scale_ref[...], gain_ref[...])
    down_ref[...] = down
    low = down.astype(jnp.bfloat16)
    dlow_ref[...] = jnp.sum(low.astype(jnp.float32), axis=0, keepdims=True)
    gather_blocks(low, all_ref, send.at[pl.ds(3, 3)], recv.at[pl.ds(3, 3)], me)
    for copy in copies:
        copy.wait()

def stage_scratch(block):
    return [pltpu.VMEM((3,) + block, jnp.bfloat16), DMA((6,)), DMA((6,))]

def f32(*shape): return jax.ShapeDtypeStruct(shape, jnp.float32)
def bf16(*shape): return jax.ShapeDtypeStruct(shape, jnp.bfloat16)

def forward_stage_call(part, base, gain, shift, eps, ident):
    parts, rows, cols = part.shape
    return comm_call(functools.partial(forward_stage, eps=eps),
        (f32(rows, cols), f32(rows, cols), f32(rows, 1), bf16(parts, rows, cols)), stage_scratch((rows, cols)), ident,
        part, base, gain, shift, name="forward_stage")

def top_stage_call(part, base, up, gain, shift, eps, ident):
    parts, rows, cols = part.shape
    return comm_call(functools.partial(top_stage, eps=eps),
        (bf16(rows, cols), f32(rows, cols), f32(1, cols), f32(1, cols), bf16(parts, rows, cols)), stage_scratch((rows, cols)), ident,
        part, base, up, gain, shift, name="top_stage")

def backward_stage_call(part, base, unit, scale, gain, ident, kinds=(), jobs=()):
    parts, rows, cols = part.shape
    vmem = pl.BlockSpec(memory_space=pltpu.VMEM)
    hbm = pl.BlockSpec(memory_space=pl.ANY)
    out_shape = [f32(rows, cols), f32(1, cols), f32(1, cols), f32(1, cols), bf16(parts, rows, cols)]
    scratch = stage_scratch((rows, cols))
    for kind, job in zip(kinds, jobs):
        ring = job.shape[0]
        out_shape.append(bf16(ring, *job.shape[2:]) if kind == "side" else bf16(ring - 1, *job.shape[1:]))
    if kinds:
        scratch += [DMA((len(kinds), 3)), DMA((len(kinds), 3))]
    return pl.pallas_call(
        functools.partial(backward_stage, kinds), out_shape=out_shape, in_specs=[vmem] * 5 + [hbm] * len(kinds),
        out_specs=[vmem] * 5 + [hbm] * len(kinds), scratch_shapes=scratch,
        compiler_params=pltpu.CompilerParams(collective_id=ident, has_side_effects=True, vmem_limit_bytes=24 << 20),
        name="backward_stage")(part, base, unit, scale, gain, *jobs)

def gather_channels(own_ref, all_ref, send, recv, *, chunks):
    me = lax.axis_index("filt")
    greet([{"filt": me ^ hop} for hop in (1, 2)])
    rows, cols = own_ref.shape
    size = rows // chunks

    def lanes(index):
        return pl.ds(pl.multiple_of(index * cols, cols), cols)

    far, near, relay = [], [], []
    for chunk in range(chunks):
        span = pl.ds(chunk * size, size)
        copy = remote(own_ref.at[span, :], all_ref.at[span, lanes(me)], send.at[0, chunk], recv.at[0, chunk], {"filt": me ^ 2})
        copy.start()
        far.append(copy)
    for chunk in range(chunks):
        span = pl.ds(chunk * size, size)
        copy = remote(own_ref.at[span, :], all_ref.at[span, lanes(me)], send.at[1, chunk], recv.at[1, chunk], {"filt": me ^ 1})
        copy.start()
        near.append(copy)
    all_ref[:, lanes(me)] = own_ref[...]
    for chunk in range(chunks):
        span = pl.ds(chunk * size, size)
        far[chunk].wait_recv()
        piece = all_ref.at[span, lanes(me ^ 2)]
        copy = remote(piece, piece, send.at[2, chunk], recv.at[2, chunk], {"filt": me ^ 1})
        copy.start()
        relay.append(copy)
    for chunk in range(chunks):
        far[chunk].wait_send()
        near[chunk].wait()
        relay[chunk].wait()

def gather_channels_call(own, parts, ident, chunks=4):
    rows, cols = own.shape
    return comm_call(functools.partial(gather_channels, chunks=chunks), bf16(rows, cols * parts),
        [DMA((3, chunks)), DMA((3, chunks))], ident, own, name="gather_channels")

def scatter_channels(part_ref, base_ref, out_ref, inbox, merged, send, recv, *, chunks):
    me = lax.axis_index("filt")
    greet([{"filt": me ^ hop} for hop in (1, 2)])
    rows, cols = base_ref.shape
    size = rows // chunks

    def lanes(index):
        return pl.ds(pl.multiple_of(index * cols, cols), cols)

    def hop(source, slot, chunk, peer):
        span = pl.ds(chunk * size, size)
        copy = remote(source, inbox.at[slot, span, :], send.at[slot, chunk], recv.at[slot, chunk], {"filt": peer})
        copy.start()
        return copy

    first, second, third = [], [], []
    for chunk in range(chunks):
        span = pl.ds(chunk * size, size)
        first.append(hop(part_ref.at[span, lanes(me ^ 3)], 0, chunk, me ^ 1))
    for chunk in range(chunks):
        span = pl.ds(chunk * size, size)
        second.append(hop(part_ref.at[span, lanes(me ^ 1)], 1, chunk, me ^ 1))
    for chunk in range(chunks):
        span = pl.ds(chunk * size, size)
        first[chunk].wait_recv()
        both = part_ref[span, lanes(me ^ 2)].astype(jnp.float32) + inbox[0, span, :].astype(jnp.float32)
        merged[span, :] = both.astype(jnp.bfloat16)
        third.append(hop(merged.at[span, :], 2, chunk, me ^ 2))
    for chunk in range(chunks):
        span = pl.ds(chunk * size, size)
        second[chunk].wait_recv()
        third[chunk].wait_recv()
        total = part_ref[span, lanes(me)].astype(jnp.float32) + inbox[1, span, :].astype(jnp.float32)
        total = total + inbox[2, span, :].astype(jnp.float32) + base_ref[span, :]
        out_ref[span, :] = total.astype(jnp.bfloat16)
    for copy in first + second + third:
        copy.wait_send()

def scatter_channels_call(part, base, ident, chunks=4):
    rows, cols = base.shape
    return comm_call(functools.partial(scatter_channels, chunks=chunks), bf16(rows, cols),
        [pltpu.VMEM((3, rows, cols), jnp.bfloat16), pltpu.VMEM((rows, cols), jnp.bfloat16), DMA((3, chunks)), DMA((3, chunks))],
        ident, part, base, name="scatter_channels")


class Total:
    def __init__(self, low, inbox, out, send, recv, sides=None):
        self.low, self.inbox, self.out, self.sides = low, inbox, out, sides
        self.send, self.recv = send, recv
        self.me, self.slot = lax.axis_index("filt"), lax.axis_index("dp")
        self.count = low.shape[0]
        self.copies = []

    def push(self, source, target, kind, hop, peer):
        copy = remote(source, target, self.send.at[kind, hop - 1], self.recv.at[kind, hop - 1], peer)
        copy.start()
        self.copies.append(copy)
        return copy

    def start(self, value):
        self.low[...] = value.astype(jnp.bfloat16)
        self.first = [
            self.push(self.low.at[self.slot ^ hop], self.inbox.at[hop - 1], 0, hop, {"dp": self.slot ^ hop})
            for hop in range(1, self.count)
        ]

    def combine(self):
        for copy in self.first:
            copy.wait_recv()
        total = self.low[self.slot].astype(jnp.float32)
        for hop in range(1, self.count):
            total = total + self.inbox[hop - 1].astype(jnp.float32)
        self.out[self.slot] = total.astype(jnp.bfloat16)
        if self.sides is None:
            self.spread()
            return
        self.sides[0] = total.astype(jnp.bfloat16)
        self.second = [self.push(self.sides.at[0], self.sides.at[hop], 1, hop, {"filt": self.me ^ hop}) for hop in (1, 2, 3)]

    def across(self):
        for copy in self.second:
            copy.wait_recv()
        left = self.sides[0].astype(jnp.float32) + self.sides[1].astype(jnp.float32)
        right = self.sides[2].astype(jnp.float32) + self.sides[3].astype(jnp.float32)
        self.out[self.slot] = (left + right).astype(jnp.bfloat16)
        self.spread()

    def spread(self):
        piece = self.out.at[self.slot]
        self.third = [self.push(piece, piece, 2, hop, {"dp": self.slot ^ hop}) for hop in range(1, self.count)]

    def finish(self):
        for copy in self.third:
            copy.wait_recv()
        for copy in self.copies:
            copy.wait_send()


def prologue(letters, depth, block, chunks, window, first, chars_ref, table_ref, weight_ref, limit_ref, count_ref, shard_ref,
             acts_ref, lse_ref, embed_ref, all_ref, full_ref, patch_ref, grid_ref,
             zsend, zrecv, local, ysend, yrecv, fsend, frecv):
    words = chars_ref.shape[1]
    filters = weight_ref.shape[0]
    me = lax.axis_index("filt")
    slot = lax.axis_index("dp")
    ring, side = slot // 2, slot % 2
    greet([{"filt": me ^ hop} for hop in (1, 2)] + [{"dp": slot ^ hop} for hop in (1, 2, 4, 6)])
    parts = all_ref.shape[1] // filters
    span = shard_ref.shape[0] // (chunks // 2)

    def spot(chunk):
        return pl.ds((chunk // 2) * span, span), chunk % 2

    own, far = [], []

    def start_chunk(chunk):
        if chunk >= chunks:
            return
        rows, half = spot(chunk)
        source = shard_ref.at[rows, pl.ds(pl.multiple_of(half * filters * parts + me * filters, filters), filters)]
        target = full_ref.at[half, ring, side, rows, :]
        copy = pltpu.make_async_copy(source, target, local.at[chunk])
        copy.start()
        own.append(copy)
        for hop in (2, 1, 3):
            copy = remote(source, target, zsend.at[chunk, hop - 1], zrecv.at[chunk, hop - 1], {"dp": slot ^ (2 * hop)})
            copy.start()
            far.append(copy)

    for chunk in range(window):
        start_chunk(chunk)
    cross = []

    def forward_chunk(chunk):
        rows, half = spot(chunk)
        own[chunk].wait()
        for copy in far[3 * chunk : 3 * chunk + 3]:
            copy.wait_recv()
        start_chunk(chunk + window)
        piece = full_ref.at[half, :, side, rows, :]
        copy = remote(piece, piece, ysend.at[chunk], yrecv.at[chunk], {"dp": slot ^ 1})
        copy.start()
        cross.append(copy)

    lead = KW - 1
    rows = KW * depth
    groups = table_ref.shape[0] // depth
    patch_ref[:, :rows, :] = jnp.zeros((patch_ref.shape[0], rows, block), jnp.bfloat16)
    ones = lax.broadcasted_iota(jnp.int32, (128 - rows, block), 0) == 0
    tail = jnp.where(ones, 1.0, 0.0).astype(jnp.bfloat16)
    patch_ref[:, rows:, :] = jnp.broadcast_to(tail[None], (patch_ref.shape[0],) + tail.shape)
    chunk = grid_ref.shape[1]
    always = letters - KW + 1
    steps = filters // chunk
    polls = {(step // steps, step % steps): step - first for step in range(first, min(first + chunks, words // block * steps))}
    gathers = ChannelGather(acts_ref, all_ref, fsend, frecv, words // block)
    for index in range(words // block):
        cols = pl.ds(index * block, block)

        def embed(position, carry):
            ids = chars_ref[pl.ds(position, 1), cols]
            low = ids & 127
            group = ids >> 7
            onehot = lax.broadcasted_iota(jnp.int32, (128, block), 0) == low
            onehot = jnp.where(onehot, 1.0, 0.0).astype(jnp.bfloat16)
            looked = nn_dot(table_ref[...], onehot)
            row = looked[:depth]
            for part in range(1, groups):
                row = jnp.where(group == part, looked[part * depth : (part + 1) * depth], row)
            row = row.astype(jnp.bfloat16)
            embed_ref[pl.ds(pl.multiple_of(position * depth, depth), depth), cols] = row
            for tap in range(KW):
                patch_ref[position + lead - tap, tap * depth : (tap + 1) * depth, :] = row
            return carry

        lax.fori_loop(0, letters, embed, 0, unroll=5)
        for start in range(0, filters, chunk):
            weight = weight_ref[start : start + chunk, :]
            limit = limit_ref[start : start + chunk, :]

            def product(position, top):
                grid = nn_dot(weight, patch_ref[position + lead])
                grid_ref[position] = grid
                return jnp.maximum(top, grid)

            top = lax.fori_loop(0, always, product, jnp.full((chunk, block), -1e30, jnp.float32), unroll=11)
            for position in range(always, letters):
                grid = nn_dot(weight, patch_ref[position + lead])
                grid = jnp.where(limit >= position, grid, -1e30)
                grid_ref[position] = grid
                top = jnp.maximum(top, grid)

            def total(position, acc):
                return acc + jnp.exp(grid_ref[position] - top)

            acc = lax.fori_loop(0, letters, total, jnp.zeros((chunk, block), jnp.float32), unroll=10)
            lse = top + jnp.log(acc)
            lse_ref[start : start + chunk, cols] = lse
            pooled = lse - count_ref[start : start + chunk, :]
            acts_ref[cols, start : start + chunk] = (pooled * normal_cdf(pooled)).astype(jnp.bfloat16).T
            poll = polls.get((index, start // chunk))
            if poll is not None:
                forward_chunk(poll)
        gathers.send(index)
    for index in range(len(polls), chunks):
        forward_chunk(index)
    for index in range(words // block):
        gathers.relay(index)
    gathers.finish()
    for copy in far:
        copy.wait_send()
    for copy in cross:
        copy.wait()

class ChannelGather:
    def __init__(self, own_ref, all_ref, send, recv, pieces):
        self.me = lax.axis_index("filt")
        self.own, self.all, self.sems = own_ref, all_ref, (send, recv)
        self.size = own_ref.shape[0] // pieces
        self.copies = []

    def view(self, index, piece):
        cols = self.own.shape[1]
        return self.all.at[pl.ds(piece * self.size, self.size), pl.ds(pl.multiple_of(index * cols, cols), cols)]

    def push(self, source, target, kind, piece, hop):
        send, recv = self.sems
        copy = remote(source, target, send.at[kind, piece], recv.at[kind, piece], {"filt": self.me ^ hop})
        copy.start()
        self.copies.append(copy)
        return copy

    def send(self, piece):
        source = self.own.at[pl.ds(piece * self.size, self.size), :]
        target = self.view(self.me, piece)
        self.push(source, target, 0, piece, 2)
        self.push(source, target, 1, piece, 1)
        cols = self.own.shape[1]
        self.all[pl.ds(piece * self.size, self.size), pl.ds(pl.multiple_of(self.me * cols, cols), cols)] = self.own[pl.ds(piece * self.size, self.size), :]

    def relay(self, piece):
        self.copies[2 * piece].wait_recv()
        view = self.view(self.me ^ 2, piece)
        self.push(view, view, 2, piece, 1)

    def finish(self):
        for index, copy in enumerate(self.copies):
            copy.wait_send()
            if index % 2 == 1 or index >= 2 * (len(self.copies) // 3):
                copy.wait_recv()

def prologue_call(ids, table, weight, limit, count, shard, parts, letters, depth, ident, block=256, chunks=8, window=2, first=2):
    words = ids.shape[1]
    filters = weight.shape[0]
    rows = shard.shape[0]
    vmem = pl.BlockSpec(memory_space=pltpu.VMEM)
    hbm = pl.BlockSpec(memory_space=pl.ANY)
    pieces = words // block
    return pl.pallas_call(
        functools.partial(prologue, letters, depth, block, chunks, window, first),
        in_specs=[vmem] * 5 + [hbm],
        out_specs=[vmem] * 4 + [hbm],
        out_shape=[bf16(words, filters), f32(filters, words), bf16(letters * depth, words), bf16(words, filters * parts),
                   bf16(2, 4, 2, rows, filters)],
        scratch_shapes=[pltpu.VMEM((letters + KW - 1, 128, block), jnp.bfloat16), pltpu.VMEM((letters, 128, block), jnp.float32),
                        DMA((chunks, 3)), DMA((chunks, 3)), DMA((chunks,)), DMA((chunks,)), DMA((chunks,)), DMA((3, pieces)), DMA((3, pieces))],
        compiler_params=pltpu.CompilerParams(collective_id=ident, has_side_effects=True, vmem_limit_bytes=48 << 20),
        name="prologue",
    )(ids, table, weight, limit, count, shard)


def sigmoid(values):
    return 1.0 / (1.0 + jnp.exp(-values))


def highway_stage(eps, slim_ref, feats_ref, wide_ref, bias_ref, acts_ref, base_ref, gain_ref, shift_ref,
                  gates_ref, hidden_ref, proj_ref, out_ref, value_ref, unit_ref, scale_ref, all_ref,
                  abox, part_ref, inbox, send, recv, asend, arecv):
    me = lax.axis_index("filt")
    greet([{"filt": me ^ hop} for hop in (1, 2, 3)])
    parts, sides, rows, dmodel = abox.shape
    copies = []
    for hop in (2, 3, 1):
        source = slim_ref.at[pl.ds(sides * (me ^ hop), sides), pl.ds(0, rows), :]
        copy = remote(source, abox.at[me], asend.at[hop - 1], arecv.at[hop - 1], {"filt": me ^ hop})
        copy.start()
        copies.append(copy)
    own = pltpu.make_async_copy(slim_ref.at[pl.ds(sides * me, sides), pl.ds(0, rows), :], abox.at[me], asend.at[3])
    own.start()
    words, filters = acts_ref.shape
    block = 256

    def mix(index, carry):
        span = pl.ds(pl.multiple_of(index * block, block), block)
        feats = feats_ref[span, :]
        turn = nn_dot(feats, wide_ref[0]) + bias_ref[:, :filters]
        gates_ref[span, :filters] = turn
        gate = nn_dot(feats, wide_ref[1]) + bias_ref[:, filters:]
        gates_ref[span, filters:] = gate
        keep = sigmoid(gate)
        mixed = keep * acts_ref[span, :].astype(jnp.float32) + (1.0 - keep) * (turn * normal_cdf(turn))
        hidden_ref[span, :] = mixed.astype(jnp.bfloat16)
        return carry

    lax.fori_loop(0, words // block, mix, 0)
    own.wait()
    for copy in copies:
        copy.wait()
    width = dmodel // parts
    size, small = proj_ref.shape[0] // (sides * parts), out_ref.shape[0] // (sides * (parts - 1))
    for part in range(parts):
        cols = slice(part * width, (part + 1) * width)
        for side in range(sides):
            for group in range(parts):
                lanes = slice(group * width, (group + 1) * width)
                start = (side * parts + group) * size
                proj_ref[start : start + size, cols] = abox[part, side, :size, lanes]
                if group < parts - 1:
                    start = (side * (parts - 1) + group) * small
                    out_ref[start : start + small, cols] = abox[part, side, size:, lanes]

    def project(index, carry):
        span = pl.ds(pl.multiple_of(index * 128, 128), 128)
        part_ref[index] = nn_dot(hidden_ref[span, :], proj_ref[...]).astype(jnp.bfloat16)
        return carry

    lax.fori_loop(0, parts, project, 0)
    total = scatter_sum(part_ref, inbox, send, recv, me) + base_ref[...]
    value, unit, scale = norm(total, gain_ref[...], shift_ref[...], eps)
    value_ref[...] = value
    unit_ref[...] = unit
    scale_ref[...] = scale
    gather_blocks(value.astype(jnp.bfloat16), all_ref, send.at[pl.ds(3, 3)], recv.at[pl.ds(3, 3)], me)


def highway_stage_call(slim, feats, wide, bias, acts, base, gain, shift, out_rows, po_rows, eps, ident):
    words, filters = acts.shape
    rows, dmodel = base.shape
    parts = words // rows
    vmem = pl.BlockSpec(memory_space=pltpu.VMEM)
    hbm = pl.BlockSpec(memory_space=pl.ANY)
    return pl.pallas_call(
        functools.partial(highway_stage, eps), in_specs=[hbm] + [vmem] * 7, out_specs=[vmem] * 8,
        out_shape=[f32(words, 2 * filters), bf16(words, filters), bf16(filters, dmodel), bf16(out_rows, dmodel), f32(rows, dmodel),
                   f32(rows, dmodel), f32(rows, 1), bf16(parts, rows, dmodel)],
        scratch_shapes=[pltpu.VMEM((parts, 2, po_rows, dmodel), jnp.bfloat16), pltpu.VMEM((parts, rows, dmodel), jnp.bfloat16)]
        + stage_scratch((rows, dmodel)) + [DMA((4,)), DMA((3,))],
        compiler_params=pltpu.CompilerParams(collective_id=ident, has_side_effects=True, vmem_limit_bytes=48 << 20),
        name="highway_stage",
    )(slim, feats, wide, bias, acts, base, gain, shift)


def highway_back(dproj_ref, proj_ref, hidden_ref, gates_ref, acts_ref, feats_ref, wide_ref, attended_ref, dmixed_ref,
                 part_ref, din_ref, grad_ref, both_ref, bias_ref, dgates_ref):
    words, filters = acts_ref.shape
    block = 128
    bias_ref[...] = jnp.zeros(bias_ref.shape, jnp.float32)

    def mix(index, carry):
        span = pl.ds(pl.multiple_of(index * block, block), block)
        dhidden = nt_dot(dproj_ref[span, :], proj_ref[...])
        turn = gates_ref[span, :filters]
        keep = sigmoid(gates_ref[span, filters:])
        below = normal_cdf(turn)
        slope = below + turn * (DENSITY * jnp.exp(-0.5 * turn * turn))
        fresh = dhidden * (1.0 - keep)
        din_ref[span, :] = dhidden * keep
        dturn = (fresh * slope).astype(jnp.bfloat16)
        dkeep = (fresh * keep * (acts_ref[span, :].astype(jnp.float32) - turn * below)).astype(jnp.bfloat16)
        dgates_ref[span, :filters] = dturn
        dgates_ref[span, filters:] = dkeep
        bias_ref[:, :filters] += jnp.sum(dturn.astype(jnp.float32), axis=0, keepdims=True)
        bias_ref[:, filters:] += jnp.sum(dkeep.astype(jnp.float32), axis=0, keepdims=True)
        return carry

    lax.fori_loop(0, words // block, mix, 0)
    piece = 512

    def grads(index, carry):
        cols = pl.ds(pl.multiple_of(index * piece, piece), piece)
        grad_ref[cols, :] = tn_dot(feats_ref[:, cols], dgates_ref[...]).astype(jnp.bfloat16)
        down = nt_dot(dgates_ref[:, :filters], wide_ref[0, cols, :]) + nt_dot(dgates_ref[:, filters:], wide_ref[1, cols, :])
        part_ref[:, cols] = down.astype(jnp.bfloat16)
        return carry

    lax.fori_loop(0, feats_ref.shape[1] // piece, grads, 0)
    parts, sides, rows, dmodel = both_ref.shape
    width = dmodel // parts
    gproj = tn_dot(hidden_ref[...], dproj_ref[...]).astype(jnp.bfloat16)
    gout = tn_dot(attended_ref[...], dmixed_ref[...]).astype(jnp.bfloat16)
    size, small = gproj.shape[0] // (sides * parts), gout.shape[0] // (sides * (parts - 1))
    for part in range(parts):
        cols = slice(part * width, (part + 1) * width)
        for side in range(sides):
            for group in range(parts):
                lanes = slice(group * width, (group + 1) * width)
                start = (side * parts + group) * size
                both_ref[part, side, :size, lanes] = gproj[start : start + size, cols]
                if group < parts - 1:
                    start = (side * (parts - 1) + group) * small
                    both_ref[part, side, size:, lanes] = gout[start : start + small, cols]
                else:
                    both_ref[part, side, size:, lanes] = jnp.zeros((rows - size, width), jnp.bfloat16)


def highway_back_call(dproj, proj, hidden, gates, acts, feats, wide, attended, dmixed, parts, po_rows):
    words, filters = acts.shape
    dmodel = dproj.shape[1]
    vmem = pl.BlockSpec(memory_space=pltpu.VMEM)
    return pl.pallas_call(
        highway_back, in_specs=[vmem] * 9, out_specs=[vmem] * 5,
        out_shape=[bf16(words, feats.shape[1]), f32(words, filters), bf16(feats.shape[1], 2 * filters), bf16(parts, 2, po_rows, dmodel), f32(1, 2 * filters)],
        scratch_shapes=[pltpu.VMEM((words, 2 * filters), jnp.bfloat16)],
        compiler_params=pltpu.CompilerParams(vmem_limit_bytes=56 << 20), name="highway_back",
        cost_estimate=pl.CostEstimate(flops=5_200_000_000, bytes_accessed=20_000_000, transcendentals=1_000_000),
    )(dproj, proj, hidden, gates, acts, feats, wide, attended, dmixed)


class RowReduce:
    def __init__(self, grad, yin, pair, zin, joined, span, sems, base=0):
        self.base, self.ready, self.after = base, [], None
        self.grad, self.yin, self.pair, self.zin, self.joined = grad, yin, pair, zin, joined
        self.span, self.sems = span, sems
        self.me, self.slot = lax.axis_index("filt"), lax.axis_index("dp")
        self.ring, self.side = self.slot // 2, self.slot % 2
        self.copies = []

    def push(self, source, target, index, peer):
        send, recv = self.sems
        copy = remote(source, target, send.at[index], recv.at[index], peer)
        copy.start()
        self.copies.append(copy)
        return copy

    def across(self):
        span = self.span
        for copy in self.ready:
            copy.wait_recv()
        self.first = self.push(
            self.grad.at[:, 1 - self.side, span, :], self.yin.at[:, span, :], 0, {"dp": self.slot ^ 1}
        )

    def along(self):
        span = self.span
        self.first.wait_recv()
        if self.after is not None:
            self.after.across()
        both = self.grad[:, self.side, span, :].astype(jnp.float32) + self.yin[:, span, :].astype(jnp.float32)
        self.pair[:, span, :] = both.astype(jnp.bfloat16)
        self.ring_out()

    def local(self):
        return pl.ds(self.span.start - self.base, self.span.size)

    def ring_out(self):
        span = self.local()
        self.rest = [
            self.push(self.pair.at[self.ring ^ hop, span, :], self.zin.at[hop - 1, span, :], hop, {"dp": self.slot ^ (2 * hop)})
            for hop in (2, 3, 1)
        ]

    def join(self):
        span = self.local()
        for copy in self.rest:
            copy.wait_recv()
        total = self.pair[self.ring, span, :].astype(jnp.float32)
        for hop in (1, 2, 3):
            total = total + self.zin[hop - 1, span, :].astype(jnp.float32)
        self.joined[self.me, self.span, :] = total.astype(jnp.bfloat16)
        self.share()

    def share(self):
        piece = self.joined.at[self.me, self.span, :]
        self.far = self.push(piece, piece, 4, {"filt": self.me ^ 2})
        self.near = self.push(piece, piece, 5, {"filt": self.me ^ 1})

    def relay(self):
        self.far.wait_recv()
        piece = self.joined.at[self.me ^ 2, self.span, :]
        self.last = self.push(piece, piece, 6, {"filt": self.me ^ 1})

    def finish(self):
        self.near.wait_recv()
        self.last.wait_recv()
        for copy in self.copies:
            copy.wait_send()


AHEAD = 2


def epilogue(letters, depth, block, *refs):
    (part_ref, base_ref, chars_ref, embed_ref, lse_ref, weight_ref, back_ref, limit_ref, count_ref, wide_ref, slim_ref,
     cross_ref, ffn_ref, pair_ref, pos_ref, few_ref,
     wide_out, slim_out, rows_out, ffn_out, conv_out, table_out, pos_out, few_out,
     inbox, merged, up_ref, patch_ref, down_ref, pull_ref, wgrad_ref, tgrad_ref, wide_y, wide_p, wide_z, slim_y, slim_p, slim_z,
     rows_ref, rows_y, rows_p, rows_z, late_z, conv_low, conv_in, table_low, table_in, table_side, pos_low, pos_in, few_low, few_in, few_side,
     csend, crecv, rsend, rrecv, tsend, trecv, asend, arecv) = refs
    me = lax.axis_index("filt")
    greet_all()
    pos = Total(pos_low, pos_in, pos_out, tsend.at[0], trecv.at[0])
    few = Total(few_low, few_in, few_out, tsend.at[1], trecv.at[1], few_side)
    conv_total = Total(conv_low, conv_in, conv_out, tsend.at[2], trecv.at[2])
    table_total = Total(table_low, table_in, table_out, tsend.at[3], trecv.at[3], table_side)
    wide_rows = wide_out.shape[1] // 4
    slim = RowReduce(slim_ref, slim_y, slim_p, slim_z, slim_out, pl.ds(0, slim_out.shape[1]), (rsend.at[4], rrecv.at[4]))
    both = RowReduce(rows_ref, rows_y, rows_p, rows_z, rows_out, pl.ds(0, rows_out.shape[1]), (rsend.at[6], rrecv.at[6]))
    wide = [
        RowReduce(wide_ref, wide_y, wide_p, wide_z, wide_out, pl.ds(index * wide_rows, wide_rows), (rsend.at[index], rrecv.at[index]))
        for index in range(4)
    ]
    early = ffn_ref.shape[0]
    ffn = RowReduce(None, None, None, None, ffn_out, pl.ds(0, early), (rsend.at[5], rrecv.at[5]))
    late = RowReduce(None, None, pair_ref, late_z, ffn_out, pl.ds(early, pair_ref.shape[1]), (rsend.at[7], rrecv.at[7]), early)
    swaps = [
        remote(cross_ref.at[me ^ hop], rows_ref.at[me], asend.at[hop - 1], arecv.at[hop - 1], {"filt": me ^ hop}) for hop in (2, 3, 1)
    ]
    both.ready = swaps
    pos.start(pos_ref[...])
    few.start(few_ref[...])
    for copy in swaps:
        copy.start()
    rows_ref[me] = cross_ref[me]
    queue = [slim, wide[0], both] + wide[1:]
    for index, item in enumerate(queue):
        item.after = queue[index + AHEAD] if index + AHEAD < len(queue) else None
    for item in queue[:AHEAD]:
        item.across()
    ffn_out[me, :early, :] = ffn_ref[...]
    late.ring_out()
    scatter = ChannelScatter(part_ref, base_ref, up_ref, inbox, merged, csend, crecv)
    scatter.run()
    pos.combine()
    few.combine()
    ffn.share()
    steps = iter([
        [slim.along, ffn.relay], [late.join], [wide[0].along, slim.join], [late.relay, slim.relay], [both.along, wide[0].join],
        [wide[0].relay, few.across], [wide[1].along, both.join], [both.relay], [], [],
    ])

    def advance():
        for step in next(steps):
            step()

    filters = weight_ref.shape[0]
    rows = KW * depth
    groups = tgrad_ref.shape[0] // (2 * depth)
    wgrad_ref[...] = jnp.zeros(wgrad_ref.shape, jnp.float32)
    tgrad_ref[...] = jnp.zeros(tgrad_ref.shape, jnp.float32)
    patch_ref[letters * depth :, :] = jnp.zeros((patch_ref.shape[0] - letters * depth, block), jnp.bfloat16)
    ones = jnp.where(lax.broadcasted_iota(jnp.int32, (128 - rows, block), 0) == 0, 1.0, 0.0).astype(jnp.bfloat16)
    always = letters - KW + 1
    quarter = always // 4
    for index in range(chars_ref.shape[1] // block):
        cols = pl.ds(index * block, block)
        patch_ref[: letters * depth, :] = embed_ref[:, cols]
        down_ref[...] = jnp.zeros(down_ref.shape, jnp.float32)
        pooled = lse_ref[:, cols] - count_ref[...]
        slope = normal_cdf(pooled) + pooled * (DENSITY * jnp.exp(-0.5 * pooled * pooled))
        pull_ref[...] = slope * up_ref[cols, :].T.astype(jnp.float32)

        def one(position, masked):
            start = position * depth
            if not isinstance(position, int):
                start = pl.multiple_of(start, depth)
            patch = jnp.concatenate([patch_ref[pl.ds(start, rows), :], ones], axis=0)
            grid = nn_dot(weight_ref[...], patch)
            spread = jnp.exp(grid - lse_ref[:, cols]) * pull_ref[...]
            if masked:
                spread = jnp.where(limit_ref[...] >= position, spread, 0.0)
            spread = spread.astype(jnp.bfloat16)
            down = nn_dot(back_ref[...], spread)
            down_ref[pl.ds(start, rows), :] += down[:rows]
            wgrad_ref[...] += nt_dot(spread, patch)

        def body(position, carry):
            one(position, False)
            return carry

        for lap in range(4):
            stop = always if lap == 3 else (lap + 1) * quarter
            lax.fori_loop(lap * quarter, stop, body, 0, unroll=11)
            advance()
        for position in range(always, letters):
            one(position, True)

        def table(position, carry):
            ids = chars_ref[pl.ds(position, 1), cols]
            low = ids & 127
            group = ids >> 7
            onehot = lax.broadcasted_iota(jnp.int32, (128, block), 0) == low
            onehot = jnp.where(onehot, 1.0, 0.0).astype(jnp.bfloat16)
            down = down_ref[pl.ds(pl.multiple_of(position * depth, depth), depth), :]
            high = down.astype(jnp.bfloat16)
            rest = (down - high.astype(jnp.float32)).astype(jnp.bfloat16)
            zero = jnp.zeros_like(high)
            parts = [jnp.where(group == part, item, zero) for item in (high, rest) for part in range(groups)]
            tgrad_ref[...] += nt_dot(jnp.concatenate(parts, axis=0), onehot)
            return carry

        lax.fori_loop(0, letters, table, 0, unroll=5)
        advance()
    table_rows = tgrad_ref.shape[0] // 2
    slices, size = table_low.shape[:2]
    conv_total.start(wgrad_ref[...].reshape(conv_low.shape))
    sums = tgrad_ref[:table_rows, :] + tgrad_ref[table_rows:, :]
    sums = jnp.concatenate([sums, jnp.zeros((slices * size - table_rows, sums.shape[1]), jnp.float32)], axis=0)
    table_total.start(sums.reshape(table_low.shape))
    for step in (
        wide[2].along, wide[1].join, wide[1].relay, wide[3].along, conv_total.combine, table_total.combine, wide[2].join,
        wide[2].relay, table_total.across, wide[3].join, wide[3].relay,
    ):
        step()
    for copy in swaps:
        copy.wait_send()
    for item in [ffn, late, slim, both, pos, few, conv_total, table_total] + wide:
        item.finish()


class ChannelScatter:
    def __init__(self, part_ref, base_ref, out_ref, inbox, merged, send, recv):
        self.part, self.base, self.out, self.inbox, self.merged = part_ref, base_ref, out_ref, inbox, merged
        self.sems = (send, recv)
        self.me = lax.axis_index("filt")

    def run(self):
        me = self.me
        rows, cols = self.base.shape
        pieces = self.sems[0].shape[1]
        size = rows // pieces

        def lanes(index):
            return pl.ds(pl.multiple_of(index * cols, cols), cols)

        def hop(source, kind, piece, peer):
            span = pl.ds(piece * size, size)
            send, recv = self.sems
            copy = remote(source, self.inbox.at[kind, span, :], send.at[kind, piece], recv.at[kind, piece], {"filt": peer})
            copy.start()
            return copy

        spans = [pl.ds(piece * size, size) for piece in range(pieces)]
        first = [hop(self.part.at[span, lanes(me ^ 3)], 0, piece, me ^ 1) for piece, span in enumerate(spans)]
        second = [hop(self.part.at[span, lanes(me ^ 1)], 1, piece, me ^ 1) for piece, span in enumerate(spans)]
        third = []
        for piece, span in enumerate(spans):
            first[piece].wait_recv()
            both = self.part[span, lanes(me ^ 2)].astype(jnp.float32) + self.inbox[0, span, :].astype(jnp.float32)
            self.merged[span, :] = both.astype(jnp.bfloat16)
            third.append(hop(self.merged.at[span, :], 2, piece, me ^ 2))
        for piece, span in enumerate(spans):
            second[piece].wait_recv()
            third[piece].wait_recv()
            total = self.part[span, lanes(me)].astype(jnp.float32) + self.inbox[1, span, :].astype(jnp.float32)
            total = total + self.inbox[2, span, :].astype(jnp.float32) + self.base[span, :]
            self.out[span, :] = total.astype(jnp.bfloat16)
        for copy in first + second + third:
            copy.wait_send()


def epilogue_call(part, base, ids, embed, lse, weight, back, limit, count, wide, slim, both, ffn, pair, pos, few, letters, depth, groups, ident, block=256):
    filters, words = lse.shape
    args = (part, base, ids, embed, lse, weight, back, limit, count, wide, slim, both, ffn, pair, pos, few)
    parts = part.shape[1] // filters
    slices = pos.shape[0]
    pieces = 4
    vmem = pl.BlockSpec(memory_space=pltpu.VMEM)
    table_size = -(-(-(-groups * depth // slices)) // 8) * 8

    def space(shape, dtype=jnp.bfloat16):
        return pltpu.VMEM(tuple(shape), dtype)

    def stages(array):
        ring, side, rows, cols = array.shape
        return [space((ring, rows, cols)), space((ring, rows, cols)), space((ring - 1, rows, cols))]

    def totals(shape, sides):
        spaces = [space(shape), space((shape[0] - 1,) + shape[1:])]
        return spaces + ([space((4,) + shape[1:])] if sides else [])

    conv_shape = (slices, filters // slices, 128)
    table_shape = (slices, table_size, 128)
    out_shape = [bf16(parts, *wide.shape[2:]), bf16(parts, *slim.shape[2:]), bf16(parts, *both.shape[2:]), bf16(parts, ffn.shape[0] + pair.shape[1], ffn.shape[1]), bf16(*conv_shape), bf16(*table_shape), bf16(*pos.shape), bf16(*few.shape)]
    padded = (letters + KW - 1) * depth
    return pl.pallas_call(
        functools.partial(epilogue, letters, depth, block),
        in_specs=[vmem] * len(args),
        out_specs=[vmem] * len(out_shape),
        out_shape=out_shape,
        scratch_shapes=[space((3, words, filters)), space((words, filters)), space((words, filters)), space((padded, block)),
                        space((padded, block), jnp.float32), space((filters, block), jnp.float32),
                        space((filters, 128), jnp.float32), space((2 * groups * depth, 128), jnp.float32)]
        + stages(wide) + stages(slim) + [space(both.shape)] + stages(both) + [space((3,) + pair.shape[1:])]
        + totals(conv_shape, False) + totals(table_shape, True) + totals(pos.shape, False) + totals(few.shape, True)
        + [DMA((3, pieces)), DMA((3, pieces)), DMA((8, 7)), DMA((8, 7)), DMA((4, 3, slices - 1)), DMA((4, 3, slices - 1)),
           DMA((3,)), DMA((3,))],
        compiler_params=pltpu.CompilerParams(collective_id=ident, has_side_effects=True, vmem_limit_bytes=56 << 20),
        name="epilogue",
    )(*args)


def assemble(depth, wide_ref, slim_ref, both_ref, ffn_ref, conv_ref, table_ref, pos_ref, few_ref, limit_ref,
             wide_out, slim_out, proj_out, out_out, inner_out, outer_out, conv_out, cbias_out, table_out, pos_out,
             hbias_out, pbias_out, gain_out, shift_out, ibias_out):
    parts = wide_ref.shape[0]
    inner_rows = inner_out.shape[0]
    proj_rows, out_rows = proj_out.shape[0] // parts, out_out.shape[0] // (parts - 1)
    filters = wide_ref.shape[2] // 2
    width = slim_ref.shape[2] // 3
    for part in range(parts):
        for half in range(2):
            start = (half * parts + part) * filters
            wide_out[:, start : start + filters] = wide_ref[part, :, half * filters : (half + 1) * filters].astype(jnp.float32)
        for block in range(3):
            start = (block * parts + part) * width
            slim_out[:, start : start + width] = slim_ref[part, :, block * width : (block + 1) * width].astype(jnp.float32)
        cols = slice(part * width, (part + 1) * width)
        for block in range(parts):
            lanes = slice(block * width, (block + 1) * width)
            proj_out[block * proj_rows : (block + 1) * proj_rows, cols] = both_ref[part, :proj_rows, lanes].astype(jnp.float32)
            if block < parts - 1:
                out_out[block * out_rows : (block + 1) * out_rows, cols] = both_ref[part, proj_rows:, lanes].astype(jnp.float32)
        units = ffn_ref.shape[1] - inner_rows
        outer_out[part * units : (part + 1) * units, :] = ffn_ref[part, inner_rows:, :].astype(jnp.float32)
        for block in range(inner_out.shape[1] // (parts * units)):
            start = (block * parts + part) * units
            inner_out[:, start : start + units] = ffn_ref[part, :inner_rows, block * units : (block + 1) * units].astype(jnp.float32)
    slices, conv_rows = conv_ref.shape[:2]
    taps = conv_out.shape[0]
    turned = conv_ref[...].reshape(slices * conv_rows, 128).astype(jnp.float32).T
    tap = lax.broadcasted_iota(jnp.int32, (taps, 1), 0) // depth
    conv_out[...] = jnp.where(tap < limit_ref[...], turned[:taps], 0.0)
    cbias_out[...] = turned[taps : taps + 1]
    table = table_ref[...].reshape(-1, 128).astype(jnp.float32)
    vocab = table_out.shape[0]
    for group in range(-(-vocab // 128)):
        stop = min(128, vocab - group * 128)
        table_out[group * 128 : group * 128 + stop, :] = table[group * depth : (group + 1) * depth].T[:stop]
    pos_out[...] = pos_ref[...].reshape(pos_out.shape).astype(jnp.float32)
    own = few_ref[lax.axis_index("dp")].astype(jnp.float32)
    size = gain_out.shape[1]
    hbias_out[...] = own[0:1, : hbias_out.shape[1]]
    pbias_out[...] = own[1:2, : pbias_out.shape[1]]
    gain_out[...] = own[2:5, :size]
    shift_out[...] = own[5:8, :size]
    ibias_out[...] = own[8:9, : ibias_out.shape[1]]


def assemble_call(wide, slim, both, ffn, conv, table, pos, few, widths, inner_rows, out_rows, taps, vocab, depth, sizes):
    args = (wide, slim, both, ffn, conv, table, pos, few, widths)
    parts = wide.shape[0]
    vmem = pl.BlockSpec(memory_space=pltpu.VMEM)
    units = ffn.shape[1] - inner_rows
    dmodel = both.shape[2]
    hb, pb, nd, ib = sizes
    proj_rows = both.shape[1] - out_rows // (parts - 1)
    out_shape = [f32(wide.shape[1], wide.shape[2] * parts), f32(slim.shape[1], slim.shape[2] * parts),
                 f32(proj_rows * parts, dmodel), f32(out_rows, dmodel), f32(inner_rows, dmodel * parts), f32(units * parts, dmodel),
                 f32(taps, widths.shape[1]), f32(1, widths.shape[1]), f32(vocab, depth), f32(pos.shape[0] * pos.shape[1], pos.shape[2]),
                 f32(1, hb), f32(1, pb), f32(3, nd), f32(3, nd), f32(1, ib)]
    return pl.pallas_call(
        functools.partial(assemble, depth), in_specs=[vmem] * len(args), out_specs=[vmem] * len(out_shape), out_shape=out_shape,
        compiler_params=pltpu.CompilerParams(vmem_limit_bytes=40 << 20), name="assemble",
    )(*args)


def exact_gaussian_activation(values):
    return jax.nn.gelu(values, approximate=False)


def gelu_back(values, upstream):
    return jax.vjp(exact_gaussian_activation, values)[1](upstream)[0]


def channel_widths(channels):
    widths = jnp.ones_like(channels)
    for power in range(6):
        widths = widths + (channels >= NF * 2**power // 64).astype(jnp.int32)
    return widths


def highway_mix(hidden, gates):
    width = hidden.shape[1]
    carry_gate = jax.nn.sigmoid(gates[:, width:])
    return carry_gate * hidden + (1.0 - carry_gate) * exact_gaussian_activation(gates[:, :width])


def swap(array, axis, bit):
    size = lax.axis_size(axis)
    return lax.ppermute(array, axis, [(index, index ^ bit) for index in range(size)])


def reduce_rows(array):
    count = lax.axis_size("dp")
    slot = lax.axis_index("dp")
    bits = count.bit_length() - 1
    rows, cols = array.shape
    if count != 1 << bits:
        return lax.psum_scatter(array.astype(jnp.bfloat16), "dp", scatter_dimension=0, tiled=True)
    array = array.reshape((2,) * bits + (rows // count, cols))
    for bit in range(bits):
        axis = bits - 1 - bit
        mine = (slot >> bit) & 1
        keep = lax.dynamic_index_in_dim(array, mine, axis, keepdims=False)
        give = lax.dynamic_index_in_dim(array, 1 - mine, axis, keepdims=False)
        got = swap(give.astype(jnp.bfloat16), "dp", 1 << bit)
        array = (keep.astype(jnp.float32) + got.astype(jnp.float32)).astype(jnp.bfloat16)
    return array


def join_parts(array):
    part = lax.axis_index("filt")
    low = (part & 1) == 1
    high = (part >> 1) == 1
    far = swap(array, "filt", 2)
    near = swap(array, "filt", 1)
    both = swap(far, "filt", 1)
    here = (jnp.where(low, near, array), jnp.where(low, array, near))
    there = (jnp.where(low, both, far), jnp.where(low, far, both))
    first = [jnp.where(high, b, a) for a, b in zip(here, there)]
    second = [jnp.where(high, a, b) for a, b in zip(here, there)]
    return first + second


def per_device(
    chars,
    lengths,
    char_table,
    conv_weight,
    conv_bias,
    highway_weight,
    highway_bias,
    proj_weight,
    proj_bias,
    position,
    norm_gain,
    norm_bias,
    query_key_value_weight,
    attention_output_weight,
    feedforward_input_weight,
    feedforward_input_bias,
    feedforward_output_weight,
    cotangent,
):
    parts = lax.axis_size("filt")
    slices = lax.axis_size("dp")
    part = lax.axis_index("filt")
    slot = lax.axis_index("dp")
    seqs, quarter, dmodel = cotangent.shape
    full_len = chars.shape[1]
    letters = chars.shape[2]
    words = seqs * full_len
    tokens = seqs * quarter
    filters = conv_weight.shape[1]
    depth = char_table.shape[1]
    heads = dmodel // HD // parts
    width = heads * HD
    inner_rows = feedforward_input_weight.shape[0]
    unit_rows = feedforward_output_weight.shape[0] // parts

    def own_columns(array, blocks):
        rows = array.shape[0]
        split = array.reshape(rows, blocks, parts, -1)
        return lax.dynamic_index_in_dim(split, part, 2, keepdims=False).reshape(rows, -1)

    def gather_rows(array):
        return lax.all_gather(array, "dp", axis=0, tiled=True)

    def groups_of(array, groups):
        array = array.reshape(groups, -1, width).transpose(1, 0, 2).reshape(-1, groups * width)
        return jnp.pad(array, ((0, 0), (0, dmodel - groups * width)))

    def rows_from_columns(both):
        both = lax.all_to_all(both.reshape(parts, -1, dmodel), "filt", split_axis=0, concat_axis=0, tiled=True)
        both = both.reshape(parts, slices // parts, po_rows, parts, width)
        both = [both[:, :, :split], both[:, :, split:, : parts - 1]]
        return [item.transpose(1, 3, 2, 0, 4).reshape(-1, dmodel) for item in both]

    def columns_from_rows(*grads):
        items = []
        for item, groups in zip(grads, (parts, parts - 1)):
            item = item.astype(jnp.bfloat16).reshape(slices // parts, groups, -1, parts, width)
            item = item.transpose(3, 0, 2, 1, 4).reshape(parts, slices // parts, -1, groups * width)
            items.append(jnp.pad(item, ((0, 0), (0, 0), (0, 0), (0, dmodel - groups * width))))
        both = jnp.concatenate(items, axis=2)
        both = lax.all_to_all(both.reshape(parts, -1, dmodel), "filt", split_axis=0, concat_axis=0, tiled=True)
        return both.reshape(slices * po_rows, dmodel)

    fast = slices == 8 and parts == 4
    hb, pb, nd = highway_bias.shape[1], proj_bias.shape[0], norm_gain.shape[1]
    small = jnp.concatenate(
        [
            highway_bias.reshape(-1),
            proj_bias,
            norm_gain.reshape(-1),
            norm_bias.reshape(-1),
            feedforward_input_bias,
        ]
    )
    small_size = small.shape[0]
    small = jnp.pad(small, (0, -small_size % dmodel))
    slim_parts = [
        groups_of(own_columns(proj_weight, 1), parts),
        groups_of(own_columns(attention_output_weight, 1), parts - 1),
        own_columns(query_key_value_weight, 3).reshape(-1, dmodel),
        small.reshape(-1, dmodel),
    ]
    split = slim_parts[0].shape[0]
    po_rows = split + slim_parts[1].shape[0]
    qkv_rows = slim_parts[2].shape[0]
    slim_all = lax.all_gather(jnp.concatenate(slim_parts, axis=0), "dp", axis=0, tiled=False)
    qkv_own = slim_all[:, po_rows : po_rows + qkv_rows].reshape(dmodel, 3 * width)
    small = slim_all[:, po_rows + qkv_rows :]
    small = small.reshape(slices, -1)[:, :small_size].astype(jnp.float32)
    cuts = [hb, hb + pb, hb + pb + 3 * nd, hb + pb + 6 * nd]
    highway_b, proj_b, gain, shift, inner_b = jnp.split(small, cuts, axis=1)
    highway_b_own = own_columns(highway_b.reshape(1, -1), 2)
    proj_b = proj_b.reshape(-1)
    gain = gain.reshape(slices, 3, nd).transpose(1, 0, 2).reshape(3, dmodel)
    shift = shift.reshape(slices, 3, nd).transpose(1, 0, 2).reshape(3, dmodel)
    inner_b_own = own_columns(inner_b.reshape(1, -1), slices)
    ffn_own = jnp.concatenate(
        [
            own_columns(feedforward_input_weight, slices),
            lax.dynamic_slice_in_dim(feedforward_output_weight, part * unit_rows, unit_rows, 0),
        ],
        axis=0,
    )

    def blocks_of(array):
        return array.astype(jnp.bfloat16).reshape(parts, tokens, -1)

    widths = channel_widths(part * filters + jnp.arange(filters, dtype=jnp.int32))
    ids, table, weight, back, limit, count = conv_prep(
        chars.reshape(words, letters), char_table, conv_weight, conv_bias, widths
    )
    if fast:
        acts, lse, embed, features, highway_own = prologue_call(
            ids, table, weight, limit, count, highway_weight[0], parts, letters, depth, 0
        )
        highway_own = highway_own.reshape(2, -1, filters)
    else:
        acts, lse, embed = conv_forward_call(ids, table, weight, limit, count, letters, depth)
        features = gather_channels_call(acts, parts, 0)
        highway_own = gather_rows(own_columns(highway_weight[0], 2))
        proj_own, out_own = rows_from_columns(slim_all[:, :po_rows])
    ffn_own, features = lax.optimization_barrier((ffn_own, features))
    ffn_all = lax.all_gather(ffn_own, "dp", axis=0, tiled=False)
    base = position.astype(jnp.float32) + proj_b[None, :]
    if fast:
        gates, hidden_low, proj_own, out_own, first, unit_zero, scale_zero, first_all = highway_stage_call(
            slim_all,
            features,
            highway_own,
            highway_b_own,
            acts,
            base,
            gain[0:1],
            shift[0:1],
            attention_output_weight.shape[0] * slices // parts,
            po_rows,
            EPS,
            1,
        )
    else:
        gates = nn_dot(features, highway_own) + highway_b_own
        feature_own = acts.astype(jnp.float32)
        hidden_low = highway_mix(feature_own, gates).astype(jnp.bfloat16)
        first, unit_zero, scale_zero, first_all = forward_stage_call(
            blocks_of(nn_dot(hidden_low, proj_own)), base, gain[0:1], shift[0:1], EPS, 1
        )
    first_all = first_all.reshape(words, dmodel)
    packed = nn_dot(first_all, qkv_own).astype(jnp.bfloat16)
    queries, keys, values = (
        packed[:, block * width : (block + 1) * width].reshape(seqs, full_len, heads, HD)
        for block in range(3)
    )
    key_ok = jnp.arange(full_len, dtype=jnp.int32)[None, :] < lengths[:, None]
    scale = HD ** (-0.5)
    scores = (
        jnp.einsum("sqhd,skhd->shqk", queries, keys, preferred_element_type=jnp.float32) * scale
    )
    scores = jnp.where(key_ok[:, None, None, :], scores, -1e30)
    row_top = jnp.max(scores, axis=-1, keepdims=True)
    log_total = row_top + jnp.log(jnp.sum(jnp.exp(scores - row_top), axis=-1, keepdims=True))
    probs = jnp.exp(scores - log_total)
    probs_low = probs.astype(jnp.bfloat16)
    attended = (
        jnp.einsum("shqk,skhd->sqhd", probs_low, values, preferred_element_type=jnp.float32)
        .astype(jnp.bfloat16)
        .reshape(words, width)
    )
    second, unit_one, scale_one, second_all = forward_stage_call(
        blocks_of(nn_dot(attended, out_own)), first, gain[1:2], shift[1:2], EPS, 2
    )
    second_all = second_all.reshape(words, dmodel)
    ffn_all, second_all = lax.optimization_barrier((ffn_all, second_all))
    inner_own = ffn_all[:, :inner_rows].reshape(dmodel, -1)
    outer_own = ffn_all[:, inner_rows:].reshape(-1, dmodel)
    inner = nn_dot(second_all, inner_own) + inner_b_own
    active = exact_gaussian_activation(inner).astype(jnp.bfloat16)
    top, d_res_two, d_gain_two, d_shift_two, d_outer = top_stage_call(
        blocks_of(nn_dot(active, outer_own)),
        second,
        cotangent.reshape(tokens, dmodel),
        gain[2:3],
        shift[2:3],
        EPS,
        3,
    )
    encoded = top.reshape(seqs, quarter, dmodel)
    d_outer = d_outer.reshape(words, dmodel)
    grad_outer = tn_dot(active, d_outer)
    d_active = nt_dot(d_outer, outer_own)
    d_inner = gelu_back(inner, d_active).astype(jnp.bfloat16)
    grad_inner = tn_dot(second_all, d_inner)
    grad_ffn = jnp.concatenate(
        [item.astype(jnp.bfloat16).reshape(slices, -1, dmodel) for item in (grad_inner, grad_outer)], axis=1
    )
    if fast:
        early = grad_ffn.shape[1] * 2 // 3
        grad_ffn = grad_ffn.reshape(4, 2, -1, dmodel)
        grad_early, grad_late = grad_ffn[:, :, :early], grad_ffn[:, :, early:]
        jobs = ("side",), (grad_early,)
    else:
        jobs = (), ()

    def pair_sum(grad, got):
        keep = lax.dynamic_index_in_dim(grad, slot % 2, 1, keepdims=False)
        return (keep.astype(jnp.float32) + got.astype(jnp.float32)).astype(jnp.bfloat16)

    grad_inner_b = jnp.sum(d_inner.astype(jnp.float32), axis=0)
    d_res_one, d_gain_one, d_shift_one, unused_sum, d_mixed, *got = backward_stage_call(
        blocks_of(nt_dot(d_inner, inner_own)), d_res_two, unit_one, scale_one, gain[1:2], 4, *jobs
    )
    if fast:
        grad_early = pair_sum(grad_early, got[0])
        jobs = ("side", "ring"), (grad_late, grad_early)
    d_mixed = d_mixed.reshape(words, dmodel)
    d_attended = nt_dot(d_mixed, out_own).astype(jnp.bfloat16)
    d_attended = d_attended.reshape(seqs, full_len, heads, HD)
    d_values = jnp.einsum(
        "shqk,sqhd->skhd", probs_low, d_attended, preferred_element_type=jnp.float32
    )
    d_probs = jnp.einsum(
        "sqhd,skhd->shqk", d_attended, values, preferred_element_type=jnp.float32
    )
    row_inner = jnp.sum(d_probs * probs, axis=-1, keepdims=True)
    d_scores = (probs * (d_probs - row_inner)).astype(jnp.bfloat16)
    d_queries = (
        jnp.einsum("shqk,skhd->sqhd", d_scores, keys, preferred_element_type=jnp.float32) * scale
    )
    d_keys = (
        jnp.einsum("shqk,sqhd->skhd", d_scores, queries, preferred_element_type=jnp.float32) * scale
    )
    d_packed = jnp.concatenate(
        [item.reshape(words, width) for item in (d_queries, d_keys, d_values)], axis=1
    ).astype(jnp.bfloat16)
    grad_qkv = tn_dot(first_all, d_packed).astype(jnp.bfloat16)
    d_summed, d_gain_zero, d_shift_zero, grad_proj_b, d_projected, *got = backward_stage_call(
        blocks_of(nt_dot(d_packed, qkv_own)), d_res_one, unit_zero, scale_zero, gain[0:1], 5, *jobs
    )
    if fast:
        grad_late = pair_sum(grad_late, got[0])
        keep = lax.dynamic_index_in_dim(grad_early, slot // 2, 0, keepdims=False)
        grad_early = sum([item.astype(jnp.float32) for item in got[1]], keep.astype(jnp.float32))
        grad_early = grad_early.astype(jnp.bfloat16)
    grad_pos = jnp.sum(d_summed.reshape(seqs, quarter, dmodel), axis=0)
    d_projected = d_projected.reshape(words, dmodel)
    if fast:
        d_partial, d_in, grad_highway, grad_both, grad_highway_b = highway_back_call(
            d_projected, proj_own, hidden_low, gates, acts, features, highway_own, attended, d_mixed, parts, po_rows
        )
    else:
        grad_both = columns_from_rows(tn_dot(hidden_low, d_projected), tn_dot(attended, d_mixed))
        d_hidden = nt_dot(d_projected, proj_own)
        d_in, d_gates = jax.vjp(highway_mix, feature_own, gates)[1](d_hidden)
        d_gates = d_gates.astype(jnp.bfloat16)
        grad_highway = tn_dot(features, d_gates).astype(jnp.bfloat16)
        grad_highway_b = jnp.sum(d_gates.astype(jnp.float32), axis=0)
        d_partial = nt_dot(d_gates, highway_own).astype(jnp.bfloat16)
    groups = table.shape[0] // depth

    def place_columns(own, blocks):
        piece = own.reshape(blocks, 1, -1)
        whole = jnp.zeros((blocks, parts, piece.shape[2]), own.dtype)
        return lax.dynamic_update_slice_in_dim(whole, piece, part, 1).reshape(-1)

    d_gain = jnp.concatenate([d_gain_zero, d_gain_one, d_gain_two])
    d_shift = jnp.concatenate([d_shift_zero, d_shift_one, d_shift_two])
    pieces = [
        place_columns(grad_highway_b, 2).reshape(slices, 1, -1),
        grad_proj_b.reshape(slices, 1, -1),
        d_gain.reshape(3, slices, nd).transpose(1, 0, 2),
        d_shift.reshape(3, slices, nd).transpose(1, 0, 2),
        place_columns(grad_inner_b, slices).reshape(slices, 1, -1),
    ]
    if fast:
        few = [jnp.pad(item, ((0, 0), (0, 0), (0, hb - item.shape[2]))) for item in pieces]
        few.append(jnp.zeros((slices, 7, hb), jnp.float32))
        few = jnp.concatenate(few, axis=1)
        wide_all, slim_all, both_all, ffn_all, conv_all, table_all, pos_all, few = epilogue_call(
            d_partial,
            d_in,
            ids,
            embed,
            lse,
            weight,
            back,
            limit,
            count,
            grad_highway.reshape(4, 2, -1, 2 * filters),
            grad_qkv.reshape(4, 2, -1, 3 * width),
            grad_both,
            grad_early,
            grad_late,
            grad_pos.reshape(slices, -1, dmodel),
            few,
            letters,
            depth,
            groups,
            6,
        )
        outs = assemble_call(
            wide_all,
            slim_all,
            both_all,
            ffn_all,
            conv_all,
            table_all,
            pos_all,
            few,
            widths[None, :],
            inner_rows,
            attention_output_weight.shape[0],
            conv_weight.shape[0],
            char_table.shape[0],
            depth,
            (hb, pb, nd, feedforward_input_bias.shape[0]),
        )
        g_highway, g_qkv, g_proj, g_out, g_inner, g_outer, conv_grad_w, conv_grad_b, g_table, grad_pos = outs[:10]
        g_highway_b, g_proj_b, g_gain, g_shift, g_inner_b = outs[10:]
        conv_grad_b, g_proj_b, g_inner_b = conv_grad_b[0], g_proj_b[0], g_inner_b[0]
    else:
        d_features = scatter_channels_call(d_partial, d_in, 6)
        conv_sums, table_sums = conv_backward_call(
            ids, embed, lse, d_features, weight, back, limit, count, groups, letters, depth
        )
        wide_all = jnp.stack(join_parts(reduce_rows(grad_highway)))
        slim_all = jnp.stack(join_parts(reduce_rows(grad_qkv)))
        both_all = jnp.stack(join_parts(reduce_rows(grad_both)))
        ffn_all = jnp.stack(join_parts(reduce_rows(grad_ffn.reshape(-1, dmodel))))
        table_sums = table_sums.reshape(2, groups * depth, -1).sum(0)
        conv_all = lax.psum(conv_sums, "dp")
        rows = jnp.concatenate([item.reshape(slices, -1) for item in pieces], axis=1)
        table_all, sums = lax.psum((table_sums, rows), ("dp", "filt"))
        grad_pos = lax.psum(grad_pos, "dp")
        own = lax.dynamic_index_in_dim(sums, slot, 0, keepdims=False)
        tap_rows = conv_weight.shape[0]
        tap_keep = (jnp.arange(tap_rows, dtype=jnp.int32) // depth)[:, None] < widths[None, :]
        conv_grad_w = jnp.where(tap_keep, conv_all[:, :tap_rows].T, 0.0)
        conv_grad_b = conv_all[:, tap_rows]
        g_table = table_all.reshape(groups, depth, 128).transpose(0, 2, 1).reshape(-1, depth)
        g_table = g_table[: char_table.shape[0]]
        g_highway_b, g_proj_b, g_gain, g_shift, g_inner_b = jnp.split(own, cuts)

        def join_columns(array, blocks, rows_here):
            array = array.reshape(parts, rows_here, blocks, -1).transpose(1, 2, 0, 3)
            return array.reshape(rows_here, -1).astype(jnp.float32)

        def join_groups(array, many):
            array = array.reshape(parts, array.shape[1], parts, width).transpose(2, 1, 0, 3)
            return array[:many].reshape(-1, dmodel).astype(jnp.float32)

        g_outer = ffn_all[:, inner_rows:].reshape(-1, dmodel).astype(jnp.float32)
        g_inner = join_columns(ffn_all[:, :inner_rows], slices, inner_rows)
        g_qkv = join_columns(slim_all, 3, query_key_value_weight.shape[0])
        g_proj = join_groups(both_all[:, :split], parts)
        g_out = join_groups(both_all[:, split:], parts - 1)
        g_highway = join_columns(wide_all, 2, highway_weight.shape[1])
    return (
        encoded,
        g_table,
        conv_grad_w,
        conv_grad_b,
        g_highway[None],
        g_highway_b.reshape(1, hb),
        g_proj,
        g_proj_b,
        grad_pos,
        g_gain.reshape(3, nd),
        g_shift.reshape(3, nd),
        g_qkv,
        g_out,
        g_inner,
        g_inner_b,
        g_outer,
    )


def solution(mesh):
    return jax.shard_map(
        per_device,
        mesh=mesh,
        in_specs=(
            P("dp", None, None),
            P("dp"),
            P(),
            P(None, "filt"),
            P("filt"),
            P(None, "dp", None),
            P(None, "dp"),
            P("dp", None),
            P("dp"),
            P("filt", None),
            P(None, "dp"),
            P(None, "dp"),
            P("dp", None),
            P("dp", None),
            P("dp", None),
            P("dp"),
            P("dp", None),
            P("dp", "filt", None),
        ),
        out_specs=(
            P("dp", "filt", None),
            P(),
            P(None, "filt"),
            P("filt"),
            P(None, "dp", None),
            P(None, "dp"),
            P("dp", None),
            P("dp"),
            P("filt", None),
            P(None, "dp"),
            P(None, "dp"),
            P("dp", None),
            P("dp", None),
            P("dp", None),
            P("dp"),
            P("dp", None),
        ),
        check_vma=False,
    )
```

```python
import functools

import jax
import jax.numpy as jnp
from jax import lax
from jax.experimental import pallas as pl
from jax.experimental.pallas import tpu as pltpu
from jax.sharding import PartitionSpec as P

KW = 7
NF = 2048
HD = 64
EPS = 1e-12
ROOT_HALF = 0.7071067811865476
DENSITY = 0.3989422804014327

def nt_dot(left, right):
    return lax.dot_general(left, right, (((1,), (1,)), ((), ())), preferred_element_type=jnp.float32)

def tn_dot(left, right):
    return lax.dot_general(left, right, (((0,), (0,)), ((), ())), preferred_element_type=jnp.float32)

def nn_dot(left, right):
    return jnp.dot(left, right, preferred_element_type=jnp.float32)

def normal_cdf(values):
    return 0.5 * (1.0 + lax.erf(values * ROOT_HALF))

def char_parts(chars_ref, position, block):
    ids = chars_ref[pl.ds(position, 1), :]
    low = ids & 127
    group = ids >> 7
    onehot = (lax.broadcasted_iota(jnp.int32, (128, block), 0) == low)
    onehot = jnp.where(onehot, 1.0, 0.0).astype(jnp.bfloat16)
    return onehot, group

def conv_forward(letters, depth, chars_ref, table_ref, weight_ref, limit_ref, count_ref,
                 acts_ref, lse_ref, embed_ref, patch_ref, grid_ref):
    block = chars_ref.shape[1]
    filters = weight_ref.shape[0]
    groups = table_ref.shape[0] // depth
    lead = KW - 1
    rows = KW * depth

    @pl.when(pl.program_id(0) == 0)
    def _():
        patch_ref[:, :rows, :] = jnp.zeros((patch_ref.shape[0], rows, block), jnp.bfloat16)
        ones = lax.broadcasted_iota(jnp.int32, (128 - rows, block), 0) == 0
        tail = jnp.where(ones, 1.0, 0.0).astype(jnp.bfloat16)
        patch_ref[:, rows:, :] = jnp.broadcast_to(tail[None], (patch_ref.shape[0],) + tail.shape)

    def embed(position, carry):
        onehot, group = char_parts(chars_ref, position, block)
        looked = nn_dot(table_ref[...], onehot)
        row = looked[:depth]
        for index in range(1, groups):
            row = jnp.where(group == index, looked[index * depth : (index + 1) * depth], row)
        row = row.astype(jnp.bfloat16)
        embed_ref[pl.ds(pl.multiple_of(position * depth, depth), depth), :] = row
        for tap in range(KW):
            patch_ref[position + lead - tap, tap * depth : (tap + 1) * depth, :] = row
        return carry

    lax.fori_loop(0, letters, embed, 0, unroll=5)
    chunk = grid_ref.shape[1]
    always = letters - KW + 1
    for start in range(0, filters, chunk):
        weight = weight_ref[start : start + chunk, :]
        limit = limit_ref[start : start + chunk, :]

        def product(position, top):
            grid = nn_dot(weight, patch_ref[position + lead])
            grid_ref[position] = grid
            return jnp.maximum(top, grid)

        top = lax.fori_loop(0, always, product, jnp.full((chunk, block), -1e30, jnp.float32), unroll=11)
        for position in range(always, letters):
            grid = nn_dot(weight, patch_ref[position + lead])
            grid = jnp.where(limit >= position, grid, -1e30)
            grid_ref[position] = grid
            top = jnp.maximum(top, grid)

        def total(position, acc):
            return acc + jnp.exp(grid_ref[position] - top)

        acc = lax.fori_loop(0, letters, total, jnp.zeros((chunk, block), jnp.float32), unroll=10)
        lse = top + jnp.log(acc)
        lse_ref[start : start + chunk, :] = lse
        pooled = lse - count_ref[start : start + chunk, :]
        acts_ref[:, start : start + chunk] = (pooled * normal_cdf(pooled)).astype(jnp.bfloat16).T

def conv_backward(letters, depth, chars_ref, embed_ref, lse_ref, up_ref, weight_ref, back_ref,
                  limit_ref, count_ref, wgrad_ref, tgrad_ref, patch_ref, down_ref, pull_ref):
    block = chars_ref.shape[1]
    filters = weight_ref.shape[0]
    lead = KW - 1
    rows = KW * depth
    groups = tgrad_ref.shape[0] // (2 * depth)
    step = pl.program_id(0)

    @pl.when(step == 0)
    def _():
        wgrad_ref[...] = jnp.zeros(wgrad_ref.shape, jnp.float32)
        tgrad_ref[...] = jnp.zeros(tgrad_ref.shape, jnp.float32)
        patch_ref[letters * depth :, :] = jnp.zeros((patch_ref.shape[0] - letters * depth, block), jnp.bfloat16)

    patch_ref[: letters * depth, :] = embed_ref[...]
    down_ref[...] = jnp.zeros(down_ref.shape, jnp.float32)
    pooled = lse_ref[...] - count_ref[...]
    slope = normal_cdf(pooled) + pooled * (DENSITY * jnp.exp(-0.5 * pooled * pooled))
    pull_ref[...] = slope * up_ref[...].T.astype(jnp.float32)
    ones = jnp.where(lax.broadcasted_iota(jnp.int32, (128 - rows, block), 0) == 0, 1.0, 0.0).astype(jnp.bfloat16)

    def one(position, masked):
        start = position * depth
        if not isinstance(position, int):
            start = pl.multiple_of(start, depth)
        patch = jnp.concatenate([patch_ref[pl.ds(start, rows), :], ones], axis=0)
        grid = nn_dot(weight_ref[...], patch)
        spread = jnp.exp(grid - lse_ref[...]) * pull_ref[...]
        if masked:
            spread = jnp.where(limit_ref[...] >= position, spread, 0.0)
        spread = spread.astype(jnp.bfloat16)
        down = nn_dot(back_ref[...], spread)
        down_ref[pl.ds(start, rows), :] += down[:rows]
        wgrad_ref[...] += nt_dot(spread, patch)

    always = letters - KW + 1

    def body(position, carry):
        one(position, False)
        return carry

    lax.fori_loop(0, always, body, 0, unroll=2)
    for position in range(always, letters):
        one(position, True)

    def table(position, carry):
        onehot, group = char_parts(chars_ref, position, block)
        down = down_ref[pl.ds(pl.multiple_of(position * depth, depth), depth), :]
        high = down.astype(jnp.bfloat16)
        low = (down - high.astype(jnp.float32)).astype(jnp.bfloat16)
        zero = jnp.zeros_like(high)
        parts = [jnp.where(group == index, item, zero) for item in (high, low) for index in range(groups)]
        tgrad_ref[...] += nt_dot(jnp.concatenate(parts, axis=0), onehot)
        return carry

    lax.fori_loop(0, letters, table, 0, unroll=5)

def conv_prep(chars, char_table, conv_weight, conv_bias, widths):
    letters = chars.shape[1]
    vocab, depth = char_table.shape
    groups = -(-vocab // 128)
    table = jnp.pad(char_table, ((0, groups * 128 - vocab), (0, 0)))
    table = table.reshape(groups, 128, depth).transpose(0, 2, 1).reshape(groups * depth, 128)
    tap = jnp.arange(conv_weight.shape[0], dtype=jnp.int32) // depth
    masked = jnp.where(tap[:, None] < widths[None, :], conv_weight, 0)
    back = jnp.concatenate([masked, conv_bias[None, :], jnp.zeros((127 - masked.shape[0], masked.shape[1]), masked.dtype)], axis=0)
    limit = (letters - widths)[:, None].astype(jnp.int32)
    count = jnp.log((letters - widths + 1).astype(jnp.float32))[:, None]
    ids = jnp.pad(chars, ((0, 0), (0, -letters % 8))).T
    return ids, table, back.T, back, limit, count

def conv_forward_call(ids, table, weight, limit, count, letters, depth, block=256):
    words = ids.shape[1]
    filters = weight.shape[0]
    full = lambda a: pl.BlockSpec(a.shape, lambda i: (0,) * a.ndim)
    return pl.pallas_call(
        functools.partial(conv_forward, letters, depth),
        grid=(words // block,),
        in_specs=[pl.BlockSpec((ids.shape[0], block), lambda i: (0, i)), full(table), full(weight), full(limit), full(count)],
        out_specs=[pl.BlockSpec((block, filters), lambda i: (i, 0)), pl.BlockSpec((filters, block), lambda i: (0, i)),
                   pl.BlockSpec((letters * depth, block), lambda i: (0, i))],
        out_shape=[jax.ShapeDtypeStruct((words, filters), jnp.bfloat16), jax.ShapeDtypeStruct((filters, words), jnp.float32),
                   jax.ShapeDtypeStruct((letters * depth, words), jnp.bfloat16)],
        scratch_shapes=[pltpu.VMEM((letters + KW - 1, 128, block), jnp.bfloat16), pltpu.VMEM((letters, 128, block), jnp.float32)],
        compiler_params=pltpu.CompilerParams(vmem_limit_bytes=48 << 20),
        name="conv_forward",
    )(ids, table, weight, limit, count)

def conv_backward_call(ids, embed, lse, up, weight, back, limit, count, groups, letters, depth, block=256):
    words = ids.shape[1]
    filters = weight.shape[0]
    full = lambda a: pl.BlockSpec(a.shape, lambda i: (0,) * a.ndim)
    return pl.pallas_call(
        functools.partial(conv_backward, letters, depth),
        grid=(words // block,),
        in_specs=[pl.BlockSpec((ids.shape[0], block), lambda i: (0, i)), pl.BlockSpec((letters * depth, block), lambda i: (0, i)),
                  pl.BlockSpec((filters, block), lambda i: (0, i)), pl.BlockSpec((block, filters), lambda i: (i, 0)),
                  full(weight), full(back), full(limit), full(count)],
        out_specs=[pl.BlockSpec((filters, 128), lambda i: (0, 0)), pl.BlockSpec((2 * groups * depth, 128), lambda i: (0, 0))],
        out_shape=[jax.ShapeDtypeStruct((filters, 128), jnp.float32), jax.ShapeDtypeStruct((2 * groups * depth, 128), jnp.float32)],
        scratch_shapes=[pltpu.VMEM(((letters + KW - 1) * depth, block), jnp.bfloat16), pltpu.VMEM(((letters + KW - 1) * depth, block), jnp.float32),
                        pltpu.VMEM((filters, block), jnp.float32)],
        compiler_params=pltpu.CompilerParams(vmem_limit_bytes=48 << 20),
        name="conv_backward",
    )(ids, embed, lse, up, weight, back, limit, count)


MESH = pl.DeviceIdType.MESH

def greet(peers):
    barrier = pltpu.get_barrier_semaphore()
    for peer in peers:
        pl.semaphore_signal(barrier, inc=1, device_id=peer, device_id_type=MESH)
    pl.semaphore_wait(barrier, len(peers))

def greet_all():
    slot, me = lax.axis_index("dp"), lax.axis_index("filt")
    count, parts = lax.axis_size("dp"), lax.axis_size("filt")
    greet([{"dp": slot ^ far, "filt": me ^ near} for far in range(count) for near in range(parts) if far or near])

def remote(source, target, send, recv, peer):
    return pltpu.make_async_remote_copy(
        src_ref=source, dst_ref=target, send_sem=send, recv_sem=recv,
        device_id=peer, device_id_type=MESH)

def comm_call(kernel, out_shape, scratch, ident, *args, name):
    vmem = pl.BlockSpec(memory_space=pltpu.VMEM)
    return pl.pallas_call(
        kernel, out_shape=out_shape, in_specs=[vmem] * len(args), out_specs=jax.tree.map(lambda _: vmem, out_shape),
        scratch_shapes=scratch,
        compiler_params=pltpu.CompilerParams(collective_id=ident, has_side_effects=True, vmem_limit_bytes=40 << 20),
        name=name)(*args)

DMA = pltpu.SemaphoreType.DMA

def scatter_sum(part_ref, inbox, send, recv, me):
    copies = []
    for hop in (3, 2, 1):
        copy = remote(part_ref.at[me ^ hop], inbox.at[hop - 1], send.at[hop - 1], recv.at[hop - 1], {"filt": me ^ hop})
        copy.start()
        copies.append(copy)
    total = part_ref[me].astype(jnp.float32)
    for copy, hop in reversed(list(zip(copies, (3, 2, 1)))):
        copy.wait()
        total = total + inbox[hop - 1].astype(jnp.float32)
    return total

def gather_blocks(low, all_ref, send, recv, me):
    all_ref[me] = low
    far = remote(all_ref.at[me], all_ref.at[me], send.at[0], recv.at[0], {"filt": me ^ 2})
    near = remote(all_ref.at[me], all_ref.at[me], send.at[1], recv.at[1], {"filt": me ^ 1})
    far.start()
    near.start()
    far.wait_recv()
    relay = remote(all_ref.at[me ^ 2], all_ref.at[me ^ 2], send.at[2], recv.at[2], {"filt": me ^ 1})
    relay.start()
    far.wait_send()
    near.wait()
    relay.wait()

def norm(values, gain, shift, eps):
    center = values - jnp.mean(values, axis=-1, keepdims=True)
    scale = lax.rsqrt(jnp.mean(center * center, axis=-1, keepdims=True) + eps)
    unit = center * scale
    return unit * gain + shift, unit, scale

def norm_back(upstream, unit, scale, gain):
    lifted = upstream * gain
    drop = jnp.mean(lifted, axis=-1, keepdims=True)
    lean = jnp.mean(lifted * unit, axis=-1, keepdims=True)
    return scale * (lifted - drop - unit * lean)

def forward_stage(part_ref, base_ref, gain_ref, shift_ref, value_ref, unit_ref, scale_ref, all_ref, inbox, send, recv, eps):
    me = lax.axis_index("filt")
    greet([{"filt": me ^ hop} for hop in (1, 2, 3)])
    total = scatter_sum(part_ref, inbox, send, recv, me) + base_ref[...]
    value, unit, scale = norm(total, gain_ref[...], shift_ref[...], eps)
    value_ref[...] = value
    unit_ref[...] = unit
    scale_ref[...] = scale
    gather_blocks(value.astype(jnp.bfloat16), all_ref, send.at[pl.ds(3, 3)], recv.at[pl.ds(3, 3)], me)

def top_stage(part_ref, base_ref, up_ref, gain_ref, shift_ref, top_ref, down_ref, dgain_ref, dshift_ref, all_ref, inbox, send, recv, eps):
    me = lax.axis_index("filt")
    greet([{"filt": me ^ hop} for hop in (1, 2, 3)])
    total = scatter_sum(part_ref, inbox, send, recv, me) + base_ref[...]
    top, unit, scale = norm(total, gain_ref[...], shift_ref[...], eps)
    top_ref[...] = top.astype(jnp.bfloat16)
    up = up_ref[...].astype(jnp.float32)
    dgain_ref[...] = jnp.sum(up * unit, axis=0, keepdims=True)
    dshift_ref[...] = jnp.sum(up, axis=0, keepdims=True)
    down = norm_back(up, unit, scale, gain_ref[...])
    down_ref[...] = down
    gather_blocks(down.astype(jnp.bfloat16), all_ref, send.at[pl.ds(3, 3)], recv.at[pl.ds(3, 3)], me)

def start_job(kind, source, target, send, recv):
    slot = lax.axis_index("dp")
    ring, side = slot // 2, slot % 2
    if kind == "side":
        moves = [(source.at[:, 1 - side], target, 1)]
    else:
        moves = [(source.at[ring ^ hop], target.at[hop - 1], 2 * hop) for hop in (2, 3, 1)]
    copies = []
    for index, (piece, place, hop) in enumerate(moves):
        copy = remote(piece, place, send.at[index], recv.at[index], {"dp": slot ^ hop})
        copy.start()
        copies.append(copy)
    return copies

def job_hops(kind):
    return (1,) if kind == "side" else (2, 4, 6)

def backward_stage(kinds, part_ref, base_ref, unit_ref, scale_ref, gain_ref, *refs):
    many = len(kinds)
    job_in, refs = refs[:many], refs[many:]
    (down_ref, dgain_ref, dshift_ref, dlow_ref, all_ref), refs = refs[:5], refs[5:]
    job_out, refs = refs[:many], refs[many:]
    inbox, send, recv = refs[:3]
    me = lax.axis_index("filt")
    slot = lax.axis_index("dp")
    hops = sorted({hop for kind in kinds for hop in job_hops(kind)})
    greet([{"filt": me ^ hop} for hop in (1, 2, 3)] + [{"dp": slot ^ hop} for hop in hops])
    copies = []
    for index, kind in enumerate(kinds):
        copies += start_job(kind, job_in[index], job_out[index], refs[3].at[index], refs[4].at[index])
    up = scatter_sum(part_ref, inbox, send, recv, me) + base_ref[...]
    unit = unit_ref[...]
    dgain_ref[...] = jnp.sum(up * unit, axis=0, keepdims=True)
    dshift_ref[...] = jnp.sum(up, axis=0, keepdims=True)
    down = norm_back(up, unit, scale_ref[...], gain_ref[...])
    down_ref[...] = down
    low = down.astype(jnp.bfloat16)
    dlow_ref[...] = jnp.sum(low.astype(jnp.float32), axis=0, keepdims=True)
    gather_blocks(low, all_ref, send.at[pl.ds(3, 3)], recv.at[pl.ds(3, 3)], me)
    for copy in copies:
        copy.wait()

def stage_scratch(block):
    return [pltpu.VMEM((3,) + block, jnp.bfloat16), DMA((6,)), DMA((6,))]

def f32(*shape): return jax.ShapeDtypeStruct(shape, jnp.float32)
def bf16(*shape): return jax.ShapeDtypeStruct(shape, jnp.bfloat16)

def forward_stage_call(part, base, gain, shift, eps, ident):
    parts, rows, cols = part.shape
    return comm_call(functools.partial(forward_stage, eps=eps),
        (f32(rows, cols), f32(rows, cols), f32(rows, 1), bf16(parts, rows, cols)), stage_scratch((rows, cols)), ident,
        part, base, gain, shift, name="forward_stage")

def top_stage_call(part, base, up, gain, shift, eps, ident):
    parts, rows, cols = part.shape
    return comm_call(functools.partial(top_stage, eps=eps),
        (bf16(rows, cols), f32(rows, cols), f32(1, cols), f32(1, cols), bf16(parts, rows, cols)), stage_scratch((rows, cols)), ident,
        part, base, up, gain, shift, name="top_stage")

def backward_stage_call(part, base, unit, scale, gain, ident, kinds=(), jobs=()):
    parts, rows, cols = part.shape
    vmem = pl.BlockSpec(memory_space=pltpu.VMEM)
    hbm = pl.BlockSpec(memory_space=pl.ANY)
    out_shape = [f32(rows, cols), f32(1, cols), f32(1, cols), f32(1, cols), bf16(parts, rows, cols)]
    scratch = stage_scratch((rows, cols))
    for kind, job in zip(kinds, jobs):
        ring = job.shape[0]
        out_shape.append(bf16(ring, *job.shape[2:]) if kind == "side" else bf16(ring - 1, *job.shape[1:]))
    if kinds:
        scratch += [DMA((len(kinds), 3)), DMA((len(kinds), 3))]
    return pl.pallas_call(
        functools.partial(backward_stage, kinds), out_shape=out_shape, in_specs=[vmem] * 5 + [hbm] * len(kinds),
        out_specs=[vmem] * 5 + [hbm] * len(kinds), scratch_shapes=scratch,
        compiler_params=pltpu.CompilerParams(collective_id=ident, has_side_effects=True, vmem_limit_bytes=24 << 20),
        name="backward_stage")(part, base, unit, scale, gain, *jobs)

def gather_channels(own_ref, all_ref, send, recv, *, chunks):
    me = lax.axis_index("filt")
    greet([{"filt": me ^ hop} for hop in (1, 2)])
    rows, cols = own_ref.shape
    size = rows // chunks

    def lanes(index):
        return pl.ds(pl.multiple_of(index * cols, cols), cols)

    far, near, relay = [], [], []
    for chunk in range(chunks):
        span = pl.ds(chunk * size, size)
        copy = remote(own_ref.at[span, :], all_ref.at[span, lanes(me)], send.at[0, chunk], recv.at[0, chunk], {"filt": me ^ 2})
        copy.start()
        far.append(copy)
    for chunk in range(chunks):
        span = pl.ds(chunk * size, size)
        copy = remote(own_ref.at[span, :], all_ref.at[span, lanes(me)], send.at[1, chunk], recv.at[1, chunk], {"filt": me ^ 1})
        copy.start()
        near.append(copy)
    all_ref[:, lanes(me)] = own_ref[...]
    for chunk in range(chunks):
        span = pl.ds(chunk * size, size)
        far[chunk].wait_recv()
        piece = all_ref.at[span, lanes(me ^ 2)]
        copy = remote(piece, piece, send.at[2, chunk], recv.at[2, chunk], {"filt": me ^ 1})
        copy.start()
        relay.append(copy)
    for chunk in range(chunks):
        far[chunk].wait_send()
        near[chunk].wait()
        relay[chunk].wait()

def gather_channels_call(own, parts, ident, chunks=4):
    rows, cols = own.shape
    return comm_call(functools.partial(gather_channels, chunks=chunks), bf16(rows, cols * parts),
        [DMA((3, chunks)), DMA((3, chunks))], ident, own, name="gather_channels")

def scatter_channels(part_ref, base_ref, out_ref, inbox, merged, send, recv, *, chunks):
    me = lax.axis_index("filt")
    greet([{"filt": me ^ hop} for hop in (1, 2)])
    rows, cols = base_ref.shape
    size = rows // chunks

    def lanes(index):
        return pl.ds(pl.multiple_of(index * cols, cols), cols)

    def hop(source, slot, chunk, peer):
        span = pl.ds(chunk * size, size)
        copy = remote(source, inbox.at[slot, span, :], send.at[slot, chunk], recv.at[slot, chunk], {"filt": peer})
        copy.start()
        return copy

    first, second, third = [], [], []
    for chunk in range(chunks):
        span = pl.ds(chunk * size, size)
        first.append(hop(part_ref.at[span, lanes(me ^ 3)], 0, chunk, me ^ 1))
    for chunk in range(chunks):
        span = pl.ds(chunk * size, size)
        second.append(hop(part_ref.at[span, lanes(me ^ 1)], 1, chunk, me ^ 1))
    for chunk in range(chunks):
        span = pl.ds(chunk * size, size)
        first[chunk].wait_recv()
        both = part_ref[span, lanes(me ^ 2)].astype(jnp.float32) + inbox[0, span, :].astype(jnp.float32)
        merged[span, :] = both.astype(jnp.bfloat16)
        third.append(hop(merged.at[span, :], 2, chunk, me ^ 2))
    for chunk in range(chunks):
        span = pl.ds(chunk * size, size)
        second[chunk].wait_recv()
        third[chunk].wait_recv()
        total = part_ref[span, lanes(me)].astype(jnp.float32) + inbox[1, span, :].astype(jnp.float32)
        total = total + inbox[2, span, :].astype(jnp.float32) + base_ref[span, :]
        out_ref[span, :] = total.astype(jnp.bfloat16)
    for copy in first + second + third:
        copy.wait_send()

def scatter_channels_call(part, base, ident, chunks=4):
    rows, cols = base.shape
    return comm_call(functools.partial(scatter_channels, chunks=chunks), bf16(rows, cols),
        [pltpu.VMEM((3, rows, cols), jnp.bfloat16), pltpu.VMEM((rows, cols), jnp.bfloat16), DMA((3, chunks)), DMA((3, chunks))],
        ident, part, base, name="scatter_channels")


class Total:
    def __init__(self, low, inbox, out, send, recv, sides=None):
        self.low, self.inbox, self.out, self.sides = low, inbox, out, sides
        self.send, self.recv = send, recv
        self.me, self.slot = lax.axis_index("filt"), lax.axis_index("dp")
        self.count = low.shape[0]
        self.copies = []

    def push(self, source, target, kind, hop, peer):
        copy = remote(source, target, self.send.at[kind, hop - 1], self.recv.at[kind, hop - 1], peer)
        copy.start()
        self.copies.append(copy)
        return copy

    def start(self, value):
        self.low[...] = value.astype(jnp.bfloat16)
        self.first = [
            self.push(self.low.at[self.slot ^ hop], self.inbox.at[hop - 1], 0, hop, {"dp": self.slot ^ hop})
            for hop in range(1, self.count)
        ]

    def combine(self):
        for copy in self.first:
            copy.wait_recv()
        total = self.low[self.slot].astype(jnp.float32)
        for hop in range(1, self.count):
            total = total + self.inbox[hop - 1].astype(jnp.float32)
        self.out[self.slot] = total.astype(jnp.bfloat16)
        if self.sides is None:
            self.spread()
            return
        self.sides[0] = total.astype(jnp.bfloat16)
        self.second = [self.push(self.sides.at[0], self.sides.at[hop], 1, hop, {"filt": self.me ^ hop}) for hop in (1, 2, 3)]

    def across(self):
        for copy in self.second:
            copy.wait_recv()
        left = self.sides[0].astype(jnp.float32) + self.sides[1].astype(jnp.float32)
        right = self.sides[2].astype(jnp.float32) + self.sides[3].astype(jnp.float32)
        self.out[self.slot] = (left + right).astype(jnp.bfloat16)
        self.spread()

    def spread(self):
        piece = self.out.at[self.slot]
        self.third = [self.push(piece, piece, 2, hop, {"dp": self.slot ^ hop}) for hop in range(1, self.count)]

    def finish(self):
        for copy in self.third:
            copy.wait_recv()
        for copy in self.copies:
            copy.wait_send()


def prologue(letters, depth, block, chunks, window, first, chars_ref, table_ref, weight_ref, limit_ref, count_ref, shard_ref,
             acts_ref, lse_ref, embed_ref, all_ref, full_ref, patch_ref, grid_ref,
             zsend, zrecv, local, ysend, yrecv, fsend, frecv):
    words = chars_ref.shape[1]
    filters = weight_ref.shape[0]
    me = lax.axis_index("filt")
    slot = lax.axis_index("dp")
    ring, side = slot // 2, slot % 2
    greet([{"filt": me ^ hop} for hop in (1, 2)] + [{"dp": slot ^ hop} for hop in (1, 2, 4, 6)])
    parts = all_ref.shape[1] // filters
    span = shard_ref.shape[0] // (chunks // 2)

    def spot(chunk):
        return pl.ds((chunk // 2) * span, span), chunk % 2

    own, far = [], []

    def start_chunk(chunk):
        if chunk >= chunks:
            return
        rows, half = spot(chunk)
        source = shard_ref.at[rows, pl.ds(pl.multiple_of(half * filters * parts + me * filters, filters), filters)]
        target = full_ref.at[half, ring, side, rows, :]
        copy = pltpu.make_async_copy(source, target, local.at[chunk])
        copy.start()
        own.append(copy)
        for hop in (2, 1, 3):
            copy = remote(source, target, zsend.at[chunk, hop - 1], zrecv.at[chunk, hop - 1], {"dp": slot ^ (2 * hop)})
            copy.start()
            far.append(copy)

    for chunk in range(window):
        start_chunk(chunk)
    cross = []

    def forward_chunk(chunk):
        rows, half = spot(chunk)
        own[chunk].wait()
        for copy in far[3 * chunk : 3 * chunk + 3]:
            copy.wait_recv()
        start_chunk(chunk + window)
        piece = full_ref.at[half, :, side, rows, :]
        copy = remote(piece, piece, ysend.at[chunk], yrecv.at[chunk], {"dp": slot ^ 1})
        copy.start()
        cross.append(copy)

    lead = KW - 1
    rows = KW * depth
    groups = table_ref.shape[0] // depth
    patch_ref[:, :rows, :] = jnp.zeros((patch_ref.shape[0], rows, block), jnp.bfloat16)
    ones = lax.broadcasted_iota(jnp.int32, (128 - rows, block), 0) == 0
    tail = jnp.where(ones, 1.0, 0.0).astype(jnp.bfloat16)
    patch_ref[:, rows:, :] = jnp.broadcast_to(tail[None], (patch_ref.shape[0],) + tail.shape)
    chunk = grid_ref.shape[1]
    always = letters - KW + 1
    steps = filters // chunk
    polls = {(step // steps, step % steps): step - first for step in range(first, min(first + chunks, words // block * steps))}
    gathers = ChannelGather(acts_ref, all_ref, fsend, frecv, words // block)
    for index in range(words // block):
        cols = pl.ds(index * block, block)

        def embed(position, carry):
            ids = chars_ref[pl.ds(position, 1), cols]
            low = ids & 127
            group = ids >> 7
            onehot = lax.broadcasted_iota(jnp.int32, (128, block), 0) == low
            onehot = jnp.where(onehot, 1.0, 0.0).astype(jnp.bfloat16)
            looked = nn_dot(table_ref[...], onehot)
            row = looked[:depth]
            for part in range(1, groups):
                row = jnp.where(group == part, looked[part * depth : (part + 1) * depth], row)
            row = row.astype(jnp.bfloat16)
            embed_ref[pl.ds(pl.multiple_of(position * depth, depth), depth), cols] = row
            for tap in range(KW):
                patch_ref[position + lead - tap, tap * depth : (tap + 1) * depth, :] = row
            return carry

        lax.fori_loop(0, letters, embed, 0, unroll=5)
        for start in range(0, filters, chunk):
            weight = weight_ref[start : start + chunk, :]
            limit = limit_ref[start : start + chunk, :]

            def product(position, top):
                grid = nn_dot(weight, patch_ref[position + lead])
                grid_ref[position] = grid
                return jnp.maximum(top, grid)

            top = lax.fori_loop(0, always, product, jnp.full((chunk, block), -1e30, jnp.float32), unroll=11)
            for position in range(always, letters):
                grid = nn_dot(weight, patch_ref[position + lead])
                grid = jnp.where(limit >= position, grid, -1e30)
                grid_ref[position] = grid
                top = jnp.maximum(top, grid)

            def total(position, acc):
                return acc + jnp.exp(grid_ref[position] - top)

            acc = lax.fori_loop(0, letters, total, jnp.zeros((chunk, block), jnp.float32), unroll=10)
            lse = top + jnp.log(acc)
            lse_ref[start : start + chunk, cols] = lse
            pooled = lse - count_ref[start : start + chunk, :]
            acts_ref[cols, start : start + chunk] = (pooled * normal_cdf(pooled)).astype(jnp.bfloat16).T
            poll = polls.get((index, start // chunk))
            if poll is not None:
                forward_chunk(poll)
        gathers.send(index)
    for index in range(len(polls), chunks):
        forward_chunk(index)
    for index in range(words // block):
        gathers.relay(index)
    gathers.finish()
    for copy in far:
        copy.wait_send()
    for copy in cross:
        copy.wait()

class ChannelGather:
    def __init__(self, own_ref, all_ref, send, recv, pieces):
        self.me = lax.axis_index("filt")
        self.own, self.all, self.sems = own_ref, all_ref, (send, recv)
        self.size = own_ref.shape[0] // pieces
        self.copies = []

    def view(self, index, piece):
        cols = self.own.shape[1]
        return self.all.at[pl.ds(piece * self.size, self.size), pl.ds(pl.multiple_of(index * cols, cols), cols)]

    def push(self, source, target, kind, piece, hop):
        send, recv = self.sems
        copy = remote(source, target, send.at[kind, piece], recv.at[kind, piece], {"filt": self.me ^ hop})
        copy.start()
        self.copies.append(copy)
        return copy

    def send(self, piece):
        source = self.own.at[pl.ds(piece * self.size, self.size), :]
        target = self.view(self.me, piece)
        self.push(source, target, 0, piece, 2)
        self.push(source, target, 1, piece, 1)
        cols = self.own.shape[1]
        self.all[pl.ds(piece * self.size, self.size), pl.ds(pl.multiple_of(self.me * cols, cols), cols)] = self.own[pl.ds(piece * self.size, self.size), :]

    def relay(self, piece):
        self.copies[2 * piece].wait_recv()
        view = self.view(self.me ^ 2, piece)
        self.push(view, view, 2, piece, 1)

    def finish(self):
        for index, copy in enumerate(self.copies):
            copy.wait_send()
            if index % 2 == 1 or index >= 2 * (len(self.copies) // 3):
                copy.wait_recv()

def prologue_call(ids, table, weight, limit, count, shard, parts, letters, depth, ident, block=256, chunks=8, window=2, first=2):
    words = ids.shape[1]
    filters = weight.shape[0]
    rows = shard.shape[0]
    vmem = pl.BlockSpec(memory_space=pltpu.VMEM)
    hbm = pl.BlockSpec(memory_space=pl.ANY)
    pieces = words // block
    return pl.pallas_call(
        functools.partial(prologue, letters, depth, block, chunks, window, first),
        in_specs=[vmem] * 5 + [hbm],
        out_specs=[vmem] * 4 + [hbm],
        out_shape=[bf16(words, filters), f32(filters, words), bf16(letters * depth, words), bf16(words, filters * parts),
                   bf16(2, 4, 2, rows, filters)],
        scratch_shapes=[pltpu.VMEM((letters + KW - 1, 128, block), jnp.bfloat16), pltpu.VMEM((letters, 128, block), jnp.float32),
                        DMA((chunks, 3)), DMA((chunks, 3)), DMA((chunks,)), DMA((chunks,)), DMA((chunks,)), DMA((3, pieces)), DMA((3, pieces))],
        compiler_params=pltpu.CompilerParams(collective_id=ident, has_side_effects=True, vmem_limit_bytes=48 << 20),
        name="prologue",
    )(ids, table, weight, limit, count, shard)


def sigmoid(values):
    return 1.0 / (1.0 + jnp.exp(-values))


def highway_stage(eps, slim_ref, feats_ref, wide_ref, bias_ref, acts_ref, base_ref, gain_ref, shift_ref,
                  gates_ref, hidden_ref, proj_ref, out_ref, value_ref, unit_ref, scale_ref, all_ref,
                  abox, part_ref, inbox, send, recv, asend, arecv):
    me = lax.axis_index("filt")
    greet([{"filt": me ^ hop} for hop in (1, 2, 3)])
    parts, sides, rows, dmodel = abox.shape
    copies = []
    size, small = proj_ref.shape[0] // (sides * parts), out_ref.shape[0] // (sides * (parts - 1))
    for index, span in enumerate((pl.ds(0, size), pl.ds(size, rows - size))):
        for hop in (2, 3, 1):
            source = slim_ref.at[pl.ds(sides * (me ^ hop), sides), span, :]
            copy = remote(source, abox.at[me, :, span, :], asend.at[index, hop - 1], arecv.at[index, hop - 1], {"filt": me ^ hop})
            copy.start()
            copies.append(copy)
    own = pltpu.make_async_copy(slim_ref.at[pl.ds(sides * me, sides), pl.ds(0, rows), :], abox.at[me], asend.at[0, 3])
    own.start()
    words, filters = acts_ref.shape
    block = 256

    def mix(index, carry):
        span = pl.ds(pl.multiple_of(index * block, block), block)
        feats = feats_ref[span, :]
        turn = nn_dot(feats, wide_ref[0]) + bias_ref[:, :filters]
        gates_ref[span, :filters] = turn
        gate = nn_dot(feats, wide_ref[1]) + bias_ref[:, filters:]
        gates_ref[span, filters:] = gate
        keep = sigmoid(gate)
        mixed = keep * acts_ref[span, :].astype(jnp.float32) + (1.0 - keep) * (turn * normal_cdf(turn))
        hidden_ref[span, :] = mixed.astype(jnp.bfloat16)
        return carry

    lax.fori_loop(0, words // block, mix, 0)
    own.wait()
    for copy in copies[:3]:
        copy.wait()
    width = dmodel // parts
    for part in range(parts):
        cols = slice(part * width, (part + 1) * width)
        for side in range(sides):
            for group in range(parts):
                lanes = slice(group * width, (group + 1) * width)
                start = (side * parts + group) * size
                proj_ref[start : start + size, cols] = abox[part, side, :size, lanes]

    def project(index, carry):
        span = pl.ds(pl.multiple_of(index * 128, 128), 128)
        part_ref[index] = nn_dot(hidden_ref[span, :], proj_ref[...]).astype(jnp.bfloat16)
        return carry

    lax.fori_loop(0, parts, project, 0)
    total = scatter_sum(part_ref, inbox, send, recv, me) + base_ref[...]
    value, unit, scale = norm(total, gain_ref[...], shift_ref[...], eps)
    value_ref[...] = value
    unit_ref[...] = unit
    scale_ref[...] = scale
    gather_blocks(value.astype(jnp.bfloat16), all_ref, send.at[pl.ds(3, 3)], recv.at[pl.ds(3, 3)], me)
    for copy in copies[3:]:
        copy.wait()
    for part in range(parts):
        cols = slice(part * width, (part + 1) * width)
        for side in range(sides):
            for group in range(parts - 1):
                start = (side * (parts - 1) + group) * small
                out_ref[start : start + small, cols] = abox[part, side, size:, group * width : (group + 1) * width]


def highway_stage_call(slim, feats, wide, bias, acts, base, gain, shift, out_rows, po_rows, eps, ident):
    words, filters = acts.shape
    rows, dmodel = base.shape
    parts = words // rows
    vmem = pl.BlockSpec(memory_space=pltpu.VMEM)
    hbm = pl.BlockSpec(memory_space=pl.ANY)
    return pl.pallas_call(
        functools.partial(highway_stage, eps), in_specs=[hbm] + [vmem] * 7, out_specs=[vmem] * 8,
        out_shape=[f32(words, 2 * filters), bf16(words, filters), bf16(filters, dmodel), bf16(out_rows, dmodel), f32(rows, dmodel),
                   f32(rows, dmodel), f32(rows, 1), bf16(parts, rows, dmodel)],
        scratch_shapes=[pltpu.VMEM((parts, 2, po_rows, dmodel), jnp.bfloat16), pltpu.VMEM((parts, rows, dmodel), jnp.bfloat16)]
        + stage_scratch((rows, dmodel)) + [DMA((2, 4)), DMA((2, 3))],
        compiler_params=pltpu.CompilerParams(collective_id=ident, has_side_effects=True, vmem_limit_bytes=48 << 20),
        name="highway_stage",
    )(slim, feats, wide, bias, acts, base, gain, shift)


class RowReduce:
    def __init__(self, grad, yin, pair, zin, joined, span, sems, base=0):
        self.base, self.ready, self.after = base, [], None
        self.grad, self.yin, self.pair, self.zin, self.joined = grad, yin, pair, zin, joined
        self.span, self.sems = span, sems
        self.me, self.slot = lax.axis_index("filt"), lax.axis_index("dp")
        self.ring, self.side = self.slot // 2, self.slot % 2
        self.copies = []

    def push(self, source, target, index, peer):
        send, recv = self.sems
        copy = remote(source, target, send.at[index], recv.at[index], peer)
        copy.start()
        self.copies.append(copy)
        return copy

    def across(self):
        span = self.span
        for copy in self.ready:
            copy.wait_recv()
        self.first = self.push(
            self.grad.at[:, 1 - self.side, span, :], self.yin.at[:, span, :], 0, {"dp": self.slot ^ 1}
        )

    def along(self):
        span = self.span
        self.first.wait_recv()
        if self.after is not None:
            self.after.across()
        both = self.grad[:, self.side, span, :].astype(jnp.float32) + self.yin[:, span, :].astype(jnp.float32)
        self.pair[:, span, :] = both.astype(jnp.bfloat16)
        self.ring_out()

    def local(self):
        return pl.ds(self.span.start - self.base, self.span.size)

    def ring_out(self):
        span = self.local()
        self.rest = [
            self.push(self.pair.at[self.ring ^ hop, span, :], self.zin.at[hop - 1, span, :], hop, {"dp": self.slot ^ (2 * hop)})
            for hop in (2, 3, 1)
        ]

    def join(self):
        span = self.local()
        for copy in self.rest:
            copy.wait_recv()
        total = self.pair[self.ring, span, :].astype(jnp.float32)
        for hop in (1, 2, 3):
            total = total + self.zin[hop - 1, span, :].astype(jnp.float32)
        self.joined[self.me, self.span, :] = total.astype(jnp.bfloat16)
        self.share()

    def share(self):
        piece = self.joined.at[self.me, self.span, :]
        self.far = self.push(piece, piece, 4, {"filt": self.me ^ 2})
        self.near = self.push(piece, piece, 5, {"filt": self.me ^ 1})

    def relay(self):
        self.far.wait_recv()
        piece = self.joined.at[self.me ^ 2, self.span, :]
        self.last = self.push(piece, piece, 6, {"filt": self.me ^ 1})

    def finish(self):
        self.near.wait_recv()
        self.last.wait_recv()
        for copy in self.copies:
            copy.wait_send()


AHEAD = 2


def epilogue(letters, depth, block, *refs):
    (dproj_ref, proj_ref, hidden_ref, gates_ref, acts_ref, feats_ref, high_ref, attended_ref, dmixed_ref, chars_ref, embed_ref, lse_ref, weight_ref, back_ref, limit_ref, count_ref, slim_ref,
     ffn_ref, pair_ref, pos_ref, few_ref,
     wide_out, slim_out, rows_out, ffn_out, conv_out, table_out, pos_out, few_out,
     bias_ref, part_ref, base_ref, dgates_ref, wide_ref, cross_ref, inbox, merged, up_ref, patch_ref, down_ref, pull_ref, wgrad_ref, tgrad_ref, wide_y, wide_p, wide_z, slim_y, slim_p, slim_z,
     rows_ref, rows_y, rows_p, rows_z, late_z, conv_low, conv_in, table_low, table_in, table_side, pos_low, pos_in, few_low, few_in, few_side,
     csend, crecv, rsend, rrecv, tsend, trecv, asend, arecv) = refs
    me = lax.axis_index("filt")
    greet_all()
    pos = Total(pos_low, pos_in, pos_out, tsend.at[0], trecv.at[0])
    few = Total(few_low, few_in, few_out, tsend.at[1], trecv.at[1], few_side)
    conv_total = Total(conv_low, conv_in, conv_out, tsend.at[2], trecv.at[2])
    table_total = Total(table_low, table_in, table_out, tsend.at[3], trecv.at[3], table_side)
    wide_rows = wide_out.shape[1] // 4
    slim = RowReduce(slim_ref, slim_y, slim_p, slim_z, slim_out, pl.ds(0, slim_out.shape[1]), (rsend.at[4], rrecv.at[4]))
    both = RowReduce(rows_ref, rows_y, rows_p, rows_z, rows_out, pl.ds(0, rows_out.shape[1]), (rsend.at[6], rrecv.at[6]))
    wide = [
        RowReduce(wide_ref, wide_y, wide_p, wide_z, wide_out, pl.ds(index * wide_rows, wide_rows), (rsend.at[index], rrecv.at[index]))
        for index in range(4)
    ]
    early = ffn_ref.shape[0]
    ffn = RowReduce(None, None, None, None, ffn_out, pl.ds(0, early), (rsend.at[5], rrecv.at[5]))
    late = RowReduce(None, None, pair_ref, late_z, ffn_out, pl.ds(early, pair_ref.shape[1]), (rsend.at[7], rrecv.at[7]), early)
    swaps = [
        remote(cross_ref.at[me ^ hop], rows_ref.at[me], asend.at[hop - 1], arecv.at[hop - 1], {"filt": me ^ hop}) for hop in (2, 3, 1)
    ]
    both.ready = swaps
    pos.start(pos_ref[...])
    queue = [slim, wide[0], wide[1], both, wide[2], wide[3]]
    for index, item in enumerate(queue):
        item.after = queue[index + AHEAD] if index + AHEAD < len(queue) else None
    slim.across()
    ffn_out[me, :early, :] = ffn_ref[...]
    late.ring_out()
    highway_mix_back(dproj_ref, proj_ref, hidden_ref, gates_ref, acts_ref, base_ref, dgates_ref, bias_ref)
    highway_grads(feats_ref, dgates_ref, wide_ref)
    for item in queue[1:AHEAD]:
        item.across()
    extra = few_ref[...]
    place, row = lax.broadcasted_iota(jnp.int32, extra.shape, 0), lax.broadcasted_iota(jnp.int32, extra.shape, 1)
    lanes = extra.shape[2]
    extra = jnp.where((row == 0) & (place == me), bias_ref[:, :lanes][None], extra)
    extra = jnp.where((row == 0) & (place == me + 4), bias_ref[:, lanes:][None], extra)
    few.start(extra)
    highway_down(dgates_ref, high_ref, part_ref)
    scatter = ChannelScatter(part_ref, base_ref, up_ref, inbox, merged, csend, crecv)
    scatter.begin()
    row_grads(hidden_ref, dproj_ref, attended_ref, dmixed_ref, cross_ref)
    rows_ref[me] = cross_ref[me]
    scatter.finish()
    pos.combine()
    few.combine()
    for copy in swaps:
        copy.start()
    ffn.share()
    steps = iter([
        [slim.along], [wide[0].along, ffn.relay], [late.join, slim.join], [wide[1].along, wide[0].join], [late.relay, slim.relay, few.across],
        [wide[0].relay, both.along], [wide[1].join], [wide[1].relay], [wide[2].along, both.join], [both.relay],
    ])

    def advance():
        for step in next(steps):
            step()

    filters = weight_ref.shape[0]
    rows = KW * depth
    groups = tgrad_ref.shape[0] // (2 * depth)
    wgrad_ref[...] = jnp.zeros(wgrad_ref.shape, jnp.float32)
    tgrad_ref[...] = jnp.zeros(tgrad_ref.shape, jnp.float32)
    patch_ref[letters * depth :, :] = jnp.zeros((patch_ref.shape[0] - letters * depth, block), jnp.bfloat16)
    ones = jnp.where(lax.broadcasted_iota(jnp.int32, (128 - rows, block), 0) == 0, 1.0, 0.0).astype(jnp.bfloat16)
    always = letters - KW + 1
    quarter = always // 4
    for index in range(chars_ref.shape[1] // block):
        cols = pl.ds(index * block, block)
        patch_ref[: letters * depth, :] = embed_ref[:, cols]
        down_ref[...] = jnp.zeros(down_ref.shape, jnp.float32)
        pooled = lse_ref[:, cols] - count_ref[...]
        slope = normal_cdf(pooled) + pooled * (DENSITY * jnp.exp(-0.5 * pooled * pooled))
        pull_ref[...] = slope * up_ref[cols, :].T.astype(jnp.float32)

        def one(position, masked):
            start = position * depth
            if not isinstance(position, int):
                start = pl.multiple_of(start, depth)
            patch = jnp.concatenate([patch_ref[pl.ds(start, rows), :], ones], axis=0)
            grid = nn_dot(weight_ref[...], patch)
            spread = jnp.exp(grid - lse_ref[:, cols]) * pull_ref[...]
            if masked:
                spread = jnp.where(limit_ref[...] >= position, spread, 0.0)
            spread = spread.astype(jnp.bfloat16)
            down = nn_dot(back_ref[...], spread)
            down_ref[pl.ds(start, rows), :] += down[:rows]
            wgrad_ref[...] += nt_dot(spread, patch)

        def body(position, carry):
            one(position, False)
            return carry

        for lap in range(4):
            stop = always if lap == 3 else (lap + 1) * quarter
            lax.fori_loop(lap * quarter, stop, body, 0, unroll=11)
            advance()
        for position in range(always, letters):
            one(position, True)

        def table(position, carry):
            ids = chars_ref[pl.ds(position, 1), cols]
            low = ids & 127
            group = ids >> 7
            onehot = lax.broadcasted_iota(jnp.int32, (128, block), 0) == low
            onehot = jnp.where(onehot, 1.0, 0.0).astype(jnp.bfloat16)
            down = down_ref[pl.ds(pl.multiple_of(position * depth, depth), depth), :]
            high = down.astype(jnp.bfloat16)
            rest = (down - high.astype(jnp.float32)).astype(jnp.bfloat16)
            zero = jnp.zeros_like(high)
            parts = [jnp.where(group == part, item, zero) for item in (high, rest) for part in range(groups)]
            tgrad_ref[...] += nt_dot(jnp.concatenate(parts, axis=0), onehot)
            return carry

        lax.fori_loop(0, letters, table, 0, unroll=5)
        advance()
    table_rows = tgrad_ref.shape[0] // 2
    slices, size = table_low.shape[:2]
    conv_total.start(wgrad_ref[...].reshape(conv_low.shape))
    sums = tgrad_ref[:table_rows, :] + tgrad_ref[table_rows:, :]
    sums = jnp.concatenate([sums, jnp.zeros((slices * size - table_rows, sums.shape[1]), jnp.float32)], axis=0)
    table_total.start(sums.reshape(table_low.shape))
    for step in (
        wide[3].along, conv_total.combine, table_total.combine, wide[2].join, wide[2].relay, table_total.across,
        wide[3].join, wide[3].relay,
    ):
        step()
    for copy in swaps:
        copy.wait_send()
    for item in [ffn, late, slim, both, pos, few, conv_total, table_total] + wide:
        item.finish()


class ChannelScatter:
    def __init__(self, part_ref, base_ref, out_ref, inbox, merged, send, recv):
        self.part, self.base, self.out, self.inbox, self.merged = part_ref, base_ref, out_ref, inbox, merged
        self.sems = (send, recv)
        self.me = lax.axis_index("filt")

    def begin(self):
        me = self.me
        rows, cols = self.base.shape
        pieces = self.sems[0].shape[1]
        size = rows // pieces

        def lanes(index):
            return pl.ds(pl.multiple_of(index * cols, cols), cols)

        def hop(source, kind, piece, peer):
            span = pl.ds(piece * size, size)
            send, recv = self.sems
            copy = remote(source, self.inbox.at[kind, span, :], send.at[kind, piece], recv.at[kind, piece], {"filt": peer})
            copy.start()
            return copy

        self.lanes, self.hop = lanes, hop
        self.spans = spans = [pl.ds(piece * size, size) for piece in range(pieces)]
        first = [hop(self.part.at[span, lanes(me ^ 3)], 0, piece, me ^ 1) for piece, span in enumerate(spans)]
        second = [hop(self.part.at[span, lanes(me ^ 1)], 1, piece, me ^ 1) for piece, span in enumerate(spans)]
        self.first, self.second = first, second

    def finish(self):
        me, lanes, hop, first, second, spans = self.me, self.lanes, self.hop, self.first, self.second, self.spans
        third = []
        for piece, span in enumerate(spans):
            first[piece].wait_recv()
            both = self.part[span, lanes(me ^ 2)].astype(jnp.float32) + self.inbox[0, span, :].astype(jnp.float32)
            self.merged[span, :] = both.astype(jnp.bfloat16)
            third.append(hop(self.merged.at[span, :], 2, piece, me ^ 2))
        for piece, span in enumerate(spans):
            second[piece].wait_recv()
            third[piece].wait_recv()
            total = self.part[span, lanes(me)].astype(jnp.float32) + self.inbox[1, span, :].astype(jnp.float32)
            total = total + self.inbox[2, span, :].astype(jnp.float32) + self.base[span, :]
            self.out[span, :] = total.astype(jnp.bfloat16)
        for copy in first + second + third:
            copy.wait_send()


def highway_mix_back(dproj_ref, proj_ref, hidden_ref, gates_ref, acts_ref, din_ref, dgates_ref, bias_ref):
    words, filters = acts_ref.shape
    block = 128
    bias_ref[...] = jnp.zeros(bias_ref.shape, jnp.float32)

    def mix(index, carry):
        span = pl.ds(pl.multiple_of(index * block, block), block)
        dhidden = nt_dot(dproj_ref[span, :], proj_ref[...])
        turn = gates_ref[span, :filters]
        keep = sigmoid(gates_ref[span, filters:])
        below = normal_cdf(turn)
        slope = below + turn * (DENSITY * jnp.exp(-0.5 * turn * turn))
        fresh = dhidden * (1.0 - keep)
        din_ref[span, :] = dhidden * keep
        dturn = (fresh * slope).astype(jnp.bfloat16)
        dkeep = (fresh * keep * (acts_ref[span, :].astype(jnp.float32) - turn * below)).astype(jnp.bfloat16)
        dgates_ref[span, :filters] = dturn
        dgates_ref[span, filters:] = dkeep
        bias_ref[:, :filters] += jnp.sum(dturn.astype(jnp.float32), axis=0, keepdims=True)
        bias_ref[:, filters:] += jnp.sum(dkeep.astype(jnp.float32), axis=0, keepdims=True)
        return carry

    lax.fori_loop(0, words // block, mix, 0)


def highway_grads(feats_ref, dgates_ref, grad_ref):
    rings, sides, rows, cols = grad_ref.shape
    piece = sides * rows

    def grads(index, carry):
        lanes = pl.ds(pl.multiple_of(index * piece, piece), piece)
        grad = tn_dot(feats_ref[:, lanes], dgates_ref[...]).astype(jnp.bfloat16)
        grad_ref[index] = grad.reshape(sides, rows, cols)
        return carry

    lax.fori_loop(0, rings, grads, 0)


def highway_down(dgates_ref, high_ref, part_ref):
    filters = high_ref.shape[2]
    piece = 512

    def down(index, carry):
        lanes = pl.ds(pl.multiple_of(index * piece, piece), piece)
        both = nt_dot(dgates_ref[:, :filters], high_ref[0, lanes, :]) + nt_dot(dgates_ref[:, filters:], high_ref[1, lanes, :])
        part_ref[:, lanes] = both.astype(jnp.bfloat16)
        return carry

    lax.fori_loop(0, part_ref.shape[1] // piece, down, 0)


def row_grads(hidden_ref, dproj_ref, attended_ref, dmixed_ref, both_ref):
    parts, sides, rows, dmodel = both_ref.shape
    width = dmodel // parts
    gproj = tn_dot(hidden_ref[...], dproj_ref[...]).astype(jnp.bfloat16)
    gout = tn_dot(attended_ref[...], dmixed_ref[...]).astype(jnp.bfloat16)
    size, small = gproj.shape[0] // (sides * parts), gout.shape[0] // (sides * (parts - 1))
    for part in range(parts):
        cols = slice(part * width, (part + 1) * width)
        for side in range(sides):
            for group in range(parts):
                lanes = slice(group * width, (group + 1) * width)
                start = (side * parts + group) * size
                both_ref[part, side, :size, lanes] = gproj[start : start + size, cols]
                if group < parts - 1:
                    start = (side * (parts - 1) + group) * small
                    both_ref[part, side, size:, lanes] = gout[start : start + small, cols]
                else:
                    both_ref[part, side, size:, lanes] = jnp.zeros((rows - size, width), jnp.bfloat16)


def epilogue_call(dproj, proj, hidden, gates, acts, feats, high, attended, dmixed, ids, embed, lse, weight, back, limit, count,
                  slim, ffn, pair, pos, few, po_rows, letters, depth, groups, ident, block=256):
    filters, words = lse.shape
    args = (dproj, proj, hidden, gates, acts, feats, high, attended, dmixed, ids, embed, lse, weight, back, limit, count,
            slim, ffn, pair, pos, few)
    channels, dmodel = feats.shape[1], dproj.shape[1]
    parts = channels // filters
    slices = pos.shape[0]
    pieces = 4
    vmem = pl.BlockSpec(memory_space=pltpu.VMEM)
    table_size = -(-(-(-groups * depth // slices)) // 8) * 8
    wide_shape = (slices // 2, 2, channels // slices, 2 * filters)
    both_shape = (slices // 2, 2, po_rows, dmodel)

    def space(shape, dtype=jnp.bfloat16):
        return pltpu.VMEM(tuple(shape), dtype)

    def stages(shape):
        ring, side, rows, cols = shape
        return [space((ring, rows, cols)), space((ring, rows, cols)), space((ring - 1, rows, cols))]

    def totals(shape, sides):
        spaces = [space(shape), space((shape[0] - 1,) + shape[1:])]
        return spaces + ([space((4,) + shape[1:])] if sides else [])

    conv_shape = (slices, filters // slices, 128)
    table_shape = (slices, table_size, 128)
    out_shape = [bf16(parts, *wide_shape[2:]), bf16(parts, *slim.shape[2:]), bf16(parts, *both_shape[2:]),
                 bf16(parts, ffn.shape[0] + pair.shape[1], ffn.shape[1]), bf16(*conv_shape), bf16(*table_shape), bf16(*pos.shape),
                 bf16(*few.shape)]
    padded = (letters + KW - 1) * depth
    return pl.pallas_call(
        functools.partial(epilogue, letters, depth, block),
        in_specs=[vmem] * len(args),
        out_specs=[vmem] * len(out_shape),
        out_shape=out_shape,
        scratch_shapes=[space((1, 2 * filters), jnp.float32), space((words, channels)), space((words, filters), jnp.float32), space((words, 2 * filters)), space(wide_shape),
                        space(both_shape), space((3, words, filters)), space((words, filters)), space((words, filters)), space((padded, block)),
                        space((padded, block), jnp.float32), space((filters, block), jnp.float32),
                        space((filters, 128), jnp.float32), space((2 * groups * depth, 128), jnp.float32)]
        + stages(wide_shape) + stages(slim.shape) + [space(both_shape)] + stages(both_shape) + [space((3,) + pair.shape[1:])]
        + totals(conv_shape, False) + totals(table_shape, True) + totals(pos.shape, False) + totals(few.shape, True)
        + [DMA((3, pieces)), DMA((3, pieces)), DMA((8, 7)), DMA((8, 7)), DMA((4, 3, slices - 1)), DMA((4, 3, slices - 1)),
           DMA((3,)), DMA((3,))],
        compiler_params=pltpu.CompilerParams(collective_id=ident, has_side_effects=True, vmem_limit_bytes=60 << 20),
        name="epilogue",
    )(*args)


def assemble(depth, wide_ref, slim_ref, both_ref, ffn_ref, conv_ref, table_ref, pos_ref, few_ref, limit_ref,
             wide_out, slim_out, proj_out, out_out, inner_out, outer_out, conv_out, cbias_out, table_out, pos_out,
             hbias_out, pbias_out, gain_out, shift_out, ibias_out):
    parts = wide_ref.shape[0]
    inner_rows = inner_out.shape[0]
    proj_rows, out_rows = proj_out.shape[0] // parts, out_out.shape[0] // (parts - 1)
    filters = wide_ref.shape[2] // 2
    width = slim_ref.shape[2] // 3
    for part in range(parts):
        for half in range(2):
            start = (half * parts + part) * filters
            wide_out[:, start : start + filters] = wide_ref[part, :, half * filters : (half + 1) * filters].astype(jnp.float32)
        for block in range(3):
            start = (block * parts + part) * width
            slim_out[:, start : start + width] = slim_ref[part, :, block * width : (block + 1) * width].astype(jnp.float32)
        cols = slice(part * width, (part + 1) * width)
        for block in range(parts):
            lanes = slice(block * width, (block + 1) * width)
            proj_out[block * proj_rows : (block + 1) * proj_rows, cols] = both_ref[part, :proj_rows, lanes].astype(jnp.float32)
            if block < parts - 1:
                out_out[block * out_rows : (block + 1) * out_rows, cols] = both_ref[part, proj_rows:, lanes].astype(jnp.float32)
        units = ffn_ref.shape[1] - inner_rows
        outer_out[part * units : (part + 1) * units, :] = ffn_ref[part, inner_rows:, :].astype(jnp.float32)
        for block in range(inner_out.shape[1] // (parts * units)):
            start = (block * parts + part) * units
            inner_out[:, start : start + units] = ffn_ref[part, :inner_rows, block * units : (block + 1) * units].astype(jnp.float32)
    slices, conv_rows = conv_ref.shape[:2]
    taps = conv_out.shape[0]
    turned = conv_ref[...].reshape(slices * conv_rows, 128).astype(jnp.float32).T
    tap = lax.broadcasted_iota(jnp.int32, (taps, 1), 0) // depth
    conv_out[...] = jnp.where(tap < limit_ref[...], turned[:taps], 0.0)
    cbias_out[...] = turned[taps : taps + 1]
    table = table_ref[...].reshape(-1, 128).astype(jnp.float32)
    vocab = table_out.shape[0]
    for group in range(-(-vocab // 128)):
        stop = min(128, vocab - group * 128)
        table_out[group * 128 : group * 128 + stop, :] = table[group * depth : (group + 1) * depth].T[:stop]
    pos_out[...] = pos_ref[...].reshape(pos_out.shape).astype(jnp.float32)
    own = few_ref[lax.axis_index("dp")].astype(jnp.float32)
    size = gain_out.shape[1]
    hbias_out[...] = own[0:1, : hbias_out.shape[1]]
    pbias_out[...] = own[1:2, : pbias_out.shape[1]]
    gain_out[...] = own[2:5, :size]
    shift_out[...] = own[5:8, :size]
    ibias_out[...] = own[8:9, : ibias_out.shape[1]]


def assemble_call(wide, slim, both, ffn, conv, table, pos, few, widths, inner_rows, out_rows, taps, vocab, depth, sizes):
    args = (wide, slim, both, ffn, conv, table, pos, few, widths)
    parts = wide.shape[0]
    vmem = pl.BlockSpec(memory_space=pltpu.VMEM)
    units = ffn.shape[1] - inner_rows
    dmodel = both.shape[2]
    hb, pb, nd, ib = sizes
    proj_rows = both.shape[1] - out_rows // (parts - 1)
    out_shape = [f32(wide.shape[1], wide.shape[2] * parts), f32(slim.shape[1], slim.shape[2] * parts),
                 f32(proj_rows * parts, dmodel), f32(out_rows, dmodel), f32(inner_rows, dmodel * parts), f32(units * parts, dmodel),
                 f32(taps, widths.shape[1]), f32(1, widths.shape[1]), f32(vocab, depth), f32(pos.shape[0] * pos.shape[1], pos.shape[2]),
                 f32(1, hb), f32(1, pb), f32(3, nd), f32(3, nd), f32(1, ib)]
    return pl.pallas_call(
        functools.partial(assemble, depth), in_specs=[vmem] * len(args), out_specs=[vmem] * len(out_shape), out_shape=out_shape,
        compiler_params=pltpu.CompilerParams(vmem_limit_bytes=40 << 20), name="assemble",
    )(*args)


def exact_gaussian_activation(values):
    return values * normal_cdf(values)


def gelu_back(values, upstream):
    density = DENSITY * jnp.exp(-0.5 * values * values)
    return upstream * (normal_cdf(values) + values * density)


def channel_widths(channels):
    widths = jnp.ones_like(channels)
    for power in range(6):
        widths = widths + (channels >= NF * 2**power // 64).astype(jnp.int32)
    return widths


def highway_mix(hidden, gates):
    width = hidden.shape[1]
    carry_gate = jax.nn.sigmoid(gates[:, width:])
    return carry_gate * hidden + (1.0 - carry_gate) * exact_gaussian_activation(gates[:, :width])


def swap(array, axis, bit):
    size = lax.axis_size(axis)
    return lax.ppermute(array, axis, [(index, index ^ bit) for index in range(size)])


def reduce_rows(array):
    count = lax.axis_size("dp")
    slot = lax.axis_index("dp")
    bits = count.bit_length() - 1
    rows, cols = array.shape
    if count != 1 << bits:
        return lax.psum_scatter(array.astype(jnp.bfloat16), "dp", scatter_dimension=0, tiled=True)
    array = array.reshape((2,) * bits + (rows // count, cols))
    for bit in range(bits):
        axis = bits - 1 - bit
        mine = (slot >> bit) & 1
        keep = lax.dynamic_index_in_dim(array, mine, axis, keepdims=False)
        give = lax.dynamic_index_in_dim(array, 1 - mine, axis, keepdims=False)
        got = swap(give.astype(jnp.bfloat16), "dp", 1 << bit)
        array = (keep.astype(jnp.float32) + got.astype(jnp.float32)).astype(jnp.bfloat16)
    return array


def join_parts(array):
    part = lax.axis_index("filt")
    low = (part & 1) == 1
    high = (part >> 1) == 1
    far = swap(array, "filt", 2)
    near = swap(array, "filt", 1)
    both = swap(far, "filt", 1)
    here = (jnp.where(low, near, array), jnp.where(low, array, near))
    there = (jnp.where(low, both, far), jnp.where(low, far, both))
    first = [jnp.where(high, b, a) for a, b in zip(here, there)]
    second = [jnp.where(high, a, b) for a, b in zip(here, there)]
    return first + second


def per_device(
    chars,
    lengths,
    char_table,
    conv_weight,
    conv_bias,
    highway_weight,
    highway_bias,
    proj_weight,
    proj_bias,
    position,
    norm_gain,
    norm_bias,
    query_key_value_weight,
    attention_output_weight,
    feedforward_input_weight,
    feedforward_input_bias,
    feedforward_output_weight,
    cotangent,
):
    parts = lax.axis_size("filt")
    slices = lax.axis_size("dp")
    part = lax.axis_index("filt")
    slot = lax.axis_index("dp")
    seqs, quarter, dmodel = cotangent.shape
    full_len = chars.shape[1]
    letters = chars.shape[2]
    words = seqs * full_len
    tokens = seqs * quarter
    filters = conv_weight.shape[1]
    depth = char_table.shape[1]
    heads = dmodel // HD // parts
    width = heads * HD
    inner_rows = feedforward_input_weight.shape[0]
    unit_rows = feedforward_output_weight.shape[0] // parts

    def own_columns(array, blocks):
        rows = array.shape[0]
        split = array.reshape(rows, blocks, parts, -1)
        return lax.dynamic_index_in_dim(split, part, 2, keepdims=False).reshape(rows, -1)

    def gather_rows(array):
        return lax.all_gather(array, "dp", axis=0, tiled=True)

    def groups_of(array, groups):
        array = array.reshape(groups, -1, width).transpose(1, 0, 2).reshape(-1, groups * width)
        return jnp.pad(array, ((0, 0), (0, dmodel - groups * width)))

    def rows_from_columns(both):
        both = lax.all_to_all(both.reshape(parts, -1, dmodel), "filt", split_axis=0, concat_axis=0, tiled=True)
        both = both.reshape(parts, slices // parts, po_rows, parts, width)
        both = [both[:, :, :split], both[:, :, split:, : parts - 1]]
        return [item.transpose(1, 3, 2, 0, 4).reshape(-1, dmodel) for item in both]

    def columns_from_rows(*grads):
        items = []
        for item, groups in zip(grads, (parts, parts - 1)):
            item = item.astype(jnp.bfloat16).reshape(slices // parts, groups, -1, parts, width)
            item = item.transpose(3, 0, 2, 1, 4).reshape(parts, slices // parts, -1, groups * width)
            items.append(jnp.pad(item, ((0, 0), (0, 0), (0, 0), (0, dmodel - groups * width))))
        both = jnp.concatenate(items, axis=2)
        both = lax.all_to_all(both.reshape(parts, -1, dmodel), "filt", split_axis=0, concat_axis=0, tiled=True)
        return both.reshape(slices * po_rows, dmodel)

    fast = slices == 8 and parts == 4
    hb, pb, nd = highway_bias.shape[1], proj_bias.shape[0], norm_gain.shape[1]
    small = jnp.concatenate(
        [
            highway_bias.reshape(-1),
            proj_bias,
            norm_gain.reshape(-1),
            norm_bias.reshape(-1),
            feedforward_input_bias,
        ]
    )
    small_size = small.shape[0]
    small = jnp.pad(small, (0, -small_size % dmodel))
    slim_parts = [
        groups_of(own_columns(proj_weight, 1), parts),
        groups_of(own_columns(attention_output_weight, 1), parts - 1),
        own_columns(query_key_value_weight, 3).reshape(-1, dmodel),
        small.reshape(-1, dmodel),
    ]
    split = slim_parts[0].shape[0]
    po_rows = split + slim_parts[1].shape[0]
    qkv_rows = slim_parts[2].shape[0]
    slim_all = lax.all_gather(jnp.concatenate(slim_parts, axis=0), "dp", axis=0, tiled=False)
    qkv_own = slim_all[:, po_rows : po_rows + qkv_rows].reshape(dmodel, 3 * width)
    small = slim_all[:, po_rows + qkv_rows :]
    small = small.reshape(slices, -1)[:, :small_size].astype(jnp.float32)
    cuts = [hb, hb + pb, hb + pb + 3 * nd, hb + pb + 6 * nd]
    highway_b, proj_b, gain, shift, inner_b = jnp.split(small, cuts, axis=1)
    highway_b_own = own_columns(highway_b.reshape(1, -1), 2)
    proj_b = proj_b.reshape(-1)
    gain = gain.reshape(slices, 3, nd).transpose(1, 0, 2).reshape(3, dmodel)
    shift = shift.reshape(slices, 3, nd).transpose(1, 0, 2).reshape(3, dmodel)
    inner_b_own = own_columns(inner_b.reshape(1, -1), slices)
    ffn_own = jnp.concatenate(
        [
            own_columns(feedforward_input_weight, slices),
            lax.dynamic_slice_in_dim(feedforward_output_weight, part * unit_rows, unit_rows, 0),
        ],
        axis=0,
    )

    def blocks_of(array):
        return array.astype(jnp.bfloat16).reshape(parts, tokens, -1)

    widths = channel_widths(part * filters + jnp.arange(filters, dtype=jnp.int32))
    ids, table, weight, back, limit, count = conv_prep(
        chars.reshape(words, letters), char_table, conv_weight, conv_bias, widths
    )
    if fast:
        acts, lse, embed, features, highway_own = prologue_call(
            ids, table, weight, limit, count, highway_weight[0], parts, letters, depth, 0
        )
        highway_own = highway_own.reshape(2, -1, filters)
    else:
        acts, lse, embed = conv_forward_call(ids, table, weight, limit, count, letters, depth)
        features = gather_channels_call(acts, parts, 0)
        highway_own = gather_rows(own_columns(highway_weight[0], 2))
        proj_own, out_own = rows_from_columns(slim_all[:, :po_rows])
    ffn_own, features = lax.optimization_barrier((ffn_own, features))
    ffn_all = lax.all_gather(ffn_own, "dp", axis=0, tiled=False)
    base = position.astype(jnp.float32) + proj_b[None, :]
    if fast:
        gates, hidden_low, proj_own, out_own, first, unit_zero, scale_zero, first_all = highway_stage_call(
            slim_all,
            features,
            highway_own,
            highway_b_own,
            acts,
            base,
            gain[0:1],
            shift[0:1],
            attention_output_weight.shape[0] * slices // parts,
            po_rows,
            EPS,
            1,
        )
    else:
        gates = nn_dot(features, highway_own) + highway_b_own
        feature_own = acts.astype(jnp.float32)
        hidden_low = highway_mix(feature_own, gates).astype(jnp.bfloat16)
        first, unit_zero, scale_zero, first_all = forward_stage_call(
            blocks_of(nn_dot(hidden_low, proj_own)), base, gain[0:1], shift[0:1], EPS, 1
        )
    first_all = first_all.reshape(words, dmodel)
    packed = nn_dot(first_all, qkv_own).astype(jnp.bfloat16)
    queries, keys, values = (
        packed[:, block * width : (block + 1) * width].reshape(seqs, full_len, heads, HD)
        for block in range(3)
    )
    key_ok = jnp.arange(full_len, dtype=jnp.int32)[None, :] < lengths[:, None]
    scale = HD ** (-0.5)
    scores = (
        jnp.einsum("sqhd,skhd->shqk", queries, keys, preferred_element_type=jnp.float32) * scale
    )
    scores = jnp.where(key_ok[:, None, None, :], scores, -1e30)
    row_top = jnp.max(scores, axis=-1, keepdims=True)
    log_total = row_top + jnp.log(jnp.sum(jnp.exp(scores - row_top), axis=-1, keepdims=True))
    probs = jnp.exp(scores - log_total)
    probs_low = probs.astype(jnp.bfloat16)
    attended = (
        jnp.einsum("shqk,skhd->sqhd", probs_low, values, preferred_element_type=jnp.float32)
        .astype(jnp.bfloat16)
        .reshape(words, width)
    )
    second, unit_one, scale_one, second_all = forward_stage_call(
        blocks_of(nn_dot(attended, out_own)), first, gain[1:2], shift[1:2], EPS, 2
    )
    second_all = second_all.reshape(words, dmodel)
    ffn_all, second_all = lax.optimization_barrier((ffn_all, second_all))
    inner_own = ffn_all[:, :inner_rows].reshape(dmodel, -1)
    outer_own = ffn_all[:, inner_rows:].reshape(-1, dmodel)
    inner = nn_dot(second_all, inner_own) + inner_b_own
    active = exact_gaussian_activation(inner).astype(jnp.bfloat16)
    top, d_res_two, d_gain_two, d_shift_two, d_outer = top_stage_call(
        blocks_of(nn_dot(active, outer_own)),
        second,
        cotangent.reshape(tokens, dmodel),
        gain[2:3],
        shift[2:3],
        EPS,
        3,
    )
    encoded = top.reshape(seqs, quarter, dmodel)
    d_outer = d_outer.reshape(words, dmodel)
    grad_outer = tn_dot(active, d_outer)
    d_active = nt_dot(d_outer, outer_own)
    d_inner = gelu_back(inner, d_active).astype(jnp.bfloat16)
    grad_inner = tn_dot(second_all, d_inner)
    grad_ffn = jnp.concatenate(
        [item.astype(jnp.bfloat16).reshape(slices, -1, dmodel) for item in (grad_inner, grad_outer)], axis=1
    )
    if fast:
        early = grad_ffn.shape[1] * 2 // 3
        grad_ffn = grad_ffn.reshape(4, 2, -1, dmodel)
        grad_early, grad_late = grad_ffn[:, :, :early], grad_ffn[:, :, early:]
        jobs = ("side",), (grad_early,)
    else:
        jobs = (), ()

    def pair_sum(grad, got):
        keep = lax.dynamic_index_in_dim(grad, slot % 2, 1, keepdims=False)
        return (keep.astype(jnp.float32) + got.astype(jnp.float32)).astype(jnp.bfloat16)

    grad_inner_b = jnp.sum(d_inner.astype(jnp.float32), axis=0)
    d_res_one, d_gain_one, d_shift_one, unused_sum, d_mixed, *got = backward_stage_call(
        blocks_of(nt_dot(d_inner, inner_own)), d_res_two, unit_one, scale_one, gain[1:2], 4, *jobs
    )
    if fast:
        grad_early = pair_sum(grad_early, got[0])
        jobs = ("side", "ring"), (grad_late, grad_early)
    d_mixed = d_mixed.reshape(words, dmodel)
    d_attended = nt_dot(d_mixed, out_own).astype(jnp.bfloat16)
    d_attended = d_attended.reshape(seqs, full_len, heads, HD)
    d_values = jnp.einsum(
        "shqk,sqhd->skhd", probs_low, d_attended, preferred_element_type=jnp.float32
    )
    d_probs = jnp.einsum(
        "sqhd,skhd->shqk", d_attended, values, preferred_element_type=jnp.float32
    )
    row_inner = jnp.sum(d_probs * probs, axis=-1, keepdims=True)
    d_scores = (probs * (d_probs - row_inner)).astype(jnp.bfloat16)
    d_queries = (
        jnp.einsum("shqk,skhd->sqhd", d_scores, keys, preferred_element_type=jnp.float32) * scale
    )
    d_keys = (
        jnp.einsum("shqk,sqhd->skhd", d_scores, queries, preferred_element_type=jnp.float32) * scale
    )
    d_packed = jnp.concatenate(
        [item.reshape(words, width) for item in (d_queries, d_keys, d_values)], axis=1
    ).astype(jnp.bfloat16)
    grad_qkv = tn_dot(first_all, d_packed).astype(jnp.bfloat16)
    d_summed, d_gain_zero, d_shift_zero, grad_proj_b, d_projected, *got = backward_stage_call(
        blocks_of(nt_dot(d_packed, qkv_own)), d_res_one, unit_zero, scale_zero, gain[0:1], 5, *jobs
    )
    if fast:
        grad_late = pair_sum(grad_late, got[0])
        keep = lax.dynamic_index_in_dim(grad_early, slot // 2, 0, keepdims=False)
        grad_early = sum([item.astype(jnp.float32) for item in got[1]], keep.astype(jnp.float32))
        grad_early = grad_early.astype(jnp.bfloat16)
    grad_pos = jnp.sum(d_summed.reshape(seqs, quarter, dmodel), axis=0)
    d_projected = d_projected.reshape(words, dmodel)
    if not fast:
        grad_both = columns_from_rows(tn_dot(hidden_low, d_projected), tn_dot(attended, d_mixed))
        d_hidden = nt_dot(d_projected, proj_own)
        d_in, d_gates = jax.vjp(highway_mix, feature_own, gates)[1](d_hidden)
        d_gates = d_gates.astype(jnp.bfloat16)
        grad_highway = tn_dot(features, d_gates).astype(jnp.bfloat16)
        grad_highway_b = jnp.sum(d_gates.astype(jnp.float32), axis=0)
        d_partial = nt_dot(d_gates, highway_own).astype(jnp.bfloat16)
    groups = table.shape[0] // depth

    def place_columns(own, blocks):
        piece = own.reshape(blocks, 1, -1)
        whole = jnp.zeros((blocks, parts, piece.shape[2]), own.dtype)
        return lax.dynamic_update_slice_in_dim(whole, piece, part, 1).reshape(-1)

    d_gain = jnp.concatenate([d_gain_zero, d_gain_one, d_gain_two])
    d_shift = jnp.concatenate([d_shift_zero, d_shift_one, d_shift_two])
    if fast:
        highway_piece = jnp.zeros((slices, 1, hb), jnp.float32)
    else:
        highway_piece = place_columns(grad_highway_b, 2).reshape(slices, 1, -1)
    pieces = [
        highway_piece,
        grad_proj_b.reshape(slices, 1, -1),
        d_gain.reshape(3, slices, nd).transpose(1, 0, 2),
        d_shift.reshape(3, slices, nd).transpose(1, 0, 2),
        place_columns(grad_inner_b, slices).reshape(slices, 1, -1),
    ]
    if fast:
        few = [jnp.pad(item, ((0, 0), (0, 0), (0, hb - item.shape[2]))) for item in pieces]
        few.append(jnp.zeros((slices, 7, hb), jnp.float32))
        few = jnp.concatenate(few, axis=1)
        wide_all, slim_all, both_all, ffn_all, conv_all, table_all, pos_all, few = epilogue_call(
            d_projected,
            proj_own,
            hidden_low,
            gates,
            acts,
            features,
            highway_own,
            attended,
            d_mixed,
            ids,
            embed,
            lse,
            weight,
            back,
            limit,
            count,
            grad_qkv.reshape(4, 2, -1, 3 * width),
            grad_early,
            grad_late,
            grad_pos.reshape(slices, -1, dmodel),
            few,
            po_rows,
            letters,
            depth,
            groups,
            6,
        )
        outs = assemble_call(
            wide_all,
            slim_all,
            both_all,
            ffn_all,
            conv_all,
            table_all,
            pos_all,
            few,
            widths[None, :],
            inner_rows,
            attention_output_weight.shape[0],
            conv_weight.shape[0],
            char_table.shape[0],
            depth,
            (hb, pb, nd, feedforward_input_bias.shape[0]),
        )
        g_highway, g_qkv, g_proj, g_out, g_inner, g_outer, conv_grad_w, conv_grad_b, g_table, grad_pos = outs[:10]
        g_highway_b, g_proj_b, g_gain, g_shift, g_inner_b = outs[10:]
        conv_grad_b, g_proj_b, g_inner_b = conv_grad_b[0], g_proj_b[0], g_inner_b[0]
    else:
        d_features = scatter_channels_call(d_partial, d_in, 6)
        conv_sums, table_sums = conv_backward_call(
            ids, embed, lse, d_features, weight, back, limit, count, groups, letters, depth
        )
        wide_all = jnp.stack(join_parts(reduce_rows(grad_highway)))
        slim_all = jnp.stack(join_parts(reduce_rows(grad_qkv)))
        both_all = jnp.stack(join_parts(reduce_rows(grad_both)))
        ffn_all = jnp.stack(join_parts(reduce_rows(grad_ffn.reshape(-1, dmodel))))
        table_sums = table_sums.reshape(2, groups * depth, -1).sum(0)
        conv_all = lax.psum(conv_sums, "dp")
        rows = jnp.concatenate([item.reshape(slices, -1) for item in pieces], axis=1)
        table_all, sums = lax.psum((table_sums, rows), ("dp", "filt"))
        grad_pos = lax.psum(grad_pos, "dp")
        own = lax.dynamic_index_in_dim(sums, slot, 0, keepdims=False)
        tap_rows = conv_weight.shape[0]
        tap_keep = (jnp.arange(tap_rows, dtype=jnp.int32) // depth)[:, None] < widths[None, :]
        conv_grad_w = jnp.where(tap_keep, conv_all[:, :tap_rows].T, 0.0)
        conv_grad_b = conv_all[:, tap_rows]
        g_table = table_all.reshape(groups, depth, 128).transpose(0, 2, 1).reshape(-1, depth)
        g_table = g_table[: char_table.shape[0]]
        g_highway_b, g_proj_b, g_gain, g_shift, g_inner_b = jnp.split(own, cuts)

        def join_columns(array, blocks, rows_here):
            array = array.reshape(parts, rows_here, blocks, -1).transpose(1, 2, 0, 3)
            return array.reshape(rows_here, -1).astype(jnp.float32)

        def join_groups(array, many):
            array = array.reshape(parts, array.shape[1], parts, width).transpose(2, 1, 0, 3)
            return array[:many].reshape(-1, dmodel).astype(jnp.float32)

        g_outer = ffn_all[:, inner_rows:].reshape(-1, dmodel).astype(jnp.float32)
        g_inner = join_columns(ffn_all[:, :inner_rows], slices, inner_rows)
        g_qkv = join_columns(slim_all, 3, query_key_value_weight.shape[0])
        g_proj = join_groups(both_all[:, :split], parts)
        g_out = join_groups(both_all[:, split:], parts - 1)
        g_highway = join_columns(wide_all, 2, highway_weight.shape[1])
    return (
        encoded,
        g_table,
        conv_grad_w,
        conv_grad_b,
        g_highway[None],
        g_highway_b.reshape(1, hb),
        g_proj,
        g_proj_b,
        grad_pos,
        g_gain.reshape(3, nd),
        g_shift.reshape(3, nd),
        g_qkv,
        g_out,
        g_inner,
        g_inner_b,
        g_outer,
    )


def solution(mesh):
    return jax.shard_map(
        per_device,
        mesh=mesh,
        in_specs=(
            P("dp", None, None),
            P("dp"),
            P(),
            P(None, "filt"),
            P("filt"),
            P(None, "dp", None),
            P(None, "dp"),
            P("dp", None),
            P("dp"),
            P("filt", None),
            P(None, "dp"),
            P(None, "dp"),
            P("dp", None),
            P("dp", None),
            P("dp", None),
            P("dp"),
            P("dp", None),
            P("dp", "filt", None),
        ),
        out_specs=(
            P("dp", "filt", None),
            P(),
            P(None, "filt"),
            P("filt"),
            P(None, "dp", None),
            P(None, "dp"),
            P("dp", None),
            P("dp"),
            P("filt", None),
            P(None, "dp"),
            P(None, "dp"),
            P("dp", None),
            P("dp", None),
            P("dp", None),
            P("dp"),
            P("dp", None),
        ),
        check_vma=False,
    )
```

```python
import functools

import jax
import jax.numpy as jnp
from jax import lax
from jax.experimental import pallas as pl
from jax.experimental.pallas import tpu as pltpu
from jax.sharding import PartitionSpec as P

KW = 7
NF = 2048
HD = 64
EPS = 1e-12
ROOT_HALF = 0.7071067811865476
DENSITY = 0.3989422804014327

def nt_dot(left, right):
    return lax.dot_general(left, right, (((1,), (1,)), ((), ())), preferred_element_type=jnp.float32)

def tn_dot(left, right):
    return lax.dot_general(left, right, (((0,), (0,)), ((), ())), preferred_element_type=jnp.float32)

def nn_dot(left, right):
    return jnp.dot(left, right, preferred_element_type=jnp.float32)

def normal_cdf(values):
    return 0.5 * (1.0 + lax.erf(values * ROOT_HALF))

def char_parts(chars_ref, position, block):
    ids = chars_ref[pl.ds(position, 1), :]
    low = ids & 127
    group = ids >> 7
    onehot = (lax.broadcasted_iota(jnp.int32, (128, block), 0) == low)
    onehot = jnp.where(onehot, 1.0, 0.0).astype(jnp.bfloat16)
    return onehot, group

def conv_forward(letters, depth, chars_ref, table_ref, weight_ref, limit_ref, count_ref,
                 acts_ref, lse_ref, embed_ref, patch_ref, grid_ref):
    block = chars_ref.shape[1]
    filters = weight_ref.shape[0]
    groups = table_ref.shape[0] // depth
    lead = KW - 1
    rows = KW * depth

    @pl.when(pl.program_id(0) == 0)
    def _():
        patch_ref[:, :rows, :] = jnp.zeros((patch_ref.shape[0], rows, block), jnp.bfloat16)
        ones = lax.broadcasted_iota(jnp.int32, (128 - rows, block), 0) == 0
        tail = jnp.where(ones, 1.0, 0.0).astype(jnp.bfloat16)
        patch_ref[:, rows:, :] = jnp.broadcast_to(tail[None], (patch_ref.shape[0],) + tail.shape)

    def embed(position, carry):
        onehot, group = char_parts(chars_ref, position, block)
        looked = nn_dot(table_ref[...], onehot)
        row = looked[:depth]
        for index in range(1, groups):
            row = jnp.where(group == index, looked[index * depth : (index + 1) * depth], row)
        row = row.astype(jnp.bfloat16)
        embed_ref[pl.ds(pl.multiple_of(position * depth, depth), depth), :] = row
        for tap in range(KW):
            patch_ref[position + lead - tap, tap * depth : (tap + 1) * depth, :] = row
        return carry

    lax.fori_loop(0, letters, embed, 0, unroll=5)
    chunk = grid_ref.shape[1]
    always = letters - KW + 1
    for start in range(0, filters, chunk):
        weight = weight_ref[start : start + chunk, :]
        limit = limit_ref[start : start + chunk, :]

        def product(position, top):
            grid = nn_dot(weight, patch_ref[position + lead])
            grid_ref[position] = grid
            return jnp.maximum(top, grid)

        top = lax.fori_loop(0, always, product, jnp.full((chunk, block), -1e30, jnp.float32), unroll=11)
        for position in range(always, letters):
            grid = nn_dot(weight, patch_ref[position + lead])
            grid = jnp.where(limit >= position, grid, -1e30)
            grid_ref[position] = grid
            top = jnp.maximum(top, grid)

        def total(position, acc):
            return acc + jnp.exp(grid_ref[position] - top)

        acc = lax.fori_loop(0, letters, total, jnp.zeros((chunk, block), jnp.float32), unroll=10)
        lse = top + jnp.log(acc)
        lse_ref[start : start + chunk, :] = lse
        pooled = lse - count_ref[start : start + chunk, :]
        acts_ref[:, start : start + chunk] = (pooled * normal_cdf(pooled)).astype(jnp.bfloat16).T

def conv_backward(letters, depth, chars_ref, embed_ref, lse_ref, up_ref, weight_ref, back_ref,
                  limit_ref, count_ref, wgrad_ref, tgrad_ref, patch_ref, down_ref, pull_ref):
    block = chars_ref.shape[1]
    filters = weight_ref.shape[0]
    lead = KW - 1
    rows = KW * depth
    groups = tgrad_ref.shape[0] // (2 * depth)
    step = pl.program_id(0)

    @pl.when(step == 0)
    def _():
        wgrad_ref[...] = jnp.zeros(wgrad_ref.shape, jnp.float32)
        tgrad_ref[...] = jnp.zeros(tgrad_ref.shape, jnp.float32)
        patch_ref[letters * depth :, :] = jnp.zeros((patch_ref.shape[0] - letters * depth, block), jnp.bfloat16)

    patch_ref[: letters * depth, :] = embed_ref[...]
    down_ref[...] = jnp.zeros(down_ref.shape, jnp.float32)
    pooled = lse_ref[...] - count_ref[...]
    slope = normal_cdf(pooled) + pooled * (DENSITY * jnp.exp(-0.5 * pooled * pooled))
    pull_ref[...] = slope * up_ref[...].T.astype(jnp.float32)
    ones = jnp.where(lax.broadcasted_iota(jnp.int32, (128 - rows, block), 0) == 0, 1.0, 0.0).astype(jnp.bfloat16)

    def one(position, masked):
        start = position * depth
        if not isinstance(position, int):
            start = pl.multiple_of(start, depth)
        patch = jnp.concatenate([patch_ref[pl.ds(start, rows), :], ones], axis=0)
        grid = nn_dot(weight_ref[...], patch)
        spread = jnp.exp(grid - lse_ref[...]) * pull_ref[...]
        if masked:
            spread = jnp.where(limit_ref[...] >= position, spread, 0.0)
        spread = spread.astype(jnp.bfloat16)
        down = nn_dot(back_ref[...], spread)
        down_ref[pl.ds(start, rows), :] += down[:rows]
        wgrad_ref[...] += nt_dot(spread, patch)

    always = letters - KW + 1

    def body(position, carry):
        one(position, False)
        return carry

    lax.fori_loop(0, always, body, 0, unroll=2)
    for position in range(always, letters):
        one(position, True)

    def table(position, carry):
        onehot, group = char_parts(chars_ref, position, block)
        down = down_ref[pl.ds(pl.multiple_of(position * depth, depth), depth), :]
        high = down.astype(jnp.bfloat16)
        low = (down - high.astype(jnp.float32)).astype(jnp.bfloat16)
        zero = jnp.zeros_like(high)
        parts = [jnp.where(group == index, item, zero) for item in (high, low) for index in range(groups)]
        tgrad_ref[...] += nt_dot(jnp.concatenate(parts, axis=0), onehot)
        return carry

    lax.fori_loop(0, letters, table, 0, unroll=5)

def conv_prep(chars, char_table, conv_weight, conv_bias, widths):
    letters = chars.shape[1]
    vocab, depth = char_table.shape
    groups = -(-vocab // 128)
    table = jnp.pad(char_table, ((0, groups * 128 - vocab), (0, 0)))
    table = table.reshape(groups, 128, depth).transpose(0, 2, 1).reshape(groups * depth, 128)
    tap = jnp.arange(conv_weight.shape[0], dtype=jnp.int32) // depth
    masked = jnp.where(tap[:, None] < widths[None, :], conv_weight, 0)
    back = jnp.concatenate([masked, conv_bias[None, :], jnp.zeros((127 - masked.shape[0], masked.shape[1]), masked.dtype)], axis=0)
    limit = (letters - widths)[:, None].astype(jnp.int32)
    count = jnp.log((letters - widths + 1).astype(jnp.float32))[:, None]
    ids = jnp.pad(chars, ((0, 0), (0, -letters % 8))).T
    return ids, table, back.T, back, limit, count

def conv_forward_call(ids, table, weight, limit, count, letters, depth, block=256):
    words = ids.shape[1]
    filters = weight.shape[0]
    full = lambda a: pl.BlockSpec(a.shape, lambda i: (0,) * a.ndim)
    return pl.pallas_call(
        functools.partial(conv_forward, letters, depth),
        grid=(words // block,),
        in_specs=[pl.BlockSpec((ids.shape[0], block), lambda i: (0, i)), full(table), full(weight), full(limit), full(count)],
        out_specs=[pl.BlockSpec((block, filters), lambda i: (i, 0)), pl.BlockSpec((filters, block), lambda i: (0, i)),
                   pl.BlockSpec((letters * depth, block), lambda i: (0, i))],
        out_shape=[jax.ShapeDtypeStruct((words, filters), jnp.bfloat16), jax.ShapeDtypeStruct((filters, words), jnp.float32),
                   jax.ShapeDtypeStruct((letters * depth, words), jnp.bfloat16)],
        scratch_shapes=[pltpu.VMEM((letters + KW - 1, 128, block), jnp.bfloat16), pltpu.VMEM((letters, 128, block), jnp.float32)],
        compiler_params=pltpu.CompilerParams(vmem_limit_bytes=48 << 20),
        name="conv_forward",
    )(ids, table, weight, limit, count)

def conv_backward_call(ids, embed, lse, up, weight, back, limit, count, groups, letters, depth, block=256):
    words = ids.shape[1]
    filters = weight.shape[0]
    full = lambda a: pl.BlockSpec(a.shape, lambda i: (0,) * a.ndim)
    return pl.pallas_call(
        functools.partial(conv_backward, letters, depth),
        grid=(words // block,),
        in_specs=[pl.BlockSpec((ids.shape[0], block), lambda i: (0, i)), pl.BlockSpec((letters * depth, block), lambda i: (0, i)),
                  pl.BlockSpec((filters, block), lambda i: (0, i)), pl.BlockSpec((block, filters), lambda i: (i, 0)),
                  full(weight), full(back), full(limit), full(count)],
        out_specs=[pl.BlockSpec((filters, 128), lambda i: (0, 0)), pl.BlockSpec((2 * groups * depth, 128), lambda i: (0, 0))],
        out_shape=[jax.ShapeDtypeStruct((filters, 128), jnp.float32), jax.ShapeDtypeStruct((2 * groups * depth, 128), jnp.float32)],
        scratch_shapes=[pltpu.VMEM(((letters + KW - 1) * depth, block), jnp.bfloat16), pltpu.VMEM(((letters + KW - 1) * depth, block), jnp.float32),
                        pltpu.VMEM((filters, block), jnp.float32)],
        compiler_params=pltpu.CompilerParams(vmem_limit_bytes=48 << 20),
        name="conv_backward",
    )(ids, embed, lse, up, weight, back, limit, count)


MESH = pl.DeviceIdType.MESH

def greet(peers):
    barrier = pltpu.get_barrier_semaphore()
    for peer in peers:
        pl.semaphore_signal(barrier, inc=1, device_id=peer, device_id_type=MESH)
    pl.semaphore_wait(barrier, len(peers))

def greet_all():
    slot, me = lax.axis_index("dp"), lax.axis_index("filt")
    count, parts = lax.axis_size("dp"), lax.axis_size("filt")
    greet([{"dp": slot ^ far, "filt": me ^ near} for far in range(count) for near in range(parts) if far or near])

def remote(source, target, send, recv, peer):
    return pltpu.make_async_remote_copy(
        src_ref=source, dst_ref=target, send_sem=send, recv_sem=recv,
        device_id=peer, device_id_type=MESH)

def comm_call(kernel, out_shape, scratch, ident, *args, name):
    vmem = pl.BlockSpec(memory_space=pltpu.VMEM)
    return pl.pallas_call(
        kernel, out_shape=out_shape, in_specs=[vmem] * len(args), out_specs=jax.tree.map(lambda _: vmem, out_shape),
        scratch_shapes=scratch,
        compiler_params=pltpu.CompilerParams(collective_id=ident, has_side_effects=True, vmem_limit_bytes=40 << 20),
        name=name)(*args)

DMA = pltpu.SemaphoreType.DMA

def scatter_sum(part_ref, inbox, send, recv, me):
    copies = []
    for hop in (3, 2, 1):
        copy = remote(part_ref.at[me ^ hop], inbox.at[hop - 1], send.at[hop - 1], recv.at[hop - 1], {"filt": me ^ hop})
        copy.start()
        copies.append(copy)
    total = part_ref[me].astype(jnp.float32)
    for copy, hop in reversed(list(zip(copies, (3, 2, 1)))):
        copy.wait()
        total = total + inbox[hop - 1].astype(jnp.float32)
    return total

def gather_blocks(low, all_ref, send, recv, me):
    all_ref[me] = low
    far = remote(all_ref.at[me], all_ref.at[me], send.at[0], recv.at[0], {"filt": me ^ 2})
    near = remote(all_ref.at[me], all_ref.at[me], send.at[1], recv.at[1], {"filt": me ^ 1})
    far.start()
    near.start()
    far.wait_recv()
    relay = remote(all_ref.at[me ^ 2], all_ref.at[me ^ 2], send.at[2], recv.at[2], {"filt": me ^ 1})
    relay.start()
    far.wait_send()
    near.wait()
    relay.wait()

def norm(values, gain, shift, eps):
    center = values - jnp.mean(values, axis=-1, keepdims=True)
    scale = lax.rsqrt(jnp.mean(center * center, axis=-1, keepdims=True) + eps)
    unit = center * scale
    return unit * gain + shift, unit, scale

def norm_back(upstream, unit, scale, gain):
    lifted = upstream * gain
    drop = jnp.mean(lifted, axis=-1, keepdims=True)
    lean = jnp.mean(lifted * unit, axis=-1, keepdims=True)
    return scale * (lifted - drop - unit * lean)

def forward_stage(part_ref, base_ref, gain_ref, shift_ref, value_ref, unit_ref, scale_ref, all_ref, inbox, send, recv, eps):
    me = lax.axis_index("filt")
    greet([{"filt": me ^ hop} for hop in (1, 2, 3)])
    total = scatter_sum(part_ref, inbox, send, recv, me) + base_ref[...]
    value, unit, scale = norm(total, gain_ref[...], shift_ref[...], eps)
    value_ref[...] = value
    unit_ref[...] = unit
    scale_ref[...] = scale
    gather_blocks(value.astype(jnp.bfloat16), all_ref, send.at[pl.ds(3, 3)], recv.at[pl.ds(3, 3)], me)

def top_stage(part_ref, base_ref, up_ref, gain_ref, shift_ref, top_ref, down_ref, dgain_ref, dshift_ref, all_ref, inbox, send, recv, eps):
    me = lax.axis_index("filt")
    greet([{"filt": me ^ hop} for hop in (1, 2, 3)])
    total = scatter_sum(part_ref, inbox, send, recv, me) + base_ref[...]
    top, unit, scale = norm(total, gain_ref[...], shift_ref[...], eps)
    top_ref[...] = top.astype(jnp.bfloat16)
    up = up_ref[...].astype(jnp.float32)
    dgain_ref[...] = jnp.sum(up * unit, axis=0, keepdims=True)
    dshift_ref[...] = jnp.sum(up, axis=0, keepdims=True)
    down = norm_back(up, unit, scale, gain_ref[...])
    down_ref[...] = down
    gather_blocks(down.astype(jnp.bfloat16), all_ref, send.at[pl.ds(3, 3)], recv.at[pl.ds(3, 3)], me)

def start_job(kind, source, target, send, recv):
    slot = lax.axis_index("dp")
    ring, side = slot // 2, slot % 2
    if kind == "side":
        moves = [(source.at[:, 1 - side], target, 1)]
    else:
        moves = [(source.at[ring ^ hop], target.at[hop - 1], 2 * hop) for hop in (2, 3, 1)]
    copies = []
    for index, (piece, place, hop) in enumerate(moves):
        copy = remote(piece, place, send.at[index], recv.at[index], {"dp": slot ^ hop})
        copy.start()
        copies.append(copy)
    return copies

def job_hops(kind):
    return (1,) if kind == "side" else (2, 4, 6)

def backward_stage(kinds, part_ref, base_ref, unit_ref, scale_ref, gain_ref, *refs):
    many = len(kinds)
    job_in, refs = refs[:many], refs[many:]
    (down_ref, dgain_ref, dshift_ref, dlow_ref, all_ref), refs = refs[:5], refs[5:]
    job_out, refs = refs[:many], refs[many:]
    inbox, send, recv = refs[:3]
    me = lax.axis_index("filt")
    slot = lax.axis_index("dp")
    hops = sorted({hop for kind in kinds for hop in job_hops(kind)})
    greet([{"filt": me ^ hop} for hop in (1, 2, 3)] + [{"dp": slot ^ hop} for hop in hops])
    copies = []
    for index, kind in enumerate(kinds):
        copies += start_job(kind, job_in[index], job_out[index], refs[3].at[index], refs[4].at[index])
    up = scatter_sum(part_ref, inbox, send, recv, me) + base_ref[...]
    unit = unit_ref[...]
    dgain_ref[...] = jnp.sum(up * unit, axis=0, keepdims=True)
    dshift_ref[...] = jnp.sum(up, axis=0, keepdims=True)
    down = norm_back(up, unit, scale_ref[...], gain_ref[...])
    down_ref[...] = down
    low = down.astype(jnp.bfloat16)
    dlow_ref[...] = jnp.sum(low.astype(jnp.float32), axis=0, keepdims=True)
    gather_blocks(low, all_ref, send.at[pl.ds(3, 3)], recv.at[pl.ds(3, 3)], me)
    for copy in copies:
        copy.wait()

def stage_scratch(block):
    return [pltpu.VMEM((3,) + block, jnp.bfloat16), DMA((6,)), DMA((6,))]

def f32(*shape): return jax.ShapeDtypeStruct(shape, jnp.float32)
def bf16(*shape): return jax.ShapeDtypeStruct(shape, jnp.bfloat16)

def forward_stage_call(part, base, gain, shift, eps, ident):
    parts, rows, cols = part.shape
    return comm_call(functools.partial(forward_stage, eps=eps),
        (f32(rows, cols), f32(rows, cols), f32(rows, 1), bf16(parts, rows, cols)), stage_scratch((rows, cols)), ident,
        part, base, gain, shift, name="forward_stage")

def top_stage_call(part, base, up, gain, shift, eps, ident):
    parts, rows, cols = part.shape
    return comm_call(functools.partial(top_stage, eps=eps),
        (bf16(rows, cols), f32(rows, cols), f32(1, cols), f32(1, cols), bf16(parts, rows, cols)), stage_scratch((rows, cols)), ident,
        part, base, up, gain, shift, name="top_stage")

def backward_stage_call(part, base, unit, scale, gain, ident, kinds=(), jobs=()):
    parts, rows, cols = part.shape
    vmem = pl.BlockSpec(memory_space=pltpu.VMEM)
    hbm = pl.BlockSpec(memory_space=pl.ANY)
    out_shape = [f32(rows, cols), f32(1, cols), f32(1, cols), f32(1, cols), bf16(parts, rows, cols)]
    scratch = stage_scratch((rows, cols))
    for kind, job in zip(kinds, jobs):
        ring = job.shape[0]
        out_shape.append(bf16(ring, *job.shape[2:]) if kind == "side" else bf16(ring - 1, *job.shape[1:]))
    if kinds:
        scratch += [DMA((len(kinds), 3)), DMA((len(kinds), 3))]
    return pl.pallas_call(
        functools.partial(backward_stage, kinds), out_shape=out_shape, in_specs=[vmem] * 5 + [hbm] * len(kinds),
        out_specs=[vmem] * 5 + [hbm] * len(kinds), scratch_shapes=scratch,
        compiler_params=pltpu.CompilerParams(collective_id=ident, has_side_effects=True, vmem_limit_bytes=24 << 20),
        name="backward_stage")(part, base, unit, scale, gain, *jobs)

def gather_channels(own_ref, all_ref, send, recv, *, chunks):
    me = lax.axis_index("filt")
    greet([{"filt": me ^ hop} for hop in (1, 2)])
    rows, cols = own_ref.shape
    size = rows // chunks

    def lanes(index):
        return pl.ds(pl.multiple_of(index * cols, cols), cols)

    far, near, relay = [], [], []
    for chunk in range(chunks):
        span = pl.ds(chunk * size, size)
        copy = remote(own_ref.at[span, :], all_ref.at[span, lanes(me)], send.at[0, chunk], recv.at[0, chunk], {"filt": me ^ 2})
        copy.start()
        far.append(copy)
    for chunk in range(chunks):
        span = pl.ds(chunk * size, size)
        copy = remote(own_ref.at[span, :], all_ref.at[span, lanes(me)], send.at[1, chunk], recv.at[1, chunk], {"filt": me ^ 1})
        copy.start()
        near.append(copy)
    all_ref[:, lanes(me)] = own_ref[...]
    for chunk in range(chunks):
        span = pl.ds(chunk * size, size)
        far[chunk].wait_recv()
        piece = all_ref.at[span, lanes(me ^ 2)]
        copy = remote(piece, piece, send.at[2, chunk], recv.at[2, chunk], {"filt": me ^ 1})
        copy.start()
        relay.append(copy)
    for chunk in range(chunks):
        far[chunk].wait_send()
        near[chunk].wait()
        relay[chunk].wait()

def gather_channels_call(own, parts, ident, chunks=4):
    rows, cols = own.shape
    return comm_call(functools.partial(gather_channels, chunks=chunks), bf16(rows, cols * parts),
        [DMA((3, chunks)), DMA((3, chunks))], ident, own, name="gather_channels")

def scatter_channels(part_ref, base_ref, out_ref, inbox, merged, send, recv, *, chunks):
    me = lax.axis_index("filt")
    greet([{"filt": me ^ hop} for hop in (1, 2)])
    rows, cols = base_ref.shape
    size = rows // chunks

    def lanes(index):
        return pl.ds(pl.multiple_of(index * cols, cols), cols)

    def hop(source, slot, chunk, peer):
        span = pl.ds(chunk * size, size)
        copy = remote(source, inbox.at[slot, span, :], send.at[slot, chunk], recv.at[slot, chunk], {"filt": peer})
        copy.start()
        return copy

    first, second, third = [], [], []
    for chunk in range(chunks):
        span = pl.ds(chunk * size, size)
        first.append(hop(part_ref.at[span, lanes(me ^ 3)], 0, chunk, me ^ 1))
    for chunk in range(chunks):
        span = pl.ds(chunk * size, size)
        second.append(hop(part_ref.at[span, lanes(me ^ 1)], 1, chunk, me ^ 1))
    for chunk in range(chunks):
        span = pl.ds(chunk * size, size)
        first[chunk].wait_recv()
        both = part_ref[span, lanes(me ^ 2)].astype(jnp.float32) + inbox[0, span, :].astype(jnp.float32)
        merged[span, :] = both.astype(jnp.bfloat16)
        third.append(hop(merged.at[span, :], 2, chunk, me ^ 2))
    for chunk in range(chunks):
        span = pl.ds(chunk * size, size)
        second[chunk].wait_recv()
        third[chunk].wait_recv()
        total = part_ref[span, lanes(me)].astype(jnp.float32) + inbox[1, span, :].astype(jnp.float32)
        total = total + inbox[2, span, :].astype(jnp.float32) + base_ref[span, :]
        out_ref[span, :] = total.astype(jnp.bfloat16)
    for copy in first + second + third:
        copy.wait_send()

def scatter_channels_call(part, base, ident, chunks=4):
    rows, cols = base.shape
    return comm_call(functools.partial(scatter_channels, chunks=chunks), bf16(rows, cols),
        [pltpu.VMEM((3, rows, cols), jnp.bfloat16), pltpu.VMEM((rows, cols), jnp.bfloat16), DMA((3, chunks)), DMA((3, chunks))],
        ident, part, base, name="scatter_channels")


class Total:
    def __init__(self, low, inbox, out, send, recv, sides=None, shared=True):
        self.shared, self.third = shared, []
        self.low, self.inbox, self.out, self.sides = low, inbox, out, sides
        self.send, self.recv = send, recv
        self.me, self.slot = lax.axis_index("filt"), lax.axis_index("dp")
        self.count = low.shape[0]
        self.copies = []

    def push(self, source, target, kind, hop, peer):
        copy = remote(source, target, self.send.at[kind, hop - 1], self.recv.at[kind, hop - 1], peer)
        copy.start()
        self.copies.append(copy)
        return copy

    def start(self, value):
        self.low[...] = value.astype(jnp.bfloat16)
        self.first = [
            self.push(self.low.at[self.slot ^ hop], self.inbox.at[hop - 1], 0, hop, {"dp": self.slot ^ hop})
            for hop in range(1, self.count)
        ]

    def combine(self):
        for copy in self.first:
            copy.wait_recv()
        total = self.low[self.slot].astype(jnp.float32)
        for hop in range(1, self.count):
            total = total + self.inbox[hop - 1].astype(jnp.float32)
        if self.sides is None:
            self.out[self.slot] = total.astype(jnp.bfloat16)
            self.spread()
            return
        self.sides[0] = total.astype(jnp.bfloat16)
        self.second = [self.push(self.sides.at[0], self.sides.at[hop], 1, hop, {"filt": self.me ^ hop}) for hop in (1, 2, 3)]

    def across(self):
        for copy in self.second:
            copy.wait_recv()
        left = self.sides[0].astype(jnp.float32) + self.sides[1].astype(jnp.float32)
        right = self.sides[2].astype(jnp.float32) + self.sides[3].astype(jnp.float32)
        total = (left + right).astype(jnp.bfloat16)
        if self.shared:
            self.out[self.slot] = total
            self.spread()
        else:
            self.out[...] = total

    def spread(self):
        piece = self.out.at[self.slot]
        self.third = [self.push(piece, piece, 2, hop, {"dp": self.slot ^ hop}) for hop in range(1, self.count)]

    def finish(self):
        for copy in self.third:
            copy.wait_recv()
        for copy in self.copies:
            copy.wait_send()


def prologue(letters, depth, block, chunks, window, first, chars_ref, table_ref, weight_ref, limit_ref, count_ref, shard_ref,
             acts_ref, lse_ref, embed_ref, all_ref, full_ref, patch_ref, grid_ref,
             zsend, zrecv, local, ysend, yrecv, fsend, frecv):
    words = chars_ref.shape[1]
    filters = weight_ref.shape[0]
    me = lax.axis_index("filt")
    slot = lax.axis_index("dp")
    ring, side = slot // 2, slot % 2
    greet([{"filt": me ^ hop} for hop in (1, 2)] + [{"dp": slot ^ hop} for hop in (1, 2, 4, 6)])
    parts = all_ref.shape[1] // filters
    span = shard_ref.shape[0] // (chunks // 2)

    def spot(chunk):
        return pl.ds((chunk // 2) * span, span), chunk % 2

    own, far = [], []

    def start_chunk(chunk):
        if chunk >= chunks:
            return
        rows, half = spot(chunk)
        source = shard_ref.at[rows, pl.ds(pl.multiple_of(half * filters * parts + me * filters, filters), filters)]
        target = full_ref.at[half, ring, side, rows, :]
        copy = pltpu.make_async_copy(source, target, local.at[chunk])
        copy.start()
        own.append(copy)
        for hop in (2, 1, 3):
            copy = remote(source, target, zsend.at[chunk, hop - 1], zrecv.at[chunk, hop - 1], {"dp": slot ^ (2 * hop)})
            copy.start()
            far.append(copy)

    for chunk in range(window):
        start_chunk(chunk)
    cross = []

    def forward_chunk(chunk):
        rows, half = spot(chunk)
        own[chunk].wait()
        for copy in far[3 * chunk : 3 * chunk + 3]:
            copy.wait_recv()
        start_chunk(chunk + window)
        piece = full_ref.at[half, :, side, rows, :]
        copy = remote(piece, piece, ysend.at[chunk], yrecv.at[chunk], {"dp": slot ^ 1})
        copy.start()
        cross.append(copy)

    lead = KW - 1
    rows = KW * depth
    groups = table_ref.shape[0] // depth
    patch_ref[:, :rows, :] = jnp.zeros((patch_ref.shape[0], rows, block), jnp.bfloat16)
    ones = lax.broadcasted_iota(jnp.int32, (128 - rows, block), 0) == 0
    tail = jnp.where(ones, 1.0, 0.0).astype(jnp.bfloat16)
    patch_ref[:, rows:, :] = jnp.broadcast_to(tail[None], (patch_ref.shape[0],) + tail.shape)
    chunk = grid_ref.shape[1]
    always = letters - KW + 1
    steps = filters // chunk
    polls = {(step // steps, step % steps): step - first for step in range(first, min(first + chunks, words // block * steps))}
    gathers = ChannelGather(acts_ref, all_ref, fsend, frecv, words // block)
    for index in range(words // block):
        cols = pl.ds(index * block, block)

        def embed(position, carry):
            ids = chars_ref[pl.ds(position, 1), cols]
            low = ids & 127
            group = ids >> 7
            onehot = lax.broadcasted_iota(jnp.int32, (128, block), 0) == low
            onehot = jnp.where(onehot, 1.0, 0.0).astype(jnp.bfloat16)
            looked = nn_dot(table_ref[...], onehot)
            row = looked[:depth]
            for part in range(1, groups):
                row = jnp.where(group == part, looked[part * depth : (part + 1) * depth], row)
            row = row.astype(jnp.bfloat16)
            embed_ref[pl.ds(pl.multiple_of(position * depth, depth), depth), cols] = row
            for tap in range(KW):
                patch_ref[position + lead - tap, tap * depth : (tap + 1) * depth, :] = row
            return carry

        lax.fori_loop(0, letters, embed, 0, unroll=5)
        for start in range(0, filters, chunk):
            weight = weight_ref[start : start + chunk, :]
            limit = limit_ref[start : start + chunk, :]

            def product(position, top):
                grid = nn_dot(weight, patch_ref[position + lead])
                grid_ref[position] = grid
                return jnp.maximum(top, grid)

            top = lax.fori_loop(0, always, product, jnp.full((chunk, block), -1e30, jnp.float32), unroll=11)
            for position in range(always, letters):
                grid = nn_dot(weight, patch_ref[position + lead])
                grid = jnp.where(limit >= position, grid, -1e30)
                grid_ref[position] = grid
                top = jnp.maximum(top, grid)

            def total(position, acc):
                return acc + jnp.exp(grid_ref[position] - top)

            acc = lax.fori_loop(0, letters, total, jnp.zeros((chunk, block), jnp.float32), unroll=10)
            lse = top + jnp.log(acc)
            lse_ref[start : start + chunk, cols] = lse
            pooled = lse - count_ref[start : start + chunk, :]
            acts_ref[cols, start : start + chunk] = (pooled * normal_cdf(pooled)).astype(jnp.bfloat16).T
            poll = polls.get((index, start // chunk))
            if poll is not None:
                forward_chunk(poll)
        gathers.send(index)
    for index in range(len(polls), chunks):
        forward_chunk(index)
    for index in range(words // block):
        gathers.relay(index)
    gathers.finish()
    for copy in far:
        copy.wait_send()
    for copy in cross:
        copy.wait()

class ChannelGather:
    def __init__(self, own_ref, all_ref, send, recv, pieces):
        self.me = lax.axis_index("filt")
        self.own, self.all, self.sems = own_ref, all_ref, (send, recv)
        self.size = own_ref.shape[0] // pieces
        self.copies = []

    def view(self, index, piece):
        cols = self.own.shape[1]
        return self.all.at[pl.ds(piece * self.size, self.size), pl.ds(pl.multiple_of(index * cols, cols), cols)]

    def push(self, source, target, kind, piece, hop):
        send, recv = self.sems
        copy = remote(source, target, send.at[kind, piece], recv.at[kind, piece], {"filt": self.me ^ hop})
        copy.start()
        self.copies.append(copy)
        return copy

    def send(self, piece):
        source = self.own.at[pl.ds(piece * self.size, self.size), :]
        target = self.view(self.me, piece)
        self.push(source, target, 0, piece, 2)
        self.push(source, target, 1, piece, 1)
        cols = self.own.shape[1]
        self.all[pl.ds(piece * self.size, self.size), pl.ds(pl.multiple_of(self.me * cols, cols), cols)] = self.own[pl.ds(piece * self.size, self.size), :]

    def relay(self, piece):
        self.copies[2 * piece].wait_recv()
        view = self.view(self.me ^ 2, piece)
        self.push(view, view, 2, piece, 1)

    def finish(self):
        for index, copy in enumerate(self.copies):
            copy.wait_send()
            if index % 2 == 1 or index >= 2 * (len(self.copies) // 3):
                copy.wait_recv()

def prologue_call(ids, table, weight, limit, count, shard, parts, letters, depth, ident, block=256, chunks=8, window=2, first=2):
    words = ids.shape[1]
    filters = weight.shape[0]
    rows = shard.shape[0]
    vmem = pl.BlockSpec(memory_space=pltpu.VMEM)
    hbm = pl.BlockSpec(memory_space=pl.ANY)
    pieces = words // block
    return pl.pallas_call(
        functools.partial(prologue, letters, depth, block, chunks, window, first),
        in_specs=[vmem] * 5 + [hbm],
        out_specs=[vmem] * 4 + [hbm],
        out_shape=[bf16(words, filters), f32(filters, words), bf16(letters * depth, words), bf16(words, filters * parts),
                   bf16(2, 4, 2, rows, filters)],
        scratch_shapes=[pltpu.VMEM((letters + KW - 1, 128, block), jnp.bfloat16), pltpu.VMEM((letters, 128, block), jnp.float32),
                        DMA((chunks, 3)), DMA((chunks, 3)), DMA((chunks,)), DMA((chunks,)), DMA((chunks,)), DMA((3, pieces)), DMA((3, pieces))],
        compiler_params=pltpu.CompilerParams(collective_id=ident, has_side_effects=True, vmem_limit_bytes=48 << 20),
        name="prologue",
    )(ids, table, weight, limit, count, shard)


def sigmoid(values):
    return 1.0 / (1.0 + jnp.exp(-values))


def highway_stage(eps, slim_ref, feats_ref, wide_ref, bias_ref, acts_ref, base_ref, gain_ref, shift_ref,
                  gates_ref, hidden_ref, proj_ref, out_ref, value_ref, unit_ref, scale_ref, all_ref,
                  abox, part_ref, inbox, send, recv, asend, arecv):
    me = lax.axis_index("filt")
    greet([{"filt": me ^ hop} for hop in (1, 2, 3)])
    parts, sides, rows, dmodel = abox.shape
    copies = []
    size, small = proj_ref.shape[0] // (sides * parts), out_ref.shape[0] // (sides * (parts - 1))
    for index, span in enumerate((pl.ds(0, size), pl.ds(size, rows - size))):
        for hop in (2, 3, 1):
            source = slim_ref.at[pl.ds(sides * (me ^ hop), sides), span, :]
            copy = remote(source, abox.at[me, :, span, :], asend.at[index, hop - 1], arecv.at[index, hop - 1], {"filt": me ^ hop})
            copy.start()
            copies.append(copy)
    own = pltpu.make_async_copy(slim_ref.at[pl.ds(sides * me, sides), pl.ds(0, rows), :], abox.at[me], asend.at[0, 3])
    own.start()
    words, filters = acts_ref.shape
    block = 256

    def mix(index, carry):
        span = pl.ds(pl.multiple_of(index * block, block), block)
        feats = feats_ref[span, :]
        turn = nn_dot(feats, wide_ref[0]) + bias_ref[:, :filters]
        gates_ref[span, :filters] = turn
        gate = nn_dot(feats, wide_ref[1]) + bias_ref[:, filters:]
        gates_ref[span, filters:] = gate
        keep = sigmoid(gate)
        mixed = keep * acts_ref[span, :].astype(jnp.float32) + (1.0 - keep) * (turn * normal_cdf(turn))
        hidden_ref[span, :] = mixed.astype(jnp.bfloat16)
        return carry

    lax.fori_loop(0, words // block, mix, 0)
    own.wait()
    for copy in copies[:3]:
        copy.wait()
    width = dmodel // parts
    for part in range(parts):
        cols = slice(part * width, (part + 1) * width)
        for side in range(sides):
            for group in range(parts):
                lanes = slice(group * width, (group + 1) * width)
                start = (side * parts + group) * size
                proj_ref[start : start + size, cols] = abox[part, side, :size, lanes]

    def project(index, carry):
        span = pl.ds(pl.multiple_of(index * 128, 128), 128)
        part_ref[index] = nn_dot(hidden_ref[span, :], proj_ref[...]).astype(jnp.bfloat16)
        return carry

    lax.fori_loop(0, parts, project, 0)
    total = scatter_sum(part_ref, inbox, send, recv, me) + base_ref[...]
    value, unit, scale = norm(total, gain_ref[...], shift_ref[...], eps)
    value_ref[...] = value
    unit_ref[...] = unit
    scale_ref[...] = scale
    gather_blocks(value.astype(jnp.bfloat16), all_ref, send.at[pl.ds(3, 3)], recv.at[pl.ds(3, 3)], me)
    for copy in copies[3:]:
        copy.wait()
    for part in range(parts):
        cols = slice(part * width, (part + 1) * width)
        for side in range(sides):
            for group in range(parts - 1):
                start = (side * (parts - 1) + group) * small
                out_ref[start : start + small, cols] = abox[part, side, size:, group * width : (group + 1) * width]


def highway_stage_call(slim, feats, wide, bias, acts, base, gain, shift, out_rows, po_rows, eps, ident):
    words, filters = acts.shape
    rows, dmodel = base.shape
    parts = words // rows
    vmem = pl.BlockSpec(memory_space=pltpu.VMEM)
    hbm = pl.BlockSpec(memory_space=pl.ANY)
    return pl.pallas_call(
        functools.partial(highway_stage, eps), in_specs=[hbm] + [vmem] * 7, out_specs=[vmem] * 8,
        out_shape=[f32(words, 2 * filters), bf16(words, filters), bf16(filters, dmodel), bf16(out_rows, dmodel), f32(rows, dmodel),
                   f32(rows, dmodel), f32(rows, 1), bf16(parts, rows, dmodel)],
        scratch_shapes=[pltpu.VMEM((parts, 2, po_rows, dmodel), jnp.bfloat16), pltpu.VMEM((parts, rows, dmodel), jnp.bfloat16)]
        + stage_scratch((rows, dmodel)) + [DMA((2, 4)), DMA((2, 3))],
        compiler_params=pltpu.CompilerParams(collective_id=ident, has_side_effects=True, vmem_limit_bytes=48 << 20),
        name="highway_stage",
    )(slim, feats, wide, bias, acts, base, gain, shift)


class RowReduce:
    def __init__(self, grad, yin, pair, zin, joined, span, sems, base=0):
        self.base, self.ready = base, []
        self.grad, self.yin, self.pair, self.zin, self.joined = grad, yin, pair, zin, joined
        self.span, self.sems = span, sems
        self.me, self.slot = lax.axis_index("filt"), lax.axis_index("dp")
        self.ring, self.side = self.slot // 2, self.slot % 2
        self.copies = []

    def push(self, source, target, index, peer):
        send, recv = self.sems
        copy = remote(source, target, send.at[index], recv.at[index], peer)
        copy.start()
        self.copies.append(copy)
        return copy

    def across(self):
        span = self.span
        for copy in self.ready:
            copy.wait_recv()
        self.first = self.push(
            self.grad.at[:, 1 - self.side, span, :], self.yin.at[:, span, :], 0, {"dp": self.slot ^ 1}
        )

    def along(self):
        span = self.span
        self.first.wait_recv()
        both = self.grad[:, self.side, span, :].astype(jnp.float32) + self.yin[:, span, :].astype(jnp.float32)
        self.pair[:, span, :] = both.astype(jnp.bfloat16)
        self.ring_out()

    def local(self):
        return pl.ds(self.span.start - self.base, self.span.size)

    def ring_out(self):
        span = self.local()
        self.rest = [
            self.push(self.pair.at[self.ring ^ hop, span, :], self.zin.at[hop - 1, span, :], hop, {"dp": self.slot ^ (2 * hop)})
            for hop in (2, 3, 1)
        ]

    def join(self):
        span = self.local()
        for copy in self.rest:
            copy.wait_recv()
        total = self.pair[self.ring, span, :].astype(jnp.float32)
        for hop in (1, 2, 3):
            total = total + self.zin[hop - 1, span, :].astype(jnp.float32)
        self.joined[self.me, self.span, :] = total.astype(jnp.bfloat16)
        self.share()

    def share(self):
        piece = self.joined.at[self.me, self.span, :]
        self.far = self.push(piece, piece, 4, {"filt": self.me ^ 2})
        self.near = self.push(piece, piece, 5, {"filt": self.me ^ 1})

    def relay(self):
        self.far.wait_recv()
        piece = self.joined.at[self.me ^ 2, self.span, :]
        self.last = self.push(piece, piece, 6, {"filt": self.me ^ 1})

    def finish(self):
        self.near.wait_recv()
        self.last.wait_recv()
        for copy in self.copies:
            copy.wait_send()


def epilogue(letters, depth, block, *refs):
    (dproj_ref, proj_ref, hidden_ref, gates_ref, acts_ref, feats_ref, high_ref, attended_ref, dmixed_ref, chars_ref, embed_ref, lse_ref, weight_ref, back_ref, limit_ref, count_ref, slim_ref,
     ffn_ref, pair_ref, pos_ref, few_ref,
     wide_out, slim_out, rows_out, ffn_out, conv_out, table_out, pos_out, few_out,
     bias_ref, part_ref, base_ref, dgates_ref, wide_ref, cross_ref, inbox, merged, up_ref, patch_ref, down_ref, pull_ref, wgrad_ref, tgrad_ref, wide_y, wide_p, wide_z, slim_y, slim_p, slim_z,
     rows_ref, rows_y, rows_p, rows_z, late_z, conv_low, conv_in, table_low, table_in, table_side, pos_low, pos_in, few_low, few_in, few_side,
     csend, crecv, rsend, rrecv, tsend, trecv, asend, arecv) = refs
    me = lax.axis_index("filt")
    greet_all()
    pos = Total(pos_low, pos_in, pos_out, tsend.at[0], trecv.at[0])
    few = Total(few_low, few_in, few_out, tsend.at[1], trecv.at[1], few_side, False)
    conv_total = Total(conv_low, conv_in, conv_out, tsend.at[2], trecv.at[2])
    table_total = Total(table_low, table_in, table_out, tsend.at[3], trecv.at[3], table_side)
    wide_rows = wide_out.shape[1] // 4
    slim = RowReduce(slim_ref, slim_y, slim_p, slim_z, slim_out, pl.ds(0, slim_out.shape[1]), (rsend.at[4], rrecv.at[4]))
    both = RowReduce(rows_ref, rows_y, rows_p, rows_z, rows_out, pl.ds(0, rows_out.shape[1]), (rsend.at[6], rrecv.at[6]))
    wide = [
        RowReduce(wide_ref, wide_y, wide_p, wide_z, wide_out, pl.ds(index * wide_rows, wide_rows), (rsend.at[index], rrecv.at[index]))
        for index in range(4)
    ]
    early = ffn_ref.shape[0]
    ffn = RowReduce(None, None, None, None, ffn_out, pl.ds(0, early), (rsend.at[5], rrecv.at[5]))
    late = RowReduce(None, None, pair_ref, late_z, ffn_out, pl.ds(early, pair_ref.shape[1]), (rsend.at[7], rrecv.at[7]), early)
    swaps = [
        remote(cross_ref.at[me ^ hop], rows_ref.at[me], asend.at[hop - 1], arecv.at[hop - 1], {"filt": me ^ hop}) for hop in (2, 3, 1)
    ]
    both.ready = swaps
    pos.start(pos_ref[...])
    slim.across()
    ffn_out[me, :early, :] = ffn_ref[...]
    late.ring_out()
    highway_mix_back(dproj_ref, proj_ref, hidden_ref, gates_ref, acts_ref, base_ref, dgates_ref, bias_ref)
    highway_grads(feats_ref, dgates_ref, wide_ref)
    wide[0].across()
    extra = few_ref[...]
    place, row = lax.broadcasted_iota(jnp.int32, extra.shape, 0), lax.broadcasted_iota(jnp.int32, extra.shape, 1)
    lanes = extra.shape[2]
    extra = jnp.where((row == 0) & (place == me), bias_ref[:, :lanes][None], extra)
    extra = jnp.where((row == 0) & (place == me + 4), bias_ref[:, lanes:][None], extra)
    few.start(extra)
    highway_down(dgates_ref, high_ref, part_ref)
    scatter = ChannelScatter(part_ref, base_ref, up_ref, inbox, merged, csend, crecv)
    scatter.begin()
    row_grads(hidden_ref, dproj_ref, attended_ref, dmixed_ref, cross_ref)
    rows_ref[me] = cross_ref[me]
    wide[1].across()
    slim.along()
    scatter.finish()
    wide[2].across()
    wide[0].along()
    pos.combine()
    few.combine()
    for copy in swaps:
        copy.start()
    ffn.share()
    steps = iter([
        [wide[3].across, wide[1].along], [slim.join], [both.across], [wide[2].along, wide[0].join, late.join],
        [slim.relay, ffn.relay, wide[0].relay, wide[1].join], [late.relay, few.across, wide[3].along], [wide[1].relay, wide[2].join],
        [wide[2].relay], [], [],
    ])

    def advance():
        for step in next(steps):
            step()

    filters = weight_ref.shape[0]
    rows = KW * depth
    groups = tgrad_ref.shape[0] // (2 * depth)
    wgrad_ref[...] = jnp.zeros(wgrad_ref.shape, jnp.float32)
    tgrad_ref[...] = jnp.zeros(tgrad_ref.shape, jnp.float32)
    patch_ref[letters * depth :, :] = jnp.zeros((patch_ref.shape[0] - letters * depth, block), jnp.bfloat16)
    ones = jnp.where(lax.broadcasted_iota(jnp.int32, (128 - rows, block), 0) == 0, 1.0, 0.0).astype(jnp.bfloat16)
    always = letters - KW + 1
    quarter = always // 4
    for index in range(chars_ref.shape[1] // block):
        cols = pl.ds(index * block, block)
        patch_ref[: letters * depth, :] = embed_ref[:, cols]
        down_ref[...] = jnp.zeros(down_ref.shape, jnp.float32)
        pooled = lse_ref[:, cols] - count_ref[...]
        slope = normal_cdf(pooled) + pooled * (DENSITY * jnp.exp(-0.5 * pooled * pooled))
        pull_ref[...] = slope * up_ref[cols, :].T.astype(jnp.float32)

        def one(position, masked):
            start = position * depth
            if not isinstance(position, int):
                start = pl.multiple_of(start, depth)
            patch = jnp.concatenate([patch_ref[pl.ds(start, rows), :], ones], axis=0)
            grid = nn_dot(weight_ref[...], patch)
            spread = jnp.exp(grid - lse_ref[:, cols]) * pull_ref[...]
            if masked:
                spread = jnp.where(limit_ref[...] >= position, spread, 0.0)
            spread = spread.astype(jnp.bfloat16)
            down = nn_dot(back_ref[...], spread)
            down_ref[pl.ds(start, rows), :] += down[:rows]
            wgrad_ref[...] += nt_dot(spread, patch)

        def body(position, carry):
            one(position, False)
            return carry

        for lap in range(4):
            stop = always if lap == 3 else (lap + 1) * quarter
            lax.fori_loop(lap * quarter, stop, body, 0, unroll=11)
            advance()
        for position in range(always, letters):
            one(position, True)

        def table(position, carry):
            ids = chars_ref[pl.ds(position, 1), cols]
            low = ids & 127
            group = ids >> 7
            onehot = lax.broadcasted_iota(jnp.int32, (128, block), 0) == low
            onehot = jnp.where(onehot, 1.0, 0.0).astype(jnp.bfloat16)
            down = down_ref[pl.ds(pl.multiple_of(position * depth, depth), depth), :]
            high = down.astype(jnp.bfloat16)
            rest = (down - high.astype(jnp.float32)).astype(jnp.bfloat16)
            zero = jnp.zeros_like(high)
            parts = [jnp.where(group == part, item, zero) for item in (high, rest) for part in range(groups)]
            tgrad_ref[...] += nt_dot(jnp.concatenate(parts, axis=0), onehot)
            return carry

        lax.fori_loop(0, letters, table, 0, unroll=5)
        advance()
    table_rows = tgrad_ref.shape[0] // 2
    slices, size = table_low.shape[:2]
    conv_total.start(wgrad_ref[...].reshape(conv_low.shape))
    sums = tgrad_ref[:table_rows, :] + tgrad_ref[table_rows:, :]
    sums = jnp.concatenate([sums, jnp.zeros((slices * size - table_rows, sums.shape[1]), jnp.float32)], axis=0)
    table_total.start(sums.reshape(table_low.shape))
    for step in (
        both.along, wide[3].join, table_total.combine, conv_total.combine, wide[3].relay, table_total.across, both.join, both.relay,
    ):
        step()
    for copy in swaps:
        copy.wait_send()
    for item in [ffn, late, slim, both, pos, few, conv_total, table_total] + wide:
        item.finish()


class ChannelScatter:
    def __init__(self, part_ref, base_ref, out_ref, inbox, merged, send, recv):
        self.part, self.base, self.out, self.inbox, self.merged = part_ref, base_ref, out_ref, inbox, merged
        self.sems = (send, recv)
        self.me = lax.axis_index("filt")

    def begin(self):
        me = self.me
        rows, cols = self.base.shape
        pieces = self.sems[0].shape[1]
        size = rows // pieces

        def lanes(index):
            return pl.ds(pl.multiple_of(index * cols, cols), cols)

        def hop(source, kind, piece, peer):
            span = pl.ds(piece * size, size)
            send, recv = self.sems
            copy = remote(source, self.inbox.at[kind, span, :], send.at[kind, piece], recv.at[kind, piece], {"filt": peer})
            copy.start()
            return copy

        self.lanes, self.hop = lanes, hop
        self.spans = spans = [pl.ds(piece * size, size) for piece in range(pieces)]
        first = [hop(self.part.at[span, lanes(me ^ 3)], 0, piece, me ^ 1) for piece, span in enumerate(spans)]
        second = [hop(self.part.at[span, lanes(me ^ 1)], 1, piece, me ^ 1) for piece, span in enumerate(spans)]
        self.first, self.second = first, second

    def finish(self):
        me, lanes, hop, first, second, spans = self.me, self.lanes, self.hop, self.first, self.second, self.spans
        third = []
        for piece, span in enumerate(spans):
            first[piece].wait_recv()
            both = self.part[span, lanes(me ^ 2)].astype(jnp.float32) + self.inbox[0, span, :].astype(jnp.float32)
            self.merged[span, :] = both.astype(jnp.bfloat16)
            third.append(hop(self.merged.at[span, :], 2, piece, me ^ 2))
        for piece, span in enumerate(spans):
            second[piece].wait_recv()
            third[piece].wait_recv()
            total = self.part[span, lanes(me)].astype(jnp.float32) + self.inbox[1, span, :].astype(jnp.float32)
            total = total + self.inbox[2, span, :].astype(jnp.float32) + self.base[span, :]
            self.out[span, :] = total.astype(jnp.bfloat16)
        for copy in first + second + third:
            copy.wait_send()


def highway_mix_back(dproj_ref, proj_ref, hidden_ref, gates_ref, acts_ref, din_ref, dgates_ref, bias_ref):
    words, filters = acts_ref.shape
    block = 128
    bias_ref[...] = jnp.zeros(bias_ref.shape, jnp.float32)

    def mix(index, carry):
        span = pl.ds(pl.multiple_of(index * block, block), block)
        dhidden = nt_dot(dproj_ref[span, :], proj_ref[...])
        turn = gates_ref[span, :filters]
        keep = sigmoid(gates_ref[span, filters:])
        below = normal_cdf(turn)
        slope = below + turn * (DENSITY * jnp.exp(-0.5 * turn * turn))
        fresh = dhidden * (1.0 - keep)
        din_ref[span, :] = dhidden * keep
        dturn = (fresh * slope).astype(jnp.bfloat16)
        dkeep = (fresh * keep * (acts_ref[span, :].astype(jnp.float32) - turn * below)).astype(jnp.bfloat16)
        dgates_ref[span, :filters] = dturn
        dgates_ref[span, filters:] = dkeep
        bias_ref[:, :filters] += jnp.sum(dturn.astype(jnp.float32), axis=0, keepdims=True)
        bias_ref[:, filters:] += jnp.sum(dkeep.astype(jnp.float32), axis=0, keepdims=True)
        return carry

    lax.fori_loop(0, words // block, mix, 0)


def highway_grads(feats_ref, dgates_ref, grad_ref):
    rings, sides, rows, cols = grad_ref.shape
    piece = sides * rows

    def grads(index, carry):
        lanes = pl.ds(pl.multiple_of(index * piece, piece), piece)
        grad = tn_dot(feats_ref[:, lanes], dgates_ref[...]).astype(jnp.bfloat16)
        grad_ref[index] = grad.reshape(sides, rows, cols)
        return carry

    lax.fori_loop(0, rings, grads, 0)


def highway_down(dgates_ref, high_ref, part_ref):
    filters = high_ref.shape[2]
    piece = 512

    def down(index, carry):
        lanes = pl.ds(pl.multiple_of(index * piece, piece), piece)
        both = nt_dot(dgates_ref[:, :filters], high_ref[0, lanes, :]) + nt_dot(dgates_ref[:, filters:], high_ref[1, lanes, :])
        part_ref[:, lanes] = both.astype(jnp.bfloat16)
        return carry

    lax.fori_loop(0, part_ref.shape[1] // piece, down, 0)


def row_grads(hidden_ref, dproj_ref, attended_ref, dmixed_ref, both_ref):
    parts, sides, rows, dmodel = both_ref.shape
    width = dmodel // parts
    gproj = tn_dot(hidden_ref[...], dproj_ref[...]).astype(jnp.bfloat16)
    gout = tn_dot(attended_ref[...], dmixed_ref[...]).astype(jnp.bfloat16)
    size, small = gproj.shape[0] // (sides * parts), gout.shape[0] // (sides * (parts - 1))
    for part in range(parts):
        cols = slice(part * width, (part + 1) * width)
        for side in range(sides):
            for group in range(parts):
                lanes = slice(group * width, (group + 1) * width)
                start = (side * parts + group) * size
                both_ref[part, side, :size, lanes] = gproj[start : start + size, cols]
                if group < parts - 1:
                    start = (side * (parts - 1) + group) * small
                    both_ref[part, side, size:, lanes] = gout[start : start + small, cols]
                else:
                    both_ref[part, side, size:, lanes] = jnp.zeros((rows - size, width), jnp.bfloat16)


def epilogue_call(dproj, proj, hidden, gates, acts, feats, high, attended, dmixed, ids, embed, lse, weight, back, limit, count,
                  slim, ffn, pair, pos, few, po_rows, letters, depth, groups, ident, block=256):
    filters, words = lse.shape
    args = (dproj, proj, hidden, gates, acts, feats, high, attended, dmixed, ids, embed, lse, weight, back, limit, count,
            slim, ffn, pair, pos, few)
    channels, dmodel = feats.shape[1], dproj.shape[1]
    parts = channels // filters
    slices = pos.shape[0]
    pieces = 4
    vmem = pl.BlockSpec(memory_space=pltpu.VMEM)
    table_size = -(-(-(-groups * depth // slices)) // 8) * 8
    wide_shape = (slices // 2, 2, channels // slices, 2 * filters)
    both_shape = (slices // 2, 2, po_rows, dmodel)

    def space(shape, dtype=jnp.bfloat16):
        return pltpu.VMEM(tuple(shape), dtype)

    def stages(shape):
        ring, side, rows, cols = shape
        return [space((ring, rows, cols)), space((ring, rows, cols)), space((ring - 1, rows, cols))]

    def totals(shape, sides):
        spaces = [space(shape), space((shape[0] - 1,) + shape[1:])]
        return spaces + ([space((4,) + shape[1:])] if sides else [])

    conv_shape = (slices, filters // slices, 128)
    table_shape = (slices, table_size, 128)
    out_shape = [bf16(parts, *wide_shape[2:]), bf16(parts, *slim.shape[2:]), bf16(parts, *both_shape[2:]),
                 bf16(parts, ffn.shape[0] + pair.shape[1], ffn.shape[1]), bf16(*conv_shape), bf16(*table_shape), bf16(*pos.shape),
                 bf16(*few.shape[1:])]
    padded = (letters + KW - 1) * depth
    return pl.pallas_call(
        functools.partial(epilogue, letters, depth, block),
        in_specs=[vmem] * len(args),
        out_specs=[vmem] * len(out_shape),
        out_shape=out_shape,
        scratch_shapes=[space((1, 2 * filters), jnp.float32), space((words, channels)), space((words, filters), jnp.float32), space((words, 2 * filters)), space(wide_shape),
                        space(both_shape), space((3, words, filters)), space((words, filters)), space((words, filters)), space((padded, block)),
                        space((padded, block), jnp.float32), space((filters, block), jnp.float32),
                        space((filters, 128), jnp.float32), space((2 * groups * depth, 128), jnp.float32)]
        + stages(wide_shape) + stages(slim.shape) + [space(both_shape)] + stages(both_shape) + [space((3,) + pair.shape[1:])]
        + totals(conv_shape, False) + totals(table_shape, True) + totals(pos.shape, False) + totals(few.shape, True)
        + [DMA((3, pieces)), DMA((3, pieces)), DMA((8, 7)), DMA((8, 7)), DMA((4, 3, slices - 1)), DMA((4, 3, slices - 1)),
           DMA((3,)), DMA((3,))],
        compiler_params=pltpu.CompilerParams(collective_id=ident, has_side_effects=True, vmem_limit_bytes=60 << 20),
        name="epilogue",
    )(*args)


def assemble(depth, wide_ref, slim_ref, both_ref, ffn_ref, conv_ref, table_ref, pos_ref, few_ref, limit_ref,
             wide_out, slim_out, proj_out, out_out, inner_out, outer_out, conv_out, cbias_out, table_out, pos_out,
             hbias_out, pbias_out, gain_out, shift_out, ibias_out):
    parts = wide_ref.shape[0]
    inner_rows = inner_out.shape[0]
    proj_rows, out_rows = proj_out.shape[0] // parts, out_out.shape[0] // (parts - 1)
    filters = wide_ref.shape[2] // 2
    width = slim_ref.shape[2] // 3
    for part in range(parts):
        for half in range(2):
            start = (half * parts + part) * filters
            wide_out[:, start : start + filters] = wide_ref[part, :, half * filters : (half + 1) * filters].astype(jnp.float32)
        for block in range(3):
            start = (block * parts + part) * width
            slim_out[:, start : start + width] = slim_ref[part, :, block * width : (block + 1) * width].astype(jnp.float32)
        cols = slice(part * width, (part + 1) * width)
        for block in range(parts):
            lanes = slice(block * width, (block + 1) * width)
            proj_out[block * proj_rows : (block + 1) * proj_rows, cols] = both_ref[part, :proj_rows, lanes].astype(jnp.float32)
            if block < parts - 1:
                out_out[block * out_rows : (block + 1) * out_rows, cols] = both_ref[part, proj_rows:, lanes].astype(jnp.float32)
        units = ffn_ref.shape[1] - inner_rows
        outer_out[part * units : (part + 1) * units, :] = ffn_ref[part, inner_rows:, :].astype(jnp.float32)
        for block in range(inner_out.shape[1] // (parts * units)):
            start = (block * parts + part) * units
            inner_out[:, start : start + units] = ffn_ref[part, :inner_rows, block * units : (block + 1) * units].astype(jnp.float32)
    slices, conv_rows = conv_ref.shape[:2]
    taps = conv_out.shape[0]
    turned = conv_ref[...].reshape(slices * conv_rows, 128).astype(jnp.float32).T
    tap = lax.broadcasted_iota(jnp.int32, (taps, 1), 0) // depth
    conv_out[...] = jnp.where(tap < limit_ref[...], turned[:taps], 0.0)
    cbias_out[...] = turned[taps : taps + 1]
    table = table_ref[...].reshape(-1, 128).astype(jnp.float32)
    vocab = table_out.shape[0]
    for group in range(-(-vocab // 128)):
        stop = min(128, vocab - group * 128)
        table_out[group * 128 : group * 128 + stop, :] = table[group * depth : (group + 1) * depth].T[:stop]
    pos_out[...] = pos_ref[...].reshape(pos_out.shape).astype(jnp.float32)
    own = few_ref[...].astype(jnp.float32)
    size = gain_out.shape[1]
    hbias_out[...] = own[0:1, : hbias_out.shape[1]]
    pbias_out[...] = own[1:2, : pbias_out.shape[1]]
    gain_out[...] = own[2:5, :size]
    shift_out[...] = own[5:8, :size]
    ibias_out[...] = own[8:9, : ibias_out.shape[1]]


def assemble_call(wide, slim, both, ffn, conv, table, pos, few, widths, inner_rows, out_rows, taps, vocab, depth, sizes):
    args = (wide, slim, both, ffn, conv, table, pos, few, widths)
    parts = wide.shape[0]

    def whole(shape):
        return pl.BlockSpec(shape, lambda step: (0,) * len(shape))

    units = ffn.shape[1] - inner_rows
    dmodel = both.shape[2]
    hb, pb, nd, ib = sizes
    proj_rows = both.shape[1] - out_rows // (parts - 1)
    out_shape = [f32(wide.shape[1], wide.shape[2] * parts), f32(slim.shape[1], slim.shape[2] * parts),
                 f32(proj_rows * parts, dmodel), f32(out_rows, dmodel), f32(inner_rows, dmodel * parts), f32(units * parts, dmodel),
                 f32(taps, widths.shape[1]), f32(1, widths.shape[1]), f32(vocab, depth), f32(pos.shape[0] * pos.shape[1], pos.shape[2]),
                 f32(1, hb), f32(1, pb), f32(3, nd), f32(3, nd), f32(1, ib)]
    return pl.pallas_call(
        functools.partial(assemble, depth), grid=(1,), in_specs=[whole(item.shape) for item in args],
        out_specs=[whole(item.shape) for item in out_shape], out_shape=out_shape,
        compiler_params=pltpu.CompilerParams(vmem_limit_bytes=56 << 20), name="assemble",
    )(*args)


def exact_gaussian_activation(values):
    return values * normal_cdf(values)


def gelu_back(values, upstream):
    density = DENSITY * jnp.exp(-0.5 * values * values)
    return upstream * (normal_cdf(values) + values * density)


def channel_widths(channels):
    widths = jnp.ones_like(channels)
    for power in range(6):
        widths = widths + (channels >= NF * 2**power // 64).astype(jnp.int32)
    return widths


def highway_mix(hidden, gates):
    width = hidden.shape[1]
    carry_gate = jax.nn.sigmoid(gates[:, width:])
    return carry_gate * hidden + (1.0 - carry_gate) * exact_gaussian_activation(gates[:, :width])


def swap(array, axis, bit):
    size = lax.axis_size(axis)
    return lax.ppermute(array, axis, [(index, index ^ bit) for index in range(size)])


def reduce_rows(array):
    count = lax.axis_size("dp")
    slot = lax.axis_index("dp")
    bits = count.bit_length() - 1
    rows, cols = array.shape
    if count != 1 << bits:
        return lax.psum_scatter(array.astype(jnp.bfloat16), "dp", scatter_dimension=0, tiled=True)
    array = array.reshape((2,) * bits + (rows // count, cols))
    for bit in range(bits):
        axis = bits - 1 - bit
        mine = (slot >> bit) & 1
        keep = lax.dynamic_index_in_dim(array, mine, axis, keepdims=False)
        give = lax.dynamic_index_in_dim(array, 1 - mine, axis, keepdims=False)
        got = swap(give.astype(jnp.bfloat16), "dp", 1 << bit)
        array = (keep.astype(jnp.float32) + got.astype(jnp.float32)).astype(jnp.bfloat16)
    return array


def join_parts(array):
    part = lax.axis_index("filt")
    low = (part & 1) == 1
    high = (part >> 1) == 1
    far = swap(array, "filt", 2)
    near = swap(array, "filt", 1)
    both = swap(far, "filt", 1)
    here = (jnp.where(low, near, array), jnp.where(low, array, near))
    there = (jnp.where(low, both, far), jnp.where(low, far, both))
    first = [jnp.where(high, b, a) for a, b in zip(here, there)]
    second = [jnp.where(high, a, b) for a, b in zip(here, there)]
    return first + second


def per_device(
    chars,
    lengths,
    char_table,
    conv_weight,
    conv_bias,
    highway_weight,
    highway_bias,
    proj_weight,
    proj_bias,
    position,
    norm_gain,
    norm_bias,
    query_key_value_weight,
    attention_output_weight,
    feedforward_input_weight,
    feedforward_input_bias,
    feedforward_output_weight,
    cotangent,
):
    parts = lax.axis_size("filt")
    slices = lax.axis_size("dp")
    part = lax.axis_index("filt")
    slot = lax.axis_index("dp")
    seqs, quarter, dmodel = cotangent.shape
    full_len = chars.shape[1]
    letters = chars.shape[2]
    words = seqs * full_len
    tokens = seqs * quarter
    filters = conv_weight.shape[1]
    depth = char_table.shape[1]
    heads = dmodel // HD // parts
    width = heads * HD
    inner_rows = feedforward_input_weight.shape[0]
    unit_rows = feedforward_output_weight.shape[0] // parts

    def own_columns(array, blocks):
        rows = array.shape[0]
        split = array.reshape(rows, blocks, parts, -1)
        return lax.dynamic_index_in_dim(split, part, 2, keepdims=False).reshape(rows, -1)

    def gather_rows(array):
        return lax.all_gather(array, "dp", axis=0, tiled=True)

    def groups_of(array, groups):
        array = array.reshape(groups, -1, width).transpose(1, 0, 2).reshape(-1, groups * width)
        return jnp.pad(array, ((0, 0), (0, dmodel - groups * width)))

    def rows_from_columns(both):
        both = lax.all_to_all(both.reshape(parts, -1, dmodel), "filt", split_axis=0, concat_axis=0, tiled=True)
        both = both.reshape(parts, slices // parts, po_rows, parts, width)
        both = [both[:, :, :split], both[:, :, split:, : parts - 1]]
        return [item.transpose(1, 3, 2, 0, 4).reshape(-1, dmodel) for item in both]

    def columns_from_rows(*grads):
        items = []
        for item, groups in zip(grads, (parts, parts - 1)):
            item = item.astype(jnp.bfloat16).reshape(slices // parts, groups, -1, parts, width)
            item = item.transpose(3, 0, 2, 1, 4).reshape(parts, slices // parts, -1, groups * width)
            items.append(jnp.pad(item, ((0, 0), (0, 0), (0, 0), (0, dmodel - groups * width))))
        both = jnp.concatenate(items, axis=2)
        both = lax.all_to_all(both.reshape(parts, -1, dmodel), "filt", split_axis=0, concat_axis=0, tiled=True)
        return both.reshape(slices * po_rows, dmodel)

    fast = slices == 8 and parts == 4
    hb, pb, nd = highway_bias.shape[1], proj_bias.shape[0], norm_gain.shape[1]
    small = jnp.concatenate(
        [
            highway_bias.reshape(-1),
            proj_bias,
            norm_gain.reshape(-1),
            norm_bias.reshape(-1),
            feedforward_input_bias,
        ]
    )
    small_size = small.shape[0]
    small = jnp.pad(small, (0, -small_size % dmodel))
    slim_parts = [
        groups_of(own_columns(proj_weight, 1), parts),
        groups_of(own_columns(attention_output_weight, 1), parts - 1),
        own_columns(query_key_value_weight, 3).reshape(-1, dmodel),
        small.reshape(-1, dmodel),
    ]
    split = slim_parts[0].shape[0]
    po_rows = split + slim_parts[1].shape[0]
    qkv_rows = slim_parts[2].shape[0]
    slim_all = lax.all_gather(jnp.concatenate(slim_parts, axis=0), "dp", axis=0, tiled=False)
    qkv_own = slim_all[:, po_rows : po_rows + qkv_rows].reshape(dmodel, 3 * width)
    small = slim_all[:, po_rows + qkv_rows :]
    small = small.reshape(slices, -1)[:, :small_size].astype(jnp.float32)
    cuts = [hb, hb + pb, hb + pb + 3 * nd, hb + pb + 6 * nd]
    highway_b, proj_b, gain, shift, inner_b = jnp.split(small, cuts, axis=1)
    highway_b_own = own_columns(highway_b.reshape(1, -1), 2)
    proj_b = proj_b.reshape(-1)
    gain = gain.reshape(slices, 3, nd).transpose(1, 0, 2).reshape(3, dmodel)
    shift = shift.reshape(slices, 3, nd).transpose(1, 0, 2).reshape(3, dmodel)
    inner_b_own = own_columns(inner_b.reshape(1, -1), slices)
    ffn_own = jnp.concatenate(
        [
            own_columns(feedforward_input_weight, slices),
            lax.dynamic_slice_in_dim(feedforward_output_weight, part * unit_rows, unit_rows, 0),
        ],
        axis=0,
    )

    def blocks_of(array):
        return array.astype(jnp.bfloat16).reshape(parts, tokens, -1)

    widths = channel_widths(part * filters + jnp.arange(filters, dtype=jnp.int32))
    ids, table, weight, back, limit, count = conv_prep(
        chars.reshape(words, letters), char_table, conv_weight, conv_bias, widths
    )
    if fast:
        acts, lse, embed, features, highway_own = prologue_call(
            ids, table, weight, limit, count, highway_weight[0], parts, letters, depth, 0
        )
        highway_own = highway_own.reshape(2, -1, filters)
    else:
        acts, lse, embed = conv_forward_call(ids, table, weight, limit, count, letters, depth)
        features = gather_channels_call(acts, parts, 0)
        highway_own = gather_rows(own_columns(highway_weight[0], 2))
        proj_own, out_own = rows_from_columns(slim_all[:, :po_rows])
    ffn_own, features = lax.optimization_barrier((ffn_own, features))
    ffn_all = lax.all_gather(ffn_own, "dp", axis=0, tiled=False)
    base = position.astype(jnp.float32) + proj_b[None, :]
    if fast:
        gates, hidden_low, proj_own, out_own, first, unit_zero, scale_zero, first_all = highway_stage_call(
            slim_all,
            features,
            highway_own,
            highway_b_own,
            acts,
            base,
            gain[0:1],
            shift[0:1],
            attention_output_weight.shape[0] * slices // parts,
            po_rows,
            EPS,
            1,
        )
    else:
        gates = nn_dot(features, highway_own) + highway_b_own
        feature_own = acts.astype(jnp.float32)
        hidden_low = highway_mix(feature_own, gates).astype(jnp.bfloat16)
        first, unit_zero, scale_zero, first_all = forward_stage_call(
            blocks_of(nn_dot(hidden_low, proj_own)), base, gain[0:1], shift[0:1], EPS, 1
        )
    first_all = first_all.reshape(words, dmodel)
    packed = nn_dot(first_all, qkv_own).astype(jnp.bfloat16)
    queries, keys, values = (
        packed[:, block * width : (block + 1) * width].reshape(seqs, full_len, heads, HD)
        for block in range(3)
    )
    key_ok = jnp.arange(full_len, dtype=jnp.int32)[None, :] < lengths[:, None]
    scale = HD ** (-0.5)
    scores = (
        jnp.einsum("sqhd,skhd->shqk", queries, keys, preferred_element_type=jnp.float32) * scale
    )
    scores = jnp.where(key_ok[:, None, None, :], scores, -1e30)
    row_top = jnp.max(scores, axis=-1, keepdims=True)
    log_total = row_top + jnp.log(jnp.sum(jnp.exp(scores - row_top), axis=-1, keepdims=True))
    probs = jnp.exp(scores - log_total)
    probs_low = probs.astype(jnp.bfloat16)
    attended = (
        jnp.einsum("shqk,skhd->sqhd", probs_low, values, preferred_element_type=jnp.float32)
        .astype(jnp.bfloat16)
        .reshape(words, width)
    )
    second, unit_one, scale_one, second_all = forward_stage_call(
        blocks_of(nn_dot(attended, out_own)), first, gain[1:2], shift[1:2], EPS, 2
    )
    second_all = second_all.reshape(words, dmodel)
    ffn_all, second_all = lax.optimization_barrier((ffn_all, second_all))
    inner_own = ffn_all[:, :inner_rows].reshape(dmodel, -1)
    outer_own = ffn_all[:, inner_rows:].reshape(-1, dmodel)
    inner = nn_dot(second_all, inner_own) + inner_b_own
    active = exact_gaussian_activation(inner).astype(jnp.bfloat16)
    top, d_res_two, d_gain_two, d_shift_two, d_outer = top_stage_call(
        blocks_of(nn_dot(active, outer_own)),
        second,
        cotangent.reshape(tokens, dmodel),
        gain[2:3],
        shift[2:3],
        EPS,
        3,
    )
    encoded = top.reshape(seqs, quarter, dmodel)
    d_outer = d_outer.reshape(words, dmodel)
    grad_outer = tn_dot(active, d_outer)
    d_active = nt_dot(d_outer, outer_own)
    d_inner = gelu_back(inner, d_active).astype(jnp.bfloat16)
    grad_inner = tn_dot(second_all, d_inner)
    grad_ffn = jnp.concatenate(
        [item.astype(jnp.bfloat16).reshape(slices, -1, dmodel) for item in (grad_inner, grad_outer)], axis=1
    )
    if fast:
        early = grad_ffn.shape[1] * 2 // 3
        grad_ffn = grad_ffn.reshape(4, 2, -1, dmodel)
        grad_early, grad_late = grad_ffn[:, :, :early], grad_ffn[:, :, early:]
        jobs = ("side",), (grad_early,)
    else:
        jobs = (), ()

    def pair_sum(grad, got):
        keep = lax.dynamic_index_in_dim(grad, slot % 2, 1, keepdims=False)
        return (keep.astype(jnp.float32) + got.astype(jnp.float32)).astype(jnp.bfloat16)

    grad_inner_b = jnp.sum(d_inner.astype(jnp.float32), axis=0)
    d_res_one, d_gain_one, d_shift_one, unused_sum, d_mixed, *got = backward_stage_call(
        blocks_of(nt_dot(d_inner, inner_own)), d_res_two, unit_one, scale_one, gain[1:2], 4, *jobs
    )
    if fast:
        grad_early = pair_sum(grad_early, got[0])
        jobs = ("side", "ring"), (grad_late, grad_early)
    d_mixed = d_mixed.reshape(words, dmodel)
    d_attended = nt_dot(d_mixed, out_own).astype(jnp.bfloat16)
    d_attended = d_attended.reshape(seqs, full_len, heads, HD)
    d_values = jnp.einsum(
        "shqk,sqhd->skhd", probs_low, d_attended, preferred_element_type=jnp.float32
    )
    d_probs = jnp.einsum(
        "sqhd,skhd->shqk", d_attended, values, preferred_element_type=jnp.float32
    )
    row_inner = jnp.sum(d_probs * probs, axis=-1, keepdims=True)
    d_scores = (probs * (d_probs - row_inner)).astype(jnp.bfloat16)
    d_queries = (
        jnp.einsum("shqk,skhd->sqhd", d_scores, keys, preferred_element_type=jnp.float32) * scale
    )
    d_keys = (
        jnp.einsum("shqk,sqhd->skhd", d_scores, queries, preferred_element_type=jnp.float32) * scale
    )
    d_packed = jnp.concatenate(
        [item.reshape(words, width) for item in (d_queries, d_keys, d_values)], axis=1
    ).astype(jnp.bfloat16)
    grad_qkv = tn_dot(first_all, d_packed).astype(jnp.bfloat16)
    d_summed, d_gain_zero, d_shift_zero, grad_proj_b, d_projected, *got = backward_stage_call(
        blocks_of(nt_dot(d_packed, qkv_own)), d_res_one, unit_zero, scale_zero, gain[0:1], 5, *jobs
    )
    if fast:
        grad_late = pair_sum(grad_late, got[0])
        keep = lax.dynamic_index_in_dim(grad_early, slot // 2, 0, keepdims=False)
        grad_early = sum([item.astype(jnp.float32) for item in got[1]], keep.astype(jnp.float32))
        grad_early = grad_early.astype(jnp.bfloat16)
    grad_pos = jnp.sum(d_summed.reshape(seqs, quarter, dmodel), axis=0)
    d_projected = d_projected.reshape(words, dmodel)
    if not fast:
        grad_both = columns_from_rows(tn_dot(hidden_low, d_projected), tn_dot(attended, d_mixed))
        d_hidden = nt_dot(d_projected, proj_own)
        d_in, d_gates = jax.vjp(highway_mix, feature_own, gates)[1](d_hidden)
        d_gates = d_gates.astype(jnp.bfloat16)
        grad_highway = tn_dot(features, d_gates).astype(jnp.bfloat16)
        grad_highway_b = jnp.sum(d_gates.astype(jnp.float32), axis=0)
        d_partial = nt_dot(d_gates, highway_own).astype(jnp.bfloat16)
    groups = table.shape[0] // depth

    def place_columns(own, blocks):
        piece = own.reshape(blocks, 1, -1)
        whole = jnp.zeros((blocks, parts, piece.shape[2]), own.dtype)
        return lax.dynamic_update_slice_in_dim(whole, piece, part, 1).reshape(-1)

    d_gain = jnp.concatenate([d_gain_zero, d_gain_one, d_gain_two])
    d_shift = jnp.concatenate([d_shift_zero, d_shift_one, d_shift_two])
    if fast:
        highway_piece = jnp.zeros((slices, 1, hb), jnp.float32)
    else:
        highway_piece = place_columns(grad_highway_b, 2).reshape(slices, 1, -1)
    pieces = [
        highway_piece,
        grad_proj_b.reshape(slices, 1, -1),
        d_gain.reshape(3, slices, nd).transpose(1, 0, 2),
        d_shift.reshape(3, slices, nd).transpose(1, 0, 2),
        place_columns(grad_inner_b, slices).reshape(slices, 1, -1),
    ]
    if fast:
        few = [jnp.pad(item, ((0, 0), (0, 0), (0, hb - item.shape[2]))) for item in pieces]
        few.append(jnp.zeros((slices, 7, hb), jnp.float32))
        few = jnp.concatenate(few, axis=1)
        wide_all, slim_all, both_all, ffn_all, conv_all, table_all, pos_all, few = epilogue_call(
            d_projected,
            proj_own,
            hidden_low,
            gates,
            acts,
            features,
            highway_own,
            attended,
            d_mixed,
            ids,
            embed,
            lse,
            weight,
            back,
            limit,
            count,
            grad_qkv.reshape(4, 2, -1, 3 * width),
            grad_early,
            grad_late,
            grad_pos.reshape(slices, -1, dmodel),
            few,
            po_rows,
            letters,
            depth,
            groups,
            6,
        )
        outs = assemble_call(
            wide_all,
            slim_all,
            both_all,
            ffn_all,
            conv_all,
            table_all,
            pos_all,
            few,
            widths[None, :],
            inner_rows,
            attention_output_weight.shape[0],
            conv_weight.shape[0],
            char_table.shape[0],
            depth,
            (hb, pb, nd, feedforward_input_bias.shape[0]),
        )
        g_highway, g_qkv, g_proj, g_out, g_inner, g_outer, conv_grad_w, conv_grad_b, g_table, grad_pos = outs[:10]
        g_highway_b, g_proj_b, g_gain, g_shift, g_inner_b = outs[10:]
        conv_grad_b, g_proj_b, g_inner_b = conv_grad_b[0], g_proj_b[0], g_inner_b[0]
    else:
        d_features = scatter_channels_call(d_partial, d_in, 6)
        conv_sums, table_sums = conv_backward_call(
            ids, embed, lse, d_features, weight, back, limit, count, groups, letters, depth
        )
        wide_all = jnp.stack(join_parts(reduce_rows(grad_highway)))
        slim_all = jnp.stack(join_parts(reduce_rows(grad_qkv)))
        both_all = jnp.stack(join_parts(reduce_rows(grad_both)))
        ffn_all = jnp.stack(join_parts(reduce_rows(grad_ffn.reshape(-1, dmodel))))
        table_sums = table_sums.reshape(2, groups * depth, -1).sum(0)
        conv_all = lax.psum(conv_sums, "dp")
        rows = jnp.concatenate([item.reshape(slices, -1) for item in pieces], axis=1)
        table_all, sums = lax.psum((table_sums, rows), ("dp", "filt"))
        grad_pos = lax.psum(grad_pos, "dp")
        own = lax.dynamic_index_in_dim(sums, slot, 0, keepdims=False)
        tap_rows = conv_weight.shape[0]
        tap_keep = (jnp.arange(tap_rows, dtype=jnp.int32) // depth)[:, None] < widths[None, :]
        conv_grad_w = jnp.where(tap_keep, conv_all[:, :tap_rows].T, 0.0)
        conv_grad_b = conv_all[:, tap_rows]
        g_table = table_all.reshape(groups, depth, 128).transpose(0, 2, 1).reshape(-1, depth)
        g_table = g_table[: char_table.shape[0]]
        g_highway_b, g_proj_b, g_gain, g_shift, g_inner_b = jnp.split(own, cuts)

        def join_columns(array, blocks, rows_here):
            array = array.reshape(parts, rows_here, blocks, -1).transpose(1, 2, 0, 3)
            return array.reshape(rows_here, -1).astype(jnp.float32)

        def join_groups(array, many):
            array = array.reshape(parts, array.shape[1], parts, width).transpose(2, 1, 0, 3)
            return array[:many].reshape(-1, dmodel).astype(jnp.float32)

        g_outer = ffn_all[:, inner_rows:].reshape(-1, dmodel).astype(jnp.float32)
        g_inner = join_columns(ffn_all[:, :inner_rows], slices, inner_rows)
        g_qkv = join_columns(slim_all, 3, query_key_value_weight.shape[0])
        g_proj = join_groups(both_all[:, :split], parts)
        g_out = join_groups(both_all[:, split:], parts - 1)
        g_highway = join_columns(wide_all, 2, highway_weight.shape[1])
    return (
        encoded,
        g_table,
        conv_grad_w,
        conv_grad_b,
        g_highway[None],
        g_highway_b.reshape(1, hb),
        g_proj,
        g_proj_b,
        grad_pos,
        g_gain.reshape(3, nd),
        g_shift.reshape(3, nd),
        g_qkv,
        g_out,
        g_inner,
        g_inner_b,
        g_outer,
    )


def solution(mesh):
    return jax.shard_map(
        per_device,
        mesh=mesh,
        in_specs=(
            P("dp", None, None),
            P("dp"),
            P(),
            P(None, "filt"),
            P("filt"),
            P(None, "dp", None),
            P(None, "dp"),
            P("dp", None),
            P("dp"),
            P("filt", None),
            P(None, "dp"),
            P(None, "dp"),
            P("dp", None),
            P("dp", None),
            P("dp", None),
            P("dp"),
            P("dp", None),
            P("dp", "filt", None),
        ),
        out_specs=(
            P("dp", "filt", None),
            P(),
            P(None, "filt"),
            P("filt"),
            P(None, "dp", None),
            P(None, "dp"),
            P("dp", None),
            P("dp"),
            P("filt", None),
            P(None, "dp"),
            P(None, "dp"),
            P("dp", None),
            P("dp", None),
            P("dp", None),
            P("dp"),
            P("dp", None),
        ),
        check_vma=False,
    )
```

```python
import functools

import jax
import jax.numpy as jnp
from jax import lax
from jax.experimental import pallas as pl
from jax.experimental.pallas import tpu as pltpu
from jax.sharding import PartitionSpec as P

KW = 7
NF = 2048
HD = 64
EPS = 1e-12
ROOT_HALF = 0.7071067811865476
DENSITY = 0.3989422804014327

def nt_dot(left, right):
    return lax.dot_general(left, right, (((1,), (1,)), ((), ())), preferred_element_type=jnp.float32)

def tn_dot(left, right):
    return lax.dot_general(left, right, (((0,), (0,)), ((), ())), preferred_element_type=jnp.float32)

def nn_dot(left, right):
    return jnp.dot(left, right, preferred_element_type=jnp.float32)

def normal_cdf(values):
    return 0.5 * (1.0 + lax.erf(values * ROOT_HALF))

def char_parts(chars_ref, position, block):
    ids = chars_ref[pl.ds(position, 1), :]
    low = ids & 127
    group = ids >> 7
    onehot = (lax.broadcasted_iota(jnp.int32, (128, block), 0) == low)
    onehot = jnp.where(onehot, 1.0, 0.0).astype(jnp.bfloat16)
    return onehot, group

def conv_forward(letters, depth, chars_ref, table_ref, weight_ref, limit_ref, count_ref,
                 acts_ref, lse_ref, embed_ref, patch_ref, grid_ref):
    block = chars_ref.shape[1]
    filters = weight_ref.shape[0]
    groups = table_ref.shape[0] // depth
    lead = KW - 1
    rows = KW * depth

    @pl.when(pl.program_id(0) == 0)
    def _():
        patch_ref[:, :rows, :] = jnp.zeros((patch_ref.shape[0], rows, block), jnp.bfloat16)
        ones = lax.broadcasted_iota(jnp.int32, (128 - rows, block), 0) == 0
        tail = jnp.where(ones, 1.0, 0.0).astype(jnp.bfloat16)
        patch_ref[:, rows:, :] = jnp.broadcast_to(tail[None], (patch_ref.shape[0],) + tail.shape)

    def embed(position, carry):
        onehot, group = char_parts(chars_ref, position, block)
        looked = nn_dot(table_ref[...], onehot)
        row = looked[:depth]
        for index in range(1, groups):
            row = jnp.where(group == index, looked[index * depth : (index + 1) * depth], row)
        row = row.astype(jnp.bfloat16)
        embed_ref[pl.ds(pl.multiple_of(position * depth, depth), depth), :] = row
        for tap in range(KW):
            patch_ref[position + lead - tap, tap * depth : (tap + 1) * depth, :] = row
        return carry

    lax.fori_loop(0, letters, embed, 0, unroll=5)
    chunk = grid_ref.shape[1]
    always = letters - KW + 1
    for start in range(0, filters, chunk):
        weight = weight_ref[start : start + chunk, :]
        limit = limit_ref[start : start + chunk, :]

        def product(position, top):
            grid = nn_dot(weight, patch_ref[position + lead])
            grid_ref[position] = grid
            return jnp.maximum(top, grid)

        top = lax.fori_loop(0, always, product, jnp.full((chunk, block), -1e30, jnp.float32), unroll=11)
        for position in range(always, letters):
            grid = nn_dot(weight, patch_ref[position + lead])
            grid = jnp.where(limit >= position, grid, -1e30)
            grid_ref[position] = grid
            top = jnp.maximum(top, grid)

        def total(position, acc):
            return acc + jnp.exp(grid_ref[position] - top)

        acc = lax.fori_loop(0, letters, total, jnp.zeros((chunk, block), jnp.float32), unroll=10)
        lse = top + jnp.log(acc)
        lse_ref[start : start + chunk, :] = lse
        pooled = lse - count_ref[start : start + chunk, :]
        acts_ref[:, start : start + chunk] = (pooled * normal_cdf(pooled)).astype(jnp.bfloat16).T

def conv_backward(letters, depth, chars_ref, embed_ref, lse_ref, up_ref, weight_ref, back_ref,
                  limit_ref, count_ref, wgrad_ref, tgrad_ref, patch_ref, down_ref, pull_ref):
    block = chars_ref.shape[1]
    filters = weight_ref.shape[0]
    lead = KW - 1
    rows = KW * depth
    groups = tgrad_ref.shape[0] // (2 * depth)
    step = pl.program_id(0)

    @pl.when(step == 0)
    def _():
        wgrad_ref[...] = jnp.zeros(wgrad_ref.shape, jnp.float32)
        tgrad_ref[...] = jnp.zeros(tgrad_ref.shape, jnp.float32)
        patch_ref[letters * depth :, :] = jnp.zeros((patch_ref.shape[0] - letters * depth, block), jnp.bfloat16)

    patch_ref[: letters * depth, :] = embed_ref[...]
    down_ref[...] = jnp.zeros(down_ref.shape, jnp.float32)
    pooled = lse_ref[...] - count_ref[...]
    slope = normal_cdf(pooled) + pooled * (DENSITY * jnp.exp(-0.5 * pooled * pooled))
    pull_ref[...] = slope * up_ref[...].T.astype(jnp.float32)
    ones = jnp.where(lax.broadcasted_iota(jnp.int32, (128 - rows, block), 0) == 0, 1.0, 0.0).astype(jnp.bfloat16)

    def one(position, masked):
        start = position * depth
        if not isinstance(position, int):
            start = pl.multiple_of(start, depth)
        patch = jnp.concatenate([patch_ref[pl.ds(start, rows), :], ones], axis=0)
        grid = nn_dot(weight_ref[...], patch)
        spread = jnp.exp(grid - lse_ref[...]) * pull_ref[...]
        if masked:
            spread = jnp.where(limit_ref[...] >= position, spread, 0.0)
        spread = spread.astype(jnp.bfloat16)
        down = nn_dot(back_ref[...], spread)
        down_ref[pl.ds(start, rows), :] += down[:rows]
        wgrad_ref[...] += nt_dot(spread, patch)

    always = letters - KW + 1

    def body(position, carry):
        one(position, False)
        return carry

    lax.fori_loop(0, always, body, 0, unroll=2)
    for position in range(always, letters):
        one(position, True)

    def table(position, carry):
        onehot, group = char_parts(chars_ref, position, block)
        down = down_ref[pl.ds(pl.multiple_of(position * depth, depth), depth), :]
        high = down.astype(jnp.bfloat16)
        low = (down - high.astype(jnp.float32)).astype(jnp.bfloat16)
        zero = jnp.zeros_like(high)
        parts = [jnp.where(group == index, item, zero) for item in (high, low) for index in range(groups)]
        tgrad_ref[...] += nt_dot(jnp.concatenate(parts, axis=0), onehot)
        return carry

    lax.fori_loop(0, letters, table, 0, unroll=5)

def conv_prep(chars, char_table, conv_weight, conv_bias, widths):
    letters = chars.shape[1]
    vocab, depth = char_table.shape
    groups = -(-vocab // 128)
    table = jnp.pad(char_table, ((0, groups * 128 - vocab), (0, 0)))
    table = table.reshape(groups, 128, depth).transpose(0, 2, 1).reshape(groups * depth, 128)
    tap = jnp.arange(conv_weight.shape[0], dtype=jnp.int32) // depth
    masked = jnp.where(tap[:, None] < widths[None, :], conv_weight, 0)
    back = jnp.concatenate([masked, conv_bias[None, :], jnp.zeros((127 - masked.shape[0], masked.shape[1]), masked.dtype)], axis=0)
    limit = (letters - widths)[:, None].astype(jnp.int32)
    count = jnp.log((letters - widths + 1).astype(jnp.float32))[:, None]
    ids = jnp.pad(chars, ((0, 0), (0, -letters % 8))).T
    return ids, table, back.T, back, limit, count

def conv_forward_call(ids, table, weight, limit, count, letters, depth, block=256):
    words = ids.shape[1]
    filters = weight.shape[0]
    full = lambda a: pl.BlockSpec(a.shape, lambda i: (0,) * a.ndim)
    return pl.pallas_call(
        functools.partial(conv_forward, letters, depth),
        grid=(words // block,),
        in_specs=[pl.BlockSpec((ids.shape[0], block), lambda i: (0, i)), full(table), full(weight), full(limit), full(count)],
        out_specs=[pl.BlockSpec((block, filters), lambda i: (i, 0)), pl.BlockSpec((filters, block), lambda i: (0, i)),
                   pl.BlockSpec((letters * depth, block), lambda i: (0, i))],
        out_shape=[jax.ShapeDtypeStruct((words, filters), jnp.bfloat16), jax.ShapeDtypeStruct((filters, words), jnp.float32),
                   jax.ShapeDtypeStruct((letters * depth, words), jnp.bfloat16)],
        scratch_shapes=[pltpu.VMEM((letters + KW - 1, 128, block), jnp.bfloat16), pltpu.VMEM((letters, 128, block), jnp.float32)],
        compiler_params=pltpu.CompilerParams(vmem_limit_bytes=48 << 20),
        name="conv_forward",
    )(ids, table, weight, limit, count)

def conv_backward_call(ids, embed, lse, up, weight, back, limit, count, groups, letters, depth, block=256):
    words = ids.shape[1]
    filters = weight.shape[0]
    full = lambda a: pl.BlockSpec(a.shape, lambda i: (0,) * a.ndim)
    return pl.pallas_call(
        functools.partial(conv_backward, letters, depth),
        grid=(words // block,),
        in_specs=[pl.BlockSpec((ids.shape[0], block), lambda i: (0, i)), pl.BlockSpec((letters * depth, block), lambda i: (0, i)),
                  pl.BlockSpec((filters, block), lambda i: (0, i)), pl.BlockSpec((block, filters), lambda i: (i, 0)),
                  full(weight), full(back), full(limit), full(count)],
        out_specs=[pl.BlockSpec((filters, 128), lambda i: (0, 0)), pl.BlockSpec((2 * groups * depth, 128), lambda i: (0, 0))],
        out_shape=[jax.ShapeDtypeStruct((filters, 128), jnp.float32), jax.ShapeDtypeStruct((2 * groups * depth, 128), jnp.float32)],
        scratch_shapes=[pltpu.VMEM(((letters + KW - 1) * depth, block), jnp.bfloat16), pltpu.VMEM(((letters + KW - 1) * depth, block), jnp.float32),
                        pltpu.VMEM((filters, block), jnp.float32)],
        compiler_params=pltpu.CompilerParams(vmem_limit_bytes=48 << 20),
        name="conv_backward",
    )(ids, embed, lse, up, weight, back, limit, count)


MESH = pl.DeviceIdType.MESH

def greet(peers):
    barrier = pltpu.get_barrier_semaphore()
    for peer in peers:
        pl.semaphore_signal(barrier, inc=1, device_id=peer, device_id_type=MESH)
    pl.semaphore_wait(barrier, len(peers))

def greet_all():
    slot, me = lax.axis_index("dp"), lax.axis_index("filt")
    count, parts = lax.axis_size("dp"), lax.axis_size("filt")
    greet([{"dp": slot ^ far, "filt": me ^ near} for far in range(count) for near in range(parts) if far or near])

def remote(source, target, send, recv, peer):
    return pltpu.make_async_remote_copy(
        src_ref=source, dst_ref=target, send_sem=send, recv_sem=recv,
        device_id=peer, device_id_type=MESH)

def comm_call(kernel, out_shape, scratch, ident, *args, name):
    vmem = pl.BlockSpec(memory_space=pltpu.VMEM)
    return pl.pallas_call(
        kernel, out_shape=out_shape, in_specs=[vmem] * len(args), out_specs=jax.tree.map(lambda _: vmem, out_shape),
        scratch_shapes=scratch,
        compiler_params=pltpu.CompilerParams(collective_id=ident, has_side_effects=True, vmem_limit_bytes=40 << 20),
        name=name)(*args)

DMA = pltpu.SemaphoreType.DMA

def scatter_sum(part_ref, inbox, send, recv, me):
    first = remote(part_ref.at[me ^ 3], inbox.at[0], send.at[0], recv.at[0], {"filt": me ^ 1})
    second = remote(part_ref.at[me ^ 1], inbox.at[1], send.at[1], recv.at[1], {"filt": me ^ 1})
    third = remote(inbox.at[3], inbox.at[2], send.at[2], recv.at[2], {"filt": me ^ 2})
    first.start()
    second.start()
    first.wait_recv()
    inbox[3] = (part_ref[me ^ 2].astype(jnp.float32) + inbox[0].astype(jnp.float32)).astype(jnp.bfloat16)
    third.start()
    second.wait_recv()
    total = part_ref[me].astype(jnp.float32) + inbox[1].astype(jnp.float32)
    third.wait_recv()
    total = total + inbox[2].astype(jnp.float32)
    first.wait_send()
    second.wait_send()
    third.wait_send()
    return total

def gather_blocks(low, all_ref, send, recv, me):
    all_ref[me] = low
    far = remote(all_ref.at[me], all_ref.at[me], send.at[0], recv.at[0], {"filt": me ^ 2})
    near = remote(all_ref.at[me], all_ref.at[me], send.at[1], recv.at[1], {"filt": me ^ 1})
    far.start()
    near.start()
    far.wait_recv()
    relay = remote(all_ref.at[me ^ 2], all_ref.at[me ^ 2], send.at[2], recv.at[2], {"filt": me ^ 1})
    relay.start()
    far.wait_send()
    near.wait()
    relay.wait()

def norm(values, gain, shift, eps):
    center = values - jnp.mean(values, axis=-1, keepdims=True)
    scale = lax.rsqrt(jnp.mean(center * center, axis=-1, keepdims=True) + eps)
    unit = center * scale
    return unit * gain + shift, unit, scale

def norm_back(upstream, unit, scale, gain):
    lifted = upstream * gain
    drop = jnp.mean(lifted, axis=-1, keepdims=True)
    lean = jnp.mean(lifted * unit, axis=-1, keepdims=True)
    return scale * (lifted - drop - unit * lean)

def forward_stage(part_ref, base_ref, gain_ref, shift_ref, value_ref, unit_ref, scale_ref, all_ref, inbox, send, recv, eps):
    me = lax.axis_index("filt")
    greet([{"filt": me ^ hop} for hop in (1, 2, 3)])
    total = scatter_sum(part_ref, inbox, send, recv, me) + base_ref[...]
    value, unit, scale = norm(total, gain_ref[...], shift_ref[...], eps)
    value_ref[...] = value
    unit_ref[...] = unit
    scale_ref[...] = scale
    gather_blocks(value.astype(jnp.bfloat16), all_ref, send.at[pl.ds(3, 3)], recv.at[pl.ds(3, 3)], me)

def top_stage(part_ref, base_ref, up_ref, gain_ref, shift_ref, top_ref, down_ref, dgain_ref, dshift_ref, all_ref, inbox, send, recv, eps):
    me = lax.axis_index("filt")
    greet([{"filt": me ^ hop} for hop in (1, 2, 3)])
    total = scatter_sum(part_ref, inbox, send, recv, me) + base_ref[...]
    top, unit, scale = norm(total, gain_ref[...], shift_ref[...], eps)
    top_ref[...] = top.astype(jnp.bfloat16)
    up = up_ref[...].astype(jnp.float32)
    dgain_ref[...] = jnp.sum(up * unit, axis=0, keepdims=True)
    dshift_ref[...] = jnp.sum(up, axis=0, keepdims=True)
    down = norm_back(up, unit, scale, gain_ref[...])
    down_ref[...] = down
    gather_blocks(down.astype(jnp.bfloat16), all_ref, send.at[pl.ds(3, 3)], recv.at[pl.ds(3, 3)], me)

def start_job(kind, source, target, send, recv):
    slot = lax.axis_index("dp")
    ring, side = slot // 2, slot % 2
    if kind == "side":
        moves = [(source.at[:, 1 - side], target, 1)]
    else:
        moves = [(source.at[ring ^ hop], target.at[hop - 1], 2 * hop) for hop in (2, 3, 1)]
    copies = []
    for index, (piece, place, hop) in enumerate(moves):
        copy = remote(piece, place, send.at[index], recv.at[index], {"dp": slot ^ hop})
        copy.start()
        copies.append(copy)
    return copies

def job_hops(kind):
    return (1,) if kind == "side" else (2, 4, 6)

def backward_stage(kinds, part_ref, base_ref, unit_ref, scale_ref, gain_ref, *refs):
    many = len(kinds)
    job_in, refs = refs[:many], refs[many:]
    (down_ref, dgain_ref, dshift_ref, dlow_ref, all_ref), refs = refs[:5], refs[5:]
    job_out, refs = refs[:many], refs[many:]
    inbox, send, recv = refs[:3]
    me = lax.axis_index("filt")
    slot = lax.axis_index("dp")
    hops = sorted({hop for kind in kinds for hop in job_hops(kind)})
    greet([{"filt": me ^ hop} for hop in (1, 2, 3)] + [{"dp": slot ^ hop} for hop in hops])
    copies = []
    for index, kind in enumerate(kinds):
        copies += start_job(kind, job_in[index], job_out[index], refs[3].at[index], refs[4].at[index])
    up = scatter_sum(part_ref, inbox, send, recv, me) + base_ref[...]
    unit = unit_ref[...]
    dgain_ref[...] = jnp.sum(up * unit, axis=0, keepdims=True)
    dshift_ref[...] = jnp.sum(up, axis=0, keepdims=True)
    down = norm_back(up, unit, scale_ref[...], gain_ref[...])
    down_ref[...] = down
    low = down.astype(jnp.bfloat16)
    dlow_ref[...] = jnp.sum(low.astype(jnp.float32), axis=0, keepdims=True)
    gather_blocks(low, all_ref, send.at[pl.ds(3, 3)], recv.at[pl.ds(3, 3)], me)
    for copy in copies:
        copy.wait()

def stage_scratch(block):
    return [pltpu.VMEM((4,) + block, jnp.bfloat16), DMA((6,)), DMA((6,))]

def f32(*shape): return jax.ShapeDtypeStruct(shape, jnp.float32)
def bf16(*shape): return jax.ShapeDtypeStruct(shape, jnp.bfloat16)

def forward_stage_call(part, base, gain, shift, eps, ident):
    parts, rows, cols = part.shape
    return comm_call(functools.partial(forward_stage, eps=eps),
        (f32(rows, cols), f32(rows, cols), f32(rows, 1), bf16(parts, rows, cols)), stage_scratch((rows, cols)), ident,
        part, base, gain, shift, name="forward_stage")

def top_stage_call(part, base, up, gain, shift, eps, ident):
    parts, rows, cols = part.shape
    return comm_call(functools.partial(top_stage, eps=eps),
        (bf16(rows, cols), f32(rows, cols), f32(1, cols), f32(1, cols), bf16(parts, rows, cols)), stage_scratch((rows, cols)), ident,
        part, base, up, gain, shift, name="top_stage")

def backward_stage_call(part, base, unit, scale, gain, ident, kinds=(), jobs=()):
    parts, rows, cols = part.shape
    vmem = pl.BlockSpec(memory_space=pltpu.VMEM)
    hbm = pl.BlockSpec(memory_space=pl.ANY)
    out_shape = [f32(rows, cols), f32(1, cols), f32(1, cols), f32(1, cols), bf16(parts, rows, cols)]
    scratch = stage_scratch((rows, cols))
    for kind, job in zip(kinds, jobs):
        ring = job.shape[0]
        out_shape.append(bf16(ring, *job.shape[2:]) if kind == "side" else bf16(ring - 1, *job.shape[1:]))
    if kinds:
        scratch += [DMA((len(kinds), 3)), DMA((len(kinds), 3))]
    return pl.pallas_call(
        functools.partial(backward_stage, kinds), out_shape=out_shape, in_specs=[vmem] * 5 + [hbm] * len(kinds),
        out_specs=[vmem] * 5 + [hbm] * len(kinds), scratch_shapes=scratch,
        compiler_params=pltpu.CompilerParams(collective_id=ident, has_side_effects=True, vmem_limit_bytes=24 << 20),
        name="backward_stage")(part, base, unit, scale, gain, *jobs)

def gather_channels(own_ref, all_ref, send, recv, *, chunks):
    me = lax.axis_index("filt")
    greet([{"filt": me ^ hop} for hop in (1, 2)])
    rows, cols = own_ref.shape
    size = rows // chunks

    def lanes(index):
        return pl.ds(pl.multiple_of(index * cols, cols), cols)

    far, near, relay = [], [], []
    for chunk in range(chunks):
        span = pl.ds(chunk * size, size)
        copy = remote(own_ref.at[span, :], all_ref.at[span, lanes(me)], send.at[0, chunk], recv.at[0, chunk], {"filt": me ^ 2})
        copy.start()
        far.append(copy)
    for chunk in range(chunks):
        span = pl.ds(chunk * size, size)
        copy = remote(own_ref.at[span, :], all_ref.at[span, lanes(me)], send.at[1, chunk], recv.at[1, chunk], {"filt": me ^ 1})
        copy.start()
        near.append(copy)
    all_ref[:, lanes(me)] = own_ref[...]
    for chunk in range(chunks):
        span = pl.ds(chunk * size, size)
        far[chunk].wait_recv()
        piece = all_ref.at[span, lanes(me ^ 2)]
        copy = remote(piece, piece, send.at[2, chunk], recv.at[2, chunk], {"filt": me ^ 1})
        copy.start()
        relay.append(copy)
    for chunk in range(chunks):
        far[chunk].wait_send()
        near[chunk].wait()
        relay[chunk].wait()

def gather_channels_call(own, parts, ident, chunks=4):
    rows, cols = own.shape
    return comm_call(functools.partial(gather_channels, chunks=chunks), bf16(rows, cols * parts),
        [DMA((3, chunks)), DMA((3, chunks))], ident, own, name="gather_channels")

def scatter_channels(part_ref, base_ref, out_ref, inbox, merged, send, recv, *, chunks):
    me = lax.axis_index("filt")
    greet([{"filt": me ^ hop} for hop in (1, 2)])
    rows, cols = base_ref.shape
    size = rows // chunks

    def lanes(index):
        return pl.ds(pl.multiple_of(index * cols, cols), cols)

    def hop(source, slot, chunk, peer):
        span = pl.ds(chunk * size, size)
        copy = remote(source, inbox.at[slot, span, :], send.at[slot, chunk], recv.at[slot, chunk], {"filt": peer})
        copy.start()
        return copy

    first, second, third = [], [], []
    for chunk in range(chunks):
        span = pl.ds(chunk * size, size)
        first.append(hop(part_ref.at[span, lanes(me ^ 3)], 0, chunk, me ^ 1))
    for chunk in range(chunks):
        span = pl.ds(chunk * size, size)
        second.append(hop(part_ref.at[span, lanes(me ^ 1)], 1, chunk, me ^ 1))
    for chunk in range(chunks):
        span = pl.ds(chunk * size, size)
        first[chunk].wait_recv()
        both = part_ref[span, lanes(me ^ 2)].astype(jnp.float32) + inbox[0, span, :].astype(jnp.float32)
        merged[span, :] = both.astype(jnp.bfloat16)
        third.append(hop(merged.at[span, :], 2, chunk, me ^ 2))
    for chunk in range(chunks):
        span = pl.ds(chunk * size, size)
        second[chunk].wait_recv()
        third[chunk].wait_recv()
        total = part_ref[span, lanes(me)].astype(jnp.float32) + inbox[1, span, :].astype(jnp.float32)
        total = total + inbox[2, span, :].astype(jnp.float32) + base_ref[span, :]
        out_ref[span, :] = total.astype(jnp.bfloat16)
    for copy in first + second + third:
        copy.wait_send()

def scatter_channels_call(part, base, ident, chunks=4):
    rows, cols = base.shape
    return comm_call(functools.partial(scatter_channels, chunks=chunks), bf16(rows, cols),
        [pltpu.VMEM((3, rows, cols), jnp.bfloat16), pltpu.VMEM((rows, cols), jnp.bfloat16), DMA((3, chunks)), DMA((3, chunks))],
        ident, part, base, name="scatter_channels")


class Total:
    def __init__(self, low, inbox, out, send, recv, sides=None, shared=True):
        self.shared, self.third = shared, []
        self.low, self.inbox, self.out, self.sides = low, inbox, out, sides
        self.send, self.recv = send, recv
        self.me, self.slot = lax.axis_index("filt"), lax.axis_index("dp")
        self.count = low.shape[0]
        self.copies = []

    def push(self, source, target, kind, hop, peer):
        copy = remote(source, target, self.send.at[kind, hop - 1], self.recv.at[kind, hop - 1], peer)
        copy.start()
        self.copies.append(copy)
        return copy

    def start(self, value):
        self.low[...] = value.astype(jnp.bfloat16)
        self.first = [
            self.push(self.low.at[self.slot ^ hop], self.inbox.at[hop - 1], 0, hop, {"dp": self.slot ^ hop})
            for hop in range(1, self.count)
        ]

    def combine(self):
        for copy in self.first:
            copy.wait_recv()
        total = self.low[self.slot].astype(jnp.float32)
        for hop in range(1, self.count):
            total = total + self.inbox[hop - 1].astype(jnp.float32)
        if self.sides is None:
            self.out[self.slot] = total.astype(jnp.bfloat16)
            self.spread()
            return
        self.sides[0] = total.astype(jnp.bfloat16)
        self.second = [self.push(self.sides.at[0], self.sides.at[hop], 1, hop, {"filt": self.me ^ hop}) for hop in (1, 2, 3)]

    def across(self):
        for copy in self.second:
            copy.wait_recv()
        left = self.sides[0].astype(jnp.float32) + self.sides[1].astype(jnp.float32)
        right = self.sides[2].astype(jnp.float32) + self.sides[3].astype(jnp.float32)
        total = (left + right).astype(jnp.bfloat16)
        if self.shared:
            self.out[self.slot] = total
            self.spread()
        else:
            self.out[...] = total

    def spread(self):
        piece = self.out.at[self.slot]
        self.third = [self.push(piece, piece, 2, hop, {"dp": self.slot ^ hop}) for hop in range(1, self.count)]

    def finish(self):
        for copy in self.third:
            copy.wait_recv()
        for copy in self.copies:
            copy.wait_send()


def prologue(letters, depth, block, chunks, window, first, chars_ref, table_ref, weight_ref, limit_ref, count_ref, shard_ref,
             acts_ref, lse_ref, embed_ref, all_ref, full_ref, patch_ref, grid_ref,
             zsend, zrecv, local, ysend, yrecv, fsend, frecv):
    words = chars_ref.shape[1]
    filters = weight_ref.shape[0]
    me = lax.axis_index("filt")
    slot = lax.axis_index("dp")
    ring, side = slot // 2, slot % 2
    greet([{"filt": me ^ hop} for hop in (1, 2)] + [{"dp": slot ^ hop} for hop in (1, 2, 4, 6)])
    parts = all_ref.shape[1] // filters
    span = shard_ref.shape[0] // (chunks // 2)

    def spot(chunk):
        return pl.ds((chunk // 2) * span, span), chunk % 2

    own, far = [], []

    def start_chunk(chunk):
        if chunk >= chunks:
            return
        rows, half = spot(chunk)
        source = shard_ref.at[rows, pl.ds(pl.multiple_of(half * filters * parts + me * filters, filters), filters)]
        target = full_ref.at[half, ring, side, rows, :]
        copy = pltpu.make_async_copy(source, target, local.at[chunk])
        copy.start()
        own.append(copy)
        for hop in (2, 1, 3):
            copy = remote(source, target, zsend.at[chunk, hop - 1], zrecv.at[chunk, hop - 1], {"dp": slot ^ (2 * hop)})
            copy.start()
            far.append(copy)

    for chunk in range(window):
        start_chunk(chunk)
    cross = []

    def forward_chunk(chunk):
        rows, half = spot(chunk)
        own[chunk].wait()
        for copy in far[3 * chunk : 3 * chunk + 3]:
            copy.wait_recv()
        start_chunk(chunk + window)
        piece = full_ref.at[half, :, side, rows, :]
        copy = remote(piece, piece, ysend.at[chunk], yrecv.at[chunk], {"dp": slot ^ 1})
        copy.start()
        cross.append(copy)

    lead = KW - 1
    rows = KW * depth
    groups = table_ref.shape[0] // depth
    patch_ref[:, :rows, :] = jnp.zeros((patch_ref.shape[0], rows, block), jnp.bfloat16)
    ones = lax.broadcasted_iota(jnp.int32, (128 - rows, block), 0) == 0
    tail = jnp.where(ones, 1.0, 0.0).astype(jnp.bfloat16)
    patch_ref[:, rows:, :] = jnp.broadcast_to(tail[None], (patch_ref.shape[0],) + tail.shape)
    chunk = grid_ref.shape[1]
    always = letters - KW + 1
    steps = filters // chunk
    polls = {(step // steps, step % steps): step - first for step in range(first, min(first + chunks, words // block * steps))}
    gathers = ChannelGather(acts_ref, all_ref, fsend, frecv, words // block)
    for index in range(words // block):
        cols = pl.ds(index * block, block)

        def embed(position, carry):
            ids = chars_ref[pl.ds(position, 1), cols]
            low = ids & 127
            group = ids >> 7
            onehot = lax.broadcasted_iota(jnp.int32, (128, block), 0) == low
            onehot = jnp.where(onehot, 1.0, 0.0).astype(jnp.bfloat16)
            looked = nn_dot(table_ref[...], onehot)
            row = looked[:depth]
            for part in range(1, groups):
                row = jnp.where(group == part, looked[part * depth : (part + 1) * depth], row)
            row = row.astype(jnp.bfloat16)
            embed_ref[pl.ds(pl.multiple_of(position * depth, depth), depth), cols] = row
            for tap in range(KW):
                patch_ref[position + lead - tap, tap * depth : (tap + 1) * depth, :] = row
            return carry

        lax.fori_loop(0, letters, embed, 0, unroll=5)
        for start in range(0, filters, chunk):
            weight = weight_ref[start : start + chunk, :]
            limit = limit_ref[start : start + chunk, :]

            def product(position, top):
                grid = nn_dot(weight, patch_ref[position + lead])
                grid_ref[position] = grid
                return jnp.maximum(top, grid)

            top = lax.fori_loop(0, always, product, jnp.full((chunk, block), -1e30, jnp.float32), unroll=11)
            for position in range(always, letters):
                grid = nn_dot(weight, patch_ref[position + lead])
                grid = jnp.where(limit >= position, grid, -1e30)
                grid_ref[position] = grid
                top = jnp.maximum(top, grid)

            def total(position, acc):
                return acc + jnp.exp(grid_ref[position] - top)

            acc = lax.fori_loop(0, letters, total, jnp.zeros((chunk, block), jnp.float32), unroll=10)
            lse = top + jnp.log(acc)
            lse_ref[start : start + chunk, cols] = lse
            pooled = lse - count_ref[start : start + chunk, :]
            acts_ref[cols, start : start + chunk] = (pooled * normal_cdf(pooled)).astype(jnp.bfloat16).T
            poll = polls.get((index, start // chunk))
            if poll is not None:
                forward_chunk(poll)
        gathers.send(index)
    for index in range(len(polls), chunks):
        forward_chunk(index)
    for index in range(words // block):
        gathers.relay(index)
    gathers.finish()
    for copy in far:
        copy.wait_send()
    for copy in cross:
        copy.wait()

class ChannelGather:
    def __init__(self, own_ref, all_ref, send, recv, pieces):
        self.me = lax.axis_index("filt")
        self.own, self.all, self.sems = own_ref, all_ref, (send, recv)
        self.size = own_ref.shape[0] // pieces
        self.copies = []

    def view(self, index, piece):
        cols = self.own.shape[1]
        return self.all.at[pl.ds(piece * self.size, self.size), pl.ds(pl.multiple_of(index * cols, cols), cols)]

    def push(self, source, target, kind, piece, hop):
        send, recv = self.sems
        copy = remote(source, target, send.at[kind, piece], recv.at[kind, piece], {"filt": self.me ^ hop})
        copy.start()
        self.copies.append(copy)
        return copy

    def send(self, piece):
        source = self.own.at[pl.ds(piece * self.size, self.size), :]
        target = self.view(self.me, piece)
        self.push(source, target, 0, piece, 2)
        self.push(source, target, 1, piece, 1)
        cols = self.own.shape[1]
        self.all[pl.ds(piece * self.size, self.size), pl.ds(pl.multiple_of(self.me * cols, cols), cols)] = self.own[pl.ds(piece * self.size, self.size), :]

    def relay(self, piece):
        self.copies[2 * piece].wait_recv()
        view = self.view(self.me ^ 2, piece)
        self.push(view, view, 2, piece, 1)

    def finish(self):
        for index, copy in enumerate(self.copies):
            copy.wait_send()
            if index % 2 == 1 or index >= 2 * (len(self.copies) // 3):
                copy.wait_recv()

def prologue_call(ids, table, weight, limit, count, shard, parts, letters, depth, ident, block=256, chunks=8, window=2, first=2):
    words = ids.shape[1]
    filters = weight.shape[0]
    rows = shard.shape[0]
    vmem = pl.BlockSpec(memory_space=pltpu.VMEM)
    hbm = pl.BlockSpec(memory_space=pl.ANY)
    pieces = words // block
    return pl.pallas_call(
        functools.partial(prologue, letters, depth, block, chunks, window, first),
        in_specs=[vmem] * 5 + [hbm],
        out_specs=[vmem] * 4 + [hbm],
        out_shape=[bf16(words, filters), f32(filters, words), bf16(letters * depth, words), bf16(words, filters * parts),
                   bf16(2, 4, 2, rows, filters)],
        scratch_shapes=[pltpu.VMEM((letters + KW - 1, 128, block), jnp.bfloat16), pltpu.VMEM((letters, 128, block), jnp.float32),
                        DMA((chunks, 3)), DMA((chunks, 3)), DMA((chunks,)), DMA((chunks,)), DMA((chunks,)), DMA((3, pieces)), DMA((3, pieces))],
        compiler_params=pltpu.CompilerParams(collective_id=ident, has_side_effects=True, vmem_limit_bytes=48 << 20),
        name="prologue",
    )(ids, table, weight, limit, count, shard)


def sigmoid(values):
    return 1.0 / (1.0 + jnp.exp(-values))


def highway_stage(eps, slim_ref, feats_ref, wide_ref, bias_ref, acts_ref, base_ref, gain_ref, shift_ref,
                  gates_ref, hidden_ref, proj_ref, out_ref, value_ref, unit_ref, scale_ref, all_ref,
                  abox, part_ref, inbox, send, recv, asend, arecv):
    me = lax.axis_index("filt")
    greet([{"filt": me ^ hop} for hop in (1, 2, 3)])
    parts, sides, rows, dmodel = abox.shape
    copies = []
    size, small = proj_ref.shape[0] // (sides * parts), out_ref.shape[0] // (sides * (parts - 1))
    for index, span in enumerate((pl.ds(0, size), pl.ds(size, rows - size))):
        for hop in (2, 3, 1):
            source = slim_ref.at[pl.ds(sides * (me ^ hop), sides), span, :]
            copy = remote(source, abox.at[me, :, span, :], asend.at[index, hop - 1], arecv.at[index, hop - 1], {"filt": me ^ hop})
            copy.start()
            copies.append(copy)
    own = pltpu.make_async_copy(slim_ref.at[pl.ds(sides * me, sides), pl.ds(0, rows), :], abox.at[me], asend.at[0, 3])
    own.start()
    words, filters = acts_ref.shape
    block = 256

    def mix(index, carry):
        span = pl.ds(pl.multiple_of(index * block, block), block)
        feats = feats_ref[span, :]
        turn = nn_dot(feats, wide_ref[0]) + bias_ref[:, :filters]
        gates_ref[span, :filters] = turn
        gate = nn_dot(feats, wide_ref[1]) + bias_ref[:, filters:]
        gates_ref[span, filters:] = gate
        keep = sigmoid(gate)
        mixed = keep * acts_ref[span, :].astype(jnp.float32) + (1.0 - keep) * (turn * normal_cdf(turn))
        hidden_ref[span, :] = mixed.astype(jnp.bfloat16)
        return carry

    lax.fori_loop(0, words // block, mix, 0)
    own.wait()
    for copy in copies[:3]:
        copy.wait()
    width = dmodel // parts
    for part in range(parts):
        cols = slice(part * width, (part + 1) * width)
        for side in range(sides):
            for group in range(parts):
                lanes = slice(group * width, (group + 1) * width)
                start = (side * parts + group) * size
                proj_ref[start : start + size, cols] = abox[part, side, :size, lanes]

    def project(index, carry):
        span = pl.ds(pl.multiple_of(index * 128, 128), 128)
        part_ref[index] = nn_dot(hidden_ref[span, :], proj_ref[...]).astype(jnp.bfloat16)
        return carry

    lax.fori_loop(0, parts, project, 0)
    total = scatter_sum(part_ref, inbox, send, recv, me) + base_ref[...]
    value, unit, scale = norm(total, gain_ref[...], shift_ref[...], eps)
    value_ref[...] = value
    unit_ref[...] = unit
    scale_ref[...] = scale
    gather_blocks(value.astype(jnp.bfloat16), all_ref, send.at[pl.ds(3, 3)], recv.at[pl.ds(3, 3)], me)
    for copy in copies[3:]:
        copy.wait()
    for part in range(parts):
        cols = slice(part * width, (part + 1) * width)
        for side in range(sides):
            for group in range(parts - 1):
                start = (side * (parts - 1) + group) * small
                out_ref[start : start + small, cols] = abox[part, side, size:, group * width : (group + 1) * width]


def highway_stage_call(slim, feats, wide, bias, acts, base, gain, shift, out_rows, po_rows, eps, ident):
    words, filters = acts.shape
    rows, dmodel = base.shape
    parts = words // rows
    vmem = pl.BlockSpec(memory_space=pltpu.VMEM)
    hbm = pl.BlockSpec(memory_space=pl.ANY)
    return pl.pallas_call(
        functools.partial(highway_stage, eps), in_specs=[hbm] + [vmem] * 7, out_specs=[vmem] * 8,
        out_shape=[f32(words, 2 * filters), bf16(words, filters), bf16(filters, dmodel), bf16(out_rows, dmodel), f32(rows, dmodel),
                   f32(rows, dmodel), f32(rows, 1), bf16(parts, rows, dmodel)],
        scratch_shapes=[pltpu.VMEM((parts, 2, po_rows, dmodel), jnp.bfloat16), pltpu.VMEM((parts, rows, dmodel), jnp.bfloat16)]
        + stage_scratch((rows, dmodel)) + [DMA((2, 4)), DMA((2, 3))],
        compiler_params=pltpu.CompilerParams(collective_id=ident, has_side_effects=True, vmem_limit_bytes=48 << 20),
        name="highway_stage",
    )(slim, feats, wide, bias, acts, base, gain, shift)


class RowReduce:
    def __init__(self, grad, yin, pair, zin, joined, span, sems, base=0):
        self.base, self.ready = base, []
        self.grad, self.yin, self.pair, self.zin, self.joined = grad, yin, pair, zin, joined
        self.span, self.sems = span, sems
        self.me, self.slot = lax.axis_index("filt"), lax.axis_index("dp")
        self.ring, self.side = self.slot // 2, self.slot % 2
        self.copies = []

    def push(self, source, target, index, peer):
        send, recv = self.sems
        copy = remote(source, target, send.at[index], recv.at[index], peer)
        copy.start()
        self.copies.append(copy)
        return copy

    def across(self):
        span = self.span
        for copy in self.ready:
            copy.wait_recv()
        self.first = self.push(
            self.grad.at[:, 1 - self.side, span, :], self.yin.at[:, span, :], 0, {"dp": self.slot ^ 1}
        )

    def along(self):
        span = self.span
        self.first.wait_recv()
        both = self.grad[:, self.side, span, :].astype(jnp.float32) + self.yin[:, span, :].astype(jnp.float32)
        self.pair[:, span, :] = both.astype(jnp.bfloat16)
        self.ring_out()

    def local(self):
        return pl.ds(self.span.start - self.base, self.span.size)

    def ring_out(self):
        span = self.local()
        self.rest = [
            self.push(self.pair.at[self.ring ^ hop, span, :], self.zin.at[hop - 1, span, :], hop, {"dp": self.slot ^ (2 * hop)})
            for hop in (2, 3, 1)
        ]

    def join(self):
        span = self.local()
        for copy in self.rest:
            copy.wait_recv()
        total = self.pair[self.ring, span, :].astype(jnp.float32)
        for hop in (1, 2, 3):
            total = total + self.zin[hop - 1, span, :].astype(jnp.float32)
        self.joined[self.me, self.span, :] = total.astype(jnp.bfloat16)
        self.share()

    def share(self):
        piece = self.joined.at[self.me, self.span, :]
        self.far = self.push(piece, piece, 4, {"filt": self.me ^ 2})
        self.near = self.push(piece, piece, 5, {"filt": self.me ^ 1})

    def relay(self):
        self.far.wait_recv()
        piece = self.joined.at[self.me ^ 2, self.span, :]
        self.last = self.push(piece, piece, 6, {"filt": self.me ^ 1})

    def finish(self):
        self.near.wait_recv()
        self.last.wait_recv()
        for copy in self.copies:
            copy.wait_send()


def epilogue(letters, depth, block, *refs):
    (dproj_ref, proj_ref, hidden_ref, gates_ref, acts_ref, feats_ref, high_ref, attended_ref, dmixed_ref, chars_ref, embed_ref, lse_ref, weight_ref, back_ref, limit_ref, count_ref, slim_ref,
     ffn_ref, pair_ref, pos_ref, few_ref,
     wide_out, slim_out, rows_out, ffn_out, conv_out, table_out, pos_out, few_out,
     bias_ref, part_ref, base_ref, dgates_ref, wide_ref, cross_ref, inbox, merged, up_ref, patch_ref, down_ref, pull_ref, wgrad_ref, tgrad_ref, wide_y, wide_p, wide_z, slim_y, slim_p, slim_z,
     rows_ref, rows_y, rows_p, rows_z, late_z, conv_low, conv_in, table_low, table_in, table_side, pos_low, pos_in, few_low, few_in, few_side,
     csend, crecv, rsend, rrecv, tsend, trecv, asend, arecv) = refs
    me = lax.axis_index("filt")
    greet_all()
    pos = Total(pos_low, pos_in, pos_out, tsend.at[0], trecv.at[0])
    few = Total(few_low, few_in, few_out, tsend.at[1], trecv.at[1], few_side, False)
    conv_total = Total(conv_low, conv_in, conv_out, tsend.at[2], trecv.at[2])
    table_total = Total(table_low, table_in, table_out, tsend.at[3], trecv.at[3], table_side)
    wide_rows = wide_out.shape[1] // 4
    slim = RowReduce(slim_ref, slim_y, slim_p, slim_z, slim_out, pl.ds(0, slim_out.shape[1]), (rsend.at[4], rrecv.at[4]))
    both = RowReduce(rows_ref, rows_y, rows_p, rows_z, rows_out, pl.ds(0, rows_out.shape[1]), (rsend.at[6], rrecv.at[6]))
    wide = [
        RowReduce(wide_ref, wide_y, wide_p, wide_z, wide_out, pl.ds(index * wide_rows, wide_rows), (rsend.at[index], rrecv.at[index]))
        for index in range(4)
    ]
    early = ffn_ref.shape[0]
    ffn = RowReduce(None, None, None, None, ffn_out, pl.ds(0, early), (rsend.at[5], rrecv.at[5]))
    late = RowReduce(None, None, pair_ref, late_z, ffn_out, pl.ds(early, pair_ref.shape[1]), (rsend.at[7], rrecv.at[7]), early)
    swaps = [
        remote(cross_ref.at[me ^ hop], rows_ref.at[me], asend.at[hop - 1], arecv.at[hop - 1], {"filt": me ^ hop}) for hop in (2, 3, 1)
    ]
    both.ready = swaps
    pos.start(pos_ref[...])
    slim.across()
    ffn_out[me, :early, :] = ffn_ref[...]
    late.ring_out()
    highway_mix_back(dproj_ref, proj_ref, hidden_ref, gates_ref, acts_ref, base_ref, dgates_ref, bias_ref)
    highway_grads(feats_ref, dgates_ref, wide_ref)
    wide[0].across()
    extra = few_ref[...]
    place, row = lax.broadcasted_iota(jnp.int32, extra.shape, 0), lax.broadcasted_iota(jnp.int32, extra.shape, 1)
    lanes = extra.shape[2]
    extra = jnp.where((row == 0) & (place == me), bias_ref[:, :lanes][None], extra)
    extra = jnp.where((row == 0) & (place == me + 4), bias_ref[:, lanes:][None], extra)
    few.start(extra)
    highway_down(dgates_ref, high_ref, part_ref)
    scatter = ChannelScatter(part_ref, base_ref, up_ref, inbox, merged, csend, crecv)
    scatter.begin()
    row_grads(hidden_ref, dproj_ref, attended_ref, dmixed_ref, cross_ref)
    rows_ref[me] = cross_ref[me]
    wide[1].across()
    slim.along()
    scatter.finish()
    wide[2].across()
    wide[0].along()
    pos.combine()
    few.combine()
    for copy in swaps:
        copy.start()
    ffn.share()
    steps = iter([
        [wide[3].across, wide[1].along], [slim.join], [both.across], [wide[2].along, wide[0].join, late.join],
        [slim.relay, ffn.relay, wide[0].relay, wide[1].join], [late.relay, few.across, wide[3].along], [wide[1].relay, wide[2].join],
        [wide[2].relay], [], [],
    ])

    def advance():
        for step in next(steps):
            step()

    filters = weight_ref.shape[0]
    rows = KW * depth
    groups = tgrad_ref.shape[0] // (2 * depth)
    wgrad_ref[...] = jnp.zeros(wgrad_ref.shape, jnp.float32)
    tgrad_ref[...] = jnp.zeros(tgrad_ref.shape, jnp.float32)
    patch_ref[letters * depth :, :] = jnp.zeros((patch_ref.shape[0] - letters * depth, block), jnp.bfloat16)
    ones = jnp.where(lax.broadcasted_iota(jnp.int32, (128 - rows, block), 0) == 0, 1.0, 0.0).astype(jnp.bfloat16)
    always = letters - KW + 1
    quarter = always // 4
    for index in range(chars_ref.shape[1] // block):
        cols = pl.ds(index * block, block)
        patch_ref[: letters * depth, :] = embed_ref[:, cols]
        down_ref[...] = jnp.zeros(down_ref.shape, jnp.float32)
        pooled = lse_ref[:, cols] - count_ref[...]
        slope = normal_cdf(pooled) + pooled * (DENSITY * jnp.exp(-0.5 * pooled * pooled))
        pull_ref[...] = slope * up_ref[cols, :].T.astype(jnp.float32)

        def one(position, masked):
            start = position * depth
            if not isinstance(position, int):
                start = pl.multiple_of(start, depth)
            patch = jnp.concatenate([patch_ref[pl.ds(start, rows), :], ones], axis=0)
            grid = nn_dot(weight_ref[...], patch)
            spread = jnp.exp(grid - lse_ref[:, cols]) * pull_ref[...]
            if masked:
                spread = jnp.where(limit_ref[...] >= position, spread, 0.0)
            spread = spread.astype(jnp.bfloat16)
            down = nn_dot(back_ref[...], spread)
            down_ref[pl.ds(start, rows), :] += down[:rows]
            wgrad_ref[...] += nt_dot(spread, patch)

        def body(position, carry):
            one(position, False)
            return carry

        for lap in range(4):
            stop = always if lap == 3 else (lap + 1) * quarter
            lax.fori_loop(lap * quarter, stop, body, 0, unroll=11)
            advance()
        for position in range(always, letters):
            one(position, True)

        def table(position, carry):
            ids = chars_ref[pl.ds(position, 1), cols]
            low = ids & 127
            group = ids >> 7
            onehot = lax.broadcasted_iota(jnp.int32, (128, block), 0) == low
            onehot = jnp.where(onehot, 1.0, 0.0).astype(jnp.bfloat16)
            down = down_ref[pl.ds(pl.multiple_of(position * depth, depth), depth), :]
            high = down.astype(jnp.bfloat16)
            rest = (down - high.astype(jnp.float32)).astype(jnp.bfloat16)
            zero = jnp.zeros_like(high)
            parts = [jnp.where(group == part, item, zero) for item in (high, rest) for part in range(groups)]
            tgrad_ref[...] += nt_dot(jnp.concatenate(parts, axis=0), onehot)
            return carry

        lax.fori_loop(0, letters, table, 0, unroll=5)
        advance()
    table_rows = tgrad_ref.shape[0] // 2
    slices, size = table_low.shape[:2]
    conv_total.start(wgrad_ref[...].reshape(conv_low.shape))
    sums = tgrad_ref[:table_rows, :] + tgrad_ref[table_rows:, :]
    sums = jnp.concatenate([sums, jnp.zeros((slices * size - table_rows, sums.shape[1]), jnp.float32)], axis=0)
    table_total.start(sums.reshape(table_low.shape))
    for step in (
        both.along, wide[3].join, table_total.combine, conv_total.combine, wide[3].relay, table_total.across, both.join, both.relay,
    ):
        step()
    for copy in swaps:
        copy.wait_send()
    for item in [ffn, late, slim, both, pos, few, conv_total, table_total] + wide:
        item.finish()


class ChannelScatter:
    def __init__(self, part_ref, base_ref, out_ref, inbox, merged, send, recv):
        self.part, self.base, self.out, self.inbox, self.merged = part_ref, base_ref, out_ref, inbox, merged
        self.sems = (send, recv)
        self.me = lax.axis_index("filt")

    def begin(self):
        me = self.me
        rows, cols = self.base.shape
        pieces = self.sems[0].shape[1]
        size = rows // pieces

        def lanes(index):
            return pl.ds(pl.multiple_of(index * cols, cols), cols)

        def hop(source, kind, piece, peer):
            span = pl.ds(piece * size, size)
            send, recv = self.sems
            copy = remote(source, self.inbox.at[kind, span, :], send.at[kind, piece], recv.at[kind, piece], {"filt": peer})
            copy.start()
            return copy

        self.lanes, self.hop = lanes, hop
        self.spans = spans = [pl.ds(piece * size, size) for piece in range(pieces)]
        first = [hop(self.part.at[span, lanes(me ^ 3)], 0, piece, me ^ 1) for piece, span in enumerate(spans)]
        second = [hop(self.part.at[span, lanes(me ^ 1)], 1, piece, me ^ 1) for piece, span in enumerate(spans)]
        self.first, self.second = first, second

    def finish(self):
        me, lanes, hop, first, second, spans = self.me, self.lanes, self.hop, self.first, self.second, self.spans
        third = []
        for piece, span in enumerate(spans):
            first[piece].wait_recv()
            both = self.part[span, lanes(me ^ 2)].astype(jnp.float32) + self.inbox[0, span, :].astype(jnp.float32)
            self.merged[span, :] = both.astype(jnp.bfloat16)
            third.append(hop(self.merged.at[span, :], 2, piece, me ^ 2))
        for piece, span in enumerate(spans):
            second[piece].wait_recv()
            third[piece].wait_recv()
            total = self.part[span, lanes(me)].astype(jnp.float32) + self.inbox[1, span, :].astype(jnp.float32)
            total = total + self.inbox[2, span, :].astype(jnp.float32) + self.base[span, :]
            self.out[span, :] = total.astype(jnp.bfloat16)
        for copy in first + second + third:
            copy.wait_send()


def highway_mix_back(dproj_ref, proj_ref, hidden_ref, gates_ref, acts_ref, din_ref, dgates_ref, bias_ref):
    words, filters = acts_ref.shape
    block = 128
    bias_ref[...] = jnp.zeros(bias_ref.shape, jnp.float32)

    def mix(index, carry):
        span = pl.ds(pl.multiple_of(index * block, block), block)
        dhidden = nt_dot(dproj_ref[span, :], proj_ref[...])
        turn = gates_ref[span, :filters]
        keep = sigmoid(gates_ref[span, filters:])
        below = normal_cdf(turn)
        slope = below + turn * (DENSITY * jnp.exp(-0.5 * turn * turn))
        fresh = dhidden * (1.0 - keep)
        din_ref[span, :] = dhidden * keep
        dturn = (fresh * slope).astype(jnp.bfloat16)
        dkeep = (fresh * keep * (acts_ref[span, :].astype(jnp.float32) - turn * below)).astype(jnp.bfloat16)
        dgates_ref[span, :filters] = dturn
        dgates_ref[span, filters:] = dkeep
        bias_ref[:, :filters] += jnp.sum(dturn.astype(jnp.float32), axis=0, keepdims=True)
        bias_ref[:, filters:] += jnp.sum(dkeep.astype(jnp.float32), axis=0, keepdims=True)
        return carry

    lax.fori_loop(0, words // block, mix, 0)


def highway_grads(feats_ref, dgates_ref, grad_ref):
    rings, sides, rows, cols = grad_ref.shape
    piece = sides * rows

    def grads(index, carry):
        lanes = pl.ds(pl.multiple_of(index * piece, piece), piece)
        grad = tn_dot(feats_ref[:, lanes], dgates_ref[...]).astype(jnp.bfloat16)
        grad_ref[index] = grad.reshape(sides, rows, cols)
        return carry

    lax.fori_loop(0, rings, grads, 0)


def highway_down(dgates_ref, high_ref, part_ref):
    filters = high_ref.shape[2]
    piece = 512

    def down(index, carry):
        lanes = pl.ds(pl.multiple_of(index * piece, piece), piece)
        both = nt_dot(dgates_ref[:, :filters], high_ref[0, lanes, :]) + nt_dot(dgates_ref[:, filters:], high_ref[1, lanes, :])
        part_ref[:, lanes] = both.astype(jnp.bfloat16)
        return carry

    lax.fori_loop(0, part_ref.shape[1] // piece, down, 0)


def row_grads(hidden_ref, dproj_ref, attended_ref, dmixed_ref, both_ref):
    parts, sides, rows, dmodel = both_ref.shape
    width = dmodel // parts
    gproj = tn_dot(hidden_ref[...], dproj_ref[...]).astype(jnp.bfloat16)
    gout = tn_dot(attended_ref[...], dmixed_ref[...]).astype(jnp.bfloat16)
    size, small = gproj.shape[0] // (sides * parts), gout.shape[0] // (sides * (parts - 1))
    for part in range(parts):
        cols = slice(part * width, (part + 1) * width)
        for side in range(sides):
            for group in range(parts):
                lanes = slice(group * width, (group + 1) * width)
                start = (side * parts + group) * size
                both_ref[part, side, :size, lanes] = gproj[start : start + size, cols]
                if group < parts - 1:
                    start = (side * (parts - 1) + group) * small
                    both_ref[part, side, size:, lanes] = gout[start : start + small, cols]
                else:
                    both_ref[part, side, size:, lanes] = jnp.zeros((rows - size, width), jnp.bfloat16)


def epilogue_call(dproj, proj, hidden, gates, acts, feats, high, attended, dmixed, ids, embed, lse, weight, back, limit, count,
                  slim, ffn, pair, pos, few, po_rows, letters, depth, groups, ident, block=256):
    filters, words = lse.shape
    args = (dproj, proj, hidden, gates, acts, feats, high, attended, dmixed, ids, embed, lse, weight, back, limit, count,
            slim, ffn, pair, pos, few)
    channels, dmodel = feats.shape[1], dproj.shape[1]
    parts = channels // filters
    slices = pos.shape[0]
    pieces = 4
    vmem = pl.BlockSpec(memory_space=pltpu.VMEM)
    table_size = -(-(-(-groups * depth // slices)) // 8) * 8
    wide_shape = (slices // 2, 2, channels // slices, 2 * filters)
    both_shape = (slices // 2, 2, po_rows, dmodel)

    def space(shape, dtype=jnp.bfloat16):
        return pltpu.VMEM(tuple(shape), dtype)

    def stages(shape):
        ring, side, rows, cols = shape
        return [space((ring, rows, cols)), space((ring, rows, cols)), space((ring - 1, rows, cols))]

    def totals(shape, sides):
        spaces = [space(shape), space((shape[0] - 1,) + shape[1:])]
        return spaces + ([space((4,) + shape[1:])] if sides else [])

    conv_shape = (slices, filters // slices, 128)
    table_shape = (slices, table_size, 128)
    out_shape = [bf16(parts, *wide_shape[2:]), bf16(parts, *slim.shape[2:]), bf16(parts, *both_shape[2:]),
                 bf16(parts, ffn.shape[0] + pair.shape[1], ffn.shape[1]), bf16(*conv_shape), bf16(*table_shape), bf16(*pos.shape),
                 bf16(*few.shape[1:])]
    padded = (letters + KW - 1) * depth
    return pl.pallas_call(
        functools.partial(epilogue, letters, depth, block),
        in_specs=[vmem] * len(args),
        out_specs=[vmem] * len(out_shape),
        out_shape=out_shape,
        scratch_shapes=[space((1, 2 * filters), jnp.float32), space((words, channels)), space((words, filters), jnp.float32), space((words, 2 * filters)), space(wide_shape),
                        space(both_shape), space((3, words, filters)), space((words, filters)), space((words, filters)), space((padded, block)),
                        space((padded, block), jnp.float32), space((filters, block), jnp.float32),
                        space((filters, 128), jnp.float32), space((2 * groups * depth, 128), jnp.float32)]
        + stages(wide_shape) + stages(slim.shape) + [space(both_shape)] + stages(both_shape) + [space((3,) + pair.shape[1:])]
        + totals(conv_shape, False) + totals(table_shape, True) + totals(pos.shape, False) + totals(few.shape, True)
        + [DMA((3, pieces)), DMA((3, pieces)), DMA((8, 7)), DMA((8, 7)), DMA((4, 3, slices - 1)), DMA((4, 3, slices - 1)),
           DMA((3,)), DMA((3,))],
        compiler_params=pltpu.CompilerParams(collective_id=ident, has_side_effects=True, vmem_limit_bytes=60 << 20),
        name="epilogue",
    )(*args)


def assemble(depth, wide_ref, slim_ref, both_ref, ffn_ref, conv_ref, table_ref, pos_ref, few_ref, limit_ref,
             wide_out, slim_out, proj_out, out_out, inner_out, outer_out, conv_out, cbias_out, table_out, pos_out,
             hbias_out, pbias_out, gain_out, shift_out, ibias_out):
    parts = wide_ref.shape[0]
    inner_rows = inner_out.shape[0]
    proj_rows, out_rows = proj_out.shape[0] // parts, out_out.shape[0] // (parts - 1)
    filters = wide_ref.shape[2] // 2
    width = slim_ref.shape[2] // 3
    for part in range(parts):
        for half in range(2):
            start = (half * parts + part) * filters
            wide_out[:, start : start + filters] = wide_ref[part, :, half * filters : (half + 1) * filters].astype(jnp.float32)
        for block in range(3):
            start = (block * parts + part) * width
            slim_out[:, start : start + width] = slim_ref[part, :, block * width : (block + 1) * width].astype(jnp.float32)
        cols = slice(part * width, (part + 1) * width)
        for block in range(parts):
            lanes = slice(block * width, (block + 1) * width)
            proj_out[block * proj_rows : (block + 1) * proj_rows, cols] = both_ref[part, :proj_rows, lanes].astype(jnp.float32)
            if block < parts - 1:
                out_out[block * out_rows : (block + 1) * out_rows, cols] = both_ref[part, proj_rows:, lanes].astype(jnp.float32)
        units = ffn_ref.shape[1] - inner_rows
        outer_out[part * units : (part + 1) * units, :] = ffn_ref[part, inner_rows:, :].astype(jnp.float32)
        for block in range(inner_out.shape[1] // (parts * units)):
            start = (block * parts + part) * units
            inner_out[:, start : start + units] = ffn_ref[part, :inner_rows, block * units : (block + 1) * units].astype(jnp.float32)
    slices, conv_rows = conv_ref.shape[:2]
    taps = conv_out.shape[0]
    turned = conv_ref[...].reshape(slices * conv_rows, 128).astype(jnp.float32).T
    tap = lax.broadcasted_iota(jnp.int32, (taps, 1), 0) // depth
    conv_out[...] = jnp.where(tap < limit_ref[...], turned[:taps], 0.0)
    cbias_out[...] = turned[taps : taps + 1]
    table = table_ref[...].reshape(-1, 128).astype(jnp.float32)
    vocab = table_out.shape[0]
    for group in range(-(-vocab // 128)):
        stop = min(128, vocab - group * 128)
        table_out[group * 128 : group * 128 + stop, :] = table[group * depth : (group + 1) * depth].T[:stop]
    pos_out[...] = pos_ref[...].reshape(pos_out.shape).astype(jnp.float32)
    own = few_ref[...].astype(jnp.float32)
    size = gain_out.shape[1]
    hbias_out[...] = own[0:1, : hbias_out.shape[1]]
    pbias_out[...] = own[1:2, : pbias_out.shape[1]]
    gain_out[...] = own[2:5, :size]
    shift_out[...] = own[5:8, :size]
    ibias_out[...] = own[8:9, : ibias_out.shape[1]]


def assemble_call(wide, slim, both, ffn, conv, table, pos, few, widths, inner_rows, out_rows, taps, vocab, depth, sizes):
    args = (wide, slim, both, ffn, conv, table, pos, few, widths)
    parts = wide.shape[0]

    def whole(shape):
        return pl.BlockSpec(shape, lambda step: (0,) * len(shape))

    units = ffn.shape[1] - inner_rows
    dmodel = both.shape[2]
    hb, pb, nd, ib = sizes
    proj_rows = both.shape[1] - out_rows // (parts - 1)
    out_shape = [f32(wide.shape[1], wide.shape[2] * parts), f32(slim.shape[1], slim.shape[2] * parts),
                 f32(proj_rows * parts, dmodel), f32(out_rows, dmodel), f32(inner_rows, dmodel * parts), f32(units * parts, dmodel),
                 f32(taps, widths.shape[1]), f32(1, widths.shape[1]), f32(vocab, depth), f32(pos.shape[0] * pos.shape[1], pos.shape[2]),
                 f32(1, hb), f32(1, pb), f32(3, nd), f32(3, nd), f32(1, ib)]
    return pl.pallas_call(
        functools.partial(assemble, depth), grid=(1,), in_specs=[whole(item.shape) for item in args],
        out_specs=[whole(item.shape) for item in out_shape], out_shape=out_shape,
        compiler_params=pltpu.CompilerParams(vmem_limit_bytes=56 << 20), name="assemble",
    )(*args)


def exact_gaussian_activation(values):
    return values * normal_cdf(values)


def gelu_back(values, upstream):
    density = DENSITY * jnp.exp(-0.5 * values * values)
    return upstream * (normal_cdf(values) + values * density)


def channel_widths(channels):
    widths = jnp.ones_like(channels)
    for power in range(6):
        widths = widths + (channels >= NF * 2**power // 64).astype(jnp.int32)
    return widths


def highway_mix(hidden, gates):
    width = hidden.shape[1]
    carry_gate = jax.nn.sigmoid(gates[:, width:])
    return carry_gate * hidden + (1.0 - carry_gate) * exact_gaussian_activation(gates[:, :width])


def swap(array, axis, bit):
    size = lax.axis_size(axis)
    return lax.ppermute(array, axis, [(index, index ^ bit) for index in range(size)])


def reduce_rows(array):
    count = lax.axis_size("dp")
    slot = lax.axis_index("dp")
    bits = count.bit_length() - 1
    rows, cols = array.shape
    if count != 1 << bits:
        return lax.psum_scatter(array.astype(jnp.bfloat16), "dp", scatter_dimension=0, tiled=True)
    array = array.reshape((2,) * bits + (rows // count, cols))
    for bit in range(bits):
        axis = bits - 1 - bit
        mine = (slot >> bit) & 1
        keep = lax.dynamic_index_in_dim(array, mine, axis, keepdims=False)
        give = lax.dynamic_index_in_dim(array, 1 - mine, axis, keepdims=False)
        got = swap(give.astype(jnp.bfloat16), "dp", 1 << bit)
        array = (keep.astype(jnp.float32) + got.astype(jnp.float32)).astype(jnp.bfloat16)
    return array


def join_parts(array):
    part = lax.axis_index("filt")
    low = (part & 1) == 1
    high = (part >> 1) == 1
    far = swap(array, "filt", 2)
    near = swap(array, "filt", 1)
    both = swap(far, "filt", 1)
    here = (jnp.where(low, near, array), jnp.where(low, array, near))
    there = (jnp.where(low, both, far), jnp.where(low, far, both))
    first = [jnp.where(high, b, a) for a, b in zip(here, there)]
    second = [jnp.where(high, a, b) for a, b in zip(here, there)]
    return first + second


def per_device(
    chars,
    lengths,
    char_table,
    conv_weight,
    conv_bias,
    highway_weight,
    highway_bias,
    proj_weight,
    proj_bias,
    position,
    norm_gain,
    norm_bias,
    query_key_value_weight,
    attention_output_weight,
    feedforward_input_weight,
    feedforward_input_bias,
    feedforward_output_weight,
    cotangent,
):
    parts = lax.axis_size("filt")
    slices = lax.axis_size("dp")
    part = lax.axis_index("filt")
    slot = lax.axis_index("dp")
    seqs, quarter, dmodel = cotangent.shape
    full_len = chars.shape[1]
    letters = chars.shape[2]
    words = seqs * full_len
    tokens = seqs * quarter
    filters = conv_weight.shape[1]
    depth = char_table.shape[1]
    heads = dmodel // HD // parts
    width = heads * HD
    inner_rows = feedforward_input_weight.shape[0]
    unit_rows = feedforward_output_weight.shape[0] // parts

    def own_columns(array, blocks):
        rows = array.shape[0]
        split = array.reshape(rows, blocks, parts, -1)
        return lax.dynamic_index_in_dim(split, part, 2, keepdims=False).reshape(rows, -1)

    def gather_rows(array):
        return lax.all_gather(array, "dp", axis=0, tiled=True)

    def groups_of(array, groups):
        array = array.reshape(groups, -1, width).transpose(1, 0, 2).reshape(-1, groups * width)
        return jnp.pad(array, ((0, 0), (0, dmodel - groups * width)))

    def rows_from_columns(both):
        both = lax.all_to_all(both.reshape(parts, -1, dmodel), "filt", split_axis=0, concat_axis=0, tiled=True)
        both = both.reshape(parts, slices // parts, po_rows, parts, width)
        both = [both[:, :, :split], both[:, :, split:, : parts - 1]]
        return [item.transpose(1, 3, 2, 0, 4).reshape(-1, dmodel) for item in both]

    def columns_from_rows(*grads):
        items = []
        for item, groups in zip(grads, (parts, parts - 1)):
            item = item.astype(jnp.bfloat16).reshape(slices // parts, groups, -1, parts, width)
            item = item.transpose(3, 0, 2, 1, 4).reshape(parts, slices // parts, -1, groups * width)
            items.append(jnp.pad(item, ((0, 0), (0, 0), (0, 0), (0, dmodel - groups * width))))
        both = jnp.concatenate(items, axis=2)
        both = lax.all_to_all(both.reshape(parts, -1, dmodel), "filt", split_axis=0, concat_axis=0, tiled=True)
        return both.reshape(slices * po_rows, dmodel)

    fast = slices == 8 and parts == 4
    hb, pb, nd = highway_bias.shape[1], proj_bias.shape[0], norm_gain.shape[1]
    small = jnp.concatenate(
        [
            highway_bias.reshape(-1),
            proj_bias,
            norm_gain.reshape(-1),
            norm_bias.reshape(-1),
            feedforward_input_bias,
        ]
    )
    small_size = small.shape[0]
    small = jnp.pad(small, (0, -small_size % dmodel))
    slim_parts = [
        groups_of(own_columns(proj_weight, 1), parts),
        groups_of(own_columns(attention_output_weight, 1), parts - 1),
        own_columns(query_key_value_weight, 3).reshape(-1, dmodel),
        small.reshape(-1, dmodel),
    ]
    split = slim_parts[0].shape[0]
    po_rows = split + slim_parts[1].shape[0]
    qkv_rows = slim_parts[2].shape[0]
    slim_all = lax.all_gather(jnp.concatenate(slim_parts, axis=0), "dp", axis=0, tiled=False)
    qkv_own = slim_all[:, po_rows : po_rows + qkv_rows].reshape(dmodel, 3 * width)
    small = slim_all[:, po_rows + qkv_rows :]
    small = small.reshape(slices, -1)[:, :small_size].astype(jnp.float32)
    cuts = [hb, hb + pb, hb + pb + 3 * nd, hb + pb + 6 * nd]
    highway_b, proj_b, gain, shift, inner_b = jnp.split(small, cuts, axis=1)
    highway_b_own = own_columns(highway_b.reshape(1, -1), 2)
    proj_b = proj_b.reshape(-1)
    gain = gain.reshape(slices, 3, nd).transpose(1, 0, 2).reshape(3, dmodel)
    shift = shift.reshape(slices, 3, nd).transpose(1, 0, 2).reshape(3, dmodel)
    inner_b_own = own_columns(inner_b.reshape(1, -1), slices)
    ffn_own = jnp.concatenate(
        [
            own_columns(feedforward_input_weight, slices),
            lax.dynamic_slice_in_dim(feedforward_output_weight, part * unit_rows, unit_rows, 0),
        ],
        axis=0,
    )

    def blocks_of(array):
        return array.astype(jnp.bfloat16).reshape(parts, tokens, -1)

    widths = channel_widths(part * filters + jnp.arange(filters, dtype=jnp.int32))
    ids, table, weight, back, limit, count = conv_prep(
        chars.reshape(words, letters), char_table, conv_weight, conv_bias, widths
    )
    if fast:
        acts, lse, embed, features, highway_own = prologue_call(
            ids, table, weight, limit, count, highway_weight[0], parts, letters, depth, 0
        )
        highway_own = highway_own.reshape(2, -1, filters)
    else:
        acts, lse, embed = conv_forward_call(ids, table, weight, limit, count, letters, depth)
        features = gather_channels_call(acts, parts, 0)
        highway_own = gather_rows(own_columns(highway_weight[0], 2))
        proj_own, out_own = rows_from_columns(slim_all[:, :po_rows])
    ffn_own, features = lax.optimization_barrier((ffn_own, features))
    ffn_all = lax.all_gather(ffn_own, "dp", axis=0, tiled=False)
    base = position.astype(jnp.float32) + proj_b[None, :]
    if fast:
        gates, hidden_low, proj_own, out_own, first, unit_zero, scale_zero, first_all = highway_stage_call(
            slim_all,
            features,
            highway_own,
            highway_b_own,
            acts,
            base,
            gain[0:1],
            shift[0:1],
            attention_output_weight.shape[0] * slices // parts,
            po_rows,
            EPS,
            1,
        )
    else:
        gates = nn_dot(features, highway_own) + highway_b_own
        feature_own = acts.astype(jnp.float32)
        hidden_low = highway_mix(feature_own, gates).astype(jnp.bfloat16)
        first, unit_zero, scale_zero, first_all = forward_stage_call(
            blocks_of(nn_dot(hidden_low, proj_own)), base, gain[0:1], shift[0:1], EPS, 1
        )
    first_all = first_all.reshape(words, dmodel)
    packed = nn_dot(first_all, qkv_own).astype(jnp.bfloat16)
    queries, keys, values = (
        packed[:, block * width : (block + 1) * width].reshape(seqs, full_len, heads, HD)
        for block in range(3)
    )
    key_ok = jnp.arange(full_len, dtype=jnp.int32)[None, :] < lengths[:, None]
    scale = HD ** (-0.5)
    scores = (
        jnp.einsum("sqhd,skhd->shqk", queries, keys, preferred_element_type=jnp.float32) * scale
    )
    scores = jnp.where(key_ok[:, None, None, :], scores, -1e30)
    row_top = jnp.max(scores, axis=-1, keepdims=True)
    log_total = row_top + jnp.log(jnp.sum(jnp.exp(scores - row_top), axis=-1, keepdims=True))
    probs = jnp.exp(scores - log_total)
    probs_low = probs.astype(jnp.bfloat16)
    attended = (
        jnp.einsum("shqk,skhd->sqhd", probs_low, values, preferred_element_type=jnp.float32)
        .astype(jnp.bfloat16)
        .reshape(words, width)
    )
    second, unit_one, scale_one, second_all = forward_stage_call(
        blocks_of(nn_dot(attended, out_own)), first, gain[1:2], shift[1:2], EPS, 2
    )
    second_all = second_all.reshape(words, dmodel)
    ffn_all, second_all = lax.optimization_barrier((ffn_all, second_all))
    inner_own = ffn_all[:, :inner_rows].reshape(dmodel, -1)
    outer_own = ffn_all[:, inner_rows:].reshape(-1, dmodel)
    inner = nn_dot(second_all, inner_own) + inner_b_own
    active = exact_gaussian_activation(inner).astype(jnp.bfloat16)
    top, d_res_two, d_gain_two, d_shift_two, d_outer = top_stage_call(
        blocks_of(nn_dot(active, outer_own)),
        second,
        cotangent.reshape(tokens, dmodel),
        gain[2:3],
        shift[2:3],
        EPS,
        3,
    )
    encoded = top.reshape(seqs, quarter, dmodel)
    d_outer = d_outer.reshape(words, dmodel)
    grad_outer = tn_dot(active, d_outer)
    d_active = nt_dot(d_outer, outer_own)
    d_inner = gelu_back(inner, d_active).astype(jnp.bfloat16)
    grad_inner = tn_dot(second_all, d_inner)
    grad_ffn = jnp.concatenate(
        [item.astype(jnp.bfloat16).reshape(slices, -1, dmodel) for item in (grad_inner, grad_outer)], axis=1
    )
    if fast:
        early = grad_ffn.shape[1] * 2 // 3
        grad_ffn = grad_ffn.reshape(4, 2, -1, dmodel)
        grad_early, grad_late = grad_ffn[:, :, :early], grad_ffn[:, :, early:]
        jobs = ("side",), (grad_early,)
    else:
        jobs = (), ()

    def pair_sum(grad, got):
        keep = lax.dynamic_index_in_dim(grad, slot % 2, 1, keepdims=False)
        return (keep.astype(jnp.float32) + got.astype(jnp.float32)).astype(jnp.bfloat16)

    grad_inner_b = jnp.sum(d_inner.astype(jnp.float32), axis=0)
    d_res_one, d_gain_one, d_shift_one, unused_sum, d_mixed, *got = backward_stage_call(
        blocks_of(nt_dot(d_inner, inner_own)), d_res_two, unit_one, scale_one, gain[1:2], 4, *jobs
    )
    if fast:
        grad_early = pair_sum(grad_early, got[0])
        jobs = ("side", "ring"), (grad_late, grad_early)
    d_mixed = d_mixed.reshape(words, dmodel)
    d_attended = nt_dot(d_mixed, out_own).astype(jnp.bfloat16)
    d_attended = d_attended.reshape(seqs, full_len, heads, HD)
    d_values = jnp.einsum(
        "shqk,sqhd->skhd", probs_low, d_attended, preferred_element_type=jnp.float32
    )
    d_probs = jnp.einsum(
        "sqhd,skhd->shqk", d_attended, values, preferred_element_type=jnp.float32
    )
    row_inner = jnp.sum(d_probs * probs, axis=-1, keepdims=True)
    d_scores = (probs * (d_probs - row_inner)).astype(jnp.bfloat16)
    d_queries = (
        jnp.einsum("shqk,skhd->sqhd", d_scores, keys, preferred_element_type=jnp.float32) * scale
    )
    d_keys = (
        jnp.einsum("shqk,sqhd->skhd", d_scores, queries, preferred_element_type=jnp.float32) * scale
    )
    d_packed = jnp.concatenate(
        [item.reshape(words, width) for item in (d_queries, d_keys, d_values)], axis=1
    ).astype(jnp.bfloat16)
    grad_qkv = tn_dot(first_all, d_packed).astype(jnp.bfloat16)
    d_summed, d_gain_zero, d_shift_zero, grad_proj_b, d_projected, *got = backward_stage_call(
        blocks_of(nt_dot(d_packed, qkv_own)), d_res_one, unit_zero, scale_zero, gain[0:1], 5, *jobs
    )
    if fast:
        grad_late = pair_sum(grad_late, got[0])
        keep = lax.dynamic_index_in_dim(grad_early, slot // 2, 0, keepdims=False)
        grad_early = sum([item.astype(jnp.float32) for item in got[1]], keep.astype(jnp.float32))
        grad_early = grad_early.astype(jnp.bfloat16)
    grad_pos = jnp.sum(d_summed.reshape(seqs, quarter, dmodel), axis=0)
    d_projected = d_projected.reshape(words, dmodel)
    if not fast:
        grad_both = columns_from_rows(tn_dot(hidden_low, d_projected), tn_dot(attended, d_mixed))
        d_hidden = nt_dot(d_projected, proj_own)
        d_in, d_gates = jax.vjp(highway_mix, feature_own, gates)[1](d_hidden)
        d_gates = d_gates.astype(jnp.bfloat16)
        grad_highway = tn_dot(features, d_gates).astype(jnp.bfloat16)
        grad_highway_b = jnp.sum(d_gates.astype(jnp.float32), axis=0)
        d_partial = nt_dot(d_gates, highway_own).astype(jnp.bfloat16)
    groups = table.shape[0] // depth

    def place_columns(own, blocks):
        piece = own.reshape(blocks, 1, -1)
        whole = jnp.zeros((blocks, parts, piece.shape[2]), own.dtype)
        return lax.dynamic_update_slice_in_dim(whole, piece, part, 1).reshape(-1)

    d_gain = jnp.concatenate([d_gain_zero, d_gain_one, d_gain_two])
    d_shift = jnp.concatenate([d_shift_zero, d_shift_one, d_shift_two])
    if fast:
        highway_piece = jnp.zeros((slices, 1, hb), jnp.float32)
    else:
        highway_piece = place_columns(grad_highway_b, 2).reshape(slices, 1, -1)
    pieces = [
        highway_piece,
        grad_proj_b.reshape(slices, 1, -1),
        d_gain.reshape(3, slices, nd).transpose(1, 0, 2),
        d_shift.reshape(3, slices, nd).transpose(1, 0, 2),
        place_columns(grad_inner_b, slices).reshape(slices, 1, -1),
    ]
    if fast:
        few = [jnp.pad(item, ((0, 0), (0, 0), (0, hb - item.shape[2]))) for item in pieces]
        few.append(jnp.zeros((slices, 7, hb), jnp.float32))
        few = jnp.concatenate(few, axis=1)
        wide_all, slim_all, both_all, ffn_all, conv_all, table_all, pos_all, few = epilogue_call(
            d_projected,
            proj_own,
            hidden_low,
            gates,
            acts,
            features,
            highway_own,
            attended,
            d_mixed,
            ids,
            embed,
            lse,
            weight,
            back,
            limit,
            count,
            grad_qkv.reshape(4, 2, -1, 3 * width),
            grad_early,
            grad_late,
            grad_pos.reshape(slices, -1, dmodel),
            few,
            po_rows,
            letters,
            depth,
            groups,
            6,
        )
        outs = assemble_call(
            wide_all,
            slim_all,
            both_all,
            ffn_all,
            conv_all,
            table_all,
            pos_all,
            few,
            widths[None, :],
            inner_rows,
            attention_output_weight.shape[0],
            conv_weight.shape[0],
            char_table.shape[0],
            depth,
            (hb, pb, nd, feedforward_input_bias.shape[0]),
        )
        g_highway, g_qkv, g_proj, g_out, g_inner, g_outer, conv_grad_w, conv_grad_b, g_table, grad_pos = outs[:10]
        g_highway_b, g_proj_b, g_gain, g_shift, g_inner_b = outs[10:]
        conv_grad_b, g_proj_b, g_inner_b = conv_grad_b[0], g_proj_b[0], g_inner_b[0]
    else:
        d_features = scatter_channels_call(d_partial, d_in, 6)
        conv_sums, table_sums = conv_backward_call(
            ids, embed, lse, d_features, weight, back, limit, count, groups, letters, depth
        )
        wide_all = jnp.stack(join_parts(reduce_rows(grad_highway)))
        slim_all = jnp.stack(join_parts(reduce_rows(grad_qkv)))
        both_all = jnp.stack(join_parts(reduce_rows(grad_both)))
        ffn_all = jnp.stack(join_parts(reduce_rows(grad_ffn.reshape(-1, dmodel))))
        table_sums = table_sums.reshape(2, groups * depth, -1).sum(0)
        conv_all = lax.psum(conv_sums, "dp")
        rows = jnp.concatenate([item.reshape(slices, -1) for item in pieces], axis=1)
        table_all, sums = lax.psum((table_sums, rows), ("dp", "filt"))
        grad_pos = lax.psum(grad_pos, "dp")
        own = lax.dynamic_index_in_dim(sums, slot, 0, keepdims=False)
        tap_rows = conv_weight.shape[0]
        tap_keep = (jnp.arange(tap_rows, dtype=jnp.int32) // depth)[:, None] < widths[None, :]
        conv_grad_w = jnp.where(tap_keep, conv_all[:, :tap_rows].T, 0.0)
        conv_grad_b = conv_all[:, tap_rows]
        g_table = table_all.reshape(groups, depth, 128).transpose(0, 2, 1).reshape(-1, depth)
        g_table = g_table[: char_table.shape[0]]
        g_highway_b, g_proj_b, g_gain, g_shift, g_inner_b = jnp.split(own, cuts)

        def join_columns(array, blocks, rows_here):
            array = array.reshape(parts, rows_here, blocks, -1).transpose(1, 2, 0, 3)
            return array.reshape(rows_here, -1).astype(jnp.float32)

        def join_groups(array, many):
            array = array.reshape(parts, array.shape[1], parts, width).transpose(2, 1, 0, 3)
            return array[:many].reshape(-1, dmodel).astype(jnp.float32)

        g_outer = ffn_all[:, inner_rows:].reshape(-1, dmodel).astype(jnp.float32)
        g_inner = join_columns(ffn_all[:, :inner_rows], slices, inner_rows)
        g_qkv = join_columns(slim_all, 3, query_key_value_weight.shape[0])
        g_proj = join_groups(both_all[:, :split], parts)
        g_out = join_groups(both_all[:, split:], parts - 1)
        g_highway = join_columns(wide_all, 2, highway_weight.shape[1])
    return (
        encoded,
        g_table,
        conv_grad_w,
        conv_grad_b,
        g_highway[None],
        g_highway_b.reshape(1, hb),
        g_proj,
        g_proj_b,
        grad_pos,
        g_gain.reshape(3, nd),
        g_shift.reshape(3, nd),
        g_qkv,
        g_out,
        g_inner,
        g_inner_b,
        g_outer,
    )


def solution(mesh):
    return jax.shard_map(
        per_device,
        mesh=mesh,
        in_specs=(
            P("dp", None, None),
            P("dp"),
            P(),
            P(None, "filt"),
            P("filt"),
            P(None, "dp", None),
            P(None, "dp"),
            P("dp", None),
            P("dp"),
            P("filt", None),
            P(None, "dp"),
            P(None, "dp"),
            P("dp", None),
            P("dp", None),
            P("dp", None),
            P("dp"),
            P("dp", None),
            P("dp", "filt", None),
        ),
        out_specs=(
            P("dp", "filt", None),
            P(),
            P(None, "filt"),
            P("filt"),
            P(None, "dp", None),
            P(None, "dp"),
            P("dp", None),
            P("dp"),
            P("filt", None),
            P(None, "dp"),
            P(None, "dp"),
            P("dp", None),
            P("dp", None),
            P("dp", None),
            P("dp"),
            P("dp", None),
        ),
        check_vma=False,
    )
```
